32 devices in a mesh: rep: 4 (over z), shard: 8 (over y, x, core).
Axes of the slice: x: 2, y: 2, z: 4, core: 2. Of those that a mesh axis runs over, the one named last changes fastest.
Arguments:
- tokens: bfloat16 [32, 1024, 512], P(('rep', 'shard')), may hold values from -6 to 6
- step_embed: bfloat16 [32, 512], P(('rep', 'shard')), may hold values from -3 to 3
- lengths: int32 [32], P(('rep', 'shard')), may hold values from 256 to 1024, as said below
- cotangent: bfloat16 [32, 1024, 512], P(('rep', 'shard')), may hold values from -6 to 6
- ln1_gain: bfloat16 [512], P('shard'), may hold values from 0.5 to 1.5
- ln1_bias: bfloat16 [512], P('shard'), may hold values from -1.1953125 to 1.1953125
- qkv_weight: bfloat16 [512, 1536], P('shard'), may hold values from -0.25 to 0.25
- q_bias: bfloat16 [512], P('shard'), may hold values from -1.1953125 to 1.1953125
- v_bias: bfloat16 [512], P('shard'), may hold values from -1.1953125 to 1.1953125
- out_weight: bfloat16 [512, 512], P('shard'), may hold values from -4 to 4
- out_bias: bfloat16 [512], P('shard'), may hold values from -1.1953125 to 1.1953125
- ln2_gain: bfloat16 [512], P('shard'), may hold values from 0.5 to 1.5
- ln2_bias: bfloat16 [512], P('shard'), may hold values from -1.1953125 to 1.1953125
- up_weight: bfloat16 [512, 2048], P('shard'), may hold values from -0.25 to 0.25
- up_bias: bfloat16 [2048], P('shard'), may hold values from -1.1953125 to 1.1953125
- down_weight: bfloat16 [2048, 512], P('shard'), may hold values from -0.25 to 0.25
- down_bias: bfloat16 [512], P('shard'), may hold values from -1.1953125 to 1.1953125
Outputs:
- output: bfloat16 [32, 1024, 512], P(('rep', 'shard'))
- tokens_grad: float32 [32, 1024, 512], P(('rep', 'shard'))
- ln1_gain_grad: float32 [512], P('shard')
- ln1_bias_grad: float32 [512], P('shard')
- qkv_weight_grad: float32 [512, 1536], P('shard')
- q_bias_grad: float32 [512], P('shard')
- v_bias_grad: float32 [512], P('shard')
- out_weight_grad: float32 [512, 512], P('shard')
- out_bias_grad: float32 [512], P('shard')
- ln2_gain_grad: float32 [512], P('shard')
- ln2_bias_grad: float32 [512], P('shard')
- up_weight_grad: float32 [512, 2048], P('shard')
- up_bias_grad: float32 [2048], P('shard')
- down_weight_grad: float32 [2048, 512], P('shard')
- down_bias_grad: float32 [512], P('shard')
The draws below stay inside these ranges and needn't reach their ends.
Inputs may be any that keep to these rules, and one draw needn't show every extreme that they name: Sequence s holds valid characters at slots below lengths[s].
All inputs are finite; a program needn't handle non-finite values.
Results may differ from the reference program's by a relative error of at most 0.01.
Values may be sent and summed in bfloat16 or wider, within the bound.
No kernel may reach another device: no remote copies, remote signals or barrier semaphores. Data moves between devices by JAX's collectives and lax.ppermute only.
A program may use at most 192 MiB of HBM per device.

```python
import math
import jax
import jax.numpy as jnp
from jax import lax

D = 512
HEADS = 8
FF = 2048
HEAD_DIM = 64
L = 1024
SEQS = 32


def draw_lengths(key, part):
    values = jax.random.randint(key, (SEQS,), L // 4, L + 1, dtype=jnp.int32)
    values = values.at[0].set(L)
    values = values.at[1].set(L // 4)
    return values.astype(jnp.int32)


def level_of(key, shape, split, least, high):
    loudness = 1.0
    for position, shards_of in split:
        heights = jax.random.uniform(jax.random.fold_in(jax.random.fold_in(key, 6), position), (shards_of,), jnp.float32, least / len(split), high / len(split))
        loudness = loudness * jnp.repeat(jnp.exp(heights), shape[position] // shards_of).reshape((-1,) + (1,) * (len(shape) - 1 - position))
    return loudness


def scatter_about(rng, shape, deviation, reach, shards=(), kind=jnp.bfloat16):
    factor_of = level_of(rng, shape, shards, -0.22, 0.18) if shards else 1.0
    result = jax.random.normal(rng, shape, jnp.float32) * deviation * factor_of
    return jnp.minimum(jnp.maximum(result, -reach), reach).astype(kind)


def setup_inputs(seed: int = 0) -> dict:
    streams_of = jax.random.split(jax.random.key(seed), 18)
    return {
        "tokens": scatter_about(streams_of[0], (SEQS, L, D), 1.0, 6.0, ((0, 32),)),
        "step_embed": scatter_about(streams_of[1], (SEQS, D), 0.5, 3.0, ((0, 32),)),
        "lengths": draw_lengths(jax.random.fold_in(streams_of[17], 71), 0),
        "cotangent": scatter_about(streams_of[3], (SEQS, L, D), 1.0, 6.0, ((0, 32),)),
        "ln1_gain": jnp.clip(1.0 + 0.1 * jax.random.normal(streams_of[4], (D,), jnp.float32), 0.5, 1.5).astype(jnp.bfloat16),
        "ln1_bias": scatter_about(streams_of[5], (D,), 0.2, 1.1953125, ((0, 8),)),
        "qkv_weight": scatter_about(streams_of[6], (D, 3 * D), D ** -0.5, 0.25, ((0, 8),)),
        "q_bias": scatter_about(streams_of[7], (D,), 0.2, 1.1953125, ((0, 8),)),
        "v_bias": scatter_about(streams_of[8], (D,), 0.2, 1.1953125, ((0, 8),)),
        "out_weight": scatter_about(streams_of[9], (D, D), (max(D // 256, 1)) ** -0.5, 4.0, ((0, 8),)),
        "out_bias": scatter_about(streams_of[10], (D,), 0.2, 1.1953125, ((0, 8),)),
        "ln2_gain": jnp.clip(1.0 + 0.1 * jax.random.normal(streams_of[11], (D,), jnp.float32), 0.5, 1.5).astype(jnp.bfloat16),
        "ln2_bias": scatter_about(streams_of[12], (D,), 0.2, 1.1953125, ((0, 8),)),
        "up_weight": scatter_about(streams_of[13], (D, FF), D ** -0.5, 0.25, ((0, 8),)),
        "up_bias": scatter_about(streams_of[14], (FF,), 0.2, 1.1953125, ((0, 8),)),
        "down_weight": scatter_about(streams_of[15], (FF, D), (FF // 4) ** -0.5, 0.25, ((0, 8),)),
        "down_bias": scatter_about(streams_of[16], (D,), 0.2, 1.1953125, ((0, 8),)),
    }


@jax.custom_vjp
def low(v):
    return lax.optimization_barrier(v.astype(jnp.bfloat16)).astype(jnp.float32)

@jax.custom_vjp
def low_back(v):
    return v

def low_keep(v):
    return (low(v), None)

def low_pass(kept, grad):
    return (grad,)

def back_keep(v):
    return (v, None)

def back_low(kept, grad):
    return (low(grad),)
low.defvjp(low_keep, low_pass)
low_back.defvjp(back_keep, back_low)
epsilon = 1e-05
highest = lax.Precision.HIGHEST

def norm_rows(values, gain_vec, shift_vec):
    center = values - lax.optimization_barrier(jnp.mean(values, axis=-1, keepdims=True))
    spread = lax.optimization_barrier(jnp.mean(center * center, axis=-1, keepdims=True))
    return center * lax.rsqrt(spread + epsilon) * gain_vec + shift_vec

def matmul(left_operand, right_operand):
    return jnp.dot(left_operand, right_operand, precision=highest)

def attend_one(packed):
    query_rows, key_rows, value_rows, key_mask = packed
    score_scale = 1.0 / math.sqrt(HEAD_DIM)
    raw_scores = jnp.einsum('qhd,khd->hqk', query_rows, key_rows, precision=highest) * score_scale
    raw_scores = low_back(raw_scores)
    masked = jnp.where(key_mask[None, None, :], raw_scores, jnp.float32(-1e+30))
    probs = jax.nn.softmax(masked, axis=-1)
    probs_low = low(probs)
    return jnp.einsum('hqk,khd->qhd', probs_low, value_rows, precision=highest)

def reference(tokens, step_embed, lengths, cotangent, ln1_gain, ln1_bias, qkv_weight, q_bias, v_bias, out_weight, out_bias, ln2_gain, ln2_bias, up_weight, up_bias, down_weight, down_bias):
    params = tuple((item.astype(jnp.float32) for item in (ln1_gain, ln1_bias, qkv_weight, q_bias, v_bias, out_weight, out_bias, ln2_gain, ln2_bias, up_weight, up_bias, down_weight, down_bias)))
    positions = jnp.arange(L, dtype=jnp.int32)
    key_mask = positions[None, :] < lengths.astype(jnp.int32)[:, None]
    valid = key_mask.astype(jnp.float32)[..., None]
    embed = step_embed.astype(jnp.float32)
    seq_count = tokens.shape[0]

    def forward(tokens_in, g_one, b_one, query_key_value_matrix, b_query, b_value, output_matrix, b_out, g_two, b_two, up_matrix, b_up, down_matrix, b_down):
        start_x = tokens_in + embed[:, None, :]
        normed_one = low(norm_rows(start_x, g_one, b_one))
        qkv_bias = jnp.concatenate([b_query, jnp.zeros((D,), jnp.float32), b_value])
        qkv_rows = low(low_back(matmul(normed_one, query_key_value_matrix) + qkv_bias))
        query_all = qkv_rows[..., :D].reshape(seq_count, L, HEADS, HEAD_DIM)
        key_all = qkv_rows[..., D:2 * D].reshape(seq_count, L, HEADS, HEAD_DIM)
        value_all = qkv_rows[..., 2 * D:].reshape(seq_count, L, HEADS, HEAD_DIM)
        mixed = lax.map(jax.checkpoint(attend_one), (query_all, key_all, value_all, key_mask))
        mixed = low(low_back(mixed.reshape(seq_count, L, D)))
        attn_out = low_back(matmul(mixed, output_matrix) + b_out)
        middle_x = start_x + attn_out
        normed_two = low(norm_rows(middle_x, g_two, b_two))
        up_rows = low_back(matmul(normed_two, up_matrix) + b_up)
        act_rows = low(jax.nn.gelu(up_rows))
        down_rows = low_back(matmul(act_rows, down_matrix) + b_down)
        return (middle_x + down_rows) * valid
    output, pull = jax.vjp(forward, tokens.astype(jnp.float32), *params)
    grads = pull(cotangent.astype(jnp.float32))
    return (output.astype(jnp.bfloat16), grads[0], grads[1], grads[2], grads[3], grads[4], grads[5], grads[6], grads[7], grads[8], grads[9], grads[10], grads[11], grads[12], grads[13])
```

```python
import functools, math
import jax, jax.numpy as jnp
from jax import lax
from jax.experimental import pallas as pl
from jax.experimental.pallas import tpu as pltpu

f32 = jnp.float32
bf16 = jnp.bfloat16
EPS = 1e-05
HEADS = 8

def dot(a, b):
    return jnp.dot(a, b, preferred_element_type=f32)

def dot_t(a, b):
    return lax.dot_general(a, b, (((1,), (1,)), ((), ())), preferred_element_type=f32)

def cp(n=1, vmem=100):
    return pltpu.CompilerParams(dimension_semantics=("arbitrary",) * n, vmem_limit_bytes=60 * 1024 * 1024)

def norm(x):
    c = x - jnp.mean(x, axis=-1, keepdims=True)
    r = lax.rsqrt(jnp.mean(c * c, axis=-1, keepdims=True) + EPS)
    return c * r, r

def row(v, i):
    return v[i : i + 1, :].astype(f32)

def front_body(scale, tok, step, vec, w, h1t, kv, qkvt):
    D = tok.shape[-1]
    v = vec[...]
    x = tok[...].astype(f32) + step[...].astype(f32)
    n, _ = norm(x)
    h = (n * row(v, 0) + row(v, 1)).astype(bf16)
    h1t[...] = h.T
    for j in range(3):
        y = dot(h, w[:, j * D : (j + 1) * D])
        if j == 0:
            y = y + row(v, 2)
        if j == 2:
            y = y + row(v, 3)
        y = y.astype(bf16)
        if j == 0:
            y = y * bf16(scale)
        else:
            kv[:, (j - 1) * D : j * D] = y
        qkvt[j * D : (j + 1) * D, :] = y.T

def front(tok, step, vec, w, bm=256):
    T, D = tok.shape
    scale = 1.0 / math.sqrt(D // HEADS)
    full = lambda a: pl.BlockSpec(a.shape, lambda i: (0,) * a.ndim)
    return pl.pallas_call(
        functools.partial(front_body, scale),
        grid=(T // bm,),
        in_specs=[pl.BlockSpec((bm, D), lambda i: (i, 0)), full(step), full(vec), full(w)],
        out_specs=[pl.BlockSpec((D, bm), lambda i: (0, i)), pl.BlockSpec((bm, 2 * D), lambda i: (i, 0)), pl.BlockSpec((3 * D, bm), lambda i: (0, i))],
        out_shape=[jax.ShapeDtypeStruct((D, T), bf16), jax.ShapeDtypeStruct((T, 2 * D), bf16), jax.ShapeDtypeStruct((3 * D, T), bf16)],
        compiler_params=cp(), name="front",
    )(tok, step, vec, w)

def attn_fwd_body(HD, ln, k, qt, vt, et, mixed, mixedt, mixedf, linv):
    T = k.shape[0]
    bi = qt.shape[1]
    n = ln[0]
    q = qt[...]
    rid = lax.broadcasted_iota(jnp.int32, q.shape, 0) // HD
    keep = lax.broadcasted_iota(jnp.int32, (T, bi), 0) < n
    outs = []
    for h in range(2):
        s = dot(k[...], jnp.where(rid == h, q, jnp.zeros_like(q)))
        s = jnp.where(keep, s, f32(-1e30))
        m = jnp.max(s, axis=0, keepdims=True)
        e = jnp.exp(s - m).astype(bf16)
        et[h] = e
        va = jnp.concatenate([vt[h * HD : (h + 1) * HD, :], jnp.ones((16, T), bf16)], axis=0)
        o = dot(va, e)
        inv = 1.0 / o[HD : HD + 1, :]
        linv[h : h + 1, :] = inv
        outs.append(o[:HD, :] * inv)
    mt = jnp.concatenate(outs, axis=0)
    mixedf[...] = mt
    mt = mt.astype(bf16)
    mixedt[...] = mt
    mixed[...] = mt.T

def attn_fwd(ln, kv, qkvt, bi=512):
    T = kv.shape[0]
    D = kv.shape[1] // 2
    HD = D // HEADS
    PW = 2 * HD
    NP = D // PW
    return pl.pallas_call(
        functools.partial(attn_fwd_body, HD),
        grid_spec=pltpu.PrefetchScalarGridSpec(
            num_scalar_prefetch=1, grid=(NP, T // bi),
            in_specs=[pl.BlockSpec((T, PW), lambda p, i, r: (0, p)), pl.BlockSpec((PW, bi), lambda p, i, r: (p, i)), pl.BlockSpec((PW, T), lambda p, i, r: (2 * NP + p, 0))],
            out_specs=[pl.BlockSpec((2, T, bi), lambda p, i, r: (p, 0, i)), pl.BlockSpec((bi, PW), lambda p, i, r: (i, p)), pl.BlockSpec((PW, bi), lambda p, i, r: (p, i)), pl.BlockSpec((PW, bi), lambda p, i, r: (p, i)), pl.BlockSpec((None, 8, bi), lambda p, i, r: (p, 0, i))]),
        out_shape=[jax.ShapeDtypeStruct((HEADS, T, T), bf16), jax.ShapeDtypeStruct((T, D), bf16), jax.ShapeDtypeStruct((D, T), bf16), jax.ShapeDtypeStruct((D, T), f32), jax.ShapeDtypeStruct((NP, 8, T), f32)],
        compiler_params=cp(2), name="attn_fwd",
    )(ln, kv, qkvt, qkvt)

G0 = math.sqrt(2 / math.pi)
def ffn_body(ln, tok, step, vec, upb, cot, mixed, wo, wu, wd, out, act, gup, h2t, gx1, gattn, gdt, gmt, sums, upsum):
    i = pl.program_id(0)
    bm, D = tok.shape
    FF = wu.shape[1]
    v = vec[...]
    x1 = tok[...].astype(f32) + step[...].astype(f32) + dot(mixed[...], wo[...]) + row(v, 4)
    n, r = norm(x1)
    h2 = (n * row(v, 5) + row(v, 6)).astype(bf16)
    h2t[...] = h2.T
    live = (lax.broadcasted_iota(jnp.int32, (bm, 1), 0) + i * bm) < ln[0]
    gd = jnp.where(live, cot[...], jnp.zeros_like(cot))
    gdt[...] = gd.T
    acc = x1 + row(v, 7)
    gh = jnp.zeros((bm, D), f32)
    ch = 512
    @pl.when(i == 0)
    def _():
        sums[...] = jnp.zeros_like(sums)
        upsum[...] = jnp.zeros_like(upsum)
    for c in range(FF // ch):
        sl = slice(c * ch, (c + 1) * ch)
        u = dot(h2, wu[:, sl]) + upb[:, sl].astype(f32)
        u2 = u * u
        t = jnp.tanh(f32(G0) * u * (1.0 + f32(0.044715) * u2))
        half = 0.5 * (1.0 + t)
        a = (u * half).astype(bf16)
        act[:, sl] = a
        dg = half + 0.5 * u * (1.0 - t * t) * (f32(G0) * (1.0 + f32(3 * 0.044715) * u2))
        ga = dot_t(gd, wd[sl, :])
        gu = (ga * dg).astype(bf16)
        gup[:, sl] = gu
        upsum[:, sl] += jnp.sum(gu.astype(f32), axis=0, keepdims=True)
        acc = acc + dot(a, wd[sl, :])
        gh = gh + dot_t(gu, wu[:, sl])
    out[...] = jnp.where(live, acc, 0.0).astype(bf16)
    gn = gh * row(v, 5)
    gx = gd.astype(f32) + r * (gn - jnp.mean(gn, axis=-1, keepdims=True) - n * jnp.mean(gn * n, axis=-1, keepdims=True))
    gx1[...] = gx
    gab = gx.astype(bf16)
    gattn[...] = gab
    gmt[...] = dot_t(gab, wo[...]).astype(bf16).T
    s = lambda a: jnp.sum(a.astype(f32), axis=0, keepdims=True)
    sums[...] += jnp.concatenate([s(gab), s(gh * n), s(gh), s(gd), jnp.zeros((4, D), f32)], axis=0)

def ffn(ln, tok, step, vec, upb, cot, mixed, wo, wu, wd, bm=256):
    T, D = tok.shape
    FF = wu.shape[1]
    full = lambda a: pl.BlockSpec(a.shape, lambda i, r: (0,) * a.ndim)
    rows = lambda w: pl.BlockSpec((bm, w), lambda i, r: (i, 0))
    cols = lambda w: pl.BlockSpec((w, bm), lambda i, r: (0, i))
    S = jax.ShapeDtypeStruct
    return pl.pallas_call(
        ffn_body,
        grid_spec=pltpu.PrefetchScalarGridSpec(
            num_scalar_prefetch=1, grid=(T // bm,),
            in_specs=[rows(D), full(step), full(vec), full(upb), rows(D), rows(D), full(wo), full(wu), full(wd)],
            out_specs=[rows(D), rows(FF), rows(FF), cols(D), rows(D), rows(D), cols(D), cols(D), pl.BlockSpec((8, D), lambda i, r: (0, 0)), pl.BlockSpec((1, FF), lambda i, r: (0, 0))]),
        out_shape=[S((T, D), bf16), S((T, FF), bf16), S((T, FF), bf16), S((D, T), bf16), S((T, D), f32), S((T, D), bf16), S((D, T), bf16), S((D, T), bf16), S((8, D), f32), S((1, FF), f32)],
        compiler_params=cp(), name="ffn",
    )(ln, tok, step, vec, upb, cot, mixed, wo, wu, wd)

def mm_body(a, b, o):
    o[...] = dot(a[...], b[...]).astype(o.dtype)

def mm(a, b, bn=512, name="mm"):
    M, K = a.shape
    N = b.shape[1]
    bn = min(bn, N)
    return pl.pallas_call(
        mm_body, grid=(N // bn,),
        in_specs=[pl.BlockSpec((M, K), lambda j: (0, 0)), pl.BlockSpec((K, bn), lambda j: (0, j))],
        out_specs=pl.BlockSpec((M, bn), lambda j: (0, j)),
        out_shape=jax.ShapeDtypeStruct((M, N), bf16), compiler_params=cp(), name=name)(a, b)

def attn_bwd_body(HD, scale, v, kt, qt, gt, mt, linv, et, gq, gk, gv):
    T = v.shape[0]
    rid = lax.broadcasted_iota(jnp.int32, gt.shape, 0) // HD
    g = gt[...].astype(f32)
    for h in range(2):
        hs = slice(h * HD, (h + 1) * HD)
        inv = linv[h : h + 1, :]
        gs = (g * inv).astype(bf16)
        dl = jnp.sum(gs[hs, :].astype(f32) * mt[hs, :], axis=0, keepdims=True)
        dp = dot(v[...], jnp.where(rid == h, gs, jnp.zeros_like(gs)))
        e = et[h]
        ds = (e.astype(f32) * (dp - dl)).astype(bf16)
        gv[hs, :] = dot_t(gs[hs, :], e).astype(bf16)
        gk[hs, :] = dot_t(qt[hs, :], ds).astype(bf16)
        gq[hs, :] = (dot(kt[hs, :], ds) * scale).astype(bf16)

def attn_bwd(kv, qkvt, gmt, mixedt, linv, et):
    T = kv.shape[0]
    D = kv.shape[1] // 2
    HD = D // HEADS
    PW = 2 * HD
    NP = D // PW
    S = jax.ShapeDtypeStruct
    pr = lambda o: pl.BlockSpec((PW, T), lambda p: (o + p, 0))
    return pl.pallas_call(
        functools.partial(attn_bwd_body, HD, 1.0 / math.sqrt(HD)),
        grid=(NP,),
        in_specs=[pl.BlockSpec((T, PW), lambda p: (0, NP + p)), pr(NP), pr(0), pr(0), pr(0), pl.BlockSpec((None, 8, T), lambda p: (p, 0, 0)), pl.BlockSpec((2, T, T), lambda p: (p, 0, 0))],
        out_specs=[pr(0)] * 3,
        out_shape=[S((D, T), bf16)] * 3,
        compiler_params=cp(), name="attn_bwd",
    )(kv, qkvt, qkvt, gmt, mixedt, linv, et)

def wqkv_body(h1t, g, o):
    o[...] = dot_t(h1t[...], g[...])

def wqkv(h1t, g):
    return pl.pallas_call(wqkv_body, grid=(1,),
        in_specs=[pl.BlockSpec(h1t.shape, lambda i: (0, 0)), pl.BlockSpec(g.shape, lambda i: (0, 0))],
        out_specs=pl.BlockSpec((h1t.shape[0], g.shape[0]), lambda i: (0, 0)),
        out_shape=jax.ShapeDtypeStruct((h1t.shape[0], g.shape[0]), f32), compiler_params=cp(), name="wqkv")(h1t, g)

def back_body(tok, step, vec, w, gq, gk, gv, gx1, tg, sums):
    i = pl.program_id(0)
    D = tok.shape[1]
    v = vec[...]
    x = tok[...].astype(f32) + step[...].astype(f32)
    n, r = norm(x)
    gt = dot(w[:, :D], gq[...]) + dot(w[:, D : 2 * D], gk[...]) + dot(w[:, 2 * D :], gv[...])
    gh = gt.T
    gn = gh * row(v, 0)
    tg[...] = gx1[...] + r * (gn - jnp.mean(gn, axis=-1, keepdims=True) - n * jnp.mean(gn * n, axis=-1, keepdims=True))
    @pl.when(i == 0)
    def _():
        sums[...] = jnp.zeros_like(sums)
    s = lambda a: jnp.sum(a, axis=0, keepdims=True)
    sums[...] += jnp.concatenate([s(gh * n), s(gh), jnp.zeros((6, D), f32)], axis=0)

def back(tok, step, vec, w, gq, gk, gv, gx1, bm=256):
    T, D = tok.shape
    full = lambda a: pl.BlockSpec(a.shape, lambda i: (0,) * a.ndim)
    rows = lambda w: pl.BlockSpec((bm, w), lambda i: (i, 0))
    cols = lambda w: pl.BlockSpec((w, bm), lambda i: (0, i))
    S = jax.ShapeDtypeStruct
    return pl.pallas_call(back_body, grid=(T // bm,),
        in_specs=[rows(D), full(step), full(vec), full(w), cols(D), cols(D), cols(D), rows(D)],
        out_specs=[rows(D), pl.BlockSpec((8, D), lambda i: (0, 0))],
        out_shape=[S((T, D), f32), S((8, D), f32)], compiler_params=cp(), name="back")(tok, step, vec, w, gq, gk, gv, gx1)


def layer(tok, step, lens, cot, vec, upb, w_qkv, wo, wu, wd):
    tok = tok[0]
    cot = cot[0]
    D = tok.shape[1]
    h1t, kv, qkvt = front(tok, step, vec, w_qkv)
    et, mixed, mixedt, mixedf, linv = attn_fwd(lens, kv, qkvt)
    out, act, gup, h2t, gx1, gattn, gdt, gmt, sums2, upsum = ffn(lens, tok, step, vec, upb, cot, mixed, wo, wu, wd)
    gwd = mm(gdt, act, name="wdown").T
    gwu = mm(h2t, gup, name="wup")
    gwo = mm(mixedt, gattn, name="wout")
    gq, gk, gv = attn_bwd(kv, qkvt, gmt, mixedf, linv, et)
    h1a = jnp.concatenate([h1t, jnp.ones((16, h1t.shape[1]), bf16)], axis=0)
    ws = [wqkv(h1a, g) for g in (gq, gk, gv)]
    gwq = jnp.concatenate([w[:D] for w in ws], axis=1).astype(bf16)
    tg, sums1 = back(tok, step, vec, w_qkv, gq, gk, gv, gx1)
    small = jnp.stack([sums1[0], sums1[1], ws[0][D], ws[2][D], sums2[0], sums2[1], sums2[2], sums2[3]])
    return out[None], tg[None], gwq, gwo, gwu, gwd, small, upsum[0]


def shards(tokens, step_embed, lengths, cotangent, ln1_gain, ln1_bias, qkv_weight, q_bias, v_bias, out_weight, out_bias, ln2_gain, ln2_bias, up_weight, up_bias, down_weight, down_bias):
    gather = lambda a, ax=0: lax.all_gather(a, "shard", axis=ax, tiled=True)
    vec = gather(jnp.stack([ln1_gain, ln1_bias, q_bias, v_bias, out_bias, ln2_gain, ln2_bias, down_bias]), 1)
    upb = gather(up_bias[None], 1)
    w_qkv, wo, wu, wd = gather(qkv_weight), gather(out_weight), gather(up_weight), gather(down_weight)
    out, tg, gwq, gwo, gwu, gwd, small, upsum = layer(tokens, step_embed, lengths, cotangent, vec, upb, w_qkv, wo, wu, wd)
    scatter = lambda a, ax=0: lax.psum_scatter(a, "shard", scatter_dimension=ax, tiled=True)
    parts = [scatter(a) for a in (gwq, gwo, gwu, gwd)]
    sq, so, su, sd = [a.astype(f32) for a in lax.psum(tuple(parts), "rep")]
    n = lax.axis_size("shard")
    me = lax.axis_index("shard")
    small = lax.psum(small, ("rep", "shard"))
    upsum = lax.psum(upsum, ("rep", "shard"))
    w = small.shape[1] // n
    small = lax.dynamic_slice(small, (0, me * w), (8, w))
    w = upsum.shape[0] // n
    upsum = lax.dynamic_slice(upsum, (me * w,), (w,))
    return out, tg, small[0], small[1], sq, small[2], small[3], so, small[4], small[5], small[6], su, upsum, sd, small[7]


def solution(mesh):
    from jax.sharding import PartitionSpec as P

    in_specs = (
        P(("rep", "shard"), None, None),
        P(("rep", "shard"), None),
        P(("rep", "shard")),
        P(("rep", "shard"), None, None),
        P("shard"),
        P("shard"),
        P("shard", None),
        P("shard"),
        P("shard"),
        P("shard", None),
        P("shard"),
        P("shard"),
        P("shard"),
        P("shard", None),
        P("shard"),
        P("shard", None),
        P("shard"),
    )
    out_specs = (
        P(("rep", "shard"), None, None),
        P(("rep", "shard"), None, None),
        P("shard"),
        P("shard"),
        P("shard", None),
        P("shard"),
        P("shard"),
        P("shard", None),
        P("shard"),
        P("shard"),
        P("shard"),
        P("shard", None),
        P("shard"),
        P("shard", None),
        P("shard"),
    )
    return jax.shard_map(shards, mesh=mesh, in_specs=in_specs, out_specs=out_specs, check_vma=False)
```

```python
import functools, math
import jax, jax.numpy as jnp
from jax import lax
from jax.experimental import pallas as pl
from jax.experimental.pallas import tpu as pltpu

f32 = jnp.float32
bf16 = jnp.bfloat16
EPS = 1e-05
HEADS = 8

def dot(a, b):
    return jnp.dot(a, b, preferred_element_type=f32)

def dot_t(a, b):
    return lax.dot_general(a, b, (((1,), (1,)), ((), ())), preferred_element_type=f32)

def cp(n=1, vmem=100):
    return pltpu.CompilerParams(dimension_semantics=("arbitrary",) * n, vmem_limit_bytes=60 * 1024 * 1024)

def norm(x):
    c = x - jnp.mean(x, axis=-1, keepdims=True)
    r = lax.rsqrt(jnp.mean(c * c, axis=-1, keepdims=True) + EPS)
    return c * r, r

def row(v, i):
    return v[i : i + 1, :].astype(f32)


VROWS = 16
LANES = 128


def xor_perm(n, k):
    return [(i, i ^ k) for i in range(n)]


def rep_perm(x, b):
    return lax.ppermute(x, "rep", xor_perm(lax.axis_size("rep"), b))


def swap(x, k):
    return lax.ppermute(x, "shard", xor_perm(lax.axis_size("shard"), k))


def after(x, *deps):
    return lax.optimization_barrier((x,) + deps)[0]


def gather_pieces(x, n, gate=()):
    R = x.shape[0]
    cut = R // 2 // 16 * 16
    bits = [b for b in (2 << i for i in range(16)) if b < n]
    whole = {0: [(0, x)]}
    halves = {}
    ks = sorted((k for k in range(2, n, 2)), key=lambda k: (bin(k).count("1"), k))
    for k in ks:
        if bin(k).count("1") == 1:
            y = swap(x, k)
            y = after(y, *gate) if gate else y
            whole[k] = [(0, y)]
            halves[k] = (y[:cut], y[cut:])
        else:
            low = k & -k
            high = 1 << (k.bit_length() - 1)
            a = swap(halves[k ^ low][0], low)
            b = swap(halves[k ^ high][1], high)
            whole[k] = [(0, a), (cut, b)]
            halves[k] = (a, b)
    out = []
    for k in [0] + ks:
        for r0, a in whole[k]:
            out.append((k, r0, a))
            out.append((k ^ 1, r0, swap(a, 1)))
    return out


def add16(a, b):
    return (a.astype(f32) + b.astype(f32)).astype(bf16)


def pair_sum(keep, send):
    return add16(keep, swap(send, 1))


def fold(s, n, t, reverse):
    m = (n // 2).bit_length() - 1
    h = s.shape[0] // 2
    return add16(s[:h], swap(s[h:], (2 << t) if reverse else (2 << (m - 1 - t))))


def folds(n):
    return range((n // 2).bit_length() - 1)


def rep_sum(x):
    nr = lax.axis_size("rep")
    if nr == 1:
        return x.astype(f32)
    h = x.shape[0] // 2
    odd = lax.axis_index("rep") % 2
    mine = lax.dynamic_slice_in_dim(x, odd * h, h, 0)
    other = lax.dynamic_slice_in_dim(x, (1 - odd) * h, h, 0)
    s = add16(mine, rep_perm(other, 1))
    b = 2
    while b < nr:
        s = add16(s, rep_perm(s, b))
        b *= 2
    o = rep_perm(s, 1)
    lo = jnp.where(odd == 0, s, o)
    hi = jnp.where(odd == 0, o, s)
    return jnp.concatenate([lo, hi], axis=0).astype(f32)


def vector_block(vecs, upb, n):
    me = lax.axis_index("shard")
    lane = lax.broadcasted_iota(jnp.int32, (1, LANES), 1)
    rows = []
    for v in list(vecs) + [upb]:
        w = v.shape[0]
        if w >= LANES:
            rows.append(v.reshape(w // LANES, LANES))
        else:
            t = LANES // w
            rows.append(jnp.where(lane // w == me % t, jnp.tile(v, t)[None], jnp.zeros((1, LANES), bf16)))
    b = jnp.concatenate(rows, axis=0)
    return jnp.pad(b, ((0, VROWS - b.shape[0]), (0, 0)))


def pull(me, refs, meta, segs, sems):
    copies = []
    for ref, (k, r0) in zip(refs, meta):
        s = jnp.bitwise_xor(me, k)
        r1 = r0 + ref.shape[0]
        for a, c, dst, lanes in segs:
            lo, hi = max(a, r0), min(a + c, r1)
            if lo < hi:
                src = ref.at[pl.ds(lo - r0, hi - lo), pl.ds(0, lanes)]
                copies.append(pltpu.make_async_copy(src, dst(s, lo - a, hi - lo), sems.at[len(copies)]))
    return copies


def mult(x, m):
    return pl.multiple_of(x, m)


def front_body(scale, n, meta, me, tok, step, *refs):
    np_ = len(meta)
    pieces = refs[:np_]
    xht, kv, qkvt, w, vec, upb, vbuf, sems = refs[np_:]
    D = tok.shape[-1]
    r = D // n
    FF = upb.shape[1]

    @pl.when(pl.program_id(0) == 0)
    def _():
        seg = lambda j: (j * r, r, lambda s, o, c: w.at[pl.ds(mult(s * r + o, 16), c), pl.ds(j * D, D)], D)
        segs = [seg(j) for j in range(3)] + [(3 * r, VROWS, lambda s, o, c: vbuf.at[s, pl.ds(o, c)], LANES)]
        cs = pull(me[0], pieces, meta, segs, sems)
        for c in cs:
            c.start()
        for c in cs:
            c.wait()
        per = LANES // r
        tiles = [sum(vbuf[s, 0:8, :].astype(f32) for s in range(t * per, (t + 1) * per)) for t in range(D // LANES)]
        vec[...] = jnp.concatenate(tiles, axis=1)
        wu = FF // n
        if wu >= LANES:
            rows = [vbuf[s, 8 + q : 9 + q, :].astype(f32) for s in range(n) for q in range(wu // LANES)]
        else:
            per = LANES // wu
            rows = [sum(vbuf[s, 8:9, :].astype(f32) for s in range(t * per, (t + 1) * per)) for t in range(FF // LANES)]
        upb[...] = jnp.concatenate(rows, axis=1)

    v = vec[...]
    x = tok[...].astype(f32) + step[...].astype(f32)
    nx, _ = norm(x)
    xht[...] = nx.astype(bf16).T
    h = (nx * row(v, 0) + row(v, 1)).astype(bf16)
    for j in range(3):
        y = dot(h, w[:, j * D : (j + 1) * D])
        if j == 0:
            y = y + row(v, 2)
        if j == 2:
            y = y + row(v, 3)
        y = y.astype(bf16)
        if j == 0:
            y = y * bf16(scale)
        else:
            kv[:, (j - 1) * D : j * D] = y
        qkvt[j * D : (j + 1) * D, :] = y.T


S = jax.ShapeDtypeStruct
ANY = pl.BlockSpec(memory_space=pl.ANY)


def cost(flops, nbytes, tr=0):
    return pl.CostEstimate(flops=int(flops), bytes_accessed=int(nbytes), transcendentals=int(tr))


def front(me, tok, step, pieces, n, FF, bm=256):
    T, D = tok.shape
    scale = 1.0 / math.sqrt(D // HEADS)
    meta = tuple((k, r0) for k, r0, _ in pieces)
    keep = lambda *sh: pl.BlockSpec(sh, lambda i, m: (0,) * len(sh))
    return pl.pallas_call(
        functools.partial(front_body, scale, n, meta),
        grid_spec=pltpu.PrefetchScalarGridSpec(
            num_scalar_prefetch=1, grid=(T // bm,),
            in_specs=[pl.BlockSpec((bm, D), lambda i, m: (i, 0)), keep(1, D)] + [ANY] * len(pieces),
            out_specs=[pl.BlockSpec((D, bm), lambda i, m: (0, i)), pl.BlockSpec((bm, 2 * D), lambda i, m: (i, 0)), pl.BlockSpec((3 * D, bm), lambda i, m: (0, i)), keep(D, 3 * D), keep(8, D), keep(1, FF)],
            scratch_shapes=[pltpu.VMEM((n, VROWS, LANES), bf16), pltpu.SemaphoreType.DMA((8 * len(pieces),))]),
        out_shape=[S((D, T), bf16), S((T, 2 * D), bf16), S((3 * D, T), bf16), S((D, 3 * D), bf16), S((8, D), f32), S((1, FF), f32)],
        compiler_params=cp(), name="front", cost_estimate=cost(6 * T * D * D, 10 * T * D * 2),
    )(me, tok, step, *[a for _, _, a in pieces])


def attn_fwd_body(HD, ln, k, qt, vt, *refs):
    et, mixed, mixedt, mixedf, linv = refs[-5:]
    T = k.shape[0]
    bi = qt.shape[1]
    n = ln[0]
    q = qt[...]
    rid = lax.broadcasted_iota(jnp.int32, q.shape, 0) // HD
    keep = lax.broadcasted_iota(jnp.int32, (T, bi), 0) < n
    outs = []
    for h in range(2):
        s = dot(k[...], jnp.where(rid == h, q, jnp.zeros_like(q)))
        s = jnp.where(keep, s, f32(-1e30))
        m = jnp.max(s, axis=0, keepdims=True)
        e = jnp.exp(s - m).astype(bf16)
        et[h] = e
        va = jnp.concatenate([vt[h * HD : (h + 1) * HD, :], jnp.ones((16, T), bf16)], axis=0)
        o = dot(va, e)
        inv = 1.0 / o[HD : HD + 1, :]
        linv[h : h + 1, :] = inv
        outs.append(o[:HD, :] * inv)
    mt = jnp.concatenate(outs, axis=0)
    mixedf[...] = mt
    mt = mt.astype(bf16)
    mixedt[...] = mt
    mixed[...] = mt.T


def attn_fwd(ln, kv, qkvt, p0, cnt, prev, bi=512):
    T = kv.shape[0]
    D = kv.shape[1] // 2
    HD = D // HEADS
    PW = 2 * HD
    NP = D // PW
    prev = list(prev)
    return pl.pallas_call(
        functools.partial(attn_fwd_body, HD),
        grid_spec=pltpu.PrefetchScalarGridSpec(
            num_scalar_prefetch=1, grid=(cnt, T // bi),
            in_specs=[pl.BlockSpec((T, PW), lambda p, i, r: (0, p0 + p)), pl.BlockSpec((PW, bi), lambda p, i, r: (p0 + p, i)), pl.BlockSpec((PW, T), lambda p, i, r: (2 * NP + p0 + p, 0))] + [ANY] * len(prev),
            out_specs=[pl.BlockSpec((2, T, bi), lambda p, i, r: (p0 + p, 0, i)), pl.BlockSpec((bi, PW), lambda p, i, r: (i, p0 + p)), pl.BlockSpec((PW, bi), lambda p, i, r: (p0 + p, i)), pl.BlockSpec((PW, bi), lambda p, i, r: (p0 + p, i)), pl.BlockSpec((None, 8, bi), lambda p, i, r: (p0 + p, 0, i))]),
        out_shape=[S((HEADS, T, T), bf16), S((T, D), bf16), S((D, T), bf16), S((D, T), f32), S((NP, 8, T), f32)],
        input_output_aliases={4 + i: i for i in range(len(prev))},
        compiler_params=cp(2), name="attn_fwd", cost_estimate=cost(cnt * 2 * 8 * T * T * 128, cnt * 2 * T * T * 2, cnt * 2 * T * T),
    )(ln, kv, qkvt, qkvt, *prev)


G0 = math.sqrt(2 / math.pi)


def ffn_body(n, meta, ln, me, tok, step, vec, upb, cot, mixed, *refs):
    np_ = len(meta)
    pieces = refs[:np_]
    out, act, gup, h2t, gx1, gattn, gdt, gmt, sums, upsum, wo, wu, wd, sems = refs[np_:]
    i = pl.program_id(0)
    bm, D = tok.shape
    FF = wu.shape[1]
    r = D // n
    rf = FF // n

    @pl.when(i == 0)
    def _():
        seg = lambda j: (r + j * r, r, lambda s, o, c: wu.at[pl.ds(mult(s * r + o, 16), c), pl.ds(j * D, D)], D)
        segs = [(0, r, lambda s, o, c: wo.at[pl.ds(mult(s * r + o, 16), c)], D)] + [seg(j) for j in range(FF // D)]
        segs += [(r + r * (FF // D), rf, lambda s, o, c: wd.at[pl.ds(mult(s * rf + o, 16), c)], D)]
        cs = pull(me[0], pieces, meta, segs, sems)
        for c in cs:
            c.start()
        for c in cs:
            c.wait()
        sums[...] = jnp.zeros_like(sums)
        upsum[...] = jnp.zeros_like(upsum)

    v = vec[...]
    x1 = tok[...].astype(f32) + step[...].astype(f32) + dot(mixed[...], wo[...]) + row(v, 4)
    nx, rr = norm(x1)
    h2 = (nx * row(v, 5) + row(v, 6)).astype(bf16)
    h2t[...] = h2.T
    live = (lax.broadcasted_iota(jnp.int32, (bm, 1), 0) + i * bm) < ln[0]
    gd = jnp.where(live, cot[...], jnp.zeros_like(cot))
    gdt[...] = gd.T
    acc = x1 + row(v, 7)
    gh = jnp.zeros((bm, D), f32)
    ch = 512
    for c in range(FF // ch):
        sl = slice(c * ch, (c + 1) * ch)
        u = dot(h2, wu[:, sl]) + upb[:, sl]
        u2 = u * u
        t = jnp.tanh(f32(G0) * u * (1.0 + f32(0.044715) * u2))
        half = 0.5 * (1.0 + t)
        a = (u * half).astype(bf16)
        act[:, sl] = a
        dg = half + 0.5 * u * (1.0 - t * t) * (f32(G0) * (1.0 + f32(3 * 0.044715) * u2))
        ga = dot_t(gd, wd[sl, :])
        gu = (ga * dg).astype(bf16)
        gup[:, sl] = gu
        upsum[:, sl] += jnp.sum(gu.astype(f32), axis=0, keepdims=True)
        acc = acc + dot(a, wd[sl, :])
        gh = gh + dot_t(gu, wu[:, sl])
    out[...] = jnp.where(live, acc, 0.0).astype(bf16)
    gn = gh * row(v, 5)
    gx = gd.astype(f32) + rr * (gn - jnp.mean(gn, axis=-1, keepdims=True) - nx * jnp.mean(gn * nx, axis=-1, keepdims=True))
    gx1[...] = gx
    gab = gx.astype(bf16)
    gattn[...] = gab
    gmt[...] = dot_t(gab, wo[...]).astype(bf16).T
    s = lambda a: jnp.sum(a.astype(f32), axis=0, keepdims=True)
    sums[...] += jnp.concatenate([s(gab), s(gh * nx), s(gh), s(gd), jnp.zeros((4, D), f32)], axis=0)


def ffn(ln, me, tok, step, vec, upb, cot, mixed, pieces, n, bm=256):
    T, D = tok.shape
    FF = upb.shape[1]
    meta = tuple((k, r0) for k, r0, _ in pieces)
    full = lambda a: pl.BlockSpec(a.shape, lambda i, l, m: (0,) * a.ndim)
    rows = lambda w: pl.BlockSpec((bm, w), lambda i, l, m: (i, 0))
    cols = lambda w: pl.BlockSpec((w, bm), lambda i, l, m: (0, i))
    return pl.pallas_call(
        functools.partial(ffn_body, n, meta),
        grid_spec=pltpu.PrefetchScalarGridSpec(
            num_scalar_prefetch=2, grid=(T // bm,),
            in_specs=[rows(D), full(step), full(vec), full(upb), rows(D), rows(D)] + [ANY] * len(pieces),
            out_specs=[rows(D), rows(FF), rows(FF), cols(D), rows(D), rows(D), cols(D), cols(D), pl.BlockSpec((8, D), lambda i, l, m: (0, 0)), pl.BlockSpec((1, FF), lambda i, l, m: (0, 0))],
            scratch_shapes=[pltpu.VMEM((D, D), bf16), pltpu.VMEM((D, FF), bf16), pltpu.VMEM((FF, D), bf16), pltpu.SemaphoreType.DMA((8 * len(pieces),))]),
        out_shape=[S((T, D), bf16), S((T, FF), bf16), S((T, FF), bf16), S((D, T), bf16), S((T, D), f32), S((T, D), bf16), S((D, T), bf16), S((D, T), bf16), S((8, D), f32), S((1, FF), f32)],
        compiler_params=cp(), name="ffn", cost_estimate=cost(2 * T * D * (4 * FF + 2 * D), 8 * T * FF, T * FF),
    )(ln, me, tok, step, vec, upb, cot, mixed, *[a for _, _, a in pieces])


def bit_reverse(x, m):
    y = jnp.zeros_like(x)
    for t in range(m):
        y = y | (((x >> t) & 1) << (m - 1 - t))
    return y


def push(me, n, s, reverse, src, keep, send, row0, sem):
    m = (n // 2).bit_length() - 1
    k = jnp.bitwise_xor(me, s)
    p = k >> 1
    if reverse:
        p = bit_reverse(p, m)
    odd = k & 1
    put = lambda dst: pltpu.make_async_copy(src, dst.at[p, pl.ds(row0, src.shape[0])], sem)

    @pl.when(odd == 0)
    def _():
        put(keep).start()

    @pl.when(odd == 1)
    def _():
        put(send).start()


def wdown_body(n, me, gdt, act, ka, sa, dn, sems):
    j = pl.program_id(0)
    rf = act.shape[1] * dn.shape[0] // n
    per = act.shape[1] // rf
    dn[j] = dot(gdt[...], act[...]).astype(bf16).T
    for t in range(per):
        s = j * per + t
        push(me[0], n, s, False, dn.at[j, pl.ds(t * rf, rf)], ka, sa, 0, sems.at[s])

    @pl.when(j == pl.num_programs(0) - 1)
    def _():
        for s in range(n):
            pltpu.make_async_copy(dn.at[0, pl.ds(0, rf)], ka.at[0], sems.at[s]).wait()


def wdown(me, gdt, act, n):
    D, T = gdt.shape
    FF = act.shape[1]
    nc = FF // D
    A = S((n // 2, FF // n, D), bf16)
    return pl.pallas_call(
        functools.partial(wdown_body, n),
        grid_spec=pltpu.PrefetchScalarGridSpec(
            num_scalar_prefetch=1, grid=(nc,),
            in_specs=[pl.BlockSpec((D, T), lambda j, m: (0, 0)), pl.BlockSpec((T, D), lambda j, m: (0, j))],
            out_specs=[ANY] * 2,
            scratch_shapes=[pltpu.VMEM((nc, D, D), bf16), pltpu.SemaphoreType.DMA((n,))]),
        out_shape=[A, A],
        compiler_params=cp(), name="wdown", cost_estimate=cost(2 * T * D * FF, 4 * T * FF),
    )(me, gdt, act)


def wup_body(n, me, h2t, gup, mixedt, gattn, sums, upsum, kb, sb, up, wo, vr, sems):
    j = pl.program_id(0)
    D = h2t.shape[0]
    nc = up.shape[0]
    r = D // n
    i0 = me[0]
    up[j] = dot(h2t[...], gup[...]).astype(bf16)
    for s in range(n):
        push(i0, n, s, True, up.at[j, pl.ds(s * r, r)], kb, sb, mult(j * r, 16), sems.at[j * n + s])

    @pl.when(j == nc - 1)
    def _():
        wo[...] = dot(mixedt[...], gattn[...]).astype(bf16)
        vr[...] = jnp.concatenate([sums[0:4, :]] + [upsum[:, c * D : (c + 1) * D] for c in range(nc)] + [jnp.zeros((VROWS - 4 - nc, D), f32)], axis=0).astype(bf16)
        b = n * nc
        for s in range(n):
            push(i0, n, s, True, wo.at[pl.ds(s * r, r)], kb, sb, nc * r, sems.at[b + s])
            push(i0, n, s, True, vr, kb, sb, (nc + 1) * r, sems.at[b + n + s])
        for s in range(n):
            for c in range(nc):
                pltpu.make_async_copy(up.at[0, pl.ds(0, r)], kb.at[0, pl.ds(0, r)], sems.at[c * n + s]).wait()
            pltpu.make_async_copy(wo.at[pl.ds(0, r)], kb.at[0, pl.ds(0, r)], sems.at[b + s]).wait()
            pltpu.make_async_copy(vr, kb.at[0, pl.ds(0, VROWS)], sems.at[b + n + s]).wait()


def wup(me, h2t, gup, mixedt, gattn, sums, upsum, n):
    D, T = h2t.shape
    FF = gup.shape[1]
    nc = FF // D
    r = D // n
    full = lambda a: pl.BlockSpec(a.shape, lambda j, m: (0,) * a.ndim)
    B = S((n // 2, (nc + 1) * r + VROWS, D), bf16)
    return pl.pallas_call(
        functools.partial(wup_body, n),
        grid_spec=pltpu.PrefetchScalarGridSpec(
            num_scalar_prefetch=1, grid=(nc,),
            in_specs=[full(h2t), pl.BlockSpec((T, D), lambda j, m: (0, j)), full(mixedt), full(gattn), full(sums), full(upsum)],
            out_specs=[ANY] * 2,
            scratch_shapes=[pltpu.VMEM((nc, D, D), bf16), pltpu.VMEM((D, D), bf16), pltpu.VMEM((VROWS, D), bf16), pltpu.SemaphoreType.DMA((n * (nc + 2),))]),
        out_shape=[B, B],
        compiler_params=cp(), name="wup", cost_estimate=cost(2 * T * D * (FF + D), 4 * T * FF),
    )(me, h2t, gup, mixedt, gattn, sums, upsum)


def attn_bwd_body(HD, scale, v, kt, qt, gt, mt, linv, et, *refs):
    gq = refs[-1]
    T = v.shape[0]
    rid = lax.broadcasted_iota(jnp.int32, gt.shape, 0) // HD
    g = gt[...].astype(f32)
    for h in range(2):
        hs = slice(h * HD, (h + 1) * HD)
        inv = linv[h : h + 1, :]
        gs = (g * inv).astype(bf16)
        dl = jnp.sum(gs[hs, :].astype(f32) * mt[hs, :], axis=0, keepdims=True)
        dp = dot(v[...], jnp.where(rid == h, gs, jnp.zeros_like(gs)))
        e = et[h]
        ds = (e.astype(f32) * (dp - dl)).astype(bf16)
        gq[2, hs, :] = dot_t(gs[hs, :], e).astype(bf16)
        gq[1, hs, :] = dot_t(qt[hs, :], ds).astype(bf16)
        gq[0, hs, :] = (dot(kt[hs, :], ds) * scale).astype(bf16)


def attn_bwd(kv, qkvt, gmt, mixedf, linv, et, p0, cnt, prev):
    T = kv.shape[0]
    D = kv.shape[1] // 2
    HD = D // HEADS
    PW = 2 * HD
    NP = D // PW
    prev = list(prev)
    pr = lambda o: pl.BlockSpec((PW, T), lambda p: (o + p0 + p, 0))
    return pl.pallas_call(
        functools.partial(attn_bwd_body, HD, 1.0 / math.sqrt(HD)),
        grid=(cnt,),
        in_specs=[pl.BlockSpec((T, PW), lambda p: (0, NP + p0 + p)), pr(NP), pr(0), pr(0), pr(0), pl.BlockSpec((None, 8, T), lambda p: (p0 + p, 0, 0)), pl.BlockSpec((2, T, T), lambda p: (p0 + p, 0, 0))] + [ANY] * len(prev),
        out_specs=pl.BlockSpec((3, PW, T), lambda p: (0, p0 + p, 0)),
        out_shape=S((3, D, T), bf16),
        input_output_aliases={7: 0} if prev else {},
        compiler_params=cp(), name="attn_bwd", cost_estimate=cost(cnt * 2 * 16 * T * T * 128, cnt * 2 * T * T * 2),
    )(kv, qkvt, qkvt, gmt, mixedf, linv, et, *prev)


def split_rows(n, D):
    R = 3 * (D // n) + VROWS
    return R // 2 // 16 * 16, R


def wqkv_body(n, cut, me, xht, g, ka, sa, kb, sb, res, vr, sems):
    j = pl.program_id(0)
    D = g.shape[0]
    r = D // n
    i0 = me[0]
    x = jnp.concatenate([xht[...], jnp.ones((16, xht.shape[1]), bf16)], axis=0)
    y = dot_t(x, g[...]).astype(bf16)
    res[j] = y[:D]
    vr[...] = jnp.where(lax.broadcasted_iota(jnp.int32, vr.shape, 0) == j, y[D:], jnp.where(j == 0, jnp.zeros_like(y[D:]), vr[...]))

    def parts(jj):
        a, b = jj * r, jj * r + r
        if b <= cut:
            return [(False, 0, r, a)]
        if a >= cut:
            return [(True, 0, r, a - cut)]
        return [(False, 0, cut - a, a), (True, cut - a, b - cut, 0)]

    def dst(rev):
        return (kb, sb) if rev else (ka, sa)

    for jj in range(3):

        @pl.when(j == jj)
        def _():
            for s in range(n):
                for q, (rev, o, c, d) in enumerate(parts(jj)):
                    push(i0, n, s, rev, res.at[jj, pl.ds(s * r + o, c)], *dst(rev), d, sems.at[(jj * n + s) * 2 + q])

    @pl.when(j == 2)
    def _():
        for s in range(n):
            push(i0, n, s, True, vr, kb, sb, 3 * r - cut, sems.at[6 * n + s])
        for s in range(n):
            for jj in range(3):
                for q, (rev, o, c, d) in enumerate(parts(jj)):
                    pltpu.make_async_copy(res.at[0, pl.ds(0, c)], dst(rev)[0].at[0, pl.ds(0, c)], sems.at[(jj * n + s) * 2 + q]).wait()
            pltpu.make_async_copy(vr, kb.at[0, pl.ds(0, VROWS)], sems.at[6 * n + s]).wait()


def wqkv(me, xht, g, n):
    D, T = xht.shape
    cut, R = split_rows(n, D)
    A = S((n // 2, cut, D), bf16)
    B = S((n // 2, R - cut, D), bf16)
    return pl.pallas_call(
        functools.partial(wqkv_body, n, cut),
        grid_spec=pltpu.PrefetchScalarGridSpec(
            num_scalar_prefetch=1, grid=(3,),
            in_specs=[pl.BlockSpec((D, T), lambda j, m: (0, 0)), pl.BlockSpec((None, D, T), lambda j, m: (j, 0, 0))],
            out_specs=[ANY] * 4,
            scratch_shapes=[pltpu.VMEM((3, D, D), bf16), pltpu.VMEM((VROWS, D), bf16), pltpu.SemaphoreType.DMA((7 * n,))]),
        out_shape=[A, A, B, B],
        compiler_params=cp(), name="wqkv", cost_estimate=cost(6 * T * D * D, 10 * T * D),
    )(me, xht, g)


def back_body(tok, step, vec, w, g, gx1, tg):
    D = tok.shape[1]
    x = tok[...].astype(f32) + step[...].astype(f32)
    nx, rr = norm(x)
    gt = dot(w[:, :D], g[0]) + dot(w[:, D : 2 * D], g[1]) + dot(w[:, 2 * D :], g[2])
    gn = gt.T * row(vec[...], 0)
    tg[...] = gx1[...] + rr * (gn - jnp.mean(gn, axis=-1, keepdims=True) - nx * jnp.mean(gn * nx, axis=-1, keepdims=True))


def back(tok, step, vec, w, g, gx1, bm=256):
    T, D = tok.shape
    full = lambda a: pl.BlockSpec(a.shape, lambda i: (0,) * a.ndim)
    rows = pl.BlockSpec((bm, D), lambda i: (i, 0))
    return pl.pallas_call(
        back_body, grid=(T // bm,),
        in_specs=[rows, full(step), full(vec), full(w), pl.BlockSpec((3, D, bm), lambda i: (0, 0, i)), rows],
        out_specs=rows, out_shape=S((T, D), f32), compiler_params=cp(), name="back", cost_estimate=cost(6 * T * D * D, 14 * T * D),
    )(tok, step, vec, w, g, gx1)


def shards(tokens, step_embed, lengths, cotangent, ln1_gain, ln1_bias, qkv_weight, q_bias, v_bias, out_weight, out_bias, ln2_gain, ln2_bias, up_weight, up_bias, down_weight, down_bias):
    n = lax.axis_size("shard")
    me = lax.axis_index("shard").astype(jnp.int32)
    mes = me[None]
    tok, cot, step = tokens[0], cotangent[0], step_embed
    T, D = tok.shape
    r = D // n
    FF = up_bias.shape[0] * n
    nc = FF // D
    vb = vector_block([ln1_gain, ln1_bias, q_bias, v_bias, out_bias, ln2_gain, ln2_bias, down_bias], up_bias, n)
    cols = lambda a: [a[:, j * D : (j + 1) * D] for j in range(a.shape[1] // D)]
    pack1 = jnp.concatenate(cols(qkv_weight) + [jnp.pad(vb, ((0, 0), (0, D - LANES)))], axis=0)
    pack2 = jnp.concatenate([out_weight] + cols(up_weight) + [down_weight], axis=0)
    pieces1 = gather_pieces(pack1, n)
    xht, kv, qkvt, w, vec, upb = front(mes, tok, step, pieces1, n, FF)
    NP = HEADS // 2
    fw = attn_fwd(lengths, kv, qkvt, 0, NP // 2, [])
    pieces2 = gather_pieces(after(pack2, *[a for _, _, a in pieces1[1:]]), n, (fw[4],))
    et, mixed, mixedt, mixedf, linv = attn_fwd(lengths, kv, qkvt, NP // 2, NP // 2, fw)
    out, act, gup, h2t, gx1, gattn, gdt, gmt, sums, upsum = ffn(lengths, mes, tok, step, vec, upb, cot, mixed, pieces2, n)
    ka, sa = wdown(mes, gdt, act, n)
    kb, sb = wup(mes, after(h2t, ka), gup, mixedt, gattn, sums, upsum, n)
    bwd = lambda p, g, *deps: attn_bwd(kv, qkvt, after(gmt, *deps), mixedf, linv, et, p, 1, g)
    fa = pair_sum(ka, sa)
    g = bwd(0, [], kb, fa)
    fb = pair_sum(kb, sb)
    g = bwd(1, [g], fb)
    g = bwd(2, [g])
    steps = list(folds(n))
    fa = fold(fa, n, steps[0], False)
    g = bwd(3, [g], fa)
    fb = fold(fb, n, steps[0], True)
    for t in steps[1:]:
        fa = fold(fa, n, t, False)
    ka, sa, kb, sb = wqkv(mes, after(xht, fb, fa), g, n)
    for t in steps[1:]:
        fb = fold(fb, n, t, True)
    za = rep_sum(fa[0])
    qa = pair_sum(ka, sa)
    qb = pair_sum(kb, sb)
    tg = back(tok, after(step, qa, qb), vec, w, g, gx1)
    for t in steps:
        qa = fold(qa, n, t, False)
        qb = fold(qb, n, t, True)
    zb = rep_sum(fb[0])
    z2 = rep_sum(jnp.concatenate([qa[0], qb[0]], axis=0))
    rf = FF // n
    g_down = za
    z1 = jnp.concatenate([za, zb], axis=0)
    wide = lambda a, c: jnp.concatenate([a[j * r : (j + 1) * r] for j in range(c)], axis=1)
    g_up = wide(z1[rf:], nc)
    g_out = z1[rf + nc * r : rf + (nc + 1) * r]
    small = z1[rf + (nc + 1) * r :]
    own = lambda a: lax.dynamic_slice(a, (me * r,), (r,))
    g_upb = lax.dynamic_slice(small[4 : 4 + nc].reshape(-1), (me * (FF // n),), (FF // n,))
    m = wide(z2, 3)
    sq = z2[3 * r : 3 * r + 3].reshape(1, 3 * D)
    wf = qkv_weight.astype(f32)
    g_qkv = ln1_gain.astype(f32)[:, None] * m + ln1_bias.astype(f32)[:, None] * sq
    g_g1 = jnp.sum(wf * m, axis=1)
    g_b1 = jnp.sum(wf * sq, axis=1)
    return (out[None], tg[None], g_g1, g_b1, g_qkv, own(z2[3 * r]), own(z2[3 * r + 2]), g_out, own(small[0]), own(small[1]), own(small[2]), g_up, g_upb, g_down, own(small[3]))


def solution(mesh):
    from jax.sharding import PartitionSpec as P

    in_specs = (
        P(("rep", "shard"), None, None),
        P(("rep", "shard"), None),
        P(("rep", "shard")),
        P(("rep", "shard"), None, None),
        P("shard"),
        P("shard"),
        P("shard", None),
        P("shard"),
        P("shard"),
        P("shard", None),
        P("shard"),
        P("shard"),
        P("shard"),
        P("shard", None),
        P("shard"),
        P("shard", None),
        P("shard"),
    )
    out_specs = (
        P(("rep", "shard"), None, None),
        P(("rep", "shard"), None, None),
        P("shard"),
        P("shard"),
        P("shard", None),
        P("shard"),
        P("shard"),
        P("shard", None),
        P("shard"),
        P("shard"),
        P("shard"),
        P("shard", None),
        P("shard"),
        P("shard", None),
        P("shard"),
    )
    return jax.shard_map(shards, mesh=mesh, in_specs=in_specs, out_specs=out_specs, check_vma=False)
```

```python
import functools, math
import jax, jax.numpy as jnp
from jax import lax
from jax.experimental import pallas as pl
from jax.experimental.pallas import tpu as pltpu

f32 = jnp.float32
bf16 = jnp.bfloat16
EPS = 1e-05
HEADS = 8

def dot(a, b):
    return jnp.dot(a, b, preferred_element_type=f32)

def dot_t(a, b):
    return lax.dot_general(a, b, (((1,), (1,)), ((), ())), preferred_element_type=f32)

def cp(n=1, vmem=100):
    return pltpu.CompilerParams(dimension_semantics=("arbitrary",) * n, vmem_limit_bytes=60 * 1024 * 1024)

def norm(x):
    c = x - jnp.mean(x, axis=-1, keepdims=True)
    r = lax.rsqrt(jnp.mean(c * c, axis=-1, keepdims=True) + EPS)
    return c * r, r

def row(v, i):
    return v[i : i + 1, :].astype(f32)


VROWS = 16
LANES = 128


def xor_perm(n, k):
    return [(i, i ^ k) for i in range(n)]


def rep_perm(x, b):
    return lax.ppermute(x, "rep", xor_perm(lax.axis_size("rep"), b))


def swap(x, k):
    return lax.ppermute(x, "shard", xor_perm(lax.axis_size("shard"), k))


def after(x, *deps):
    return lax.optimization_barrier((x,) + deps)[0]


def gather_direct(x, n):
    out = [(0, 0, x)]
    far = [(k, swap(x, k)) for k in range(2, n, 2)]
    out += [(k, 0, y) for k, y in far]
    return out + [(k ^ 1, 0, swap(y, 1)) for k, _, y in out]


def gather_forward(x, n, gate1, gate2):
    R = x.shape[0]
    cut = R // 2 // 16 * 16
    near = []
    far = []
    halves = {}
    for k in sorted(range(2, n, 2), key=lambda k: (bin(k).count("1"), k)):
        if bin(k).count("1") == 1:
            y = after(swap(x, k), gate1)
            near.append((k, 0, y))
            halves[k] = (y[:cut], y[cut:])
        else:
            low = k & -k
            high = 1 << (k.bit_length() - 1)
            a = swap(halves[k ^ low][0], low)
            b = swap(halves[k ^ high][1], high)
            far += [(k, 0, a), (k, cut, b)]
            halves[k] = (a, b)
    near = [(0, 0, x)] + near
    late = [(k, r0, after(a, gate2)) for k, r0, a in far]
    out = near + [(k ^ 1, r0, swap(a, 1)) for k, r0, a in near]
    return out + late + [(k ^ 1, r0, swap(a, 1)) for k, r0, a in late]


def add16(a, b):
    return (a.astype(f32) + b.astype(f32)).astype(bf16)


def spread_sum(parts, *gate):
    got = [swap(parts[k], 2 * k) for k in range(len(parts) - 1, 0, -1)]
    if gate:
        got = [after(a, *gate) for a in got]
    t = parts[0].astype(f32)
    for a in got:
        t = t + a.astype(f32)
    return t.astype(bf16)


def halve(s, top, bit):
    m = s.shape[0] // 2
    keep, out = (s[:m], s[m:]) if top else (s[0::2], s[1::2])
    return keep, swap(out, bit)


def rep_half(x):
    h = x.shape[0] // 2
    odd = lax.axis_index("rep") % 2
    mine = lax.dynamic_slice_in_dim(x, odd * h, h, 0)
    other = lax.dynamic_slice_in_dim(x, (1 - odd) * h, h, 0)
    return mine, rep_perm(other, 1)


def rep_steps():
    nr = lax.axis_size("rep")
    return [b for b in (2 << i for i in range(16)) if b < nr]


def rep_join(s, o):
    odd = lax.axis_index("rep") % 2
    lo = jnp.where(odd == 0, s, o)
    hi = jnp.where(odd == 0, o, s)
    return jnp.concatenate([lo, hi], axis=0).astype(f32)


def vector_block(vecs, upb, n):
    me = lax.axis_index("shard")

    def spot(v):
        w = v.shape[1]
        if w >= LANES:
            return v.reshape(-1, LANES)
        t = LANES // w
        lane = lax.broadcasted_iota(jnp.int32, (v.shape[0], LANES), 1)
        return jnp.where(lane // w == me % t, jnp.concatenate([v] * t, axis=1), jnp.zeros((), bf16))

    b = jnp.concatenate([spot(jnp.stack(vecs)), spot(upb[None])], axis=0)
    return jnp.pad(b, ((0, VROWS - b.shape[0]), (0, 0)))


def pull(me, refs, meta, segs, sems):
    copies = []
    for ref, (k, r0) in zip(refs, meta):
        s = jnp.bitwise_xor(me, k)
        r1 = r0 + ref.shape[0]
        for a, c, dst, lanes in segs:
            lo, hi = max(a, r0), min(a + c, r1)
            if lo < hi:
                src = ref.at[pl.ds(lo - r0, hi - lo), pl.ds(0, lanes)]
                copies.append(pltpu.make_async_copy(src, dst(s, lo - a, hi - lo), sems.at[len(copies)]))
    return copies


def mult(x, m):
    return pl.multiple_of(x, m)


def front_body(scale, n, meta, me, tok, step, *refs):
    np_ = len(meta)
    pieces = refs[:np_]
    xht, kv, qkvt, w, vec, upb, vbuf, sems = refs[np_:]
    D = tok.shape[-1]
    r = D // n
    FF = upb.shape[1]
    first = pl.program_id(0) == 0
    seg = lambda j: (j * r, r, lambda s, o, c: w.at[pl.ds(mult(s * r + o, 16), c), pl.ds(j * D, D)], D)
    segs = [(3 * r, VROWS, lambda s, o, c: vbuf.at[s, pl.ds(o, c)], LANES)] + [seg(j) for j in range(3)]

    @pl.when(first)
    def _():
        for c in pull(me[0], pieces, meta, segs, sems):
            c.start()

    x = tok[...].astype(f32) + step[...].astype(f32)
    nx, _ = norm(x)
    xht[...] = nx.astype(bf16).T

    @pl.when(first)
    def _():
        for c in pull(me[0], pieces, meta, segs, sems):
            c.wait()
        per = LANES // r
        tiles = [sum(vbuf[s, 0:8, :].astype(f32) for s in range(t * per, (t + 1) * per)) for t in range(D // LANES)]
        vec[...] = jnp.concatenate(tiles, axis=1)
        wu = FF // n
        if wu >= LANES:
            rows = [vbuf[s, 8 + q : 9 + q, :].astype(f32) for s in range(n) for q in range(wu // LANES)]
        else:
            per = LANES // wu
            rows = [sum(vbuf[s, 8:9, :].astype(f32) for s in range(t * per, (t + 1) * per)) for t in range(FF // LANES)]
        upb[...] = jnp.concatenate(rows, axis=1)

    v = vec[...]
    h = (nx * row(v, 0) + row(v, 1)).astype(bf16)
    for j in range(3):
        y = dot(h, w[:, j * D : (j + 1) * D])
        if j == 0:
            y = y + row(v, 2)
        if j == 2:
            y = y + row(v, 3)
        y = y.astype(bf16)
        if j == 0:
            y = y * bf16(scale)
        else:
            kv[:, (j - 1) * D : j * D] = y
        qkvt[j * D : (j + 1) * D, :] = y.T


S = jax.ShapeDtypeStruct
ANY = pl.BlockSpec(memory_space=pl.ANY)


def cost(flops, nbytes, tr=0):
    return pl.CostEstimate(flops=int(flops), bytes_accessed=int(nbytes), transcendentals=int(tr))


def front(me, tok, step, pieces, n, FF, bm=512):
    T, D = tok.shape
    scale = 1.0 / math.sqrt(D // HEADS)
    meta = tuple((k, r0) for k, r0, _ in pieces)
    keep = lambda *sh: pl.BlockSpec(sh, lambda i, m: (0,) * len(sh))
    return pl.pallas_call(
        functools.partial(front_body, scale, n, meta),
        grid_spec=pltpu.PrefetchScalarGridSpec(
            num_scalar_prefetch=1, grid=(T // bm,),
            in_specs=[pl.BlockSpec((bm, D), lambda i, m: (i, 0)), keep(1, D)] + [ANY] * len(pieces),
            out_specs=[pl.BlockSpec((D, bm), lambda i, m: (0, i)), pl.BlockSpec((bm, 2 * D), lambda i, m: (i, 0)), pl.BlockSpec((3 * D, bm), lambda i, m: (0, i)), keep(D, 3 * D), keep(8, D), keep(1, FF)],
            scratch_shapes=[pltpu.VMEM((n, VROWS, LANES), bf16), pltpu.SemaphoreType.DMA((8 * len(pieces),))]),
        out_shape=[S((D, T), bf16), S((T, 2 * D), bf16), S((3 * D, T), bf16), S((D, 3 * D), bf16), S((8, D), f32), S((1, FF), f32)],
        compiler_params=cp(), name="front", cost_estimate=cost(6 * T * D * D, 10 * T * D * 2),
    )(me, tok, step, *[a for _, _, a in pieces])


def attn_fwd_body(HD, bi, CR, ln, k, qt, vt, *refs):
    et, mixed, mixedt, mixedf, linv, scr, ka = refs[-7:]
    T, PW = k.shape
    n = ln[0]
    rid = lax.broadcasted_iota(jnp.int32, (PW, bi), 0)
    lane = lax.broadcasted_iota(jnp.int32, (T, PW), 1)
    rows = lax.broadcasted_iota(jnp.int32, (T, PW), 0)
    ka[:, :PW] = k[...]
    ka[:, PW:] = jnp.where((lane == 0) & (rows >= n), f32(-1e30), f32(0)).astype(bf16)
    ones = jnp.where(rid == 0, f32(1), f32(0)).astype(bf16)
    va = [jnp.concatenate([vt[h * HD : (h + 1) * HD, :], jnp.ones((16, T), bf16)], axis=0) for h in range(2)]
    tasks = [(b, h) for b in range(T // bi) for h in range(2)]
    nch = T // CR

    def query(t):
        b, h = tasks[t]
        q = qt[:, b * bi : (b + 1) * bi]
        return jnp.concatenate([jnp.where(rid // HD == h, q, jnp.zeros_like(q)), ones], axis=0)

    def score(t, c, q):
        s = dot(ka[c * CR : (c + 1) * CR, :], q)
        scr[t % 2, c * CR : (c + 1) * CR, :] = s
        return jnp.max(s, axis=0, keepdims=True)

    q = query(0)
    m = functools.reduce(jnp.maximum, [score(0, c, q) for c in range(nch)])
    half = None
    for t, (b, h) in enumerate(tasks):
        sl = slice(b * bi, (b + 1) * bi)
        more = t + 1 < len(tasks)
        if more:
            q = query(t + 1)
        nxt = []
        for c in range(nch):
            cs = slice(c * CR, (c + 1) * CR)
            if more:
                nxt.append(score(t + 1, c, q))
            et[h, cs, sl] = jnp.exp(scr[t % 2, cs, :] - m).astype(bf16)
        o = dot(va[h], et[h, :, sl])
        if more:
            m = functools.reduce(jnp.maximum, nxt)
        inv = 1.0 / o[HD : HD + 1, :]
        linv[h : h + 1, sl] = inv
        o = o[:HD, :] * inv
        if h == 0:
            half = o
        else:
            mt = jnp.concatenate([half, o], axis=0)
            mixedf[:, sl] = mt
            mt = mt.astype(bf16)
            mixedt[:, sl] = mt
            mixed[sl, :] = mt.T


def attn_fwd(ln, kv, qkvt, p0, cnt, prev):
    T = kv.shape[0]
    D = kv.shape[1] // 2
    HD = D // HEADS
    PW = 2 * HD
    NP = D // PW
    bi = min(512, T)
    prev = list(prev)
    return pl.pallas_call(
        functools.partial(attn_fwd_body, HD, bi, min(256, T)),
        grid_spec=pltpu.PrefetchScalarGridSpec(
            num_scalar_prefetch=1, grid=(cnt,),
            in_specs=[pl.BlockSpec((T, PW), lambda p, r: (0, p0 + p)), pl.BlockSpec((PW, T), lambda p, r: (p0 + p, 0)), pl.BlockSpec((PW, T), lambda p, r: (2 * NP + p0 + p, 0))] + [ANY] * len(prev),
            out_specs=[pl.BlockSpec((2, T, T), lambda p, r: (p0 + p, 0, 0)), pl.BlockSpec((T, PW), lambda p, r: (0, p0 + p)), pl.BlockSpec((PW, T), lambda p, r: (p0 + p, 0)), pl.BlockSpec((PW, T), lambda p, r: (p0 + p, 0)), pl.BlockSpec((None, 8, T), lambda p, r: (p0 + p, 0, 0))],
            scratch_shapes=[pltpu.VMEM((2, T, bi), f32), pltpu.VMEM((T, 2 * PW), bf16)]),
        out_shape=[S((HEADS, T, T), bf16), S((T, D), bf16), S((D, T), bf16), S((D, T), f32), S((NP, 8, T), f32)],
        input_output_aliases={4 + i: i for i in range(len(prev))},
        compiler_params=cp(), name="attn_fwd", cost_estimate=cost(cnt * 2 * 8 * T * T * 128, cnt * 2 * T * T * 2, cnt * 2 * T * T),
    )(ln, kv, qkvt, qkvt, *prev)


G0 = math.sqrt(2 / math.pi)


def push(me, n, s, src, keep, send, row0, sem):
    k = jnp.bitwise_xor(me, s)
    p = k >> 1
    put = lambda dst: pltpu.make_async_copy(src, dst.at[p, pl.ds(row0, src.shape[0])], sem)

    @pl.when(k & 1 == 0)
    def _():
        put(keep).start()

    @pl.when(k & 1 == 1)
    def _():
        put(send).start()


def ffn_body(n, meta, ch, ln, me, tok, step, vec, upb, cot, mixed, mixedt, *refs):
    np_ = len(meta)
    pieces = refs[:np_]
    out, gx1, gmt, keep, send, wo, wu, wd, act, gup, h2t, gdt, gattn, sums, upsum, dn, up, gwo, vr, sems, psems = refs[np_:]
    i = pl.program_id(0)
    bm, D = tok.shape
    FF = wu.shape[1]
    r = D // n
    rf = FF // n
    nf = FF // D
    i0 = me[0]
    ro = pl.ds(mult(i * bm, 128), bm)
    first = i == 0
    seg = lambda j: (r + j * r, r, lambda s, o, c: wu.at[pl.ds(mult(s * r + o, 16), c), pl.ds(j * D, D)], D)
    segs = [(0, r, lambda s, o, c: wo.at[pl.ds(mult(s * r + o, 16), c)], D)] + [seg(j) for j in range(nf)]
    segs += [(r + r * nf, rf, lambda s, o, c: wd.at[pl.ds(mult(s * rf + o, 16), c)], D)]

    @pl.when(first)
    def _():
        for c in pull(i0, pieces, meta, segs, sems):
            c.start()
        sums[...] = jnp.zeros_like(sums)
        upsum[...] = jnp.zeros_like(upsum)
        for c in pull(i0, pieces, meta, segs, sems):
            c.wait()

    v = vec[...]
    x1 = tok[...].astype(f32) + step[...].astype(f32) + dot(mixed[...], wo[...]) + row(v, 4)
    nx, rr = norm(x1)
    h2 = (nx * row(v, 5) + row(v, 6)).astype(bf16)
    live = (lax.broadcasted_iota(jnp.int32, (bm, 1), 0) + i * bm) < ln[0]
    gd = jnp.where(live, cot[...], jnp.zeros_like(cot))
    acc = x1 + row(v, 7)
    gh = None
    nc = FF // ch
    sl = [slice(c * ch, (c + 1) * ch) for c in range(nc)]
    lead = lambda c: (dot(h2, wu[:, sl[c]]), dot_t(gd, wd[sl[c], :]))
    nxt = lead(0)
    h2t[:, ro] = h2.T
    gdt[:, ro] = gd.T
    for c in range(nc):
        u, ga = nxt
        nxt = lead(c + 1) if c + 1 < nc else None
        u = u + upb[:, sl[c]]
        u2 = u * u
        t = jnp.tanh(u * (f32(G0) + f32(G0 * 0.044715) * u2))
        half = 0.5 + 0.5 * t
        a = (u * half).astype(bf16)
        act[ro, sl[c]] = a
        dg = half + u * (half * (1.0 - half)) * (f32(2 * G0) + f32(6 * 0.044715 * G0) * u2)
        gu = (ga * dg).astype(bf16)
        gup[ro, sl[c]] = gu
        upsum[:, sl[c]] += jnp.sum(gu.astype(f32), axis=0, keepdims=True)
        acc = acc + dot(a, wd[sl[c], :])
        p = dot_t(gu, wu[:, sl[c]])
        gh = p if gh is None else gh + p
    out[...] = jnp.where(live, acc, 0.0).astype(bf16)
    gn = gh * row(v, 5)
    gx = gd.astype(f32) + rr * (gn - jnp.mean(gn, axis=-1, keepdims=True) - nx * jnp.mean(gn * nx, axis=-1, keepdims=True))
    gx1[...] = gx
    gab = gx.astype(bf16)
    gattn[ro, :] = gab
    gmt[...] = dot_t(gab, wo[...]).astype(bf16).T
    s_ = lambda a: jnp.sum(a.astype(f32), axis=0, keepdims=True)
    sums[...] += jnp.concatenate([s_(gab), s_(gh * nx), s_(gh), s_(gd), jnp.zeros((4, D), f32)], axis=0)

    @pl.when(i == pl.num_programs(0) - 1)
    def _():
        per = D // rf
        o_up, o_out, o_vec = rf, rf + nf * r, rf + (nf + 1) * r
        for j in range(nf):
            dn[j] = dot(gdt[...], act[:, j * D : (j + 1) * D]).astype(bf16).T
            for t in range(per):
                push(i0, n, j * per + t, dn.at[j, pl.ds(t * rf, rf)], keep, send, 0, psems.at[j * per + t])
            up[j] = dot(h2t[...], gup[:, j * D : (j + 1) * D]).astype(bf16)
            for s in range(n):
                push(i0, n, s, up.at[j, pl.ds(s * r, r)], keep, send, o_up + j * r, psems.at[n * (1 + j) + s])
        gwo[...] = dot(mixedt[...], gattn[...]).astype(bf16)
        vr[...] = jnp.concatenate([sums[0:4, :]] + [upsum[:, c * D : (c + 1) * D] for c in range(nf)] + [jnp.zeros((VROWS - 4 - nf, D), f32)], axis=0).astype(bf16)
        b = n * (1 + nf)
        for s in range(n):
            push(i0, n, s, gwo.at[pl.ds(s * r, r)], keep, send, o_out, psems.at[b + s])
            push(i0, n, s, vr, keep, send, o_vec, psems.at[b + n + s])
        done = lambda src, q: pltpu.make_async_copy(src, keep.at[0, pl.ds(0, src.shape[0])], psems.at[q]).wait()
        for s in range(n):
            done(dn.at[0, pl.ds(0, rf)], s)
            for c in range(nf):
                done(up.at[0, pl.ds(0, r)], n * (1 + c) + s)
            done(gwo.at[pl.ds(0, r)], b + s)
            done(vr, b + n + s)


def ffn(ln, me, tok, step, vec, upb, cot, mixed, mixedt, pieces, n):
    T, D = tok.shape
    FF = upb.shape[1]
    bm = min(512, T)
    nf = FF // D
    r = D // n
    meta = tuple((k, r0) for k, r0, _ in pieces)
    full = lambda a: pl.BlockSpec(a.shape, lambda i, l, m: (0,) * a.ndim)
    rows = pl.BlockSpec((bm, D), lambda i, l, m: (i, 0))
    B = S((n // 2, FF // n + (nf + 1) * r + VROWS, D), bf16)
    V = pltpu.VMEM
    return pl.pallas_call(
        functools.partial(ffn_body, n, meta, min(1024, FF)),
        grid_spec=pltpu.PrefetchScalarGridSpec(
            num_scalar_prefetch=2, grid=(T // bm,),
            in_specs=[rows, full(step), full(vec), full(upb), rows, rows, full(mixedt)] + [ANY] * len(pieces),
            out_specs=[rows, rows, pl.BlockSpec((D, bm), lambda i, l, m: (0, i)), ANY, ANY],
            scratch_shapes=[V((D, D), bf16), V((D, FF), bf16), V((FF, D), bf16), V((T, FF), bf16), V((T, FF), bf16), V((D, T), bf16), V((D, T), bf16), V((T, D), bf16), V((8, D), f32), V((1, FF), f32), V((nf, D, D), bf16), V((nf, D, D), bf16), V((D, D), bf16), V((VROWS, D), bf16), pltpu.SemaphoreType.DMA((8 * len(pieces),)), pltpu.SemaphoreType.DMA((n * (nf + 3),))]),
        out_shape=[S((T, D), bf16), S((T, D), f32), S((D, T), bf16), B, B],
        compiler_params=cp(), name="ffn", cost_estimate=cost(2 * T * D * (6 * FF + 3 * D), 16 * T * D, T * FF),
    )(ln, me, tok, step, vec, upb, cot, mixed, mixedt, *[a for _, _, a in pieces])


def attn_bwd_body(HD, scale, CR, v, kt, qt, gt, mt, linv, et, *refs):
    gq, ds = refs[-2:]
    T = v.shape[0]
    rid = lax.broadcasted_iota(jnp.int32, gt.shape, 0) // HD
    g = gt[...].astype(f32)
    q = qt[...]
    gv = gk = None
    for h in range(2):
        hs = slice(h * HD, (h + 1) * HD)
        gs = (g * linv[h : h + 1, :]).astype(bf16)
        gm = jnp.where(rid == h, gs, jnp.zeros_like(gs))
        dl = jnp.sum(gs[hs, :].astype(f32) * mt[hs, :], axis=0, keepdims=True)
        for c in range(T // CR):
            cs = slice(c * CR, (c + 1) * CR)
            ds[h, cs, :] = (et[h, cs, :].astype(f32) * (dot(v[cs, :], gm) - dl)).astype(bf16)
        a = dot(et[h], gm.T)
        b = dot(ds[h], jnp.where(rid == h, q, jnp.zeros_like(q)).T)
        gv = a if gv is None else gv + a
        gk = b if gk is None else gk + b
        gq[0, hs, :] = (dot(kt[hs, :], ds[h]) * scale).astype(bf16)
    gq[2] = gv.astype(bf16).T
    gq[1] = gk.astype(bf16).T


def attn_bwd(kv, qkvt, gmt, mixedf, linv, et, p0, cnt, prev):
    T = kv.shape[0]
    D = kv.shape[1] // 2
    HD = D // HEADS
    PW = 2 * HD
    NP = D // PW
    prev = list(prev)
    pr = lambda o: pl.BlockSpec((PW, T), lambda p: (o + p0 + p, 0))
    return pl.pallas_call(
        functools.partial(attn_bwd_body, HD, 1.0 / math.sqrt(HD), min(256, T)),
        grid=(cnt,),
        scratch_shapes=[pltpu.VMEM((2, T, T), bf16)],
        in_specs=[pl.BlockSpec((T, PW), lambda p: (0, NP + p0 + p)), pr(NP), pr(0), pr(0), pr(0), pl.BlockSpec((None, 8, T), lambda p: (p0 + p, 0, 0)), pl.BlockSpec((2, T, T), lambda p: (p0 + p, 0, 0))] + [ANY] * len(prev),
        out_specs=pl.BlockSpec((3, PW, T), lambda p: (0, p0 + p, 0)),
        out_shape=S((3, D, T), bf16),
        input_output_aliases={7: 0} if prev else {},
        compiler_params=cp(), name="attn_bwd", cost_estimate=cost(cnt * 2 * 16 * T * T * 128, cnt * 2 * T * T * 2),
    )(kv, qkvt, qkvt, gmt, mixedf, linv, et, *prev)


def wqkv_body(n, me, xht, g, keep, send, res, vr, sems):
    j = pl.program_id(0)
    D = g.shape[0]
    r = D // n
    i0 = me[0]
    x = jnp.concatenate([xht[...], jnp.ones((16, xht.shape[1]), bf16)], axis=0)
    y = dot_t(x, g[...]).astype(bf16)
    res[j] = y[:D]
    vr[...] = jnp.where(lax.broadcasted_iota(jnp.int32, vr.shape, 0) == j, y[D:], jnp.where(j == 0, jnp.zeros_like(y[D:]), vr[...]))
    for s in range(n):
        push(i0, n, s, res.at[j, pl.ds(s * r, r)], keep, send, mult(j * r, 16), sems.at[j * n + s])

    @pl.when(j == 2)
    def _():
        for s in range(n):
            push(i0, n, s, vr, keep, send, 3 * r, sems.at[3 * n + s])
        for s in range(n):
            for q in range(3):
                pltpu.make_async_copy(res.at[0, pl.ds(0, r)], keep.at[0, pl.ds(0, r)], sems.at[q * n + s]).wait()
            pltpu.make_async_copy(vr, keep.at[0, pl.ds(0, VROWS)], sems.at[3 * n + s]).wait()


def wqkv(me, xht, g, n):
    D, T = xht.shape
    A = S((n // 2, 3 * (D // n) + VROWS, D), bf16)
    return pl.pallas_call(
        functools.partial(wqkv_body, n),
        grid_spec=pltpu.PrefetchScalarGridSpec(
            num_scalar_prefetch=1, grid=(3,),
            in_specs=[pl.BlockSpec((D, T), lambda j, m: (0, 0)), pl.BlockSpec((None, D, T), lambda j, m: (j, 0, 0))],
            out_specs=[ANY] * 2,
            scratch_shapes=[pltpu.VMEM((3, D, D), bf16), pltpu.VMEM((VROWS, D), bf16), pltpu.SemaphoreType.DMA((4 * n,))]),
        out_shape=[A, A],
        compiler_params=cp(), name="wqkv", cost_estimate=cost(6 * T * D * D, 10 * T * D),
    )(me, xht, g)


def back_body(tok, step, vec, w, g, gx1, tg):
    D = tok.shape[1]
    x = tok[...].astype(f32) + step[...].astype(f32)
    nx, rr = norm(x)
    gt = dot(w[:, :D], g[0]) + dot(w[:, D : 2 * D], g[1]) + dot(w[:, 2 * D :], g[2])
    gn = gt.T * row(vec[...], 0)
    tg[...] = gx1[...] + rr * (gn - jnp.mean(gn, axis=-1, keepdims=True) - nx * jnp.mean(gn * nx, axis=-1, keepdims=True))


def back(tok, step, vec, w, g, gx1, bm=512):
    T, D = tok.shape
    full = lambda a: pl.BlockSpec(a.shape, lambda i: (0,) * a.ndim)
    rows = pl.BlockSpec((bm, D), lambda i: (i, 0))
    return pl.pallas_call(
        back_body, grid=(T // bm,),
        in_specs=[rows, full(step), full(vec), full(w), pl.BlockSpec((3, D, bm), lambda i: (0, 0, i)), rows],
        out_specs=rows, out_shape=S((T, D), f32), compiler_params=cp(), name="back", cost_estimate=cost(6 * T * D * D, 14 * T * D),
    )(tok, step, vec, w, g, gx1)


def shards(tokens, step_embed, lengths, cotangent, ln1_gain, ln1_bias, qkv_weight, q_bias, v_bias, out_weight, out_bias, ln2_gain, ln2_bias, up_weight, up_bias, down_weight, down_bias):
    n = lax.axis_size("shard")
    me = lax.axis_index("shard").astype(jnp.int32)
    mes = me[None]
    tok, cot, step = tokens[0], cotangent[0], step_embed
    T, D = tok.shape
    r = D // n
    FF = up_bias.shape[0] * n
    nc = FF // D
    vb = vector_block([ln1_gain, ln1_bias, q_bias, v_bias, out_bias, ln2_gain, ln2_bias, down_bias], up_bias, n)
    cols = lambda a: [a[:, j * D : (j + 1) * D] for j in range(a.shape[1] // D)]
    pack1 = jnp.concatenate(cols(qkv_weight) + [jnp.pad(vb, ((0, 0), (0, D - LANES)))], axis=0)
    pack2 = jnp.concatenate([out_weight] + cols(up_weight) + [down_weight], axis=0)
    pieces1 = gather_direct(pack1, n)
    xht, kv, qkvt, w, vec, upb = front(mes, tok, step, pieces1, n, FF)
    NP = HEADS // 2
    fw = attn_fwd(lengths, kv, qkvt, 0, NP // 2, [])
    fw2 = attn_fwd(lengths, kv, qkvt, NP // 2, NP // 2, fw)
    et, mixed, mixedt, mixedf, linv = fw2
    pieces2 = gather_forward(after(pack2, *[a for _, _, a in pieces1[1:]]), n, fw[4], linv)
    out, gx1, gmt, keep, send = ffn(lengths, mes, tok, step, vec, upb, cot, mixed, mixedt, pieces2, n)
    bwd = lambda p, c, g, *deps: attn_bwd(kv, qkvt, after(gmt, *deps) if deps else gmt, mixedf, linv, et, p, c, g)
    R = keep.shape[1]
    ra = R // 2 // 8 * 8
    got = swap(send, 1)
    g = bwd(0, 1, [])
    got = after(got, g)
    sa = add16(keep[:, :ra], got[:, :ra])
    sb = add16(keep[:, ra:], got[:, ra:])
    g = bwd(1, NP - 1, [g], sa, sb)
    m = (n // 2).bit_length() - 1
    for t in range(m):
        ka, ga = halve(sa, True, 1 << (m - t))
        kb, gb = halve(sb, False, 2 << t)
        dep = g if t == 0 else keep
        sa = add16(ka, after(ga, dep))
        sb = add16(kb, after(gb, dep))
        if t == 0:
            keep, send = wqkv(mes, after(xht, sa, sb), g, n)
    ua, ub = sa[0], sb[0]
    got = after(swap(send, 1), ua, ub)
    parts = [add16(keep[k], got[k]) for k in range(n // 2)]
    ma, ga = rep_half(ua)
    mb, gb = rep_half(ub)
    tg = back(tok, after(step, ua, ub, *parts), vec, w, g, gx1)
    za = add16(ma, after(ga, tg))
    zb = add16(mb, after(gb, tg))
    own2 = spread_sum(parts, za, zb)
    m2, g2 = rep_half(own2)
    z2 = add16(m2, g2)
    for b in rep_steps():
        za = add16(za, after(rep_perm(za, b), z2))
        zb = add16(zb, rep_perm(zb, b))
        z2 = add16(z2, after(rep_perm(z2, b), za, zb))
    z1 = jnp.concatenate([rep_join(za, rep_perm(za, 1)), rep_join(zb, rep_perm(zb, 1))], axis=0)
    z2 = rep_join(z2, rep_perm(z2, 1))
    rf = FF // n
    g_down = z1[:rf]
    wide = lambda a, c: jnp.concatenate([a[j * r : (j + 1) * r] for j in range(c)], axis=1)
    g_up = wide(z1[rf:], nc)
    g_out = z1[rf + nc * r : rf + (nc + 1) * r]
    small = z1[rf + (nc + 1) * r :]
    own = lambda a: lax.dynamic_slice(a, (me * r,), (r,))
    g_upb = lax.dynamic_slice(small[4 : 4 + nc].reshape(-1), (me * (FF // n),), (FF // n,))
    m = wide(z2, 3)
    sq = z2[3 * r : 3 * r + 3].reshape(1, 3 * D)
    wf = qkv_weight.astype(f32)
    g_qkv = ln1_gain.astype(f32)[:, None] * m + ln1_bias.astype(f32)[:, None] * sq
    g_g1 = jnp.sum(wf * m, axis=1)
    g_b1 = jnp.sum(wf * sq, axis=1)
    return (out[None], tg[None], g_g1, g_b1, g_qkv, own(z2[3 * r]), own(z2[3 * r + 2]), g_out, own(small[0]), own(small[1]), own(small[2]), g_up, g_upb, g_down, own(small[3]))


def solution(mesh):
    from jax.sharding import PartitionSpec as P

    in_specs = (
        P(("rep", "shard"), None, None),
        P(("rep", "shard"), None),
        P(("rep", "shard")),
        P(("rep", "shard"), None, None),
        P("shard"),
        P("shard"),
        P("shard", None),
        P("shard"),
        P("shard"),
        P("shard", None),
        P("shard"),
        P("shard"),
        P("shard"),
        P("shard", None),
        P("shard"),
        P("shard", None),
        P("shard"),
    )
    out_specs = (
        P(("rep", "shard"), None, None),
        P(("rep", "shard"), None, None),
        P("shard"),
        P("shard"),
        P("shard", None),
        P("shard"),
        P("shard"),
        P("shard", None),
        P("shard"),
        P("shard"),
        P("shard"),
        P("shard", None),
        P("shard"),
        P("shard", None),
        P("shard"),
    )
    return jax.shard_map(shards, mesh=mesh, in_specs=in_specs, out_specs=out_specs, check_vma=False)
```

```python
import functools, math
import jax, jax.numpy as jnp
from jax import lax
from jax.experimental import pallas as pl
from jax.experimental.pallas import tpu as pltpu

f32 = jnp.float32
bf16 = jnp.bfloat16
EPS = 1e-05
HEADS = 8

def dot(a, b):
    return jnp.dot(a, b, preferred_element_type=f32)

def dot_t(a, b):
    return lax.dot_general(a, b, (((1,), (1,)), ((), ())), preferred_element_type=f32)

def cp(n=1, vmem=100):
    return pltpu.CompilerParams(dimension_semantics=("arbitrary",) * n, vmem_limit_bytes=60 * 1024 * 1024)

def norm(x):
    c = x - jnp.mean(x, axis=-1, keepdims=True)
    r = lax.rsqrt(jnp.mean(c * c, axis=-1, keepdims=True) + EPS)
    return c * r, r

def row(v, i):
    return v[i : i + 1, :].astype(f32)


VROWS = 16
LANES = 128


def xor_perm(n, k):
    return [(i, i ^ k) for i in range(n)]


def rep_perm(x, b):
    return lax.ppermute(x, "rep", xor_perm(lax.axis_size("rep"), b))


def swap(x, k):
    return lax.ppermute(x, "shard", xor_perm(lax.axis_size("shard"), k))


def after(x, *deps):
    return lax.optimization_barrier((x,) + deps)[0]


def gather_direct(x, n):
    out = [(0, 0, x)]
    far = [(k, swap(x, k)) for k in range(2, n, 2)]
    out += [(k, 0, y) for k, y in far]
    return out + [(k ^ 1, 0, swap(y, 1)) for k, _, y in out]


def gather_forward(x, n, gate1, gate2):
    R = x.shape[0]
    cut = R // 2 // 16 * 16
    near = []
    far = []
    halves = {}
    for k in sorted(range(2, n, 2), key=lambda k: (bin(k).count("1"), k)):
        if bin(k).count("1") == 1:
            y = after(swap(x, k), gate1)
            near.append((k, 0, y))
            halves[k] = (y[:cut], y[cut:])
        else:
            low = k & -k
            high = 1 << (k.bit_length() - 1)
            a = swap(halves[k ^ low][0], low)
            b = swap(halves[k ^ high][1], high)
            far += [(k, 0, a), (k, cut, b)]
            halves[k] = (a, b)
    near = [(0, 0, x)] + near
    late = [(k, r0, after(a, gate2)) for k, r0, a in far]
    out = near + [(k ^ 1, r0, swap(a, 1)) for k, r0, a in near]
    return out + late + [(k ^ 1, r0, swap(a, 1)) for k, r0, a in late]


def add16(a, b):
    return (a.astype(f32) + b.astype(f32)).astype(bf16)


def spread(parts):
    return [swap(parts[k], 2 * k) for k in range(len(parts) - 1, 0, -1)]


def total(own, got):
    t = own.astype(f32)
    for a in got:
        t = t + a.astype(f32)
    return t.astype(bf16)


def rep_half(x):
    h = x.shape[0] // 2
    odd = lax.axis_index("rep") % 2
    mine = lax.dynamic_slice_in_dim(x, odd * h, h, 0)
    other = lax.dynamic_slice_in_dim(x, (1 - odd) * h, h, 0)
    return mine, rep_perm(other, 1), other


def rep_steps():
    nr = lax.axis_size("rep")
    return [b for b in (2 << i for i in range(16)) if b < nr]


def pack_first_body(me, w, upb, *refs):
    vecs = refs[:-1]
    out = refs[-1]
    r, W = w.shape
    D = out.shape[1]
    for j in range(W // D):
        out[j * r : (j + 1) * r, :] = w[:, j * D : (j + 1) * D]

    def spot(v):
        w_ = v.shape[1]
        if w_ >= LANES:
            return [v[:, q * LANES : (q + 1) * LANES] for q in range(w_ // LANES)]
        t = LANES // w_
        lane = lax.broadcasted_iota(jnp.int32, (1, LANES), 1)
        return [jnp.where(lane // w_ == me[0] % t, jnp.concatenate([v] * t, axis=1), jnp.zeros((1, LANES), f32))]

    rows = [a for v in vecs for a in spot(v[...].astype(f32))] + spot(upb[...].astype(f32))
    b = jnp.concatenate(rows + [jnp.zeros((VROWS - len(rows), LANES), f32)], axis=0).astype(bf16)
    out[W // D * r :, :] = jnp.concatenate([b, jnp.zeros((VROWS, D - LANES), bf16)], axis=1)


def whole(n):
    return [pl.BlockSpec(memory_space=pltpu.VMEM)] * n


def pack_first(me, w, vecs, upb, D):
    return pl.pallas_call(
        pack_first_body,
        in_specs=[pl.BlockSpec(memory_space=pltpu.SMEM)] + whole(2 + len(vecs)), out_specs=whole(1)[0],
        out_shape=S((w.size // D + VROWS, D), bf16), compiler_params=pltpu.CompilerParams(vmem_limit_bytes=8 << 20), name="pack_first", cost_estimate=cost(0, 4 * w.size),
    )(me, w, upb[None], *[v[None] for v in vecs])


def pack_rest_body(wo, wu, wd, out):
    r, D = wo.shape
    out[:r, :] = wo[...]
    for j in range(wu.shape[1] // D):
        out[(1 + j) * r : (2 + j) * r, :] = wu[:, j * D : (j + 1) * D]
    out[(1 + wu.shape[1] // D) * r :, :] = wd[...]


def pack_rest(wo, wu, wd):
    D = wo.shape[1]
    return pl.pallas_call(
        pack_rest_body, in_specs=whole(3), out_specs=whole(1)[0],
        out_shape=S(((wo.size + wu.size + wd.size) // D, D), bf16), compiler_params=pltpu.CompilerParams(vmem_limit_bytes=8 << 20), name="pack_rest", cost_estimate=cost(0, 4 * wu.size),
    )(wo, wu, wd)


def own_lanes(tiles, me, w):
    pick = lambda i: sum(jnp.where(i == t, a, jnp.zeros_like(a)) for t, a in enumerate(tiles))
    if w >= LANES:
        q = w // LANES
        return jnp.concatenate([pick(me * q + c) for c in range(q)], axis=1)
    per = LANES // w
    x = pick(me // per)
    off = me % per
    return sum(jnp.where(off == o, x[:, o * w : (o + 1) * w], 0.0) for o in range(per))


def rows_of(lo, hi, a, b):
    h = lo.shape[0]
    if b <= h:
        return lo[a:b, :]
    if a >= h:
        return hi[a - h : b - h, :]
    return jnp.concatenate([lo[a:h, :], hi[: b - h, :]], axis=0)


def finish_rest_body(r, rf, n, ids, sa, oa, sb, ob, down, up, out, upb, *vecs):
    D = out.shape[1]
    nf = up.shape[1] // D

    def run(la, ha, lb, hb):
        f = lambda x, y, a, b: rows_of(x, y, a, b).astype(f32)
        down[...] = f(la, ha, 0, rf)
        out[...] = f(la, ha, rf, rf + r)
        for j in range(nf):
            up[:, j * D : (j + 1) * D] = f(lb, hb, j * r, (j + 1) * r)
        v = f(lb, hb, nf * r, nf * r + VROWS)
        me = ids[0]
        tiles = [v[0:8, t * LANES : (t + 1) * LANES] for t in range(D // LANES)]
        x = own_lanes(tiles, me, r)
        for q, ref in enumerate(vecs):
            ref[...] = x[q : q + 1, :]
        tiles = [v[4 + q : 5 + q, t * LANES : (t + 1) * LANES] for q in range(nf) for t in range(D // LANES)]
        upb[...] = own_lanes(tiles, me, nf * D // n)

    @pl.when(ids[1] == 0)
    def _():
        run(sa, oa, sb, ob)

    @pl.when(ids[1] == 1)
    def _():
        run(oa, sa, ob, sb)


def finish_rest(ids, sa, oa, sb, ob, r, rf, nf, n):
    D = sa.shape[1]
    row1 = lambda w: S((1, w), f32)
    return pl.pallas_call(
        functools.partial(finish_rest_body, r, rf, n),
        in_specs=[pl.BlockSpec(memory_space=pltpu.SMEM)] + whole(4), out_specs=whole(8),
        out_shape=[S((rf, D), f32), S((r, nf * D), f32), S((r, D), f32), row1(nf * D // n)] + [row1(r)] * 4,
        compiler_params=pltpu.CompilerParams(vmem_limit_bytes=16 << 20), name="finish_rest", cost_estimate=cost(0, 8 * sa.size),
    )(ids, sa, oa, sb, ob)


def finish_first_body(ids, s, o, w, gain, bias, qkv, gg, gb, qb, vb):
    r, W = w.shape
    D = s.shape[1]

    def run(lo, hi):
        f = lambda a, b: rows_of(lo, hi, a, b).astype(f32)
        v = f(3 * r, 3 * r + VROWS)
        nt = D // LANES
        accg = accb = jnp.zeros((r, LANES), f32)
        col = lambda g: jnp.concatenate([g[...].astype(f32), jnp.zeros((7, r), f32)], axis=0).T[:, 0:1]
        cg, cb = col(gain), col(bias)
        for j in range(3):
            m = f(j * r, (j + 1) * r)
            sq = v[j : j + 1, :]
            ww = w[:, j * D : (j + 1) * D].astype(f32)
            qkv[:, j * D : (j + 1) * D] = cg * m + cb * sq
            pg, pb = ww * m, ww * sq
            accg = accg + sum(pg[:, t * LANES : (t + 1) * LANES] for t in range(nt))
            accb = accb + sum(pb[:, t * LANES : (t + 1) * LANES] for t in range(nt))
        gg[...] = jnp.sum(accg.T, axis=0, keepdims=True)
        gb[...] = jnp.sum(accb.T, axis=0, keepdims=True)
        x = own_lanes([v[0:8, t * LANES : (t + 1) * LANES] for t in range(nt)], ids[0], r)
        qb[...] = x[0:1, :]
        vb[...] = x[2:3, :]

    @pl.when(ids[1] == 0)
    def _():
        run(s, o)

    @pl.when(ids[1] == 1)
    def _():
        run(o, s)


def finish_first(ids, s, o, w, gain, bias):
    r, W = w.shape
    return pl.pallas_call(
        finish_first_body,
        in_specs=[pl.BlockSpec(memory_space=pltpu.SMEM)] + whole(5), out_specs=whole(5),
        out_shape=[S((r, W), f32)] + [S((1, r), f32)] * 4,
        compiler_params=pltpu.CompilerParams(vmem_limit_bytes=16 << 20), name="finish_first", cost_estimate=cost(0, 8 * w.size),
    )(ids, s, o, w, gain[None], bias[None])


def pull(me, refs, meta, segs, sems):
    copies = []
    for ref, (k, r0) in zip(refs, meta):
        s = jnp.bitwise_xor(me, k)
        r1 = r0 + ref.shape[0]
        for a, c, dst, lanes in segs:
            lo, hi = max(a, r0), min(a + c, r1)
            if lo < hi:
                src = ref.at[pl.ds(lo - r0, hi - lo), pl.ds(0, lanes)]
                copies.append(pltpu.make_async_copy(src, dst(s, lo - a, hi - lo), sems.at[len(copies)]))
    return copies


def mult(x, m):
    return pl.multiple_of(x, m)


def front_body(scale, n, meta, me, tok, step, *refs):
    np_ = len(meta)
    pieces = refs[:np_]
    xht, kv, qkvt, w, vec, upb, vbuf, sems = refs[np_:]
    D = tok.shape[-1]
    r = D // n
    FF = upb.shape[1]
    first = pl.program_id(0) == 0
    seg = lambda j: (j * r, r, lambda s, o, c: w.at[pl.ds(mult(s * r + o, 16), c), pl.ds(j * D, D)], D)
    segs = [(3 * r, VROWS, lambda s, o, c: vbuf.at[s, pl.ds(o, c)], LANES)] + [seg(j) for j in range(3)]

    @pl.when(first)
    def _():
        for c in pull(me[0], pieces, meta, segs, sems):
            c.start()

    x = tok[...].astype(f32) + step[...].astype(f32)
    nx, _ = norm(x)
    xht[...] = nx.astype(bf16).T

    @pl.when(first)
    def _():
        for c in pull(me[0], pieces, meta, segs, sems):
            c.wait()
        per = LANES // r
        tiles = [sum(vbuf[s, 0:8, :].astype(f32) for s in range(t * per, (t + 1) * per)) for t in range(D // LANES)]
        vec[...] = jnp.concatenate(tiles, axis=1)
        wu = FF // n
        if wu >= LANES:
            rows = [vbuf[s, 8 + q : 9 + q, :].astype(f32) for s in range(n) for q in range(wu // LANES)]
        else:
            per = LANES // wu
            rows = [sum(vbuf[s, 8:9, :].astype(f32) for s in range(t * per, (t + 1) * per)) for t in range(FF // LANES)]
        upb[...] = jnp.concatenate(rows, axis=1)

    v = vec[...]
    h = (nx * row(v, 0) + row(v, 1)).astype(bf16)
    for j in range(3):
        y = dot(h, w[:, j * D : (j + 1) * D])
        if j == 0:
            y = y + row(v, 2)
        if j == 2:
            y = y + row(v, 3)
        y = y.astype(bf16)
        if j == 0:
            y = y * bf16(scale)
        else:
            kv[:, (j - 1) * D : j * D] = y
        qkvt[j * D : (j + 1) * D, :] = y.T


S = jax.ShapeDtypeStruct
ANY = pl.BlockSpec(memory_space=pl.ANY)


def cost(flops, nbytes, tr=0):
    return pl.CostEstimate(flops=int(flops), bytes_accessed=int(nbytes), transcendentals=int(tr))


def front(me, tok, step, pieces, n, FF, bm=512):
    T, D = tok.shape
    scale = 1.0 / math.sqrt(D // HEADS)
    meta = tuple((k, r0) for k, r0, _ in pieces)
    keep = lambda *sh: pl.BlockSpec(sh, lambda i, m: (0,) * len(sh))
    return pl.pallas_call(
        functools.partial(front_body, scale, n, meta),
        grid_spec=pltpu.PrefetchScalarGridSpec(
            num_scalar_prefetch=1, grid=(T // bm,),
            in_specs=[pl.BlockSpec((bm, D), lambda i, m: (i, 0)), keep(1, D)] + [ANY] * len(pieces),
            out_specs=[pl.BlockSpec((D, bm), lambda i, m: (0, i)), pl.BlockSpec((bm, 2 * D), lambda i, m: (i, 0)), pl.BlockSpec((3 * D, bm), lambda i, m: (0, i)), keep(D, 3 * D), keep(8, D), keep(1, FF)],
            scratch_shapes=[pltpu.VMEM((n, VROWS, LANES), bf16), pltpu.SemaphoreType.DMA((8 * len(pieces),))]),
        out_shape=[S((D, T), bf16), S((T, 2 * D), bf16), S((3 * D, T), bf16), S((D, 3 * D), bf16), S((8, D), f32), S((1, FF), f32)],
        compiler_params=cp(), name="front", cost_estimate=cost(6 * T * D * D, 10 * T * D * 2),
    )(me, tok, step, *[a for _, _, a in pieces])


def attn_fwd_body(HD, bi, CR, ln, k, qt, vt, *refs):
    et, mixed, mixedt, mixedf, linv, scr, ka = refs[-7:]
    T, PW = k.shape
    n = ln[0]
    rid = lax.broadcasted_iota(jnp.int32, (PW, bi), 0)
    lane = lax.broadcasted_iota(jnp.int32, (T, PW), 1)
    rows = lax.broadcasted_iota(jnp.int32, (T, PW), 0)
    ka[:, :PW] = k[...]
    ka[:, PW:] = jnp.where((lane == 0) & (rows >= n), f32(-1e30), f32(0)).astype(bf16)
    ones = jnp.where(rid == 0, f32(1), f32(0)).astype(bf16)
    va = [jnp.concatenate([vt[h * HD : (h + 1) * HD, :], jnp.ones((16, T), bf16)], axis=0) for h in range(2)]
    tasks = [(b, h) for b in range(T // bi) for h in range(2)]
    nch = T // CR

    def query(t):
        b, h = tasks[t]
        q = qt[:, b * bi : (b + 1) * bi]
        return jnp.concatenate([jnp.where(rid // HD == h, q, jnp.zeros_like(q)), ones], axis=0)

    def score(t, c, q):
        s = dot(ka[c * CR : (c + 1) * CR, :], q)
        scr[t % 2, c * CR : (c + 1) * CR, :] = s
        return jnp.max(s, axis=0, keepdims=True)

    q = query(0)
    m = functools.reduce(jnp.maximum, [score(0, c, q) for c in range(nch)])
    half = None
    for t, (b, h) in enumerate(tasks):
        sl = slice(b * bi, (b + 1) * bi)
        more = t + 1 < len(tasks)
        if more:
            q = query(t + 1)
        nxt = []
        for c in range(nch):
            cs = slice(c * CR, (c + 1) * CR)
            if more:
                nxt.append(score(t + 1, c, q))
            et[h, cs, sl] = jnp.exp(scr[t % 2, cs, :] - m).astype(bf16)
        o = dot(va[h], et[h, :, sl])
        if more:
            m = functools.reduce(jnp.maximum, nxt)
        inv = 1.0 / o[HD : HD + 1, :]
        linv[h : h + 1, sl] = inv
        o = o[:HD, :] * inv
        if h == 0:
            half = o
        else:
            mt = jnp.concatenate([half, o], axis=0)
            mixedf[:, sl] = mt
            mt = mt.astype(bf16)
            mixedt[:, sl] = mt
            mixed[sl, :] = mt.T


def attn_fwd(ln, kv, qkvt, p0, cnt, prev):
    T = kv.shape[0]
    D = kv.shape[1] // 2
    HD = D // HEADS
    PW = 2 * HD
    NP = D // PW
    bi = min(512, T)
    prev = list(prev)
    return pl.pallas_call(
        functools.partial(attn_fwd_body, HD, bi, min(256, T)),
        grid_spec=pltpu.PrefetchScalarGridSpec(
            num_scalar_prefetch=1, grid=(cnt,),
            in_specs=[pl.BlockSpec((T, PW), lambda p, r: (0, p0 + p)), pl.BlockSpec((PW, T), lambda p, r: (p0 + p, 0)), pl.BlockSpec((PW, T), lambda p, r: (2 * NP + p0 + p, 0))] + [ANY] * len(prev),
            out_specs=[pl.BlockSpec((2, T, T), lambda p, r: (p0 + p, 0, 0)), pl.BlockSpec((T, PW), lambda p, r: (0, p0 + p)), pl.BlockSpec((PW, T), lambda p, r: (p0 + p, 0)), pl.BlockSpec((PW, T), lambda p, r: (p0 + p, 0)), pl.BlockSpec((None, 8, T), lambda p, r: (p0 + p, 0, 0))],
            scratch_shapes=[pltpu.VMEM((2, T, bi), f32), pltpu.VMEM((T, 2 * PW), bf16)]),
        out_shape=[S((HEADS, T, T), bf16), S((T, D), bf16), S((D, T), bf16), S((D, T), f32), S((NP, 8, T), f32)],
        input_output_aliases={4 + i: i for i in range(len(prev))},
        compiler_params=cp(), name="attn_fwd", cost_estimate=cost(cnt * 2 * 8 * T * T * 128, cnt * 2 * T * T * 2, cnt * 2 * T * T),
    )(ln, kv, qkvt, qkvt, *prev)


G0 = math.sqrt(2 / math.pi)


def bit_reverse(x, m):
    y = jnp.zeros_like(x)
    for t in range(m):
        y = y | (((x >> t) & 1) << (m - 1 - t))
    return y


def push(me, n, s, src, keep, send, row0, sem, reverse=False):
    k = jnp.bitwise_xor(me, s)
    p = k >> 1
    if reverse:
        p = bit_reverse(p, (n // 2).bit_length() - 1)
    put = lambda dst: pltpu.make_async_copy(src, dst.at[p, pl.ds(row0, src.shape[0])], sem)

    @pl.when(k & 1 == 0)
    def _():
        put(keep).start()

    @pl.when(k & 1 == 1)
    def _():
        put(send).start()


def ffn_body(n, meta, ch, ln, me, tok, step, vec, upb, cot, mixed, mixedt, *refs):
    np_ = len(meta)
    pieces = refs[:np_]
    out, gx1, gmt, keep, send, wo, wu, wd, act, gup, h2t, gdt, gattn, sums, upsum, dn, up, gwo, vr, sems, psems = refs[np_:]
    i = pl.program_id(0)
    bm, D = tok.shape
    FF = wu.shape[1]
    r = D // n
    rf = FF // n
    nf = FF // D
    i0 = me[0]
    ro = pl.ds(mult(i * bm, 128), bm)
    first = i == 0
    seg = lambda j: (r + j * r, r, lambda s, o, c: wu.at[pl.ds(mult(s * r + o, 16), c), pl.ds(j * D, D)], D)
    segs = [(0, r, lambda s, o, c: wo.at[pl.ds(mult(s * r + o, 16), c)], D)] + [seg(j) for j in range(nf)]
    segs += [(r + r * nf, rf, lambda s, o, c: wd.at[pl.ds(mult(s * rf + o, 16), c)], D)]

    @pl.when(first)
    def _():
        for c in pull(i0, pieces, meta, segs, sems):
            c.start()
        sums[...] = jnp.zeros_like(sums)
        upsum[...] = jnp.zeros_like(upsum)
        for c in pull(i0, pieces, meta, segs, sems):
            c.wait()

    v = vec[...]
    x1 = tok[...].astype(f32) + step[...].astype(f32) + dot(mixed[...], wo[...]) + row(v, 4)
    nx, rr = norm(x1)
    h2 = (nx * row(v, 5) + row(v, 6)).astype(bf16)
    live = (lax.broadcasted_iota(jnp.int32, (bm, 1), 0) + i * bm) < ln[0]
    gd = jnp.where(live, cot[...], jnp.zeros_like(cot))
    acc = x1 + row(v, 7)
    gh = None
    nc = FF // ch
    sl = [slice(c * ch, (c + 1) * ch) for c in range(nc)]
    lead = lambda c: (dot(h2, wu[:, sl[c]]), dot_t(gd, wd[sl[c], :]))
    nxt = lead(0)
    h2t[:, ro] = h2.T
    gdt[:, ro] = gd.T
    for c in range(nc):
        u, ga = nxt
        nxt = lead(c + 1) if c + 1 < nc else None
        u = u + upb[:, sl[c]]
        u2 = u * u
        t = jnp.tanh(u * (f32(G0) + f32(G0 * 0.044715) * u2))
        half = 0.5 + 0.5 * t
        a = (u * half).astype(bf16)
        act[ro, sl[c]] = a
        dg = half + u * (half * (1.0 - half)) * (f32(2 * G0) + f32(6 * 0.044715 * G0) * u2)
        gu = (ga * dg).astype(bf16)
        gup[ro, sl[c]] = gu
        upsum[:, sl[c]] += jnp.sum(gu.astype(f32), axis=0, keepdims=True)
        acc = acc + dot(a, wd[sl[c], :])
        p = dot_t(gu, wu[:, sl[c]])
        gh = p if gh is None else gh + p
    out[...] = jnp.where(live, acc, 0.0).astype(bf16)
    gn = gh * row(v, 5)
    gx = gd.astype(f32) + rr * (gn - jnp.mean(gn, axis=-1, keepdims=True) - nx * jnp.mean(gn * nx, axis=-1, keepdims=True))
    gx1[...] = gx
    gab = gx.astype(bf16)
    gattn[ro, :] = gab
    gmt[...] = dot_t(gab, wo[...]).astype(bf16).T
    s_ = lambda a: jnp.sum(a.astype(f32), axis=0, keepdims=True)
    sums[...] += jnp.concatenate([s_(gab), s_(gh * nx), s_(gh), s_(gd), jnp.zeros((4, D), f32)], axis=0)

    @pl.when(i == pl.num_programs(0) - 1)
    def _():
        per = D // rf
        o_out, o_up, o_vec = rf, rf + r, rf + (nf + 1) * r
        for j in range(nf):
            dn[j] = dot(gdt[...], act[:, j * D : (j + 1) * D]).astype(bf16).T
            for t in range(per):
                push(i0, n, j * per + t, dn.at[j, pl.ds(t * rf, rf)], keep, send, 0, psems.at[j * per + t])
            up[j] = dot(h2t[...], gup[:, j * D : (j + 1) * D]).astype(bf16)
            for s in range(n):
                push(i0, n, s, up.at[j, pl.ds(s * r, r)], keep, send, o_up + j * r, psems.at[n * (1 + j) + s], True)
        gwo[...] = dot(mixedt[...], gattn[...]).astype(bf16)
        vr[...] = jnp.concatenate([sums[0:4, :]] + [upsum[:, c * D : (c + 1) * D] for c in range(nf)] + [jnp.zeros((VROWS - 4 - nf, D), f32)], axis=0).astype(bf16)
        b = n * (1 + nf)
        for s in range(n):
            push(i0, n, s, gwo.at[pl.ds(s * r, r)], keep, send, o_out, psems.at[b + s])
            push(i0, n, s, vr, keep, send, o_vec, psems.at[b + n + s], True)
        done = lambda src, q: pltpu.make_async_copy(src, keep.at[0, pl.ds(0, src.shape[0])], psems.at[q]).wait()
        for s in range(n):
            done(dn.at[0, pl.ds(0, rf)], s)
            for c in range(nf):
                done(up.at[0, pl.ds(0, r)], n * (1 + c) + s)
            done(gwo.at[pl.ds(0, r)], b + s)
            done(vr, b + n + s)


def ffn(ln, me, tok, step, vec, upb, cot, mixed, mixedt, pieces, n):
    T, D = tok.shape
    FF = upb.shape[1]
    bm = min(512, T)
    nf = FF // D
    r = D // n
    meta = tuple((k, r0) for k, r0, _ in pieces)
    full = lambda a: pl.BlockSpec(a.shape, lambda i, l, m: (0,) * a.ndim)
    rows = pl.BlockSpec((bm, D), lambda i, l, m: (i, 0))
    B = S((n // 2, FF // n + (nf + 1) * r + VROWS, D), bf16)
    V = pltpu.VMEM
    return pl.pallas_call(
        functools.partial(ffn_body, n, meta, min(1024, FF)),
        grid_spec=pltpu.PrefetchScalarGridSpec(
            num_scalar_prefetch=2, grid=(T // bm,),
            in_specs=[rows, full(step), full(vec), full(upb), rows, rows, full(mixedt)] + [ANY] * len(pieces),
            out_specs=[rows, rows, pl.BlockSpec((D, bm), lambda i, l, m: (0, i)), ANY, ANY],
            scratch_shapes=[V((D, D), bf16), V((D, FF), bf16), V((FF, D), bf16), V((T, FF), bf16), V((T, FF), bf16), V((D, T), bf16), V((D, T), bf16), V((T, D), bf16), V((8, D), f32), V((1, FF), f32), V((nf, D, D), bf16), V((nf, D, D), bf16), V((D, D), bf16), V((VROWS, D), bf16), pltpu.SemaphoreType.DMA((8 * len(pieces),)), pltpu.SemaphoreType.DMA((n * (nf + 3),))]),
        out_shape=[S((T, D), bf16), S((T, D), f32), S((D, T), bf16), B, B],
        compiler_params=cp(), name="ffn", cost_estimate=cost(2 * T * D * (6 * FF + 3 * D), 16 * T * D, T * FF),
    )(ln, me, tok, step, vec, upb, cot, mixed, mixedt, *[a for _, _, a in pieces])


def attn_bwd_body(HD, scale, CR, v, kt, qt, gt, mt, linv, et, *refs):
    gq, ds = refs[-2:]
    T = v.shape[0]
    rid = lax.broadcasted_iota(jnp.int32, gt.shape, 0) // HD
    g = gt[...].astype(f32)
    q = qt[...]
    gv = gk = None
    for h in range(2):
        hs = slice(h * HD, (h + 1) * HD)
        gs = (g * linv[h : h + 1, :]).astype(bf16)
        gm = jnp.where(rid == h, gs, jnp.zeros_like(gs))
        dl = jnp.sum(gs[hs, :].astype(f32) * mt[hs, :], axis=0, keepdims=True)
        for c in range(T // CR):
            cs = slice(c * CR, (c + 1) * CR)
            ds[h, cs, :] = (et[h, cs, :].astype(f32) * (dot(v[cs, :], gm) - dl)).astype(bf16)
        a = dot(et[h], gm.T)
        b = dot(ds[h], jnp.where(rid == h, q, jnp.zeros_like(q)).T)
        gv = a if gv is None else gv + a
        gk = b if gk is None else gk + b
        gq[0, hs, :] = (dot(kt[hs, :], ds[h]) * scale).astype(bf16)
    gq[2] = gv.astype(bf16).T
    gq[1] = gk.astype(bf16).T


def attn_bwd(kv, qkvt, gmt, mixedf, linv, et, p0, cnt, prev):
    T = kv.shape[0]
    D = kv.shape[1] // 2
    HD = D // HEADS
    PW = 2 * HD
    NP = D // PW
    prev = list(prev)
    pr = lambda o: pl.BlockSpec((PW, T), lambda p: (o + p0 + p, 0))
    return pl.pallas_call(
        functools.partial(attn_bwd_body, HD, 1.0 / math.sqrt(HD), min(256, T)),
        grid=(cnt,),
        scratch_shapes=[pltpu.VMEM((2, T, T), bf16)],
        in_specs=[pl.BlockSpec((T, PW), lambda p: (0, NP + p0 + p)), pr(NP), pr(0), pr(0), pr(0), pl.BlockSpec((None, 8, T), lambda p: (p0 + p, 0, 0)), pl.BlockSpec((2, T, T), lambda p: (p0 + p, 0, 0))] + [ANY] * len(prev),
        out_specs=pl.BlockSpec((3, PW, T), lambda p: (0, p0 + p, 0)),
        out_shape=S((3, D, T), bf16),
        input_output_aliases={7: 0} if prev else {},
        compiler_params=cp(), name="attn_bwd", cost_estimate=cost(cnt * 2 * 16 * T * T * 128, cnt * 2 * T * T * 2),
    )(kv, qkvt, qkvt, gmt, mixedf, linv, et, *prev)


def wqkv_body(n, me, xht, g, keep, send, res, vr, sems):
    j = pl.program_id(0)
    D = g.shape[0]
    r = D // n
    i0 = me[0]
    x = jnp.concatenate([xht[...], jnp.ones((16, xht.shape[1]), bf16)], axis=0)
    y = dot_t(x, g[...]).astype(bf16)
    res[j] = y[:D]
    vr[...] = jnp.where(lax.broadcasted_iota(jnp.int32, vr.shape, 0) == j, y[D:], jnp.where(j == 0, jnp.zeros_like(y[D:]), vr[...]))
    for s in range(n):
        push(i0, n, s, res.at[j, pl.ds(s * r, r)], keep, send, mult(j * r, 16), sems.at[j * n + s])

    @pl.when(j == 2)
    def _():
        for s in range(n):
            push(i0, n, s, vr, keep, send, 3 * r, sems.at[3 * n + s])
        for s in range(n):
            for q in range(3):
                pltpu.make_async_copy(res.at[0, pl.ds(0, r)], keep.at[0, pl.ds(0, r)], sems.at[q * n + s]).wait()
            pltpu.make_async_copy(vr, keep.at[0, pl.ds(0, VROWS)], sems.at[3 * n + s]).wait()


def wqkv(me, xht, g, n):
    D, T = xht.shape
    A = S((n // 2, 3 * (D // n) + VROWS, D), bf16)
    return pl.pallas_call(
        functools.partial(wqkv_body, n),
        grid_spec=pltpu.PrefetchScalarGridSpec(
            num_scalar_prefetch=1, grid=(3,),
            in_specs=[pl.BlockSpec((D, T), lambda j, m: (0, 0)), pl.BlockSpec((None, D, T), lambda j, m: (j, 0, 0))],
            out_specs=[ANY] * 2,
            scratch_shapes=[pltpu.VMEM((3, D, D), bf16), pltpu.VMEM((VROWS, D), bf16), pltpu.SemaphoreType.DMA((4 * n,))]),
        out_shape=[A, A],
        compiler_params=cp(), name="wqkv", cost_estimate=cost(6 * T * D * D, 10 * T * D),
    )(me, xht, g)


def back_body(tok, step, vec, w, g, gx1, tg):
    D = tok.shape[1]
    x = tok[...].astype(f32) + step[...].astype(f32)
    nx, rr = norm(x)
    gt = dot(w[:, :D], g[0]) + dot(w[:, D : 2 * D], g[1]) + dot(w[:, 2 * D :], g[2])
    gn = gt.T * row(vec[...], 0)
    tg[...] = gx1[...] + rr * (gn - jnp.mean(gn, axis=-1, keepdims=True) - nx * jnp.mean(gn * nx, axis=-1, keepdims=True))


def back(tok, step, vec, w, g, gx1, bm=512):
    T, D = tok.shape
    full = lambda a: pl.BlockSpec(a.shape, lambda i: (0,) * a.ndim)
    rows = pl.BlockSpec((bm, D), lambda i: (i, 0))
    return pl.pallas_call(
        back_body, grid=(T // bm,),
        in_specs=[rows, full(step), full(vec), full(w), pl.BlockSpec((3, D, bm), lambda i: (0, 0, i)), rows],
        out_specs=rows, out_shape=S((T, D), f32), compiler_params=cp(), name="back", cost_estimate=cost(6 * T * D * D, 14 * T * D),
    )(tok, step, vec, w, g, gx1)


def shards(tokens, step_embed, lengths, cotangent, ln1_gain, ln1_bias, qkv_weight, q_bias, v_bias, out_weight, out_bias, ln2_gain, ln2_bias, up_weight, up_bias, down_weight, down_bias):
    n = lax.axis_size("shard")
    me = lax.axis_index("shard").astype(jnp.int32)
    mes = me[None]
    tok, cot, step = tokens[0], cotangent[0], step_embed
    T, D = tok.shape
    r = D // n
    FF = up_bias.shape[0] * n
    nc = FF // D
    rf = FF // n
    pack1 = pack_first(mes, qkv_weight, [ln1_gain, ln1_bias, q_bias, v_bias, out_bias, ln2_gain, ln2_bias, down_bias], up_bias, D)
    pack2 = pack_rest(out_weight, up_weight, down_weight)
    pieces1 = gather_direct(pack1, n)
    xht, kv, qkvt, w, vec, upb = front(mes, tok, step, pieces1, n, FF)
    NP = HEADS // 2
    fw = attn_fwd(lengths, kv, qkvt, 0, NP // 2, [])
    fw2 = attn_fwd(lengths, kv, qkvt, NP // 2, NP // 2, fw)
    et, mixed, mixedt, mixedf, linv = fw2
    pieces2 = gather_forward(after(pack2, *[a for _, _, a in pieces1[1:]]), n, fw[4], linv)
    out, gx1, gmt, keep, send = ffn(lengths, mes, tok, step, vec, upb, cot, mixed, mixedt, pieces2, n)
    bwd = lambda p, c, g, *deps: attn_bwd(kv, qkvt, after(gmt, *deps) if deps else gmt, mixedf, linv, et, p, c, g)
    ra = rf + r
    got = swap(send, 1)
    g = bwd(0, 1, [])
    got = after(got, g)
    h = n // 4
    add = lambda a, b, k: add16(a[k], b[k])
    rows_a, rows_b = slice(0, ra), slice(ra, None)
    lo, hi = slice(0, h), slice(h, None)
    ka, xa, kb, xb = [add(keep, got, k) for k in ((lo, rows_a), (hi, rows_a), (lo, rows_b), (hi, rows_b))]
    g = bwd(1, NP - 1, [g], ka, xa, kb, xb)
    m = (n // 2).bit_length() - 1
    ga, gb = swap(xa, 2 << (m - 1)), swap(xb, 2)
    for t in range(1, m):
        dep = g if t == 1 else keep
        ga, gb = after(ga, dep), after(gb, dep)
        h //= 2
        lo, hi = slice(0, h), slice(h, None)
        ka, xa = add(ka, ga, lo), add(ka, ga, hi)
        kb, xb = add(kb, gb, lo), add(kb, gb, hi)
        ga, gb = swap(xa, 2 << (m - 1 - t)), swap(xb, 2 << t)
        if t == 1:
            keep, send = wqkv(mes, after(xht, ka, xa, kb, xb), g, n)
    got = swap(send, 1)
    p2 = [add16(keep[k], got[k]) for k in range(n // 2)]
    far2 = spread(p2)
    ua = add16(ka, after(ga, keep))[0]
    ub = add16(kb, after(gb, keep))[0]
    ma, oa, xa = rep_half(ua)
    mb, ob, xb = rep_half(ub)
    tg = back(tok, after(step, xa, xb), vec, w, g, gx1)
    za = add16(ma, after(oa, tg))
    zb = add16(mb, after(ob, tg))
    own2 = total(p2[0], [after(a, za, zb) for a in far2])
    m2, o2, _ = rep_half(own2)
    z2 = add16(m2, o2)
    for b in rep_steps():
        pa, pb = rep_perm(za, b), rep_perm(zb, b)
        za = add16(za, after(pa, z2))
        z2 = add16(z2, after(rep_perm(z2, b), za))
        zb = add16(zb, after(pb, z2))
    oa, ob, o2 = rep_perm(za, 1), rep_perm(zb, 1), rep_perm(z2, 1)
    ids = jnp.stack([me, (lax.axis_index("rep") % 2).astype(jnp.int32)])
    g_qkv, g_g1, g_b1, g_q, g_v = finish_first(ids, z2, o2, qkv_weight, ln1_gain, ln1_bias)
    g_down, g_up, g_out, g_upb, g_ob, g_g2, g_b2, g_db = finish_rest(ids, za, oa, zb, ob, r, rf, nc, n)
    flat = lambda a: a.reshape(-1)
    return (out[None], tg[None], flat(g_g1), flat(g_b1), g_qkv, flat(g_q), flat(g_v), g_out, flat(g_ob), flat(g_g2), flat(g_b2), g_up, flat(g_upb), g_down, flat(g_db))


def solution(mesh):
    from jax.sharding import PartitionSpec as P

    in_specs = (
        P(("rep", "shard"), None, None),
        P(("rep", "shard"), None),
        P(("rep", "shard")),
        P(("rep", "shard"), None, None),
        P("shard"),
        P("shard"),
        P("shard", None),
        P("shard"),
        P("shard"),
        P("shard", None),
        P("shard"),
        P("shard"),
        P("shard"),
        P("shard", None),
        P("shard"),
        P("shard", None),
        P("shard"),
    )
    out_specs = (
        P(("rep", "shard"), None, None),
        P(("rep", "shard"), None, None),
        P("shard"),
        P("shard"),
        P("shard", None),
        P("shard"),
        P("shard"),
        P("shard", None),
        P("shard"),
        P("shard"),
        P("shard"),
        P("shard", None),
        P("shard"),
        P("shard", None),
        P("shard"),
    )
    return jax.shard_map(shards, mesh=mesh, in_specs=in_specs, out_specs=out_specs, check_vma=False)
```

```python
import functools, math
import jax, jax.numpy as jnp
from jax import lax
from jax.experimental import pallas as pl
from jax.experimental.pallas import tpu as pltpu

f32 = jnp.float32
bf16 = jnp.bfloat16
EPS = 1e-05
HEADS = 8

def dot(a, b):
    return jnp.dot(a, b, preferred_element_type=f32)

def dot_t(a, b):
    return lax.dot_general(a, b, (((1,), (1,)), ((), ())), preferred_element_type=f32)

def cp(n=1, vmem=100):
    return pltpu.CompilerParams(dimension_semantics=("arbitrary",) * n, vmem_limit_bytes=60 * 1024 * 1024)

def norm(x):
    c = x - jnp.mean(x, axis=-1, keepdims=True)
    r = lax.rsqrt(jnp.mean(c * c, axis=-1, keepdims=True) + EPS)
    return c * r, r

def row(v, i):
    return v[i : i + 1, :].astype(f32)


VROWS = 16
LANES = 128


def xor_perm(n, k):
    return [(i, i ^ k) for i in range(n)]


def rep_perm(x, b):
    return lax.ppermute(x, "rep", xor_perm(lax.axis_size("rep"), b))


def swap(x, k):
    return lax.ppermute(x, "shard", xor_perm(lax.axis_size("shard"), k))


def after(x, *deps):
    return lax.optimization_barrier((x,) + deps)[0]


def gather_direct(x, n, *gate):
    out = [(0, 0, x)]
    far = [(k, swap(x, k)) for k in range(2, n, 2)]
    out += [(k, 0, after(y, *gate) if gate else y) for k, y in far]
    return out + [(k ^ 1, 0, swap(y, 1)) for k, _, y in out]


def gather_forward(x, n, gate1, gate2):
    R = x.shape[0]
    cut = R // 2 // 16 * 16
    near = []
    far = []
    halves = {}
    for k in sorted(range(2, n, 2), key=lambda k: (bin(k).count("1"), k)):
        if bin(k).count("1") == 1:
            y = after(swap(x, k), gate1)
            near.append((k, 0, y))
            halves[k] = (y[:cut], y[cut:])
        else:
            low = k & -k
            high = 1 << (k.bit_length() - 1)
            a = swap(halves[k ^ low][0], low)
            b = swap(halves[k ^ high][1], high)
            far += [(k, 0, a), (k, cut, b)]
            halves[k] = (a, b)
    near = [(0, 0, x)] + near
    late = [(k, r0, after(a, gate2)) for k, r0, a in far]
    out = near + [(k ^ 1, r0, swap(a, 1)) for k, r0, a in near]
    return out + late + [(k ^ 1, r0, swap(a, 1)) for k, r0, a in late]


def add16(a, b):
    return (a.astype(f32) + b.astype(f32)).astype(bf16)


def spread(parts):
    return [swap(parts[k], 2 * k) for k in range(len(parts) - 1, 0, -1)]


def total(own, got):
    t = own.astype(f32)
    for a in got:
        t = t + a.astype(f32)
    return t.astype(bf16)


def rep_half(x):
    h = x.shape[0] // 2
    odd = lax.axis_index("rep") % 2
    mine = lax.dynamic_slice_in_dim(x, odd * h, h, 0)
    other = lax.dynamic_slice_in_dim(x, (1 - odd) * h, h, 0)
    return mine, rep_perm(other, 1), other


def rep_steps():
    nr = lax.axis_size("rep")
    return [b for b in (2 << i for i in range(16)) if b < nr]


GROUPS = 2


def pack_first_body(me, w, upb, *refs):
    vecs = refs[:-GROUPS]
    outs = refs[-GROUPS:]
    r, W = w.shape
    D = W // 3
    gw = D // GROUPS
    for g, out in enumerate(outs):
        for j in range(3):
            out[j * r : (j + 1) * r, :] = w[:, j * D + g * gw : j * D + (g + 1) * gw]

    def spot(v):
        w_ = v.shape[1]
        if w_ >= LANES:
            return [v[:, q * LANES : (q + 1) * LANES] for q in range(w_ // LANES)]
        t = LANES // w_
        lane = lax.broadcasted_iota(jnp.int32, (1, LANES), 1)
        return [jnp.where(lane // w_ == me[0] % t, jnp.concatenate([v] * t, axis=1), jnp.zeros((1, LANES), f32))]

    rows = [a for v in vecs for a in spot(v[...].astype(f32))] + spot(upb[...].astype(f32))
    b = jnp.concatenate(rows + [jnp.zeros((VROWS - len(rows), LANES), f32)], axis=0).astype(bf16)
    outs[0][3 * r :, :] = jnp.concatenate([b, jnp.zeros((VROWS, gw - LANES), bf16)], axis=1)


def whole(n):
    return [pl.BlockSpec(memory_space=pltpu.VMEM)] * n


def once(*arrays):
    return [pl.BlockSpec(a.shape, lambda i, *m, nd=len(a.shape): (0,) * nd) for a in arrays]


def pack_first(me, w, vecs, upb):
    r, W = w.shape
    gw = W // 3 // GROUPS
    args = [w, upb[None]] + [v[None] for v in vecs]
    outs = [S((3 * r + (VROWS if g == 0 else 0), gw), bf16) for g in range(GROUPS)]
    return pl.pallas_call(
        pack_first_body,
        grid_spec=pltpu.PrefetchScalarGridSpec(num_scalar_prefetch=1, grid=(1,), in_specs=once(*args), out_specs=once(*outs)),
        out_shape=outs, compiler_params=pltpu.CompilerParams(vmem_limit_bytes=8 << 20), name="pack_first", cost_estimate=cost(0, 4 * w.size),
    )(me, *args)


def pack_rest_body(wo, wu, wd, out):
    r, D = wo.shape
    out[:r, :] = wo[...]
    for j in range(wu.shape[1] // D):
        out[(1 + j) * r : (2 + j) * r, :] = wu[:, j * D : (j + 1) * D]
    out[(1 + wu.shape[1] // D) * r :, :] = wd[...]


def pack_rest(wo, wu, wd):
    D = wo.shape[1]
    out = S(((wo.size + wu.size + wd.size) // D, D), bf16)
    return pl.pallas_call(
        pack_rest_body, grid=(1,), in_specs=once(wo, wu, wd), out_specs=once(out)[0],
        out_shape=out, compiler_params=pltpu.CompilerParams(vmem_limit_bytes=8 << 20), name="pack_rest", cost_estimate=cost(0, 4 * wu.size),
    )(wo, wu, wd)


def own_lanes(tiles, me, w):
    pick = lambda i: sum(jnp.where(i == t, a, jnp.zeros_like(a)) for t, a in enumerate(tiles))
    if w >= LANES:
        q = w // LANES
        return jnp.concatenate([pick(me * q + c) for c in range(q)], axis=1)
    per = LANES // w
    x = pick(me // per)
    off = me % per
    return sum(jnp.where(off == o, x[:, o * w : (o + 1) * w], 0.0) for o in range(per))


def rows_of(lo, hi, a, b):
    h = lo.shape[0]
    if b <= h:
        return lo[a:b, :]
    if a >= h:
        return hi[a - h : b - h, :]
    return jnp.concatenate([lo[a:h, :], hi[: b - h, :]], axis=0)


def finish_rest_body(r, rf, n, ids, sa, oa, sb, ob, down, up, out, upb, *vecs):
    D = out.shape[1]
    nf = up.shape[1] // D

    def run(la, ha, lb, hb):
        f = lambda x, y, a, b: rows_of(x, y, a, b).astype(f32)
        down[...] = f(la, ha, 0, rf)
        out[...] = f(la, ha, rf, rf + r)
        for j in range(nf):
            up[:, j * D : (j + 1) * D] = f(lb, hb, j * r, (j + 1) * r)
        v = f(lb, hb, nf * r, nf * r + VROWS)
        me = ids[0]
        tiles = [v[0:8, t * LANES : (t + 1) * LANES] for t in range(D // LANES)]
        x = own_lanes(tiles, me, r)
        for q, ref in enumerate(vecs):
            ref[...] = x[q : q + 1, :]
        tiles = [v[4 + q : 5 + q, t * LANES : (t + 1) * LANES] for q in range(nf) for t in range(D // LANES)]
        upb[...] = own_lanes(tiles, me, nf * D // n)

    @pl.when(ids[1] == 0)
    def _():
        run(sa, oa, sb, ob)

    @pl.when(ids[1] == 1)
    def _():
        run(oa, sa, ob, sb)


def finish_rest(ids, sa, oa, sb, ob, r, rf, nf, n):
    D = sa.shape[1]
    row1 = lambda w: S((1, w), f32)
    return pl.pallas_call(
        functools.partial(finish_rest_body, r, rf, n),
        in_specs=[pl.BlockSpec(memory_space=pltpu.SMEM)] + whole(4), out_specs=whole(8),
        out_shape=[S((rf, D), f32), S((r, nf * D), f32), S((r, D), f32), row1(nf * D // n)] + [row1(r)] * 4,
        compiler_params=pltpu.CompilerParams(vmem_limit_bytes=16 << 20), name="finish_rest", cost_estimate=cost(0, 8 * sa.size),
    )(ids, sa, oa, sb, ob)


def finish_first_body(ids, s, o, w, gain, bias, qkv, gg, gb, qb, vb):
    r, W = w.shape
    D = s.shape[1]

    def run(lo, hi):
        f = lambda a, b: rows_of(lo, hi, a, b).astype(f32)
        v = f(3 * r, 3 * r + VROWS)
        nt = D // LANES
        accg = accb = jnp.zeros((r, LANES), f32)
        col = lambda g: jnp.concatenate([g[...].astype(f32), jnp.zeros((7, r), f32)], axis=0).T[:, 0:1]
        cg, cb = col(gain), col(bias)
        for j in range(3):
            m = f(j * r, (j + 1) * r)
            sq = v[j : j + 1, :]
            ww = w[:, j * D : (j + 1) * D].astype(f32)
            qkv[:, j * D : (j + 1) * D] = cg * m + cb * sq
            pg, pb = ww * m, ww * sq
            accg = accg + sum(pg[:, t * LANES : (t + 1) * LANES] for t in range(nt))
            accb = accb + sum(pb[:, t * LANES : (t + 1) * LANES] for t in range(nt))
        gg[...] = jnp.sum(accg.T, axis=0, keepdims=True)
        gb[...] = jnp.sum(accb.T, axis=0, keepdims=True)
        x = own_lanes([v[0:8, t * LANES : (t + 1) * LANES] for t in range(nt)], ids[0], r)
        qb[...] = x[0:1, :]
        vb[...] = x[2:3, :]

    @pl.when(ids[1] == 0)
    def _():
        run(s, o)

    @pl.when(ids[1] == 1)
    def _():
        run(o, s)


def finish_first(ids, s, o, w, gain, bias):
    r, W = w.shape
    return pl.pallas_call(
        finish_first_body,
        in_specs=[pl.BlockSpec(memory_space=pltpu.SMEM)] + whole(5), out_specs=whole(5),
        out_shape=[S((r, W), f32)] + [S((1, r), f32)] * 4,
        compiler_params=pltpu.CompilerParams(vmem_limit_bytes=16 << 20), name="finish_first", cost_estimate=cost(0, 8 * w.size),
    )(ids, s, o, w, gain[None], bias[None])


def pull(me, refs, meta, segs, sems):
    copies = []
    for ref, (k, r0) in zip(refs, meta):
        s = jnp.bitwise_xor(me, k)
        r1 = r0 + ref.shape[0]
        for a, c, dst, lanes in segs:
            lo, hi = max(a, r0), min(a + c, r1)
            if lo < hi:
                src = ref.at[pl.ds(lo - r0, hi - lo), pl.ds(0, lanes)]
                copies.append(pltpu.make_async_copy(src, dst(s, lo - a, hi - lo), sems.at[len(copies)]))
    return copies


def mult(x, m):
    return pl.multiple_of(x, m)


def project(v, h, w, kv, qkvt, grp, scale):
    gw = w.shape[1] // 3
    bias = lambda i: v[i : i + 1, grp * gw : (grp + 1) * gw]
    for j in range(3):
        y = dot(h, w[:, j * gw : (j + 1) * gw])
        if j == 0:
            y = y + bias(2)
        if j == 2:
            y = y + bias(3)
        y = y.astype(bf16)
        if j == 0:
            y = y * bf16(scale)
        else:
            kv[j - 1] = y
        qkvt[j] = y.T


def weight_segs(w, r):
    gw = w.shape[1] // 3
    seg = lambda j: (j * r, r, lambda s, o, c: w.at[pl.ds(mult(s * r + o, 16), c), pl.ds(j * gw, gw)], gw)
    return [seg(j) for j in range(3)]


def front_body(scale, n, meta, me, tok, step, *refs):
    np_ = len(meta)
    pieces = refs[:np_]
    xht, hs, kv, qkvt, w, vec, upb, vbuf, sems = refs[np_:]
    D = tok.shape[-1]
    r = D // n
    FF = upb.shape[1]
    first = pl.program_id(0) == 0
    segs = [(3 * r, VROWS, lambda s, o, c: vbuf.at[s, pl.ds(o, c)], LANES)] + weight_segs(w, r)

    @pl.when(first)
    def _():
        for c in pull(me[0], pieces, meta, segs, sems):
            c.start()

    x = tok[...].astype(f32) + step[...].astype(f32)
    nx, _ = norm(x)
    xht[...] = nx.astype(bf16).T

    @pl.when(first)
    def _():
        for c in pull(me[0], pieces, meta, segs, sems):
            c.wait()
        per = LANES // r
        tiles = [sum(vbuf[s, 0:8, :].astype(f32) for s in range(t * per, (t + 1) * per)) for t in range(D // LANES)]
        vec[...] = jnp.concatenate(tiles, axis=1)
        wu = FF // n
        if wu >= LANES:
            rows = [vbuf[s, 8 + q : 9 + q, :].astype(f32) for s in range(n) for q in range(wu // LANES)]
        else:
            per = LANES // wu
            rows = [sum(vbuf[s, 8:9, :].astype(f32) for s in range(t * per, (t + 1) * per)) for t in range(FF // LANES)]
        upb[...] = jnp.concatenate(rows, axis=1)

    v = vec[...]
    h = (nx * row(v, 0) + row(v, 1)).astype(bf16)
    hs[...] = h
    project(v, h, w, kv, qkvt, 0, scale)


def front_next_body(scale, n, meta, grp, me, hs, vec, *refs):
    np_ = len(meta)
    pieces = refs[:np_]
    kv, qkvt, w, sems = refs[np_ + 2 :]

    @pl.when(pl.program_id(0) == 0)
    def _():
        cs = pull(me[0], pieces, meta, weight_segs(w, w.shape[0] // n), sems)
        for c in cs:
            c.start()
        for c in cs:
            c.wait()

    project(vec[...], hs[...], w, kv, qkvt, grp, scale)


S = jax.ShapeDtypeStruct
ANY = pl.BlockSpec(memory_space=pl.ANY)


def cost(flops, nbytes, tr=0):
    return pl.CostEstimate(flops=int(flops), bytes_accessed=int(nbytes), transcendentals=int(tr))


def front(me, tok, step, pieces, n, FF, bm=512):
    T, D = tok.shape
    scale = 1.0 / math.sqrt(D // HEADS)
    gw = D // GROUPS
    meta = tuple((k, r0) for k, r0, _ in pieces)
    keep = lambda *sh: pl.BlockSpec(sh, lambda i, m: (0,) * len(sh))
    return pl.pallas_call(
        functools.partial(front_body, scale, n, meta),
        grid_spec=pltpu.PrefetchScalarGridSpec(
            num_scalar_prefetch=1, grid=(T // bm,),
            in_specs=[pl.BlockSpec((bm, D), lambda i, m: (i, 0)), keep(1, D)] + [ANY] * len(pieces),
            out_specs=[pl.BlockSpec((D, bm), lambda i, m: (0, i)), pl.BlockSpec((bm, D), lambda i, m: (i, 0)), pl.BlockSpec((2, bm, gw), lambda i, m: (0, i, 0)), pl.BlockSpec((3, gw, bm), lambda i, m: (0, 0, i)), keep(D, 3 * gw), keep(8, D), keep(1, FF)],
            scratch_shapes=[pltpu.VMEM((n, VROWS, LANES), bf16), pltpu.SemaphoreType.DMA((8 * len(pieces),))]),
        out_shape=[S((D, T), bf16), S((T, D), bf16), S((2, T, D), bf16), S((3, D, T), bf16), S((D, 3 * gw), bf16), S((8, D), f32), S((1, FF), f32)],
        compiler_params=cp(), name="front", cost_estimate=cost(6 * T * D * gw, 8 * T * D),
    )(me, tok, step, *[a for _, _, a in pieces])


def front_next(me, hs, vec, pieces, kv, qkvt, grp, n, bm=512):
    T, D = hs.shape
    scale = 1.0 / math.sqrt(D // HEADS)
    gw = D // GROUPS
    meta = tuple((k, r0) for k, r0, _ in pieces)
    q = len(pieces)
    return pl.pallas_call(
        functools.partial(front_next_body, scale, n, meta, grp),
        grid_spec=pltpu.PrefetchScalarGridSpec(
            num_scalar_prefetch=1, grid=(T // bm,),
            in_specs=[pl.BlockSpec((bm, D), lambda i, m: (i, 0)), pl.BlockSpec(vec.shape, lambda i, m: (0, 0))] + [ANY] * (q + 2),
            out_specs=[pl.BlockSpec((2, bm, gw), lambda i, m: (0, i, grp)), pl.BlockSpec((3, gw, bm), lambda i, m: (0, grp, i)), pl.BlockSpec((D, 3 * gw), lambda i, m: (0, 0))],
            scratch_shapes=[pltpu.SemaphoreType.DMA((8 * q,))]),
        out_shape=[S((2, T, D), bf16), S((3, D, T), bf16), S((D, 3 * gw), bf16)],
        input_output_aliases={3 + q: 0, 4 + q: 1},
        compiler_params=cp(), name="front_next", cost_estimate=cost(6 * T * D * gw, 6 * T * D),
    )(me, hs, vec, *[a for _, _, a in pieces], kv, qkvt)


def attn_fwd_body(HD, bi, CR, ln, k, qt, vt, *refs):
    et, mixed, mixedt, mixedf, linv, scr, ka = refs[-7:]
    T, PW = k.shape
    n = ln[0]
    rid = lax.broadcasted_iota(jnp.int32, (PW, bi), 0)
    lane = lax.broadcasted_iota(jnp.int32, (T, PW), 1)
    rows = lax.broadcasted_iota(jnp.int32, (T, PW), 0)
    ka[:, :PW] = k[...]
    ka[:, PW:] = jnp.where((lane == 0) & (rows >= n), f32(-1e30), f32(0)).astype(bf16)
    ones = jnp.where(rid == 0, f32(1), f32(0)).astype(bf16)
    va = [jnp.concatenate([vt[h * HD : (h + 1) * HD, :], jnp.ones((16, T), bf16)], axis=0) for h in range(2)]
    tasks = [(b, h) for b in range(T // bi) for h in range(2)]
    nch = T // CR

    def query(t):
        b, h = tasks[t]
        q = qt[:, b * bi : (b + 1) * bi]
        return jnp.concatenate([jnp.where(rid // HD == h, q, jnp.zeros_like(q)), ones], axis=0)

    def score(t, c, q):
        s = dot(ka[c * CR : (c + 1) * CR, :], q)
        scr[t % 2, c * CR : (c + 1) * CR, :] = s
        return jnp.max(s, axis=0, keepdims=True)

    q = query(0)
    m = functools.reduce(jnp.maximum, [score(0, c, q) for c in range(nch)])
    half = None
    for t, (b, h) in enumerate(tasks):
        sl = slice(b * bi, (b + 1) * bi)
        more = t + 1 < len(tasks)
        if more:
            q = query(t + 1)
        nxt = []
        for c in range(nch):
            cs = slice(c * CR, (c + 1) * CR)
            if more:
                nxt.append(score(t + 1, c, q))
            et[h, cs, sl] = jnp.exp(scr[t % 2, cs, :] - m).astype(bf16)
        o = dot(va[h], et[h, :, sl])
        if more:
            m = functools.reduce(jnp.maximum, nxt)
        inv = 1.0 / o[HD : HD + 1, :]
        linv[h : h + 1, sl] = inv
        o = o[:HD, :] * inv
        if h == 0:
            half = o
        else:
            mt = jnp.concatenate([half, o], axis=0)
            mixedf[:, sl] = mt
            mt = mt.astype(bf16)
            mixedt[:, sl] = mt
            mixed[sl, :] = mt.T


def attn_fwd(ln, kv, qkvt, p0, cnt, prev):
    _, T, D = kv.shape
    HD = D // HEADS
    PW = 2 * HD
    NP = D // PW
    bi = min(512, T)
    prev = list(prev)
    return pl.pallas_call(
        functools.partial(attn_fwd_body, HD, bi, min(256, T)),
        grid_spec=pltpu.PrefetchScalarGridSpec(
            num_scalar_prefetch=1, grid=(cnt,),
            in_specs=[pl.BlockSpec((None, T, PW), lambda p, r: (0, 0, p0 + p)), pl.BlockSpec((None, PW, T), lambda p, r: (0, p0 + p, 0)), pl.BlockSpec((None, PW, T), lambda p, r: (2, p0 + p, 0))] + [ANY] * len(prev),
            out_specs=[pl.BlockSpec((2, T, T), lambda p, r: (p0 + p, 0, 0)), pl.BlockSpec((T, PW), lambda p, r: (0, p0 + p)), pl.BlockSpec((PW, T), lambda p, r: (p0 + p, 0)), pl.BlockSpec((PW, T), lambda p, r: (p0 + p, 0)), pl.BlockSpec((None, 8, T), lambda p, r: (p0 + p, 0, 0))],
            scratch_shapes=[pltpu.VMEM((2, T, bi), f32), pltpu.VMEM((T, 2 * PW), bf16)]),
        out_shape=[S((HEADS, T, T), bf16), S((T, D), bf16), S((D, T), bf16), S((D, T), f32), S((NP, 8, T), f32)],
        input_output_aliases={4 + i: i for i in range(len(prev))},
        compiler_params=cp(), name="attn_fwd", cost_estimate=cost(cnt * 2 * 8 * T * T * 128, cnt * 2 * T * T * 2, cnt * 2 * T * T),
    )(ln, kv, qkvt, qkvt, *prev)


G0 = math.sqrt(2 / math.pi)


def bit_reverse(x, m):
    y = jnp.zeros_like(x)
    for t in range(m):
        y = y | (((x >> t) & 1) << (m - 1 - t))
    return y


def push(me, n, s, src, keep, send, row0, sem, reverse=False):
    k = jnp.bitwise_xor(me, s)
    p = k >> 1
    if reverse:
        p = bit_reverse(p, (n // 2).bit_length() - 1)
    put = lambda dst: pltpu.make_async_copy(src, dst.at[p, pl.ds(row0, src.shape[0])], sem)

    @pl.when(k & 1 == 0)
    def _():
        put(keep).start()

    @pl.when(k & 1 == 1)
    def _():
        put(send).start()


def ffn_body(n, meta, ch, ln, me, tok, step, vec, upb, cot, mixed, mixedt, *refs):
    np_ = len(meta)
    pieces = refs[:np_]
    out, gx1, gmt, keep, send, wo, wu, wd, act, gup, h2t, gdt, gattn, sums, upsum, dn, up, gwo, vr, sems, psems = refs[np_:]
    i = pl.program_id(0)
    bm, D = tok.shape
    FF = wu.shape[1]
    r = D // n
    rf = FF // n
    nf = FF // D
    i0 = me[0]
    ro = pl.ds(mult(i * bm, 128), bm)
    first = i == 0
    seg = lambda j: (r + j * r, r, lambda s, o, c: wu.at[pl.ds(mult(s * r + o, 16), c), pl.ds(j * D, D)], D)
    segs = [(0, r, lambda s, o, c: wo.at[pl.ds(mult(s * r + o, 16), c)], D)] + [seg(j) for j in range(nf)]
    segs += [(r + r * nf, rf, lambda s, o, c: wd.at[pl.ds(mult(s * rf + o, 16), c)], D)]

    @pl.when(first)
    def _():
        for c in pull(i0, pieces, meta, segs, sems):
            c.start()
        sums[...] = jnp.zeros_like(sums)
        upsum[...] = jnp.zeros_like(upsum)
        for c in pull(i0, pieces, meta, segs, sems):
            c.wait()

    v = vec[...]
    x1 = tok[...].astype(f32) + step[...].astype(f32) + dot(mixed[...], wo[...]) + row(v, 4)
    nx, rr = norm(x1)
    h2 = (nx * row(v, 5) + row(v, 6)).astype(bf16)
    live = (lax.broadcasted_iota(jnp.int32, (bm, 1), 0) + i * bm) < ln[0]
    gd = jnp.where(live, cot[...], jnp.zeros_like(cot))
    acc = x1 + row(v, 7)
    gh = None
    nc = FF // ch
    sl = [slice(c * ch, (c + 1) * ch) for c in range(nc)]
    lead = lambda c: (dot(h2, wu[:, sl[c]]), dot_t(gd, wd[sl[c], :]))
    nxt = lead(0)
    h2t[:, ro] = h2.T
    gdt[:, ro] = gd.T
    for c in range(nc):
        u, ga = nxt
        nxt = lead(c + 1) if c + 1 < nc else None
        u = u + upb[:, sl[c]]
        u2 = u * u
        t = jnp.tanh(u * (f32(G0) + f32(G0 * 0.044715) * u2))
        half = 0.5 + 0.5 * t
        a = (u * half).astype(bf16)
        act[ro, sl[c]] = a
        dg = half + u * (half * (1.0 - half)) * (f32(2 * G0) + f32(6 * 0.044715 * G0) * u2)
        gu = (ga * dg).astype(bf16)
        gup[ro, sl[c]] = gu
        upsum[:, sl[c]] += jnp.sum(gu.astype(f32), axis=0, keepdims=True)
        acc = acc + dot(a, wd[sl[c], :])
        p = dot_t(gu, wu[:, sl[c]])
        gh = p if gh is None else gh + p
    out[...] = jnp.where(live, acc, 0.0).astype(bf16)
    gn = gh * row(v, 5)
    gx = gd.astype(f32) + rr * (gn - jnp.mean(gn, axis=-1, keepdims=True) - nx * jnp.mean(gn * nx, axis=-1, keepdims=True))
    gx1[...] = gx
    gab = gx.astype(bf16)
    gattn[ro, :] = gab
    gmt[...] = dot_t(gab, wo[...]).astype(bf16).T
    s_ = lambda a: jnp.sum(a.astype(f32), axis=0, keepdims=True)
    sums[...] += jnp.concatenate([s_(gab), s_(gh * nx), s_(gh), s_(gd), jnp.zeros((4, D), f32)], axis=0)

    @pl.when(i == pl.num_programs(0) - 1)
    def _():
        per = D // rf
        o_out, o_up, o_vec = rf, rf + r, rf + (nf + 1) * r
        for j in range(nf):
            dn[j] = dot(gdt[...], act[:, j * D : (j + 1) * D]).astype(bf16).T
            for t in range(per):
                push(i0, n, j * per + t, dn.at[j, pl.ds(t * rf, rf)], keep, send, 0, psems.at[j * per + t])
            up[j] = dot(h2t[...], gup[:, j * D : (j + 1) * D]).astype(bf16)
            for s in range(n):
                push(i0, n, s, up.at[j, pl.ds(s * r, r)], keep, send, o_up + j * r, psems.at[n * (1 + j) + s], True)
        gwo[...] = dot(mixedt[...], gattn[...]).astype(bf16)
        vr[...] = jnp.concatenate([sums[0:4, :]] + [upsum[:, c * D : (c + 1) * D] for c in range(nf)] + [jnp.zeros((VROWS - 4 - nf, D), f32)], axis=0).astype(bf16)
        b = n * (1 + nf)
        for s in range(n):
            push(i0, n, s, gwo.at[pl.ds(s * r, r)], keep, send, o_out, psems.at[b + s])
            push(i0, n, s, vr, keep, send, o_vec, psems.at[b + n + s], True)
        done = lambda src, q: pltpu.make_async_copy(src, keep.at[0, pl.ds(0, src.shape[0])], psems.at[q]).wait()
        for s in range(n):
            done(dn.at[0, pl.ds(0, rf)], s)
            for c in range(nf):
                done(up.at[0, pl.ds(0, r)], n * (1 + c) + s)
            done(gwo.at[pl.ds(0, r)], b + s)
            done(vr, b + n + s)


def ffn(ln, me, tok, step, vec, upb, cot, mixed, mixedt, pieces, n):
    T, D = tok.shape
    FF = upb.shape[1]
    bm = min(512, T)
    nf = FF // D
    r = D // n
    meta = tuple((k, r0) for k, r0, _ in pieces)
    full = lambda a: pl.BlockSpec(a.shape, lambda i, l, m: (0,) * a.ndim)
    rows = pl.BlockSpec((bm, D), lambda i, l, m: (i, 0))
    B = S((n // 2, FF // n + (nf + 1) * r + VROWS, D), bf16)
    V = pltpu.VMEM
    return pl.pallas_call(
        functools.partial(ffn_body, n, meta, min(1024, FF)),
        grid_spec=pltpu.PrefetchScalarGridSpec(
            num_scalar_prefetch=2, grid=(T // bm,),
            in_specs=[rows, full(step), full(vec), full(upb), rows, rows, full(mixedt)] + [ANY] * len(pieces),
            out_specs=[rows, rows, pl.BlockSpec((D, bm), lambda i, l, m: (0, i)), ANY, ANY],
            scratch_shapes=[V((D, D), bf16), V((D, FF), bf16), V((FF, D), bf16), V((T, FF), bf16), V((T, FF), bf16), V((D, T), bf16), V((D, T), bf16), V((T, D), bf16), V((8, D), f32), V((1, FF), f32), V((nf, D, D), bf16), V((nf, D, D), bf16), V((D, D), bf16), V((VROWS, D), bf16), pltpu.SemaphoreType.DMA((8 * len(pieces),)), pltpu.SemaphoreType.DMA((n * (nf + 3),))]),
        out_shape=[S((T, D), bf16), S((T, D), f32), S((D, T), bf16), B, B],
        compiler_params=cp(), name="ffn", cost_estimate=cost(2 * T * D * (6 * FF + 3 * D), 16 * T * D, T * FF),
    )(ln, me, tok, step, vec, upb, cot, mixed, mixedt, *[a for _, _, a in pieces])


def attn_bwd_body(HD, scale, CR, v, kt, qt, gt, mt, linv, et, *refs):
    gq, ds = refs[-2:]
    T = v.shape[0]
    rid = lax.broadcasted_iota(jnp.int32, gt.shape, 0) // HD
    g = gt[...].astype(f32)
    q = qt[...]
    gv = gk = None
    for h in range(2):
        hs = slice(h * HD, (h + 1) * HD)
        gs = (g * linv[h : h + 1, :]).astype(bf16)
        gm = jnp.where(rid == h, gs, jnp.zeros_like(gs))
        dl = jnp.sum(gs[hs, :].astype(f32) * mt[hs, :], axis=0, keepdims=True)
        for c in range(T // CR):
            cs = slice(c * CR, (c + 1) * CR)
            ds[h, cs, :] = (et[h, cs, :].astype(f32) * (dot(v[cs, :], gm) - dl)).astype(bf16)
        a = dot(et[h], gm.T)
        b = dot(ds[h], jnp.where(rid == h, q, jnp.zeros_like(q)).T)
        gv = a if gv is None else gv + a
        gk = b if gk is None else gk + b
        gq[0, hs, :] = (dot(kt[hs, :], ds[h]) * scale).astype(bf16)
    gq[2] = gv.astype(bf16).T
    gq[1] = gk.astype(bf16).T


def attn_bwd(kv, qkvt, gmt, mixedf, linv, et, p0, cnt, prev):
    _, T, D = kv.shape
    HD = D // HEADS
    PW = 2 * HD
    NP = D // PW
    prev = list(prev)
    pr = pl.BlockSpec((PW, T), lambda p: (p0 + p, 0))
    of = lambda j: pl.BlockSpec((None, PW, T), lambda p: (j, p0 + p, 0))
    return pl.pallas_call(
        functools.partial(attn_bwd_body, HD, 1.0 / math.sqrt(HD), min(256, T)),
        grid=(cnt,),
        scratch_shapes=[pltpu.VMEM((2, T, T), bf16)],
        in_specs=[pl.BlockSpec((None, T, PW), lambda p: (1, 0, p0 + p)), of(1), of(0), pr, pr, pl.BlockSpec((None, 8, T), lambda p: (p0 + p, 0, 0)), pl.BlockSpec((2, T, T), lambda p: (p0 + p, 0, 0))] + [ANY] * len(prev),
        out_specs=pl.BlockSpec((3, PW, T), lambda p: (0, p0 + p, 0)),
        out_shape=S((3, D, T), bf16),
        input_output_aliases={7: 0} if prev else {},
        compiler_params=cp(), name="attn_bwd", cost_estimate=cost(cnt * 2 * 16 * T * T * 128, cnt * 2 * T * T * 2),
    )(kv, qkvt, qkvt, gmt, mixedf, linv, et, *prev)


def wqkv_body(n, me, xht, g, keep, send, res, vr, sems):
    j = pl.program_id(0)
    D = g.shape[0]
    r = D // n
    i0 = me[0]
    x = jnp.concatenate([xht[...], jnp.ones((16, xht.shape[1]), bf16)], axis=0)
    y = dot_t(x, g[...]).astype(bf16)
    res[j] = y[:D]
    vr[...] = jnp.where(lax.broadcasted_iota(jnp.int32, vr.shape, 0) == j, y[D:], jnp.where(j == 0, jnp.zeros_like(y[D:]), vr[...]))
    for s in range(n):
        push(i0, n, s, res.at[j, pl.ds(s * r, r)], keep, send, mult(j * r, 16), sems.at[j * n + s])

    @pl.when(j == 2)
    def _():
        for s in range(n):
            push(i0, n, s, vr, keep, send, 3 * r, sems.at[3 * n + s])
        for s in range(n):
            for q in range(3):
                pltpu.make_async_copy(res.at[0, pl.ds(0, r)], keep.at[0, pl.ds(0, r)], sems.at[q * n + s]).wait()
            pltpu.make_async_copy(vr, keep.at[0, pl.ds(0, VROWS)], sems.at[3 * n + s]).wait()


def wqkv(me, xht, g, n):
    D, T = xht.shape
    A = S((n // 2, 3 * (D // n) + VROWS, D), bf16)
    return pl.pallas_call(
        functools.partial(wqkv_body, n),
        grid_spec=pltpu.PrefetchScalarGridSpec(
            num_scalar_prefetch=1, grid=(3,),
            in_specs=[pl.BlockSpec((D, T), lambda j, m: (0, 0)), pl.BlockSpec((None, D, T), lambda j, m: (j, 0, 0))],
            out_specs=[ANY] * 2,
            scratch_shapes=[pltpu.VMEM((3, D, D), bf16), pltpu.VMEM((VROWS, D), bf16), pltpu.SemaphoreType.DMA((4 * n,))]),
        out_shape=[A, A],
        compiler_params=cp(), name="wqkv", cost_estimate=cost(6 * T * D * D, 10 * T * D),
    )(me, xht, g)


def back_body(tok, step, vec, g, gx1, *refs):
    ws, tg = refs[:-1], refs[-1]
    D = tok.shape[1]
    gw = D // GROUPS
    x = tok[...].astype(f32) + step[...].astype(f32)
    nx, rr = norm(x)
    gt = sum(dot(w[:, j * gw : (j + 1) * gw], g[j, q * gw : (q + 1) * gw, :]) for q, w in enumerate(ws) for j in range(3))
    gn = gt.T * row(vec[...], 0)
    tg[...] = gx1[...] + rr * (gn - jnp.mean(gn, axis=-1, keepdims=True) - nx * jnp.mean(gn * nx, axis=-1, keepdims=True))


def back(tok, step, vec, ws, g, gx1, bm=512):
    T, D = tok.shape
    full = lambda a: pl.BlockSpec(a.shape, lambda i: (0,) * a.ndim)
    rows = pl.BlockSpec((bm, D), lambda i: (i, 0))
    return pl.pallas_call(
        back_body, grid=(T // bm,),
        in_specs=[rows, full(step), full(vec), pl.BlockSpec((3, D, bm), lambda i: (0, 0, i)), rows] + [full(w) for w in ws],
        out_specs=rows, out_shape=S((T, D), f32), compiler_params=cp(), name="back", cost_estimate=cost(6 * T * D * D, 14 * T * D),
    )(tok, step, vec, g, gx1, *ws)


def shards(tokens, step_embed, lengths, cotangent, ln1_gain, ln1_bias, qkv_weight, q_bias, v_bias, out_weight, out_bias, ln2_gain, ln2_bias, up_weight, up_bias, down_weight, down_bias):
    n = lax.axis_size("shard")
    me = lax.axis_index("shard").astype(jnp.int32)
    mes = me[None]
    tok, cot, step = tokens[0], cotangent[0], step_embed
    T, D = tok.shape
    r = D // n
    FF = up_bias.shape[0] * n
    nc = FF // D
    rf = FF // n
    packs = pack_first(mes, qkv_weight, [ln1_gain, ln1_bias, q_bias, v_bias, out_bias, ln2_gain, ln2_bias, down_bias], up_bias)
    pack2 = pack_rest(out_weight, up_weight, down_weight)
    NP = HEADS // 2
    GP = NP // GROUPS
    arrays = lambda ps: [a for _, _, a in ps[1:]]
    pieces = gather_direct(packs[0], n)
    xht, hs, kv, qkvt, wa, vec, upb = front(mes, tok, after(step, pack2), pieces, n, FF)
    nextp = gather_direct(packs[1], n, vec)
    fw = attn_fwd(lengths, kv, qkvt, 0, GP, [])
    kv, qkvt, wb = front_next(mes, hs, after(vec, fw[4]), nextp, kv, qkvt, 1, n)
    fw2 = attn_fwd(lengths, kv, qkvt, GP, NP - GP, fw)
    ws = [wa, wb]
    et, mixed, mixedt, mixedf, linv = fw2
    pieces2 = gather_forward(after(pack2, vec, *arrays(nextp)), n, wb, linv)
    out, gx1, gmt, keep, send = ffn(lengths, mes, tok, step, vec, upb, cot, mixed, mixedt, pieces2, n)
    bwd = lambda p, c, g, *deps: attn_bwd(kv, qkvt, after(gmt, *deps) if deps else gmt, mixedf, linv, et, p, c, g)
    ra = rf + r
    got = swap(send, 1)
    g = bwd(0, 1, [])
    got = after(got, g)
    h = n // 4
    add = lambda a, b, k: add16(a[k], b[k])
    rows_a, rows_b = slice(0, ra), slice(ra, None)
    lo, hi = slice(0, h), slice(h, None)
    ka, xa, kb, xb = [add(keep, got, k) for k in ((lo, rows_a), (hi, rows_a), (lo, rows_b), (hi, rows_b))]
    g = bwd(1, NP - 1, [g], ka, xa, kb, xb)
    m = (n // 2).bit_length() - 1
    ga, gb = swap(xa, 2 << (m - 1)), swap(xb, 2)
    for t in range(1, m):
        dep = g if t == 1 else keep
        ga, gb, _ = lax.optimization_barrier((ga, gb, dep))
        h //= 2
        lo, hi = slice(0, h), slice(h, None)
        ka, xa = add(ka, ga, lo), add(ka, ga, hi)
        kb, xb = add(kb, gb, lo), add(kb, gb, hi)
        ga, gb = swap(xa, 2 << (m - 1 - t)), swap(xb, 2 << t)
        if t == 1:
            keep, send = wqkv(mes, after(xht, ka, xa, kb, xb), g, n)
    got = swap(send, 1)
    p2 = [add16(keep[k], got[k]) for k in range(n // 2)]
    far2 = spread(p2)
    ga, gb, _ = lax.optimization_barrier((ga, gb, keep))
    ua = add16(ka, ga)[0]
    ub = add16(kb, gb)[0]
    ua, ub = lax.optimization_barrier((ua, ub))
    ma, oa, xa = rep_half(ua)
    mb, ob, xb = rep_half(ub)
    za = add16(ma, after(oa, p2[1]))
    zb = add16(mb, after(ob, p2[1]))
    tg = back(tok, after(step, za, zb, *p2[1:]), vec, ws, g, gx1)
    own2 = total(p2[0], [after(a, tg) for a in far2])
    m2, o2, x2 = rep_half(own2)
    z2 = add16(m2, o2)
    for b in rep_steps():
        pa, pb, pz = rep_perm(za, b), rep_perm(zb, b), rep_perm(z2, b)
        za = add16(za, after(pa, x2))
        zb = add16(zb, after(pb, x2))
        z2 = add16(z2, after(pz, za, zb))
    oa, ob, o2 = rep_perm(za, 1), rep_perm(zb, 1), rep_perm(z2, 1)
    ids = jnp.stack([me, (lax.axis_index("rep") % 2).astype(jnp.int32)])
    g_down, g_up, g_out, g_upb, g_ob, g_g2, g_b2, g_db = finish_rest(ids, za, oa, zb, ob, r, rf, nc, n)
    g_qkv, g_g1, g_b1, g_q, g_v = finish_first(ids, z2, after(o2, g_out), qkv_weight, ln1_gain, ln1_bias)
    flat = lambda a: a.reshape(-1)
    return (out[None], tg[None], flat(g_g1), flat(g_b1), g_qkv, flat(g_q), flat(g_v), g_out, flat(g_ob), flat(g_g2), flat(g_b2), g_up, flat(g_upb), g_down, flat(g_db))


def solution(mesh):
    from jax.sharding import PartitionSpec as P

    in_specs = (
        P(("rep", "shard"), None, None),
        P(("rep", "shard"), None),
        P(("rep", "shard")),
        P(("rep", "shard"), None, None),
        P("shard"),
        P("shard"),
        P("shard", None),
        P("shard"),
        P("shard"),
        P("shard", None),
        P("shard"),
        P("shard"),
        P("shard"),
        P("shard", None),
        P("shard"),
        P("shard", None),
        P("shard"),
    )
    out_specs = (
        P(("rep", "shard"), None, None),
        P(("rep", "shard"), None, None),
        P("shard"),
        P("shard"),
        P("shard", None),
        P("shard"),
        P("shard"),
        P("shard", None),
        P("shard"),
        P("shard"),
        P("shard"),
        P("shard", None),
        P("shard"),
        P("shard", None),
        P("shard"),
    )
    return jax.shard_map(shards, mesh=mesh, in_specs=in_specs, out_specs=out_specs, check_vma=False)
```

```python
import functools, math
import jax, jax.numpy as jnp
from jax import lax
from jax.experimental import pallas as pl
from jax.experimental.pallas import tpu as pltpu

f32 = jnp.float32
bf16 = jnp.bfloat16
EPS = 1e-05
HEADS = 8

def dot(a, b):
    return jnp.dot(a, b, preferred_element_type=f32)

def dot_t(a, b):
    return lax.dot_general(a, b, (((1,), (1,)), ((), ())), preferred_element_type=f32)

def cp(n=1, vmem=100):
    return pltpu.CompilerParams(dimension_semantics=("arbitrary",) * n, vmem_limit_bytes=60 * 1024 * 1024)

def norm(x):
    c = x - jnp.mean(x, axis=-1, keepdims=True)
    r = lax.rsqrt(jnp.mean(c * c, axis=-1, keepdims=True) + EPS)
    return c * r, r

def row(v, i):
    return v[i : i + 1, :].astype(f32)


VROWS = 16
LANES = 128


def xor_perm(n, k):
    return [(i, i ^ k) for i in range(n)]


def rep_perm(x, b):
    return lax.ppermute(x, "rep", xor_perm(lax.axis_size("rep"), b))


def swap(x, k):
    return lax.ppermute(x, "shard", xor_perm(lax.axis_size("shard"), k))


def after(x, *deps):
    return lax.optimization_barrier((x,) + deps)[0]


def gather_direct(x, n, *gate):
    out = [(0, 0, x)]
    far = [(k, swap(x, k)) for k in range(2, n, 2)]
    out += [(k, 0, after(y, *gate) if gate else y) for k, y in far]
    return out + [(k ^ 1, 0, swap(y, 1)) for k, _, y in out]


def gather_forward(x, n, gate1, gate2):
    R = x.shape[0]
    cut = R // 2 // 16 * 16
    near = []
    far = []
    halves = {}
    for k in sorted(range(2, n, 2), key=lambda k: (bin(k).count("1"), k)):
        if bin(k).count("1") == 1:
            y = after(swap(x, k), gate1)
            near.append((k, 0, y))
            halves[k] = (y[:cut], y[cut:])
        else:
            low = k & -k
            high = 1 << (k.bit_length() - 1)
            a = swap(halves[k ^ low][0], low)
            b = swap(halves[k ^ high][1], high)
            far += [(k, 0, a), (k, cut, b)]
            halves[k] = (a, b)
    near = [(0, 0, x)] + near
    late = [(k, r0, after(a, gate2)) for k, r0, a in far]
    out = near + [(k ^ 1, r0, swap(a, 1)) for k, r0, a in near]
    return out + late + [(k ^ 1, r0, swap(a, 1)) for k, r0, a in late]


def add16(a, b):
    return (a.astype(f32) + b.astype(f32)).astype(bf16)


def spread(parts):
    return [swap(parts[k], 2 * k) for k in range(len(parts) - 1, 0, -1)]


def total(own, got):
    t = own.astype(f32)
    for a in got:
        t = t + a.astype(f32)
    return t.astype(bf16)


def rep_half(x):
    h = x.shape[0] // 2
    odd = lax.axis_index("rep") % 2
    mine = lax.dynamic_slice_in_dim(x, odd * h, h, 0)
    other = lax.dynamic_slice_in_dim(x, (1 - odd) * h, h, 0)
    return mine, rep_perm(other, 1), other


def rep_steps():
    nr = lax.axis_size("rep")
    return [b for b in (2 << i for i in range(16)) if b < nr]


GROUPS = 1


def pack_first_body(me, w, upb, *refs):
    vecs = refs[:-GROUPS]
    outs = refs[-GROUPS:]
    r, W = w.shape
    D = W // 3
    gw = D // GROUPS
    for g, out in enumerate(outs):
        for j in range(3):
            out[j * r : (j + 1) * r, :] = w[:, j * D + g * gw : j * D + (g + 1) * gw]

    def spot(v):
        w_ = v.shape[1]
        if w_ >= LANES:
            return [v[:, q * LANES : (q + 1) * LANES] for q in range(w_ // LANES)]
        t = LANES // w_
        lane = lax.broadcasted_iota(jnp.int32, (1, LANES), 1)
        return [jnp.where(lane // w_ == me[0] % t, jnp.concatenate([v] * t, axis=1), jnp.zeros((1, LANES), f32))]

    rows = [a for v in vecs for a in spot(v[...].astype(f32))] + spot(upb[...].astype(f32))
    b = jnp.concatenate(rows + [jnp.zeros((VROWS - len(rows), LANES), f32)], axis=0).astype(bf16)
    outs[0][3 * r :, :] = jnp.concatenate([b, jnp.zeros((VROWS, gw - LANES), bf16)], axis=1) if gw > LANES else b


def whole(n):
    return [pl.BlockSpec(memory_space=pltpu.VMEM)] * n


def once(*arrays):
    return [pl.BlockSpec(a.shape, lambda i, *m, nd=len(a.shape): (0,) * nd) for a in arrays]


def pack_first(me, w, vecs, upb):
    r, W = w.shape
    gw = W // 3 // GROUPS
    args = [w, upb[None]] + [v[None] for v in vecs]
    outs = [S((3 * r + (VROWS if g == 0 else 0), gw), bf16) for g in range(GROUPS)]
    return pl.pallas_call(
        pack_first_body,
        grid_spec=pltpu.PrefetchScalarGridSpec(num_scalar_prefetch=1, grid=(1,), in_specs=once(*args), out_specs=once(*outs)),
        out_shape=outs, compiler_params=cp(), name="pack_first", cost_estimate=cost(0, 4 * w.size),
    )(me, *args)


def pack_rest_body(wo, wu, wd, out):
    r, D = wo.shape
    out[:r, :] = wo[...]
    for j in range(wu.shape[1] // D):
        out[(1 + j) * r : (2 + j) * r, :] = wu[:, j * D : (j + 1) * D]
    out[(1 + wu.shape[1] // D) * r :, :] = wd[...]


def pack_rest(wo, wu, wd):
    D = wo.shape[1]
    out = S(((wo.size + wu.size + wd.size) // D, D), bf16)
    return pl.pallas_call(
        pack_rest_body, grid=(1,), in_specs=once(wo, wu, wd), out_specs=once(out)[0],
        out_shape=out, compiler_params=cp(), name="pack_rest", cost_estimate=cost(0, 4 * wu.size),
    )(wo, wu, wd)


def own_lanes(tiles, me, w):
    pick = lambda i: sum(jnp.where(i == t, a, jnp.zeros_like(a)) for t, a in enumerate(tiles))
    if w >= LANES:
        q = w // LANES
        return jnp.concatenate([pick(me * q + c) for c in range(q)], axis=1)
    per = LANES // w
    x = pick(me // per)
    off = me % per
    return sum(jnp.where(off == o, x[:, o * w : (o + 1) * w], 0.0) for o in range(per))


def rows_of(lo, hi, a, b):
    h = lo.shape[0]
    if b <= h:
        return lo[a:b, :]
    if a >= h:
        return hi[a - h : b - h, :]
    return jnp.concatenate([lo[a:h, :], hi[: b - h, :]], axis=0)


def finish_rest_body(r, rf, n, ids, s, o, down, up, out, upb, *vecs):
    D = out.shape[1]
    nf = up.shape[1] // D

    def run(lo, hi):
        f = lambda a, b: rows_of(lo, hi, a, b).astype(f32)
        down[...] = f(0, rf)
        out[...] = f(rf, rf + r)
        for j in range(nf):
            up[:, j * D : (j + 1) * D] = f(rf + (j + 1) * r, rf + (j + 2) * r)
        b = rf + (nf + 1) * r
        v = f(b, b + VROWS)
        me = ids[0]
        tiles = [v[0:8, t * LANES : (t + 1) * LANES] for t in range(D // LANES)]
        x = own_lanes(tiles, me, r)
        for q, ref in enumerate(vecs):
            ref[...] = x[q : q + 1, :]
        tiles = [v[4 + q : 5 + q, t * LANES : (t + 1) * LANES] for q in range(nf) for t in range(D // LANES)]
        upb[...] = own_lanes(tiles, me, nf * D // n)

    @pl.when(ids[1] == 0)
    def _():
        run(s, o)

    @pl.when(ids[1] == 1)
    def _():
        run(o, s)


def finish_rest(ids, s, o, r, rf, nf, n):
    D = s.shape[1]
    row1 = lambda w: S((1, w), f32)
    return pl.pallas_call(
        functools.partial(finish_rest_body, r, rf, n),
        in_specs=[pl.BlockSpec(memory_space=pltpu.SMEM)] + whole(2), out_specs=whole(8),
        out_shape=[S((rf, D), f32), S((r, nf * D), f32), S((r, D), f32), row1(nf * D // n)] + [row1(r)] * 4,
        compiler_params=pltpu.CompilerParams(vmem_limit_bytes=16 << 20), name="finish_rest", cost_estimate=cost(0, 8 * s.size),
    )(ids, s, o)


def finish_first_body(ids, s, o, w, gain, bias, qkv, gg, gb, qb, vb):
    r, W = w.shape
    D = s.shape[1]

    def run(lo, hi):
        f = lambda a, b: rows_of(lo, hi, a, b).astype(f32)
        v = f(3 * r, 3 * r + VROWS)
        nt = D // LANES
        accg = accb = jnp.zeros((r, LANES), f32)
        col = lambda g: jnp.concatenate([g[...].astype(f32), jnp.zeros((7, r), f32)], axis=0).T[:, 0:1]
        cg, cb = col(gain), col(bias)
        for j in range(3):
            m = f(j * r, (j + 1) * r)
            sq = v[j : j + 1, :]
            ww = w[:, j * D : (j + 1) * D].astype(f32)
            qkv[:, j * D : (j + 1) * D] = cg * m + cb * sq
            pg, pb = ww * m, ww * sq
            accg = accg + sum(pg[:, t * LANES : (t + 1) * LANES] for t in range(nt))
            accb = accb + sum(pb[:, t * LANES : (t + 1) * LANES] for t in range(nt))
        gg[...] = jnp.sum(accg.T, axis=0, keepdims=True)
        gb[...] = jnp.sum(accb.T, axis=0, keepdims=True)
        x = own_lanes([v[0:8, t * LANES : (t + 1) * LANES] for t in range(nt)], ids[0], r)
        qb[...] = x[0:1, :]
        vb[...] = x[2:3, :]

    @pl.when(ids[1] == 0)
    def _():
        run(s, o)

    @pl.when(ids[1] == 1)
    def _():
        run(o, s)


def finish_first(ids, s, o, w, gain, bias):
    r, W = w.shape
    return pl.pallas_call(
        finish_first_body,
        in_specs=[pl.BlockSpec(memory_space=pltpu.SMEM)] + whole(5), out_specs=whole(5),
        out_shape=[S((r, W), f32)] + [S((1, r), f32)] * 4,
        compiler_params=pltpu.CompilerParams(vmem_limit_bytes=16 << 20), name="finish_first", cost_estimate=cost(0, 8 * w.size),
    )(ids, s, o, w, gain[None], bias[None])


def pull(me, refs, meta, segs, sems):
    copies = []
    for ref, (k, r0) in zip(refs, meta):
        s = jnp.bitwise_xor(me, k)
        r1 = r0 + ref.shape[0]
        for a, c, dst, lanes in segs:
            lo, hi = max(a, r0), min(a + c, r1)
            if lo < hi:
                src = ref.at[pl.ds(lo - r0, hi - lo), pl.ds(0, lanes)]
                copies.append(pltpu.make_async_copy(src, dst(s, lo - a, hi - lo), sems.at[len(copies)]))
    return copies


def mult(x, m):
    return pl.multiple_of(x, m)


def project(v, h, w, kv, qkvt, grp, scale):
    gw = w.shape[1] // 3
    bias = lambda i: v[i : i + 1, grp * gw : (grp + 1) * gw]
    for j in range(3):
        y = dot(h, w[:, j * gw : (j + 1) * gw])
        if j == 0:
            y = y + bias(2)
        if j == 2:
            y = y + bias(3)
        y = y.astype(bf16)
        if j == 0:
            y = y * bf16(scale)
        else:
            kv[j - 1] = y
        qkvt[j] = y.T


def weight_segs(w, r):
    gw = w.shape[1] // 3
    seg = lambda j: (j * r, r, lambda s, o, c: w.at[pl.ds(mult(s * r + o, 16), c), pl.ds(j * gw, gw)], gw)
    return [seg(j) for j in range(3)]


def start_body(tok, step, nx, xht):
    n, _ = norm(tok[...].astype(f32) + step[...].astype(f32))
    nx[...] = n
    xht[...] = n.astype(bf16).T


def start(tok, step, bm=256):
    T, D = tok.shape
    rows = pl.BlockSpec((bm, D), lambda i: (i, 0))
    return pl.pallas_call(
        start_body, grid=(T // bm,),
        in_specs=[rows, pl.BlockSpec((1, D), lambda i: (0, 0))], out_specs=[rows, pl.BlockSpec((D, bm), lambda i: (0, i))],
        out_shape=[S((T, D), f32), S((D, T), bf16)], compiler_params=cp(), name="start", cost_estimate=cost(20 * T * D, 8 * T * D),
    )(tok, step)


def front_body(scale, n, meta, me, nx, *refs):
    np_ = len(meta)
    pieces = refs[:np_]
    kv, qkvt, w, vec, upb, vbuf, sems = refs[np_:]
    D = nx.shape[-1]
    r = D // n
    FF = upb.shape[1]
    segs = [(3 * r, VROWS, lambda s, o, c: vbuf.at[s, pl.ds(o, c)], LANES)] + weight_segs(w, r)

    @pl.when(pl.program_id(0) == 0)
    def _():
        cs = pull(me[0], pieces, meta, segs, sems)
        for c in cs:
            c.start()
        for c in cs:
            c.wait()
        per = LANES // r
        tiles = [sum(vbuf[s, 0:8, :].astype(f32) for s in range(t * per, (t + 1) * per)) for t in range(D // LANES)]
        vec[...] = jnp.concatenate(tiles, axis=1)
        wu = FF // n
        if wu >= LANES:
            rows = [vbuf[s, 8 + q : 9 + q, :].astype(f32) for s in range(n) for q in range(wu // LANES)]
        else:
            per = LANES // wu
            rows = [sum(vbuf[s, 8:9, :].astype(f32) for s in range(t * per, (t + 1) * per)) for t in range(FF // LANES)]
        upb[...] = jnp.concatenate(rows, axis=1)

    v = vec[...]
    h = (nx[...] * row(v, 0) + row(v, 1)).astype(bf16)
    project(v, h, w, kv, qkvt, 0, scale)


S = jax.ShapeDtypeStruct
ANY = pl.BlockSpec(memory_space=pl.ANY)


def cost(flops, nbytes, tr=0):
    return pl.CostEstimate(flops=int(flops), bytes_accessed=int(nbytes), transcendentals=int(tr))


def front(me, nx, pieces, n, FF, bm=512):
    T, D = nx.shape
    scale = 1.0 / math.sqrt(D // HEADS)
    meta = tuple((k, r0) for k, r0, _ in pieces)
    keep = lambda *sh: pl.BlockSpec(sh, lambda i, m: (0,) * len(sh))
    return pl.pallas_call(
        functools.partial(front_body, scale, n, meta),
        grid_spec=pltpu.PrefetchScalarGridSpec(
            num_scalar_prefetch=1, grid=(T // bm,),
            in_specs=[pl.BlockSpec((bm, D), lambda i, m: (i, 0))] + [ANY] * len(pieces),
            out_specs=[pl.BlockSpec((2, bm, D), lambda i, m: (0, i, 0)), pl.BlockSpec((3, D, bm), lambda i, m: (0, 0, i)), keep(D, 3 * D), keep(8, D), keep(1, FF)],
            scratch_shapes=[pltpu.VMEM((n, VROWS, LANES), bf16), pltpu.SemaphoreType.DMA((8 * len(pieces),))]),
        out_shape=[S((2, T, D), bf16), S((3, D, T), bf16), S((D, 3 * D), bf16), S((8, D), f32), S((1, FF), f32)],
        compiler_params=cp(), name="front", cost_estimate=cost(6 * T * D * D, 12 * T * D),
    )(me, nx, *[a for _, _, a in pieces])


def attn_fwd_body(HD, bi, CR, ln, k, qt, vt, *refs):
    et, mixed, mixedt, mixedf, linv, scr, ka = refs[-7:]
    T, PW = k.shape
    n = ln[0]
    rid = lax.broadcasted_iota(jnp.int32, (PW, bi), 0)
    lane = lax.broadcasted_iota(jnp.int32, (T, PW), 1)
    rows = lax.broadcasted_iota(jnp.int32, (T, PW), 0)
    ka[:, :PW] = k[...]
    ka[:, PW:] = jnp.where((lane == 0) & (rows >= n), f32(-1e30), f32(0)).astype(bf16)
    ones = jnp.where(rid == 0, f32(1), f32(0)).astype(bf16)
    va = [jnp.concatenate([vt[h * HD : (h + 1) * HD, :], jnp.ones((16, T), bf16)], axis=0) for h in range(2)]
    tasks = [(b, h) for b in range(T // bi) for h in range(2)]
    nch = T // CR

    def query(t):
        b, h = tasks[t]
        q = qt[:, b * bi : (b + 1) * bi]
        return jnp.concatenate([jnp.where(rid // HD == h, q, jnp.zeros_like(q)), ones], axis=0)

    def score(t, c, q):
        s = dot(ka[c * CR : (c + 1) * CR, :], q)
        scr[t % 2, c * CR : (c + 1) * CR, :] = s
        return jnp.max(s, axis=0, keepdims=True)

    q = query(0)
    m = functools.reduce(jnp.maximum, [score(0, c, q) for c in range(nch)])
    half = None
    for t, (b, h) in enumerate(tasks):
        sl = slice(b * bi, (b + 1) * bi)
        more = t + 1 < len(tasks)
        if more:
            q = query(t + 1)
        nxt = []
        for c in range(nch):
            cs = slice(c * CR, (c + 1) * CR)
            if more:
                nxt.append(score(t + 1, c, q))
            et[h, cs, sl] = jnp.exp(scr[t % 2, cs, :] - m).astype(bf16)
        o = dot(va[h], et[h, :, sl])
        if more:
            m = functools.reduce(jnp.maximum, nxt)
        inv = 1.0 / o[HD : HD + 1, :]
        linv[h : h + 1, sl] = inv
        o = o[:HD, :] * inv
        if h == 0:
            half = o
        else:
            mt = jnp.concatenate([half, o], axis=0)
            mixedf[:, sl] = mt
            mt = mt.astype(bf16)
            mixedt[:, sl] = mt
            mixed[sl, :] = mt.T


def attn_fwd(ln, kv, qkvt, p0, cnt, prev):
    _, T, D = kv.shape
    HD = D // HEADS
    PW = 2 * HD
    NP = D // PW
    bi = min(512, T)
    prev = list(prev)
    return pl.pallas_call(
        functools.partial(attn_fwd_body, HD, bi, min(256, T)),
        grid_spec=pltpu.PrefetchScalarGridSpec(
            num_scalar_prefetch=1, grid=(cnt,),
            in_specs=[pl.BlockSpec((None, T, PW), lambda p, r: (0, 0, p0 + p)), pl.BlockSpec((None, PW, T), lambda p, r: (0, p0 + p, 0)), pl.BlockSpec((None, PW, T), lambda p, r: (2, p0 + p, 0))] + [ANY] * len(prev),
            out_specs=[pl.BlockSpec((2, T, T), lambda p, r: (p0 + p, 0, 0)), pl.BlockSpec((T, PW), lambda p, r: (0, p0 + p)), pl.BlockSpec((PW, T), lambda p, r: (p0 + p, 0)), pl.BlockSpec((PW, T), lambda p, r: (p0 + p, 0)), pl.BlockSpec((None, 8, T), lambda p, r: (p0 + p, 0, 0))],
            scratch_shapes=[pltpu.VMEM((2, T, bi), f32), pltpu.VMEM((T, 2 * PW), bf16)]),
        out_shape=[S((HEADS, T, T), bf16), S((T, D), bf16), S((D, T), bf16), S((D, T), f32), S((NP, 8, T), f32)],
        input_output_aliases={4 + i: i for i in range(len(prev))},
        compiler_params=cp(), name="attn_fwd", cost_estimate=cost(cnt * 2 * 8 * T * T * 128, cnt * 2 * T * T * 2, cnt * 2 * T * T),
    )(ln, kv, qkvt, qkvt, *prev)


G0 = math.sqrt(2 / math.pi)


def bit_reverse(x, m):
    y = jnp.zeros_like(x)
    for t in range(m):
        y = y | (((x >> t) & 1) << (m - 1 - t))
    return y


def push(me, n, s, src, keep, send, row0, sem, reverse=False):
    k = jnp.bitwise_xor(me, s)
    p = k >> 1
    if reverse:
        p = bit_reverse(p, (n // 2).bit_length() - 1)
    put = lambda dst: pltpu.make_async_copy(src, dst.at[p, pl.ds(row0, src.shape[0])], sem)

    @pl.when(k & 1 == 0)
    def _():
        put(keep).start()

    @pl.when(k & 1 == 1)
    def _():
        put(send).start()


def ffn_body(n, meta, ch, ln, me, tok, step, vec, upb, cot, mixed, mixedt, *refs):
    np_ = len(meta)
    pieces = refs[:np_]
    out, gx1, gmt, keep, send, wo, wu, wd, act, gup, h2t, gdt, gattn, sums, upsum, dn, up, gwo, vr, sems, psems = refs[np_:]
    i = pl.program_id(0)
    bm, D = tok.shape
    FF = wu.shape[1]
    r = D // n
    rf = FF // n
    nf = FF // D
    i0 = me[0]
    ro = pl.ds(mult(i * bm, 128), bm)
    first = i == 0
    seg = lambda j: (r + j * r, r, lambda s, o, c: wu.at[pl.ds(mult(s * r + o, 16), c), pl.ds(j * D, D)], D)
    segs = [(0, r, lambda s, o, c: wo.at[pl.ds(mult(s * r + o, 16), c)], D)] + [seg(j) for j in range(nf)]
    segs += [(r + r * nf, rf, lambda s, o, c: wd.at[pl.ds(mult(s * rf + o, 16), c)], D)]

    @pl.when(first)
    def _():
        for c in pull(i0, pieces, meta, segs, sems):
            c.start()
        sums[...] = jnp.zeros_like(sums)
        upsum[...] = jnp.zeros_like(upsum)
        for c in pull(i0, pieces, meta, segs, sems):
            c.wait()

    v = vec[...]
    x1 = tok[...].astype(f32) + step[...].astype(f32) + dot(mixed[...], wo[...]) + row(v, 4)
    nx, rr = norm(x1)
    h2 = (nx * row(v, 5) + row(v, 6)).astype(bf16)
    live = (lax.broadcasted_iota(jnp.int32, (bm, 1), 0) + i * bm) < ln[0]
    gd = jnp.where(live, cot[...], jnp.zeros_like(cot))
    acc = x1 + row(v, 7)
    gh = None
    nc = FF // ch
    sl = [slice(c * ch, (c + 1) * ch) for c in range(nc)]
    lead = lambda c: (dot(h2, wu[:, sl[c]]), dot_t(gd, wd[sl[c], :]))
    nxt = lead(0)
    h2t[:, ro] = h2.T
    gdt[:, ro] = gd.T
    for c in range(nc):
        u, ga = nxt
        nxt = lead(c + 1) if c + 1 < nc else None
        u = u + upb[:, sl[c]]
        u2 = u * u
        t = jnp.tanh(u * (f32(G0) + f32(G0 * 0.044715) * u2))
        half = 0.5 + 0.5 * t
        a = (u * half).astype(bf16)
        act[ro, sl[c]] = a
        dg = half + u * (half * (1.0 - half)) * (f32(2 * G0) + f32(6 * 0.044715 * G0) * u2)
        gu = (ga * dg).astype(bf16)
        gup[ro, sl[c]] = gu
        upsum[:, sl[c]] += jnp.sum(gu.astype(f32), axis=0, keepdims=True)
        acc = acc + dot(a, wd[sl[c], :])
        p = dot_t(gu, wu[:, sl[c]])
        gh = p if gh is None else gh + p
    out[...] = jnp.where(live, acc, 0.0).astype(bf16)
    gn = gh * row(v, 5)
    gx = gd.astype(f32) + rr * (gn - jnp.mean(gn, axis=-1, keepdims=True) - nx * jnp.mean(gn * nx, axis=-1, keepdims=True))
    gx1[...] = gx
    gab = gx.astype(bf16)
    gattn[ro, :] = gab
    gmt[...] = dot_t(gab, wo[...]).astype(bf16).T
    s_ = lambda a: jnp.sum(a.astype(f32), axis=0, keepdims=True)
    sums[...] += jnp.concatenate([s_(gab), s_(gh * nx), s_(gh), s_(gd), jnp.zeros((4, D), f32)], axis=0)

    @pl.when(i == pl.num_programs(0) - 1)
    def _():
        per = D // rf
        o_out, o_up, o_vec = rf, rf + r, rf + (nf + 1) * r
        for j in range(nf):
            dn[j] = dot(gdt[...], act[:, j * D : (j + 1) * D]).astype(bf16).T
            for t in range(per):
                push(i0, n, j * per + t, dn.at[j, pl.ds(t * rf, rf)], keep, send, 0, psems.at[j * per + t])
            up[j] = dot(h2t[...], gup[:, j * D : (j + 1) * D]).astype(bf16)
            for s in range(n):
                push(i0, n, s, up.at[j, pl.ds(s * r, r)], keep, send, o_up + j * r, psems.at[n * (1 + j) + s], True)
        gwo[...] = dot(mixedt[...], gattn[...]).astype(bf16)
        vr[...] = jnp.concatenate([sums[0:4, :]] + [upsum[:, c * D : (c + 1) * D] for c in range(nf)] + [jnp.zeros((VROWS - 4 - nf, D), f32)], axis=0).astype(bf16)
        b = n * (1 + nf)
        for s in range(n):
            push(i0, n, s, gwo.at[pl.ds(s * r, r)], keep, send, o_out, psems.at[b + s])
            push(i0, n, s, vr, keep, send, o_vec, psems.at[b + n + s], True)
        done = lambda src, q: pltpu.make_async_copy(src, keep.at[0, pl.ds(0, src.shape[0])], psems.at[q]).wait()
        for s in range(n):
            done(dn.at[0, pl.ds(0, rf)], s)
            for c in range(nf):
                done(up.at[0, pl.ds(0, r)], n * (1 + c) + s)
            done(gwo.at[pl.ds(0, r)], b + s)
            done(vr, b + n + s)


def ffn(ln, me, tok, step, vec, upb, cot, mixed, mixedt, pieces, n):
    T, D = tok.shape
    FF = upb.shape[1]
    bm = min(512, T)
    nf = FF // D
    r = D // n
    meta = tuple((k, r0) for k, r0, _ in pieces)
    full = lambda a: pl.BlockSpec(a.shape, lambda i, l, m: (0,) * a.ndim)
    rows = pl.BlockSpec((bm, D), lambda i, l, m: (i, 0))
    B = S((n // 2, FF // n + (nf + 1) * r + VROWS, D), bf16)
    V = pltpu.VMEM
    return pl.pallas_call(
        functools.partial(ffn_body, n, meta, min(1024, FF)),
        grid_spec=pltpu.PrefetchScalarGridSpec(
            num_scalar_prefetch=2, grid=(T // bm,),
            in_specs=[rows, full(step), full(vec), full(upb), rows, rows, full(mixedt)] + [ANY] * len(pieces),
            out_specs=[rows, rows, pl.BlockSpec((D, bm), lambda i, l, m: (0, i)), ANY, ANY],
            scratch_shapes=[V((D, D), bf16), V((D, FF), bf16), V((FF, D), bf16), V((T, FF), bf16), V((T, FF), bf16), V((D, T), bf16), V((D, T), bf16), V((T, D), bf16), V((8, D), f32), V((1, FF), f32), V((nf, D, D), bf16), V((nf, D, D), bf16), V((D, D), bf16), V((VROWS, D), bf16), pltpu.SemaphoreType.DMA((8 * len(pieces),)), pltpu.SemaphoreType.DMA((n * (nf + 3),))]),
        out_shape=[S((T, D), bf16), S((T, D), f32), S((D, T), bf16), B, B],
        compiler_params=cp(), name="ffn", cost_estimate=cost(2 * T * D * (6 * FF + 3 * D), 16 * T * D, T * FF),
    )(ln, me, tok, step, vec, upb, cot, mixed, mixedt, *[a for _, _, a in pieces])


def attn_bwd_body(HD, scale, CR, v, kt, qt, gt, mt, linv, et, *refs):
    gq, ds = refs[-2:]
    T = v.shape[0]
    rid = lax.broadcasted_iota(jnp.int32, gt.shape, 0) // HD
    g = gt[...].astype(f32)
    q = qt[...]
    gv = gk = None
    for h in range(2):
        hs = slice(h * HD, (h + 1) * HD)
        gs = (g * linv[h : h + 1, :]).astype(bf16)
        gm = jnp.where(rid == h, gs, jnp.zeros_like(gs))
        dl = jnp.sum(gs[hs, :].astype(f32) * mt[hs, :], axis=0, keepdims=True)
        for c in range(T // CR):
            cs = slice(c * CR, (c + 1) * CR)
            ds[h, cs, :] = (et[h, cs, :].astype(f32) * (dot(v[cs, :], gm) - dl)).astype(bf16)
        a = dot(et[h], gm.T)
        b = dot(ds[h], jnp.where(rid == h, q, jnp.zeros_like(q)).T)
        gv = a if gv is None else gv + a
        gk = b if gk is None else gk + b
        gq[0, hs, :] = (dot(kt[hs, :], ds[h]) * scale).astype(bf16)
    gq[2] = gv.astype(bf16).T
    gq[1] = gk.astype(bf16).T


def attn_bwd(kv, qkvt, gmt, mixedf, linv, et, p0, cnt, prev):
    _, T, D = kv.shape
    HD = D // HEADS
    PW = 2 * HD
    NP = D // PW
    prev = list(prev)
    pr = pl.BlockSpec((PW, T), lambda p: (p0 + p, 0))
    of = lambda j: pl.BlockSpec((None, PW, T), lambda p: (j, p0 + p, 0))
    return pl.pallas_call(
        functools.partial(attn_bwd_body, HD, 1.0 / math.sqrt(HD), min(256, T)),
        grid=(cnt,),
        scratch_shapes=[pltpu.VMEM((2, T, T), bf16)],
        in_specs=[pl.BlockSpec((None, T, PW), lambda p: (1, 0, p0 + p)), of(1), of(0), pr, pr, pl.BlockSpec((None, 8, T), lambda p: (p0 + p, 0, 0)), pl.BlockSpec((2, T, T), lambda p: (p0 + p, 0, 0))] + [ANY] * len(prev),
        out_specs=pl.BlockSpec((3, PW, T), lambda p: (0, p0 + p, 0)),
        out_shape=S((3, D, T), bf16),
        input_output_aliases={7: 0} if prev else {},
        compiler_params=cp(), name="attn_bwd", cost_estimate=cost(cnt * 2 * 16 * T * T * 128, cnt * 2 * T * T * 2),
    )(kv, qkvt, qkvt, gmt, mixedf, linv, et, *prev)


def wqkv_body(n, me, xht, g, keep, send, res, vr, sems):
    j = pl.program_id(0)
    D = g.shape[0]
    r = D // n
    i0 = me[0]
    x = jnp.concatenate([xht[...], jnp.ones((16, xht.shape[1]), bf16)], axis=0)
    y = dot_t(x, g[...]).astype(bf16)
    res[j] = y[:D]
    vr[...] = jnp.where(lax.broadcasted_iota(jnp.int32, vr.shape, 0) == j, y[D:], jnp.where(j == 0, jnp.zeros_like(y[D:]), vr[...]))
    for s in range(n):
        push(i0, n, s, res.at[j, pl.ds(s * r, r)], keep, send, mult(j * r, 16), sems.at[j * n + s])

    @pl.when(j == 2)
    def _():
        for s in range(n):
            push(i0, n, s, vr, keep, send, 3 * r, sems.at[3 * n + s])
        for s in range(n):
            for q in range(3):
                pltpu.make_async_copy(res.at[0, pl.ds(0, r)], keep.at[0, pl.ds(0, r)], sems.at[q * n + s]).wait()
            pltpu.make_async_copy(vr, keep.at[0, pl.ds(0, VROWS)], sems.at[3 * n + s]).wait()


def wqkv(me, xht, g, n):
    D, T = xht.shape
    A = S((n // 2, 3 * (D // n) + VROWS, D), bf16)
    return pl.pallas_call(
        functools.partial(wqkv_body, n),
        grid_spec=pltpu.PrefetchScalarGridSpec(
            num_scalar_prefetch=1, grid=(3,),
            in_specs=[pl.BlockSpec((D, T), lambda j, m: (0, 0)), pl.BlockSpec((None, D, T), lambda j, m: (j, 0, 0))],
            out_specs=[ANY] * 2,
            scratch_shapes=[pltpu.VMEM((3, D, D), bf16), pltpu.VMEM((VROWS, D), bf16), pltpu.SemaphoreType.DMA((4 * n,))]),
        out_shape=[A, A],
        compiler_params=cp(), name="wqkv", cost_estimate=cost(6 * T * D * D, 10 * T * D),
    )(me, xht, g)


def back_body(tok, step, vec, g, gx1, *refs):
    ws, tg = refs[:-1], refs[-1]
    D = tok.shape[1]
    gw = D // GROUPS
    x = tok[...].astype(f32) + step[...].astype(f32)
    nx, rr = norm(x)
    gt = sum(dot(w[:, j * gw : (j + 1) * gw], g[j, q * gw : (q + 1) * gw, :]) for q, w in enumerate(ws) for j in range(3))
    gn = gt.T * row(vec[...], 0)
    tg[...] = gx1[...] + rr * (gn - jnp.mean(gn, axis=-1, keepdims=True) - nx * jnp.mean(gn * nx, axis=-1, keepdims=True))


def back(tok, step, vec, ws, g, gx1, bm=512):
    T, D = tok.shape
    full = lambda a: pl.BlockSpec(a.shape, lambda i: (0,) * a.ndim)
    rows = pl.BlockSpec((bm, D), lambda i: (i, 0))
    return pl.pallas_call(
        back_body, grid=(T // bm,),
        in_specs=[rows, full(step), full(vec), pl.BlockSpec((3, D, bm), lambda i: (0, 0, i)), rows] + [full(w) for w in ws],
        out_specs=rows, out_shape=S((T, D), f32), compiler_params=cp(), name="back", cost_estimate=cost(6 * T * D * D, 14 * T * D),
    )(tok, step, vec, g, gx1, *ws)


def shards(tokens, step_embed, lengths, cotangent, ln1_gain, ln1_bias, qkv_weight, q_bias, v_bias, out_weight, out_bias, ln2_gain, ln2_bias, up_weight, up_bias, down_weight, down_bias):
    n = lax.axis_size("shard")
    me = lax.axis_index("shard").astype(jnp.int32)
    mes = me[None]
    tok, cot, step = tokens[0], cotangent[0], step_embed
    T, D = tok.shape
    r = D // n
    FF = up_bias.shape[0] * n
    nc = FF // D
    rf = FF // n
    packs = pack_first(mes, qkv_weight, [ln1_gain, ln1_bias, q_bias, v_bias, out_bias, ln2_gain, ln2_bias, down_bias], up_bias)
    pack2 = pack_rest(out_weight, up_weight, down_weight)
    NP = HEADS // 2
    nx, xht = start(tok, step)
    pieces = gather_direct(packs[0], n, xht, pack2)
    kv, qkvt, w, vec, upb = front(mes, nx, pieces, n, FF)
    fw = attn_fwd(lengths, kv, qkvt, 0, NP // 2, [])
    fw2 = attn_fwd(lengths, kv, qkvt, NP // 2, NP // 2, fw)
    et, mixed, mixedt, mixedf, linv = fw2
    pieces2 = gather_forward(after(pack2, *[a for _, _, a in pieces[1:]]), n, fw[4], linv)
    out, gx1, gmt, keep, send = ffn(lengths, mes, tok, step, vec, upb, cot, mixed, mixedt, pieces2, n)
    bwd = lambda p, c, g, *deps: attn_bwd(kv, qkvt, after(gmt, *deps) if deps else gmt, mixedf, linv, et, p, c, g)
    ra = rf + r
    got = swap(send, 1)
    g = bwd(0, 1, [])
    got = after(got, g)
    h = n // 4
    add = lambda a, b, k: add16(a[k], b[k])
    rows_a, rows_b = slice(0, ra), slice(ra, None)
    lo, hi = slice(0, h), slice(h, None)
    ka, xa, kb, xb = [add(keep, got, k) for k in ((lo, rows_a), (hi, rows_a), (lo, rows_b), (hi, rows_b))]
    g = bwd(1, NP - 1, [g], ka, xa, kb, xb)
    m = (n // 2).bit_length() - 1
    ga, gb = swap(xa, 2 << (m - 1)), swap(xb, 2)
    for t in range(1, m):
        dep = g if t == 1 else keep
        ga, gb, _ = lax.optimization_barrier((ga, gb, dep))
        h //= 2
        lo, hi = slice(0, h), slice(h, None)
        ka, xa = add(ka, ga, lo), add(ka, ga, hi)
        kb, xb = add(kb, gb, lo), add(kb, gb, hi)
        ga, gb = swap(xa, 2 << (m - 1 - t)), swap(xb, 2 << t)
        if t == 1:
            keep, send = wqkv(mes, after(xht, ka, xa, kb, xb), g, n)
    got = swap(send, 1)
    p2 = [add16(keep[k], got[k]) for k in range(n // 2)]
    far2 = spread(p2)
    ga, gb, _ = lax.optimization_barrier((ga, gb, keep))
    got = swap(send, 1)
    p2 = [add16(keep[k], got[k]) for k in range(n // 2)]
    far2 = spread(p2)
    own1 = jnp.concatenate([add16(ka, ga)[0], add16(kb, gb)[0]], axis=0)
    m1, o1, x1 = rep_half(own1)
    z1 = add16(m1, after(o1, *p2[1:]))
    tg = back(tok, after(step, z1, *p2[1:]), vec, [w], g, gx1)
    own2 = total(p2[0], [after(a, tg) for a in far2])
    m2, o2, x2 = rep_half(own2)
    z2 = add16(m2, o2)
    for b in rep_steps():
        pa, pz = rep_perm(z1, b), rep_perm(z2, b)
        z1 = add16(z1, after(pa, x2))
        z2 = add16(z2, after(pz, z1))
    o1, o2 = rep_perm(z1, 1), rep_perm(z2, 1)
    ids = jnp.stack([me, (lax.axis_index("rep") % 2).astype(jnp.int32)])
    g_down, g_up, g_out, g_upb, g_ob, g_g2, g_b2, g_db = finish_rest(ids, z1, o1, r, rf, nc, n)
    g_qkv, g_g1, g_b1, g_q, g_v = finish_first(ids, z2, after(o2, g_out), qkv_weight, ln1_gain, ln1_bias)
    flat = lambda a: a.reshape(-1)
    return (out[None], tg[None], flat(g_g1), flat(g_b1), g_qkv, flat(g_q), flat(g_v), g_out, flat(g_ob), flat(g_g2), flat(g_b2), g_up, flat(g_upb), g_down, flat(g_db))


def solution(mesh):
    from jax.sharding import PartitionSpec as P

    in_specs = (
        P(("rep", "shard"), None, None),
        P(("rep", "shard"), None),
        P(("rep", "shard")),
        P(("rep", "shard"), None, None),
        P("shard"),
        P("shard"),
        P("shard", None),
        P("shard"),
        P("shard"),
        P("shard", None),
        P("shard"),
        P("shard"),
        P("shard"),
        P("shard", None),
        P("shard"),
        P("shard", None),
        P("shard"),
    )
    out_specs = (
        P(("rep", "shard"), None, None),
        P(("rep", "shard"), None, None),
        P("shard"),
        P("shard"),
        P("shard", None),
        P("shard"),
        P("shard"),
        P("shard", None),
        P("shard"),
        P("shard"),
        P("shard"),
        P("shard", None),
        P("shard"),
        P("shard", None),
        P("shard"),
    )
    return jax.shard_map(shards, mesh=mesh, in_specs=in_specs, out_specs=out_specs, check_vma=False)
```

```python
import functools, math
import jax, jax.numpy as jnp
from jax import lax
from jax.experimental import pallas as pl
from jax.experimental.pallas import tpu as pltpu

f32 = jnp.float32
bf16 = jnp.bfloat16
EPS = 1e-05
HEADS = 8

def dot(a, b):
    return jnp.dot(a, b, preferred_element_type=f32)

def dot_t(a, b):
    return lax.dot_general(a, b, (((1,), (1,)), ((), ())), preferred_element_type=f32)

def cp(n=1, vmem=100):
    return pltpu.CompilerParams(dimension_semantics=("arbitrary",) * n, vmem_limit_bytes=60 * 1024 * 1024)

def norm(x):
    c = x - jnp.mean(x, axis=-1, keepdims=True)
    r = lax.rsqrt(jnp.mean(c * c, axis=-1, keepdims=True) + EPS)
    return c * r, r

def row(v, i):
    return v[i : i + 1, :].astype(f32)


VROWS = 16
LANES = 128


def xor_perm(n, k):
    return [(i, i ^ k) for i in range(n)]


def rep_perm(x, b):
    return lax.ppermute(x, "rep", xor_perm(lax.axis_size("rep"), b))


def swap(x, k):
    return lax.ppermute(x, "shard", xor_perm(lax.axis_size("shard"), k))


def after(x, *deps):
    return lax.optimization_barrier((x,) + deps)[0]


def gather_direct(x, n, *gate):
    out = [(0, 0, x)]
    far = [(k, swap(x, k)) for k in range(2, n, 2)]
    out += [(k, 0, after(y, *gate) if gate else y) for k, y in far]
    return out + [(k ^ 1, 0, swap(y, 1)) for k, _, y in out]


def gather_forward(x, n, gate1, gate2):
    R = x.shape[0]
    cut = R // 2 // 16 * 16
    near = []
    far = []
    halves = {}
    for k in sorted(range(2, n, 2), key=lambda k: (bin(k).count("1"), k)):
        if bin(k).count("1") == 1:
            y = after(swap(x, k), gate1)
            near.append((k, 0, y))
            halves[k] = (y[:cut], y[cut:])
        else:
            low = k & -k
            high = 1 << (k.bit_length() - 1)
            a = swap(halves[k ^ low][0], low)
            b = swap(halves[k ^ high][1], high)
            far += [(k, 0, a), (k, cut, b)]
            halves[k] = (a, b)
    near = [(0, 0, x)] + near
    late = [(k, r0, after(a, gate2)) for k, r0, a in far]
    out = near + [(k ^ 1, r0, swap(a, 1)) for k, r0, a in near]
    return out + late + [(k ^ 1, r0, swap(a, 1)) for k, r0, a in late]


def add16(a, b):
    return a + b


def spread(parts):
    return [swap(parts[k], 2 * k) for k in range(len(parts) - 1, 0, -1)]


def total(own, got):
    t = own.astype(f32)
    for a in got:
        t = t + a.astype(f32)
    return t.astype(bf16)


def rep_half(x):
    h = x.shape[0] // 2
    odd = lax.axis_index("rep") % 2
    mine = lax.dynamic_slice_in_dim(x, odd * h, h, 0)
    other = lax.dynamic_slice_in_dim(x, (1 - odd) * h, h, 0)
    return mine, rep_perm(other, 1), other


def rep_steps():
    nr = lax.axis_size("rep")
    return [b for b in (2 << i for i in range(16)) if b < nr]


GROUPS = 1


def pack_first_body(me, w, upb, *refs):
    vecs = refs[:-GROUPS]
    outs = refs[-GROUPS:]
    r, W = w.shape
    D = W // 3
    gw = D // GROUPS
    for g, out in enumerate(outs):
        for j in range(3):
            out[j * r : (j + 1) * r, :] = w[:, j * D + g * gw : j * D + (g + 1) * gw]

    def spot(v):
        w_ = v.shape[1]
        if w_ >= LANES:
            return [v[:, q * LANES : (q + 1) * LANES] for q in range(w_ // LANES)]
        t = LANES // w_
        lane = lax.broadcasted_iota(jnp.int32, (1, LANES), 1)
        return [jnp.where(lane // w_ == me[0] % t, jnp.concatenate([v] * t, axis=1), jnp.zeros((1, LANES), f32))]

    rows = [a for v in vecs for a in spot(v[...].astype(f32))] + spot(upb[...].astype(f32))
    b = jnp.concatenate(rows + [jnp.zeros((VROWS - len(rows), LANES), f32)], axis=0).astype(bf16)
    outs[0][3 * r :, :] = jnp.concatenate([b, jnp.zeros((VROWS, gw - LANES), bf16)], axis=1) if gw > LANES else b


def whole(n):
    return [pl.BlockSpec(memory_space=pltpu.VMEM)] * n


def once(*arrays):
    return [pl.BlockSpec(a.shape, lambda i, *m, nd=len(a.shape): (0,) * nd) for a in arrays]


def pack_first(me, w, vecs, upb):
    r, W = w.shape
    gw = W // 3 // GROUPS
    args = [w, upb[None]] + [v[None] for v in vecs]
    outs = [S((3 * r + (VROWS if g == 0 else 0), gw), bf16) for g in range(GROUPS)]
    return pl.pallas_call(
        pack_first_body,
        grid_spec=pltpu.PrefetchScalarGridSpec(num_scalar_prefetch=1, grid=(1,), in_specs=once(*args), out_specs=once(*outs)),
        out_shape=outs, compiler_params=cp(), name="pack_first", cost_estimate=cost(0, 4 * w.size),
    )(me, *args)


def pack_rest_body(wo, wu, wd, out):
    r, D = wo.shape
    out[:r, :] = wo[...]
    for j in range(wu.shape[1] // D):
        out[(1 + j) * r : (2 + j) * r, :] = wu[:, j * D : (j + 1) * D]
    out[(1 + wu.shape[1] // D) * r :, :] = wd[...]


def pack_rest(wo, wu, wd):
    D = wo.shape[1]
    out = S(((wo.size + wu.size + wd.size) // D, D), bf16)
    return pl.pallas_call(
        pack_rest_body, grid=(1,), in_specs=once(wo, wu, wd), out_specs=once(out)[0],
        out_shape=out, compiler_params=cp(), name="pack_rest", cost_estimate=cost(0, 4 * wu.size),
    )(wo, wu, wd)


def own_lanes(tiles, me, w):
    pick = lambda i: sum(jnp.where(i == t, a, jnp.zeros_like(a)) for t, a in enumerate(tiles))
    if w >= LANES:
        q = w // LANES
        return jnp.concatenate([pick(me * q + c) for c in range(q)], axis=1)
    per = LANES // w
    x = pick(me // per)
    off = me % per
    return sum(jnp.where(off == o, x[:, o * w : (o + 1) * w], 0.0) for o in range(per))


def rows_of(lo, hi, a, b):
    h = lo.shape[0]
    if b <= h:
        return lo[a:b, :]
    if a >= h:
        return hi[a - h : b - h, :]
    return jnp.concatenate([lo[a:h, :], hi[: b - h, :]], axis=0)


def finish_rest_body(r, rf, n, ids, s, o, down, up, out, upb, *vecs):
    D = out.shape[1]
    nf = up.shape[1] // D

    def run(lo, hi):
        f = lambda a, b: rows_of(lo, hi, a, b).astype(f32)
        down[...] = f(0, rf)
        out[...] = f(rf, rf + r)
        for j in range(nf):
            up[:, j * D : (j + 1) * D] = f(rf + (j + 1) * r, rf + (j + 2) * r)
        b = rf + (nf + 1) * r
        v = f(b, b + VROWS)
        me = ids[0]
        tiles = [v[0:8, t * LANES : (t + 1) * LANES] for t in range(D // LANES)]
        x = own_lanes(tiles, me, r)
        for q, ref in enumerate(vecs):
            ref[...] = x[q : q + 1, :]
        tiles = [v[4 + q : 5 + q, t * LANES : (t + 1) * LANES] for q in range(nf) for t in range(D // LANES)]
        upb[...] = own_lanes(tiles, me, nf * D // n)

    @pl.when(ids[1] == 0)
    def _():
        run(s, o)

    @pl.when(ids[1] == 1)
    def _():
        run(o, s)


def finish_rest(ids, s, o, r, rf, nf, n):
    D = s.shape[1]
    row1 = lambda w: S((1, w), f32)
    return pl.pallas_call(
        functools.partial(finish_rest_body, r, rf, n),
        in_specs=[pl.BlockSpec(memory_space=pltpu.SMEM)] + whole(2), out_specs=whole(8),
        out_shape=[S((rf, D), f32), S((r, nf * D), f32), S((r, D), f32), row1(nf * D // n)] + [row1(r)] * 4,
        compiler_params=pltpu.CompilerParams(vmem_limit_bytes=16 << 20), name="finish_rest", cost_estimate=cost(0, 8 * s.size),
    )(ids, s, o)


def finish_first_body(ids, s, o, w, gain, bias, qkv, gg, gb, qb, vb):
    r, W = w.shape
    D = s.shape[1]

    def run(lo, hi):
        f = lambda a, b: rows_of(lo, hi, a, b).astype(f32)
        v = f(3 * r, 3 * r + VROWS)
        nt = D // LANES
        accg = accb = jnp.zeros((r, LANES), f32)
        col = lambda g: jnp.concatenate([g[...].astype(f32), jnp.zeros((7, r), f32)], axis=0).T[:, 0:1]
        cg, cb = col(gain), col(bias)
        for j in range(3):
            m = f(j * r, (j + 1) * r)
            sq = v[j : j + 1, :]
            ww = w[:, j * D : (j + 1) * D].astype(f32)
            qkv[:, j * D : (j + 1) * D] = cg * m + cb * sq
            pg, pb = ww * m, ww * sq
            accg = accg + sum(pg[:, t * LANES : (t + 1) * LANES] for t in range(nt))
            accb = accb + sum(pb[:, t * LANES : (t + 1) * LANES] for t in range(nt))
        gg[...] = jnp.sum(accg.T, axis=0, keepdims=True)
        gb[...] = jnp.sum(accb.T, axis=0, keepdims=True)
        x = own_lanes([v[0:8, t * LANES : (t + 1) * LANES] for t in range(nt)], ids[0], r)
        qb[...] = x[0:1, :]
        vb[...] = x[2:3, :]

    @pl.when(ids[1] == 0)
    def _():
        run(s, o)

    @pl.when(ids[1] == 1)
    def _():
        run(o, s)


def finish_first(ids, s, o, w, gain, bias):
    r, W = w.shape
    return pl.pallas_call(
        finish_first_body,
        in_specs=[pl.BlockSpec(memory_space=pltpu.SMEM)] + whole(5), out_specs=whole(5),
        out_shape=[S((r, W), f32)] + [S((1, r), f32)] * 4,
        compiler_params=pltpu.CompilerParams(vmem_limit_bytes=16 << 20), name="finish_first", cost_estimate=cost(0, 8 * w.size),
    )(ids, s, o, w, gain[None], bias[None])


def pull(me, refs, meta, segs, sems):
    copies = []
    for ref, (k, r0) in zip(refs, meta):
        s = jnp.bitwise_xor(me, k)
        r1 = r0 + ref.shape[0]
        for a, c, dst, lanes in segs:
            lo, hi = max(a, r0), min(a + c, r1)
            if lo < hi:
                src = ref.at[pl.ds(lo - r0, hi - lo), pl.ds(0, lanes)]
                copies.append(pltpu.make_async_copy(src, dst(s, lo - a, hi - lo), sems.at[len(copies)]))
    return copies


def mult(x, m):
    return pl.multiple_of(x, m)


def weight_segs(w, r):
    gw = w.shape[1] // 3
    seg = lambda j: (j * r, r, lambda s, o, c: w.at[pl.ds(mult(s * r + o, 16), c), pl.ds(j * gw, gw)], gw)
    return [seg(j) for j in range(3)]


def start_body(tok, step, nx, xht):
    n, _ = norm(tok[...].astype(f32) + step[...].astype(f32))
    nx[...] = n
    xht[...] = n.astype(bf16).T


def start(tok, step, bm=256):
    T, D = tok.shape
    rows = pl.BlockSpec((bm, D), lambda i: (i, 0))
    return pl.pallas_call(
        start_body, grid=(T // bm,),
        in_specs=[rows, pl.BlockSpec((1, D), lambda i: (0, 0))], out_specs=[rows, pl.BlockSpec((D, bm), lambda i: (0, i))],
        out_shape=[S((T, D), f32), S((D, T), bf16)], compiler_params=cp(), name="start", cost_estimate=cost(20 * T * D, 8 * T * D),
    )(tok, step)


def front_body(scale, n, meta, me, nx, *refs):
    np_ = len(meta)
    pieces = refs[:np_]
    kv, qkvt, wout, vec, upb, nv, h, w, vbuf, sems, own = refs[np_:]
    T, D = nv.shape
    r = D // n
    FF = upb.shape[1]
    i = pl.program_id(0)
    cw = kv.shape[2]
    per_j = D // cw
    segs = [(3 * r, VROWS, lambda s, o, c: vbuf.at[s, pl.ds(o, c)], LANES)] + weight_segs(w, r)
    load = pltpu.make_async_copy(nx, nv, own.at[0])
    save = pltpu.make_async_copy(w, wout, own.at[1])

    @pl.when(i == 0)
    def _():
        cs = pull(me[0], pieces, meta, segs, sems)
        for c in cs:
            c.start()
        load.start()
        for c in cs:
            c.wait()
        save.start()
        per = LANES // r
        tiles = [sum(vbuf[s, 0:8, :].astype(f32) for s in range(t * per, (t + 1) * per)) for t in range(D // LANES)]
        vec[...] = jnp.concatenate(tiles, axis=1)
        wu = FF // n
        if wu >= LANES:
            rows = [vbuf[s, 8 + q : 9 + q, :].astype(f32) for s in range(n) for q in range(wu // LANES)]
        else:
            per = LANES // wu
            rows = [sum(vbuf[s, 8:9, :].astype(f32) for s in range(t * per, (t + 1) * per)) for t in range(FF // LANES)]
        upb[...] = jnp.concatenate(rows, axis=1)
        load.wait()
        v = vec[...]
        h[...] = (nv[...] * row(v, 0) + row(v, 1)).astype(bf16)

    cols = pl.ds(mult(i * cw, 128), cw)
    y = dot(h[...], w[:, cols])
    here = pl.ds(mult((i % per_j) * cw, 128), cw)
    kind = i // per_j
    y = (y + jnp.where(kind == 0, vec[2:3, here], jnp.where(kind == 2, vec[3:4, here], 0.0))).astype(bf16)
    kv[0] = y
    qkvt[0] = jnp.where(kind == 0, y * bf16(scale), y).T

    @pl.when(i == pl.num_programs(0) - 1)
    def _():
        save.wait()


S = jax.ShapeDtypeStruct
ANY = pl.BlockSpec(memory_space=pl.ANY)


def cost(flops, nbytes, tr=0):
    return pl.CostEstimate(flops=int(flops), bytes_accessed=int(nbytes), transcendentals=int(tr))


def front(me, nx, pieces, n, FF, cw=256):
    T, D = nx.shape
    scale = 1.0 / math.sqrt(D // HEADS)
    meta = tuple((k, r0) for k, r0, _ in pieces)
    q = D // cw
    keep = lambda *sh: pl.BlockSpec(sh, lambda i, m: (0,) * len(sh))
    rest = lambda i: jnp.maximum(i - q, 0)
    V = pltpu.VMEM
    return pl.pallas_call(
        functools.partial(front_body, scale, n, meta),
        grid_spec=pltpu.PrefetchScalarGridSpec(
            num_scalar_prefetch=1, grid=(3 * q,),
            in_specs=[ANY] * (1 + len(pieces)),
            out_specs=[pl.BlockSpec((1, T, cw), lambda i, m: (rest(i) // q, 0, rest(i) % q)), pl.BlockSpec((1, cw, T), lambda i, m: (i // q, i % q, 0)), ANY, keep(8, D), keep(1, FF)],
            scratch_shapes=[V((T, D), f32), V((T, D), bf16), V((D, 3 * D), bf16), V((n, VROWS, LANES), bf16), pltpu.SemaphoreType.DMA((8 * len(pieces),)), pltpu.SemaphoreType.DMA((2,))]),
        out_shape=[S((2, T, D), bf16), S((3, D, T), bf16), S((D, 3 * D), bf16), S((8, D), f32), S((1, FF), f32)],
        compiler_params=cp(), name="front", cost_estimate=cost(6 * T * D * D, 12 * T * D),
    )(me, nx, *[a for _, _, a in pieces])


def attn_fwd_body(HD, bi, CR, ln, k, qt, vt, *refs):
    et, mixed, mixedt, mixedf, linv, scr, ka = refs[-7:]
    T, PW = k.shape
    n = ln[0]
    rid = lax.broadcasted_iota(jnp.int32, (PW, bi), 0)
    lane = lax.broadcasted_iota(jnp.int32, (T, PW), 1)
    rows = lax.broadcasted_iota(jnp.int32, (T, PW), 0)
    ka[:, :PW] = k[...]
    ka[:, PW:] = jnp.where((lane == 0) & (rows >= n), f32(-1e30), f32(0)).astype(bf16)
    ones = jnp.where(rid == 0, f32(1), f32(0)).astype(bf16)
    va = [jnp.concatenate([vt[h * HD : (h + 1) * HD, :], jnp.ones((16, T), bf16)], axis=0) for h in range(2)]
    tasks = [(b, h) for b in range(T // bi) for h in range(2)]
    nch = T // CR

    def query(t):
        b, h = tasks[t]
        q = qt[:, b * bi : (b + 1) * bi]
        return jnp.concatenate([jnp.where(rid // HD == h, q, jnp.zeros_like(q)), ones], axis=0)

    def score(t, c, q):
        s = dot(ka[c * CR : (c + 1) * CR, :], q)
        scr[t % 2, c * CR : (c + 1) * CR, :] = s
        return jnp.max(s, axis=0, keepdims=True)

    q = query(0)
    m = functools.reduce(jnp.maximum, [score(0, c, q) for c in range(nch)])
    half = None
    for t, (b, h) in enumerate(tasks):
        sl = slice(b * bi, (b + 1) * bi)
        more = t + 1 < len(tasks)
        if more:
            q = query(t + 1)
        nxt = []
        for c in range(nch):
            cs = slice(c * CR, (c + 1) * CR)
            if more:
                nxt.append(score(t + 1, c, q))
            et[h, cs, sl] = jnp.exp(scr[t % 2, cs, :] - m).astype(bf16)
        o = dot(va[h], et[h, :, sl])
        if more:
            m = functools.reduce(jnp.maximum, nxt)
        inv = 1.0 / o[HD : HD + 1, :]
        linv[h : h + 1, sl] = inv
        o = o[:HD, :] * inv
        if h == 0:
            half = o
        else:
            mt = jnp.concatenate([half, o], axis=0)
            mixedf[:, sl] = mt
            mt = mt.astype(bf16)
            mixedt[:, sl] = mt
            mixed[sl, :] = mt.T


def attn_fwd(ln, kv, qkvt, p0, cnt, prev):
    _, T, D = kv.shape
    HD = D // HEADS
    PW = 2 * HD
    NP = D // PW
    bi = min(512, T)
    prev = list(prev)
    return pl.pallas_call(
        functools.partial(attn_fwd_body, HD, bi, min(256, T)),
        grid_spec=pltpu.PrefetchScalarGridSpec(
            num_scalar_prefetch=1, grid=(cnt,),
            in_specs=[pl.BlockSpec((None, T, PW), lambda p, r: (0, 0, p0 + p)), pl.BlockSpec((None, PW, T), lambda p, r: (0, p0 + p, 0)), pl.BlockSpec((None, PW, T), lambda p, r: (2, p0 + p, 0))] + [ANY] * len(prev),
            out_specs=[pl.BlockSpec((2, T, T), lambda p, r: (p0 + p, 0, 0)), pl.BlockSpec((T, PW), lambda p, r: (0, p0 + p)), pl.BlockSpec((PW, T), lambda p, r: (p0 + p, 0)), pl.BlockSpec((PW, T), lambda p, r: (p0 + p, 0)), pl.BlockSpec((None, 8, T), lambda p, r: (p0 + p, 0, 0))],
            scratch_shapes=[pltpu.VMEM((2, T, bi), f32), pltpu.VMEM((T, 2 * PW), bf16)]),
        out_shape=[S((HEADS, T, T), bf16), S((T, D), bf16), S((D, T), bf16), S((D, T), f32), S((NP, 8, T), f32)],
        input_output_aliases={4 + i: i for i in range(len(prev))},
        compiler_params=cp(), name="attn_fwd", cost_estimate=cost(cnt * 2 * 8 * T * T * 128, cnt * 2 * T * T * 2, cnt * 2 * T * T),
    )(ln, kv, qkvt, qkvt, *prev)


G0 = math.sqrt(2 / math.pi)


def bit_reverse(x, m):
    y = jnp.zeros_like(x)
    for t in range(m):
        y = y | (((x >> t) & 1) << (m - 1 - t))
    return y


def push(me, n, s, src, keep, send, row0, sem, reverse=False):
    k = jnp.bitwise_xor(me, s)
    p = k >> 1
    if reverse:
        p = bit_reverse(p, (n // 2).bit_length() - 1)
    put = lambda dst: pltpu.make_async_copy(src, dst.at[p, pl.ds(row0, src.shape[0])], sem)

    @pl.when(k & 1 == 0)
    def _():
        put(keep).start()

    @pl.when(k & 1 == 1)
    def _():
        put(send).start()


def ffn_body(n, meta, ch, ln, me, tok, step, vec, upb, cot, mixed, mixedt, *refs):
    np_ = len(meta)
    pieces = refs[:np_]
    out, gx1, gmt, keep, send, wo, wu, wd, act, gup, h2t, gdt, gattn, sums, upsum, dn, up, gwo, vr, mtv, sems, psems = refs[np_:]
    i = pl.program_id(0)
    bm, D = tok.shape
    FF = wu.shape[1]
    r = D // n
    rf = FF // n
    nf = FF // D
    i0 = me[0]
    ro = pl.ds(mult(i * bm, 128), bm)
    first = i == 0
    seg = lambda j: (r + j * r, r, lambda s, o, c: wu.at[pl.ds(mult(s * r + o, 16), c), pl.ds(j * D, D)], D)
    seg_o = [(0, r, lambda s, o, c: wo.at[pl.ds(mult(s * r + o, 16), c)], D)]
    seg_u = [seg(j) for j in range(nf)]
    seg_d = [(r + r * nf, rf, lambda s, o, c: wd.at[pl.ds(mult(s * rf + o, 16), c)], D)]
    q = sems.shape[0] // 4
    parts = [(seg_o, sems.at[pl.ds(0, q)]), (seg_d, sems.at[pl.ds(q, q)]), (seg_u, sems.at[pl.ds(2 * q, 2 * q)])]
    load = pltpu.make_async_copy(mixedt, mtv, psems.at[psems.shape[0] - 1])

    @pl.when(first)
    def _():
        for sg, sm in parts:
            for c in pull(i0, pieces, meta, sg, sm):
                c.start()
        load.start()
        sums[...] = jnp.zeros_like(sums)
        upsum[...] = jnp.zeros_like(upsum)
        for c in pull(i0, pieces, meta, *parts[0]):
            c.wait()

    v = vec[...]
    x1 = tok[...].astype(f32) + step[...].astype(f32) + dot(mixed[...], wo[...]) + row(v, 4)
    nx, rr = norm(x1)
    h2 = (nx * row(v, 5) + row(v, 6)).astype(bf16)
    live = (lax.broadcasted_iota(jnp.int32, (bm, 1), 0) + i * bm) < ln[0]
    gd = jnp.where(live, cot[...], jnp.zeros_like(cot))
    acc = x1 + row(v, 7)
    gh = None
    nc = FF // ch
    sl = [slice(c * ch, (c + 1) * ch) for c in range(nc)]
    lead = lambda c: (dot(h2, wu[:, sl[c]]), dot_t(gd, wd[sl[c], :]))
    h2t[:, ro] = h2.T
    gdt[:, ro] = gd.T

    @pl.when(first)
    def _():
        for sg, sm in parts[1:]:
            for c in pull(i0, pieces, meta, sg, sm):
                c.wait()

    nxt = lead(0)
    for c in range(nc):
        u, ga = nxt
        nxt = lead(c + 1) if c + 1 < nc else None
        u = u + upb[:, sl[c]]
        u2 = u * u
        t = jnp.tanh(u * (f32(G0) + f32(G0 * 0.044715) * u2))
        half = 0.5 + 0.5 * t
        a = (u * half).astype(bf16)
        act[ro, sl[c]] = a
        dg = half + u * (half * (1.0 - half)) * (f32(2 * G0) + f32(6 * 0.044715 * G0) * u2)
        gu = (ga * dg).astype(bf16)
        gup[ro, sl[c]] = gu
        upsum[:, sl[c]] += jnp.sum(gu.astype(f32), axis=0, keepdims=True)
        acc = acc + dot(a, wd[sl[c], :])
        p = dot_t(gu, wu[:, sl[c]])
        gh = p if gh is None else gh + p
    out[...] = jnp.where(live, acc, 0.0).astype(bf16)
    gn = gh * row(v, 5)
    gx = gd.astype(f32) + rr * (gn - jnp.mean(gn, axis=-1, keepdims=True) - nx * jnp.mean(gn * nx, axis=-1, keepdims=True))
    gx1[...] = gx
    gab = gx.astype(bf16)
    gattn[ro, :] = gab
    gmt[...] = dot_t(gab, wo[...]).astype(bf16).T
    s_ = lambda a: jnp.sum(a.astype(f32), axis=0, keepdims=True)
    sums[...] += jnp.concatenate([s_(gab), s_(gh * nx), s_(gh), s_(gd), jnp.zeros((4, D), f32)], axis=0)

    @pl.when(i == pl.num_programs(0) - 1)
    def _():
        per = D // rf
        o_out, o_up, o_vec = rf, rf + r, rf + (nf + 1) * r
        for j in range(nf):
            dn[j] = dot(gdt[...], act[:, j * D : (j + 1) * D]).astype(bf16).T
            for t in range(per):
                push(i0, n, j * per + t, dn.at[j, pl.ds(t * rf, rf)], keep, send, 0, psems.at[j * per + t])
            up[j] = dot(h2t[...], gup[:, j * D : (j + 1) * D]).astype(bf16)
            for s in range(n):
                push(i0, n, s, up.at[j, pl.ds(s * r, r)], keep, send, o_up + j * r, psems.at[n * (1 + j) + s], True)
        load.wait()
        gwo[...] = dot(mtv[...], gattn[...]).astype(bf16)
        vr[...] = jnp.concatenate([sums[0:4, :]] + [upsum[:, c * D : (c + 1) * D] for c in range(nf)] + [jnp.zeros((VROWS - 4 - nf, D), f32)], axis=0).astype(bf16)
        b = n * (1 + nf)
        for s in range(n):
            push(i0, n, s, gwo.at[pl.ds(s * r, r)], keep, send, o_out, psems.at[b + s])
            push(i0, n, s, vr, keep, send, o_vec, psems.at[b + n + s], True)
        done = lambda src, q: pltpu.make_async_copy(src, keep.at[0, pl.ds(0, src.shape[0])], psems.at[q]).wait()
        for s in range(n):
            done(dn.at[0, pl.ds(0, rf)], s)
            for c in range(nf):
                done(up.at[0, pl.ds(0, r)], n * (1 + c) + s)
            done(gwo.at[pl.ds(0, r)], b + s)
            done(vr, b + n + s)


def ffn(ln, me, tok, step, vec, upb, cot, mixed, mixedt, pieces, n):
    T, D = tok.shape
    FF = upb.shape[1]
    bm = min(512, T)
    nf = FF // D
    r = D // n
    meta = tuple((k, r0) for k, r0, _ in pieces)
    full = lambda a: pl.BlockSpec(a.shape, lambda i, l, m: (0,) * a.ndim)
    rows = pl.BlockSpec((bm, D), lambda i, l, m: (i, 0))
    B = S((n // 2, FF // n + (nf + 1) * r + VROWS, D), bf16)
    V = pltpu.VMEM
    return pl.pallas_call(
        functools.partial(ffn_body, n, meta, min(1024, FF)),
        grid_spec=pltpu.PrefetchScalarGridSpec(
            num_scalar_prefetch=2, grid=(T // bm,),
            in_specs=[rows, full(step), full(vec), full(upb), rows, rows, ANY] + [ANY] * len(pieces),
            out_specs=[rows, rows, pl.BlockSpec((D, bm), lambda i, l, m: (0, i)), ANY, ANY],
            scratch_shapes=[V((D, D), bf16), V((D, FF), bf16), V((FF, D), bf16), V((T, FF), bf16), V((T, FF), bf16), V((D, T), bf16), V((D, T), bf16), V((T, D), bf16), V((8, D), f32), V((1, FF), f32), V((nf, D, D), bf16), V((nf, D, D), bf16), V((D, D), bf16), V((VROWS, D), bf16), V((D, T), bf16), pltpu.SemaphoreType.DMA((16 * len(pieces),)), pltpu.SemaphoreType.DMA((n * (nf + 3) + 1,))]),
        out_shape=[S((T, D), bf16), S((T, D), f32), S((D, T), bf16), B, B],
        compiler_params=cp(), name="ffn", cost_estimate=cost(2 * T * D * (6 * FF + 3 * D), 16 * T * D, T * FF),
    )(ln, me, tok, step, vec, upb, cot, mixed, mixedt, *[a for _, _, a in pieces])


def attn_bwd_body(HD, scale, CR, v, kt, qt, gt, mt, linv, et, *refs):
    gq, ds = refs[-2:]
    T = v.shape[0]
    rid = lax.broadcasted_iota(jnp.int32, gt.shape, 0) // HD
    g = gt[...].astype(f32)
    q = qt[...]
    gv = gk = None
    for h in range(2):
        hs = slice(h * HD, (h + 1) * HD)
        gs = (g * linv[h : h + 1, :]).astype(bf16)
        gm = jnp.where(rid == h, gs, jnp.zeros_like(gs))
        dl = jnp.sum(gs[hs, :].astype(f32) * mt[hs, :], axis=0, keepdims=True)
        for c in range(T // CR):
            cs = slice(c * CR, (c + 1) * CR)
            ds[h, cs, :] = (et[h, cs, :].astype(f32) * (dot(v[cs, :], gm) - dl)).astype(bf16)
        a = dot(et[h], gm.T)
        b = dot(ds[h], jnp.where(rid == h, q, jnp.zeros_like(q)).T)
        gv = a if gv is None else gv + a
        gk = b if gk is None else gk + b
        gq[0, hs, :] = (dot(kt[hs, :], ds[h]) * scale).astype(bf16)
    gq[2] = gv.astype(bf16).T
    gq[1] = gk.astype(bf16).T


def attn_bwd(kv, qkvt, gmt, mixedf, linv, et, p0, cnt, prev):
    _, T, D = kv.shape
    HD = D // HEADS
    PW = 2 * HD
    NP = D // PW
    prev = list(prev)
    pr = pl.BlockSpec((PW, T), lambda p: (p0 + p, 0))
    of = lambda j: pl.BlockSpec((None, PW, T), lambda p: (j, p0 + p, 0))
    return pl.pallas_call(
        functools.partial(attn_bwd_body, HD, 1.0 / math.sqrt(HD), min(256, T)),
        grid=(cnt,),
        scratch_shapes=[pltpu.VMEM((2, T, T), bf16)],
        in_specs=[pl.BlockSpec((None, T, PW), lambda p: (1, 0, p0 + p)), of(1), of(0), pr, pr, pl.BlockSpec((None, 8, T), lambda p: (p0 + p, 0, 0)), pl.BlockSpec((2, T, T), lambda p: (p0 + p, 0, 0))] + [ANY] * len(prev),
        out_specs=pl.BlockSpec((3, PW, T), lambda p: (0, p0 + p, 0)),
        out_shape=S((3, D, T), bf16),
        input_output_aliases={7: 0} if prev else {},
        compiler_params=cp(), name="attn_bwd", cost_estimate=cost(cnt * 2 * 16 * T * T * 128, cnt * 2 * T * T * 2),
    )(kv, qkvt, qkvt, gmt, mixedf, linv, et, *prev)


def wqkv_body(n, me, xht, g, keep, send, res, vr, sems):
    j = pl.program_id(0)
    D = g.shape[0]
    r = D // n
    i0 = me[0]
    x = jnp.concatenate([xht[...], jnp.ones((16, xht.shape[1]), bf16)], axis=0)
    y = dot_t(x, g[...]).astype(bf16)
    res[j] = y[:D]
    vr[...] = jnp.where(lax.broadcasted_iota(jnp.int32, vr.shape, 0) == j, y[D:], jnp.where(j == 0, jnp.zeros_like(y[D:]), vr[...]))
    for s in range(n):
        push(i0, n, s, res.at[j, pl.ds(s * r, r)], keep, send, mult(j * r, 16), sems.at[j * n + s])

    @pl.when(j == 2)
    def _():
        for s in range(n):
            push(i0, n, s, vr, keep, send, 3 * r, sems.at[3 * n + s])
        for s in range(n):
            for q in range(3):
                pltpu.make_async_copy(res.at[0, pl.ds(0, r)], keep.at[0, pl.ds(0, r)], sems.at[q * n + s]).wait()
            pltpu.make_async_copy(vr, keep.at[0, pl.ds(0, VROWS)], sems.at[3 * n + s]).wait()


def wqkv(me, xht, g, n):
    D, T = xht.shape
    A = S((n // 2, 3 * (D // n) + VROWS, D), bf16)
    return pl.pallas_call(
        functools.partial(wqkv_body, n),
        grid_spec=pltpu.PrefetchScalarGridSpec(
            num_scalar_prefetch=1, grid=(3,),
            in_specs=[pl.BlockSpec((D, T), lambda j, m: (0, 0)), pl.BlockSpec((None, D, T), lambda j, m: (j, 0, 0))],
            out_specs=[ANY] * 2,
            scratch_shapes=[pltpu.VMEM((3, D, D), bf16), pltpu.VMEM((VROWS, D), bf16), pltpu.SemaphoreType.DMA((4 * n,))]),
        out_shape=[A, A],
        compiler_params=cp(), name="wqkv", cost_estimate=cost(6 * T * D * D, 10 * T * D),
    )(me, xht, g)


def back_body(tok, step, vec, g, gx1, *refs):
    ws, tg = refs[:-1], refs[-1]
    D = tok.shape[1]
    gw = D // GROUPS
    x = tok[...].astype(f32) + step[...].astype(f32)
    nx, rr = norm(x)
    gt = sum(dot(w[:, j * gw : (j + 1) * gw], g[j, q * gw : (q + 1) * gw, :]) for q, w in enumerate(ws) for j in range(3))
    gn = gt.T * row(vec[...], 0)
    tg[...] = gx1[...] + rr * (gn - jnp.mean(gn, axis=-1, keepdims=True) - nx * jnp.mean(gn * nx, axis=-1, keepdims=True))


def back(tok, step, vec, ws, g, gx1, bm=512):
    T, D = tok.shape
    full = lambda a: pl.BlockSpec(a.shape, lambda i: (0,) * a.ndim)
    rows = pl.BlockSpec((bm, D), lambda i: (i, 0))
    return pl.pallas_call(
        back_body, grid=(T // bm,),
        in_specs=[rows, full(step), full(vec), pl.BlockSpec((3, D, bm), lambda i: (0, 0, i)), rows] + [full(w) for w in ws],
        out_specs=rows, out_shape=S((T, D), f32), compiler_params=cp(), name="back", cost_estimate=cost(6 * T * D * D, 14 * T * D),
    )(tok, step, vec, g, gx1, *ws)


def shards(tokens, step_embed, lengths, cotangent, ln1_gain, ln1_bias, qkv_weight, q_bias, v_bias, out_weight, out_bias, ln2_gain, ln2_bias, up_weight, up_bias, down_weight, down_bias):
    n = lax.axis_size("shard")
    me = lax.axis_index("shard").astype(jnp.int32)
    mes = me[None]
    tok, cot, step = tokens[0], cotangent[0], step_embed
    T, D = tok.shape
    r = D // n
    FF = up_bias.shape[0] * n
    nc = FF // D
    rf = FF // n
    packs = pack_first(mes, qkv_weight, [ln1_gain, ln1_bias, q_bias, v_bias, out_bias, ln2_gain, ln2_bias, down_bias], up_bias)
    pack2 = pack_rest(out_weight, up_weight, down_weight)
    NP = HEADS // 2
    nx, xht = start(tok, step)
    pieces = gather_direct(packs[0], n, xht, pack2)
    kv, qkvt, w, vec, upb = front(mes, nx, pieces, n, FF)
    fw = attn_fwd(lengths, kv, qkvt, 0, NP // 2, [])
    fw2 = attn_fwd(lengths, kv, qkvt, NP // 2, NP // 2, fw)
    et, mixed, mixedt, mixedf, linv = fw2
    pieces2 = gather_forward(after(pack2, *[a for _, _, a in pieces[1:]]), n, fw[4], linv)
    out, gx1, gmt, keep, send = ffn(lengths, mes, tok, step, vec, upb, cot, mixed, mixedt, pieces2, n)
    bwd = lambda p, c, g, *deps: attn_bwd(kv, qkvt, after(gmt, *deps) if deps else gmt, mixedf, linv, et, p, c, g)
    ra = rf + r
    got = swap(send, 1)
    g = bwd(0, 1, [])
    got = after(got, g)
    h = n // 4
    add = lambda a, b, k: add16(a[k], b[k])
    rows_a, rows_b = slice(0, ra), slice(ra, None)
    lo, hi = slice(0, h), slice(h, None)
    ka, xa, kb, xb = [add(keep, got, k) for k in ((lo, rows_a), (hi, rows_a), (lo, rows_b), (hi, rows_b))]
    g = bwd(1, NP - 1, [g], ka, xa, kb, xb)
    m = (n // 2).bit_length() - 1
    ga, gb = swap(xa, 2 << (m - 1)), swap(xb, 2)
    for t in range(1, m):
        dep = g if t == 1 else keep
        ga, gb, _ = lax.optimization_barrier((ga, gb, dep))
        h //= 2
        lo, hi = slice(0, h), slice(h, None)
        ka, xa = add(ka, ga, lo), add(ka, ga, hi)
        kb, xb = add(kb, gb, lo), add(kb, gb, hi)
        ga, gb = swap(xa, 2 << (m - 1 - t)), swap(xb, 2 << t)
        if t == 1:
            keep, send = wqkv(mes, after(xht, ka, xa, kb, xb), g, n)
    got = swap(send, 1)
    p2 = [add16(keep[k], got[k]) for k in range(n // 2)]
    far2 = spread(p2)
    ga, gb, _ = lax.optimization_barrier((ga, gb, keep))
    got = swap(send, 1)
    p2 = [add16(keep[k], got[k]) for k in range(n // 2)]
    far2 = spread(p2)
    own1 = jnp.concatenate([add16(ka, ga)[0], add16(kb, gb)[0]], axis=0)
    m1, o1, x1 = rep_half(own1)
    z1 = add16(m1, after(o1, *p2[1:]))
    tg = back(tok, after(step, z1, *p2[1:]), vec, [w], g, gx1)
    own2 = total(p2[0], [after(a, tg) for a in far2])
    m2, o2, x2 = rep_half(own2)
    steps = rep_steps()
    z2 = None if steps else add16(m2, o2)
    for b in steps:
        z1 = add16(z1, after(rep_perm(z1, b), x2))
        if z2 is None:
            z2 = add16(m2, after(o2, z1))
        pz = rep_perm(z2, b)
        z2 = add16(z2, after(pz, z1))
    o1, o2 = rep_perm(z1, 1), rep_perm(z2, 1)
    ids = jnp.stack([me, (lax.axis_index("rep") % 2).astype(jnp.int32)])
    g_down, g_up, g_out, g_upb, g_ob, g_g2, g_b2, g_db = finish_rest(ids, z1, o1, r, rf, nc, n)
    g_qkv, g_g1, g_b1, g_q, g_v = finish_first(ids, z2, after(o2, g_out), qkv_weight, ln1_gain, ln1_bias)
    flat = lambda a: a.reshape(-1)
    return (out[None], tg[None], flat(g_g1), flat(g_b1), g_qkv, flat(g_q), flat(g_v), g_out, flat(g_ob), flat(g_g2), flat(g_b2), g_up, flat(g_upb), g_down, flat(g_db))


def solution(mesh):
    from jax.sharding import PartitionSpec as P

    in_specs = (
        P(("rep", "shard"), None, None),
        P(("rep", "shard"), None),
        P(("rep", "shard")),
        P(("rep", "shard"), None, None),
        P("shard"),
        P("shard"),
        P("shard", None),
        P("shard"),
        P("shard"),
        P("shard", None),
        P("shard"),
        P("shard"),
        P("shard"),
        P("shard", None),
        P("shard"),
        P("shard", None),
        P("shard"),
    )
    out_specs = (
        P(("rep", "shard"), None, None),
        P(("rep", "shard"), None, None),
        P("shard"),
        P("shard"),
        P("shard", None),
        P("shard"),
        P("shard"),
        P("shard", None),
        P("shard"),
        P("shard"),
        P("shard"),
        P("shard", None),
        P("shard"),
        P("shard", None),
        P("shard"),
    )
    return jax.shard_map(shards, mesh=mesh, in_specs=in_specs, out_specs=out_specs, check_vma=False)
```

```python
import functools, math
import jax, jax.numpy as jnp
from jax import lax
from jax.experimental import pallas as pl
from jax.experimental.pallas import tpu as pltpu

f32 = jnp.float32
bf16 = jnp.bfloat16
EPS = 1e-05
HEADS = 8

def dot(a, b):
    return jnp.dot(a, b, preferred_element_type=f32)

def dot_t(a, b):
    return lax.dot_general(a, b, (((1,), (1,)), ((), ())), preferred_element_type=f32)

def cp(n=1, vmem=100):
    return pltpu.CompilerParams(dimension_semantics=("arbitrary",) * n, vmem_limit_bytes=60 * 1024 * 1024)

def norm(x):
    c = x - jnp.mean(x, axis=-1, keepdims=True)
    r = lax.rsqrt(jnp.mean(c * c, axis=-1, keepdims=True) + EPS)
    return c * r, r

def row(v, i):
    return v[i : i + 1, :].astype(f32)


VROWS = 16
LANES = 128


def xor_perm(n, k):
    return [(i, i ^ k) for i in range(n)]


def rep_perm(x, b):
    return lax.ppermute(x, "rep", xor_perm(lax.axis_size("rep"), b))


def swap(x, k):
    return lax.ppermute(x, "shard", xor_perm(lax.axis_size("shard"), k))


def after(x, *deps):
    return lax.optimization_barrier((x,) + deps)[0]


def gather_direct(x, n, *gate):
    out = [(0, 0, x)]
    far = [(k, swap(x, k)) for k in range(2, n, 2)]
    out += [(k, 0, after(y, *gate) if gate else y) for k, y in far]
    return out + [(k ^ 1, 0, swap(y, 1)) for k, _, y in out]


def gather_forward(x, n, gate1, gate2):
    R = x.shape[0]
    cut = R // 2 // 16 * 16
    near = []
    far = []
    halves = {}
    for k in sorted(range(2, n, 2), key=lambda k: (bin(k).count("1"), k)):
        if bin(k).count("1") == 1:
            y = after(swap(x, k), gate1)
            near.append((k, 0, y))
            halves[k] = (y[:cut], y[cut:])
        else:
            low = k & -k
            high = 1 << (k.bit_length() - 1)
            a = swap(halves[k ^ low][0], low)
            b = swap(halves[k ^ high][1], high)
            far += [(k, 0, a), (k, cut, b)]
            halves[k] = (a, b)
    near = [(0, 0, x)] + near
    late = [(k, r0, after(a, gate2)) for k, r0, a in far]
    out = near + [(k ^ 1, r0, swap(a, 1)) for k, r0, a in near]
    return out + late + [(k ^ 1, r0, swap(a, 1)) for k, r0, a in late]


def add16(a, b):
    return a + b


def spread(parts):
    return [swap(parts[k], 2 * k) for k in range(len(parts) - 1, 0, -1)]


def total(own, got):
    t = own.astype(f32)
    for a in got:
        t = t + a.astype(f32)
    return t.astype(bf16)


def rep_half(x):
    h = x.shape[0] // 2
    odd = lax.axis_index("rep") % 2
    mine = lax.dynamic_slice_in_dim(x, odd * h, h, 0)
    other = lax.dynamic_slice_in_dim(x, (1 - odd) * h, h, 0)
    return mine, rep_perm(other, 1), other


def rep_steps():
    nr = lax.axis_size("rep")
    return [b for b in (2 << i for i in range(16)) if b < nr]


def pack_body(nv, me, wo, wu, wd, upb, *refs):
    vecs, (block, out) = refs[:nv], refs[nv:]

    def spot(v):
        w_ = v.shape[1]
        if w_ >= LANES:
            return [v[:, q * LANES : (q + 1) * LANES] for q in range(w_ // LANES)]
        t = LANES // w_
        lane = lax.broadcasted_iota(jnp.int32, (1, LANES), 1)
        return [jnp.where(lane // w_ == me[0] % t, jnp.concatenate([v] * t, axis=1), jnp.zeros((1, LANES), f32))]

    rows = [a for v in vecs for a in spot(v[...].astype(f32))] + spot(upb[...].astype(f32))
    block[...] = jnp.concatenate(rows + [jnp.zeros((VROWS - len(rows), LANES), f32)], axis=0).astype(bf16)
    r, D = wo.shape
    out[:r, :] = wo[...]
    for j in range(wu.shape[1] // D):
        out[(1 + j) * r : (2 + j) * r, :] = wu[:, j * D : (j + 1) * D]
    out[(1 + wu.shape[1] // D) * r :, :] = wd[...]


def whole(n):
    return [pl.BlockSpec(memory_space=pltpu.VMEM)] * n


def once(*arrays):
    return [pl.BlockSpec(a.shape, lambda i, *m, nd=len(a.shape): (0,) * nd) for a in arrays]


def pack(me, vecs, upb, wo, wu, wd):
    args = [wo, wu, wd, upb[None]] + [v[None] for v in vecs]
    D = wo.shape[1]
    outs = [S((VROWS, LANES), bf16), S(((wo.size + wu.size + wd.size) // D, D), bf16)]
    return pl.pallas_call(
        functools.partial(pack_body, len(vecs)),
        grid_spec=pltpu.PrefetchScalarGridSpec(num_scalar_prefetch=1, grid=(1,), in_specs=once(*args), out_specs=once(*outs)),
        out_shape=outs, compiler_params=cp(), name="pack", cost_estimate=cost(0, 4 * wu.size),
    )(me, *args)


def own_lanes(tiles, me, w):
    pick = lambda i: sum(jnp.where(i == t, a, jnp.zeros_like(a)) for t, a in enumerate(tiles))
    if w >= LANES:
        q = w // LANES
        return jnp.concatenate([pick(me * q + c) for c in range(q)], axis=1)
    per = LANES // w
    x = pick(me // per)
    off = me % per
    return sum(jnp.where(off == o, x[:, o * w : (o + 1) * w], 0.0) for o in range(per))


def rows_of(lo, hi, a, b):
    h = lo.shape[0]
    if b <= h:
        return lo[a:b, :]
    if a >= h:
        return hi[a - h : b - h, :]
    return jnp.concatenate([lo[a:h, :], hi[: b - h, :]], axis=0)


def finish_rest_body(r, rf, n, ids, s, o, down, up, out, upb, *vecs):
    D = out.shape[1]
    nf = up.shape[1] // D

    def run(lo, hi):
        f = lambda a, b: rows_of(lo, hi, a, b).astype(f32)
        down[...] = f(0, rf)
        out[...] = f(rf, rf + r)
        for j in range(nf):
            up[:, j * D : (j + 1) * D] = f(rf + (j + 1) * r, rf + (j + 2) * r)
        b = rf + (nf + 1) * r
        v = f(b, b + VROWS)
        me = ids[0]
        tiles = [v[0:8, t * LANES : (t + 1) * LANES] for t in range(D // LANES)]
        x = own_lanes(tiles, me, r)
        for q, ref in enumerate(vecs):
            ref[...] = x[q : q + 1, :]
        tiles = [v[4 + q : 5 + q, t * LANES : (t + 1) * LANES] for q in range(nf) for t in range(D // LANES)]
        upb[...] = own_lanes(tiles, me, nf * D // n)

    @pl.when(ids[1] == 0)
    def _():
        run(s, o)

    @pl.when(ids[1] == 1)
    def _():
        run(o, s)


def finish_rest(ids, s, o, r, rf, nf, n):
    D = s.shape[1]
    row1 = lambda w: S((1, w), f32)
    return pl.pallas_call(
        functools.partial(finish_rest_body, r, rf, n),
        in_specs=[pl.BlockSpec(memory_space=pltpu.SMEM)] + whole(2), out_specs=whole(8),
        out_shape=[S((rf, D), f32), S((r, nf * D), f32), S((r, D), f32), row1(nf * D // n)] + [row1(r)] * 4,
        compiler_params=pltpu.CompilerParams(vmem_limit_bytes=16 << 20), name="finish_rest", cost_estimate=cost(0, 8 * s.size),
    )(ids, s, o)


def finish_first_body(ids, s, o, w, gain, bias, qkv, gg, gb, qb, vb):
    r, W = w.shape
    D = s.shape[1]

    def run(lo, hi):
        f = lambda a, b: rows_of(lo, hi, a, b).astype(f32)
        v = f(3 * r, 3 * r + VROWS)
        nt = D // LANES
        accg = accb = jnp.zeros((r, LANES), f32)
        col = lambda g: jnp.concatenate([g[...].astype(f32), jnp.zeros((7, r), f32)], axis=0).T[:, 0:1]
        cg, cb = col(gain), col(bias)
        for j in range(3):
            m = f(j * r, (j + 1) * r)
            sq = v[j : j + 1, :]
            ww = w[:, j * D : (j + 1) * D].astype(f32)
            qkv[:, j * D : (j + 1) * D] = cg * m + cb * sq
            pg, pb = ww * m, ww * sq
            accg = accg + sum(pg[:, t * LANES : (t + 1) * LANES] for t in range(nt))
            accb = accb + sum(pb[:, t * LANES : (t + 1) * LANES] for t in range(nt))
        gg[...] = jnp.sum(accg.T, axis=0, keepdims=True)
        gb[...] = jnp.sum(accb.T, axis=0, keepdims=True)
        x = own_lanes([v[0:8, t * LANES : (t + 1) * LANES] for t in range(nt)], ids[0], r)
        qb[...] = x[0:1, :]
        vb[...] = x[2:3, :]

    @pl.when(ids[1] == 0)
    def _():
        run(s, o)

    @pl.when(ids[1] == 1)
    def _():
        run(o, s)


def finish_first(ids, s, o, w, gain, bias):
    r, W = w.shape
    return pl.pallas_call(
        finish_first_body,
        in_specs=[pl.BlockSpec(memory_space=pltpu.SMEM)] + whole(5), out_specs=whole(5),
        out_shape=[S((r, W), f32)] + [S((1, r), f32)] * 4,
        compiler_params=pltpu.CompilerParams(vmem_limit_bytes=16 << 20), name="finish_first", cost_estimate=cost(0, 8 * w.size),
    )(ids, s, o, w, gain[None], bias[None])


def pull(me, refs, meta, segs, sems):
    copies = []
    for ref, (k, r0) in zip(refs, meta):
        s = jnp.bitwise_xor(me, k)
        r1 = r0 + ref.shape[0]
        for a, c, dst, lanes in segs:
            lo, hi = max(a, r0), min(a + c, r1)
            if lo < hi:
                src = ref.at[pl.ds(lo - r0, hi - lo), pl.ds(0, lanes)]
                copies.append(pltpu.make_async_copy(src, dst(s, lo - a, hi - lo), sems.at[len(copies)]))
    return copies


def mult(x, m):
    return pl.multiple_of(x, m)


def start_body(tok, step, nx, xht):
    n, _ = norm(tok[...].astype(f32) + step[...].astype(f32))
    nx[...] = n
    xht[...] = n.astype(bf16).T


def start(tok, step, bm=256):
    T, D = tok.shape
    rows = pl.BlockSpec((bm, D), lambda i: (i, 0))
    return pl.pallas_call(
        start_body, grid=(T // bm,),
        in_specs=[rows, pl.BlockSpec((1, D), lambda i: (0, 0))], out_specs=[rows, pl.BlockSpec((D, bm), lambda i: (0, i))],
        out_shape=[S((T, D), f32), S((D, T), bf16)], compiler_params=cp(), name="start", cost_estimate=cost(20 * T * D, 8 * T * D),
    )(tok, step)


def front_body(scale, n, meta, vmeta, me, nx, *refs):
    np_ = len(meta)
    pieces = refs[:np_]
    vpieces = refs[np_ : np_ + len(vmeta)]
    kv, qkvt, wout, vec, upb, nv, h, w, vbuf, sems, own = refs[np_ + len(vmeta) :]
    T, D = nv.shape
    r = D // n
    FF = upb.shape[1]
    i = pl.program_id(0)
    cw = kv.shape[2]
    per_j = D // cw
    vsegs = [(0, VROWS, lambda s, o, c: vbuf.at[s, pl.ds(o, c)], LANES)]
    wsegs = [(0, r, lambda s, o, c: w.at[pl.ds(mult(s * r + o, 16), c)], 3 * D)]
    half = sems.shape[0] // 2
    load = pltpu.make_async_copy(nx, nv, own.at[0])
    save = pltpu.make_async_copy(w, wout, own.at[1])

    @pl.when(i == 0)
    def _():
        cs = pull(me[0], vpieces, vmeta, vsegs, sems.at[pl.ds(0, half)])
        cs += pull(me[0], pieces, meta, wsegs, sems.at[pl.ds(half, half)])
        load.start()
        for c in cs:
            c.start()
        for c in cs:
            c.wait()
        save.start()
        per = LANES // r
        tiles = [sum(vbuf[s, 0:8, :].astype(f32) for s in range(t * per, (t + 1) * per)) for t in range(D // LANES)]
        vec[...] = jnp.concatenate(tiles, axis=1)
        wu = FF // n
        if wu >= LANES:
            rows = [vbuf[s, 8 + q : 9 + q, :].astype(f32) for s in range(n) for q in range(wu // LANES)]
        else:
            per = LANES // wu
            rows = [sum(vbuf[s, 8:9, :].astype(f32) for s in range(t * per, (t + 1) * per)) for t in range(FF // LANES)]
        upb[...] = jnp.concatenate(rows, axis=1)
        load.wait()
        v = vec[...]
        h[...] = (nv[...] * row(v, 0) + row(v, 1)).astype(bf16)

    cols = pl.ds(mult(i * cw, 128), cw)
    y = dot(h[...], w[:, cols])
    here = pl.ds(mult((i % per_j) * cw, 128), cw)
    kind = i // per_j
    y = (y + jnp.where(kind == 0, vec[2:3, here], jnp.where(kind == 2, vec[3:4, here], 0.0))).astype(bf16)
    kv[0] = y
    qkvt[0] = jnp.where(kind == 0, y * bf16(scale), y).T

    @pl.when(i == pl.num_programs(0) - 1)
    def _():
        save.wait()


S = jax.ShapeDtypeStruct
ANY = pl.BlockSpec(memory_space=pl.ANY)


def cost(flops, nbytes, tr=0):
    return pl.CostEstimate(flops=int(flops), bytes_accessed=int(nbytes), transcendentals=int(tr))


def front(me, nx, pieces, vpieces, n, FF, cw=512):
    T, D = nx.shape
    scale = 1.0 / math.sqrt(D // HEADS)
    meta = tuple((k, r0) for k, r0, _ in pieces)
    vmeta = tuple((k, r0) for k, r0, _ in vpieces)
    q = D // cw
    keep = lambda *sh: pl.BlockSpec(sh, lambda i, m: (0,) * len(sh))
    rest = lambda i: jnp.maximum(i - q, 0)
    V = pltpu.VMEM
    return pl.pallas_call(
        functools.partial(front_body, scale, n, meta, vmeta),
        grid_spec=pltpu.PrefetchScalarGridSpec(
            num_scalar_prefetch=1, grid=(3 * q,),
            in_specs=[ANY] * (1 + len(pieces) + len(vpieces)),
            out_specs=[pl.BlockSpec((1, T, cw), lambda i, m: (rest(i) // q, 0, rest(i) % q)), pl.BlockSpec((1, cw, T), lambda i, m: (i // q, i % q, 0)), ANY, keep(8, D), keep(1, FF)],
            scratch_shapes=[V((T, D), f32), V((T, D), bf16), V((D, 3 * D), bf16), V((n, VROWS, LANES), bf16), pltpu.SemaphoreType.DMA((8 * len(pieces),)), pltpu.SemaphoreType.DMA((2,))]),
        out_shape=[S((2, T, D), bf16), S((3, D, T), bf16), S((D, 3 * D), bf16), S((8, D), f32), S((1, FF), f32)],
        compiler_params=cp(), name="front", cost_estimate=cost(6 * T * D * D, 12 * T * D),
    )(me, nx, *[a for _, _, a in pieces + vpieces])


def attn_fwd_body(HD, bi, CR, p0, ln, k, qt, vt, *refs):
    et, mixed, mixedt, mixedf, linv, scr, ka, eb, esem = refs[-9:]
    T, PW = k.shape
    n = ln[0]
    p = pl.program_id(0)
    last = p == pl.num_programs(0) - 1
    rid = lax.broadcasted_iota(jnp.int32, (PW, bi), 0)
    lane = lax.broadcasted_iota(jnp.int32, (T, PW), 1)
    rows = lax.broadcasted_iota(jnp.int32, (T, PW), 0)
    ka[:, :PW] = k[...]
    ka[:, PW:] = jnp.where((lane == 0) & (rows >= n), f32(-1e30), f32(0)).astype(bf16)
    ones = jnp.where(rid == 0, f32(1), f32(0)).astype(bf16)
    va = [jnp.concatenate([vt[h * HD : (h + 1) * HD, :], jnp.ones((16, T), bf16)], axis=0) for h in range(2)]
    tasks = [(b, h) for b in range(T // bi) for h in range(2)]
    nch = T // CR

    def query(t):
        b, h = tasks[t]
        q = qt[:, b * bi : (b + 1) * bi]
        return jnp.concatenate([jnp.where(rid // HD == h, q, jnp.zeros_like(q)), ones], axis=0)

    def score(t, c, q):
        s = dot(ka[c * CR : (c + 1) * CR, :], q)
        scr[t % 2, c * CR : (c + 1) * CR, :] = s
        return jnp.max(s, axis=0, keepdims=True)

    q = query(0)
    m = functools.reduce(jnp.maximum, [score(0, c, q) for c in range(nch)])
    half = None
    for t, (b, h) in enumerate(tasks):
        sl = slice(b * bi, (b + 1) * bi)
        more = t + 1 < len(tasks)
        put = pltpu.make_async_copy(eb.at[t % 2], et.at[2 * (p0 + p) + h, :, pl.ds(b * bi, bi)], esem.at[t % 2])
        if t < 2:

            @pl.when(p > 0)
            def _():
                put.wait()

        else:
            put.wait()
        if more:
            q = query(t + 1)
        nxt = []
        for c in range(nch):
            cs = slice(c * CR, (c + 1) * CR)
            if more:
                nxt.append(score(t + 1, c, q))
            eb[t % 2, cs, :] = jnp.exp(scr[t % 2, cs, :] - m).astype(bf16)
        put.start()
        o = dot(va[h], eb[t % 2])
        if more:
            m = functools.reduce(jnp.maximum, nxt)
        inv = 1.0 / o[HD : HD + 1, :]
        linv[h : h + 1, sl] = inv
        o = o[:HD, :] * inv
        if h == 0:
            half = o
        else:
            mt = jnp.concatenate([half, o], axis=0)
            mixedf[:, sl] = mt
            mt = mt.astype(bf16)
            mixedt[:, sl] = mt
            mixed[sl, :] = mt.T

    @pl.when(last)
    def _():
        for q in range(2):
            pltpu.make_async_copy(eb.at[q], et.at[0, :, pl.ds(0, bi)], esem.at[q]).wait()


def attn_fwd(ln, kv, qkvt, p0, cnt, prev):
    _, T, D = kv.shape
    HD = D // HEADS
    PW = 2 * HD
    NP = D // PW
    bi = min(512, T)
    prev = list(prev)
    return pl.pallas_call(
        functools.partial(attn_fwd_body, HD, bi, min(256, T), p0),
        grid_spec=pltpu.PrefetchScalarGridSpec(
            num_scalar_prefetch=1, grid=(cnt,),
            in_specs=[pl.BlockSpec((None, T, PW), lambda p, r: (0, 0, p0 + p)), pl.BlockSpec((None, PW, T), lambda p, r: (0, p0 + p, 0)), pl.BlockSpec((None, PW, T), lambda p, r: (2, p0 + p, 0))] + [ANY] * len(prev),
            out_specs=[ANY, pl.BlockSpec((T, PW), lambda p, r: (0, p0 + p)), pl.BlockSpec((PW, T), lambda p, r: (p0 + p, 0)), pl.BlockSpec((PW, T), lambda p, r: (p0 + p, 0)), pl.BlockSpec((None, 8, T), lambda p, r: (p0 + p, 0, 0))],
            scratch_shapes=[pltpu.VMEM((2, T, bi), f32), pltpu.VMEM((T, 2 * PW), bf16), pltpu.VMEM((2, T, bi), bf16), pltpu.SemaphoreType.DMA((2,))]),
        out_shape=[S((HEADS, T, T), bf16), S((T, D), bf16), S((D, T), bf16), S((D, T), f32), S((NP, 8, T), f32)],
        input_output_aliases={4 + i: i for i in range(len(prev))},
        compiler_params=cp(), name="attn_fwd", cost_estimate=cost(cnt * 2 * 8 * T * T * 128, cnt * 2 * T * T * 2, cnt * 2 * T * T),
    )(ln, kv, qkvt, qkvt, *prev)


G0 = math.sqrt(2 / math.pi)


def bit_reverse(x, m):
    y = jnp.zeros_like(x)
    for t in range(m):
        y = y | (((x >> t) & 1) << (m - 1 - t))
    return y


def push(me, n, s, src, keep, send, row0, sem, reverse=False):
    k = jnp.bitwise_xor(me, s)
    p = k >> 1
    if reverse:
        p = bit_reverse(p, (n // 2).bit_length() - 1)
    put = lambda dst: pltpu.make_async_copy(src, dst.at[p, pl.ds(row0, src.shape[0])], sem)

    @pl.when(k & 1 == 0)
    def _():
        put(keep).start()

    @pl.when(k & 1 == 1)
    def _():
        put(send).start()


def ffn_body(n, meta, ch, ln, me, tok, step, vec, upb, cot, mixed, mixedt, *refs):
    np_ = len(meta)
    pieces = refs[:np_]
    out, gx1, gmt, keep, send, wo, wu, wd, act, gup, h2t, gdt, gattn, sums, upsum, dn, up, gwo, vr, mtv, sems, psems = refs[np_:]
    i = pl.program_id(0)
    bm, D = tok.shape
    FF = wu.shape[1]
    r = D // n
    rf = FF // n
    nf = FF // D
    i0 = me[0]
    ro = pl.ds(mult(i * bm, 128), bm)
    first = i == 0
    seg = lambda j: (r + j * r, r, lambda s, o, c: wu.at[pl.ds(mult(s * r + o, 16), c), pl.ds(j * D, D)], D)
    seg_o = [(0, r, lambda s, o, c: wo.at[pl.ds(mult(s * r + o, 16), c)], D)]
    seg_u = [seg(j) for j in range(nf)]
    seg_d = [(r + r * nf, rf, lambda s, o, c: wd.at[pl.ds(mult(s * rf + o, 16), c)], D)]
    q = sems.shape[0] // 4
    parts = [(seg_o, sems.at[pl.ds(0, q)]), (seg_d, sems.at[pl.ds(q, q)]), (seg_u, sems.at[pl.ds(2 * q, 2 * q)])]
    load = pltpu.make_async_copy(mixedt, mtv, psems.at[psems.shape[0] - 1])

    @pl.when(first)
    def _():
        for sg, sm in parts:
            for c in pull(i0, pieces, meta, sg, sm):
                c.start()
        load.start()
        sums[...] = jnp.zeros_like(sums)
        upsum[...] = jnp.zeros_like(upsum)
        for c in pull(i0, pieces, meta, *parts[0]):
            c.wait()

    v = vec[...]
    x1 = tok[...].astype(f32) + step[...].astype(f32) + dot(mixed[...], wo[...]) + row(v, 4)
    nx, rr = norm(x1)
    h2 = (nx * row(v, 5) + row(v, 6)).astype(bf16)
    live = (lax.broadcasted_iota(jnp.int32, (bm, 1), 0) + i * bm) < ln[0]
    gd = jnp.where(live, cot[...], jnp.zeros_like(cot))
    acc = x1 + row(v, 7)
    nc = FF // ch
    sl = [slice(c * ch, (c + 1) * ch) for c in range(nc)]
    lead = lambda c: (dot(h2, wu[:, sl[c]]), dot_t(gd, wd[sl[c], :]))
    h2t[:, ro] = h2.T
    gdt[:, ro] = gd.T

    @pl.when(first)
    def _():
        for sg, sm in parts[1:]:
            for c in pull(i0, pieces, meta, sg, sm):
                c.wait()

    nxt = lead(0)
    for c in range(nc):
        u, ga = nxt
        nxt = lead(c + 1) if c + 1 < nc else None
        u = u + upb[:, sl[c]]
        u2 = u * u
        t = jnp.tanh(u * (f32(G0) + f32(G0 * 0.044715) * u2))
        half = 0.5 + 0.5 * t
        a = (u * half).astype(bf16)
        act[ro, sl[c]] = a
        dg = half + u * (half * (1.0 - half)) * (f32(2 * G0) + f32(6 * 0.044715 * G0) * u2)
        gu = (ga * dg).astype(bf16)
        gup[ro, sl[c]] = gu
        upsum[:, sl[c]] += jnp.sum(gu.astype(f32), axis=0, keepdims=True)
    gh = dot_t(gup[ro, :], wu[...])
    gn = gh * row(v, 5)
    gx = gd.astype(f32) + rr * (gn - jnp.mean(gn, axis=-1, keepdims=True) - nx * jnp.mean(gn * nx, axis=-1, keepdims=True))
    gx1[...] = gx
    gab = gx.astype(bf16)
    gattn[ro, :] = gab
    gmt[...] = dot_t(gab, wo[...]).astype(bf16).T
    acc = acc + dot(act[ro, :], wd[...])
    out[...] = jnp.where(live, acc, 0.0).astype(bf16)
    s_ = lambda a: jnp.sum(a.astype(f32), axis=0, keepdims=True)
    sums[...] += jnp.concatenate([s_(gab), s_(gh * nx), s_(gh), s_(gd), jnp.zeros((4, D), f32)], axis=0)

    @pl.when(i == pl.num_programs(0) - 1)
    def _():
        per = D // rf
        o_out, o_up, o_vec = rf, rf + r, rf + (nf + 1) * r
        for j in range(nf):
            dn[j] = dot(gdt[...], act[:, j * D : (j + 1) * D]).astype(bf16).T
            for t in range(per):
                push(i0, n, j * per + t, dn.at[j, pl.ds(t * rf, rf)], keep, send, 0, psems.at[j * per + t])
            up[j] = dot(h2t[...], gup[:, j * D : (j + 1) * D]).astype(bf16)
            for s in range(n):
                push(i0, n, s, up.at[j, pl.ds(s * r, r)], keep, send, o_up + j * r, psems.at[n * (1 + j) + s], True)
        load.wait()
        gwo[...] = dot(mtv[...], gattn[...]).astype(bf16)
        vr[...] = jnp.concatenate([sums[0:4, :]] + [upsum[:, c * D : (c + 1) * D] for c in range(nf)] + [jnp.zeros((VROWS - 4 - nf, D), f32)], axis=0).astype(bf16)
        b = n * (1 + nf)
        for s in range(n):
            push(i0, n, s, gwo.at[pl.ds(s * r, r)], keep, send, o_out, psems.at[b + s])
            push(i0, n, s, vr, keep, send, o_vec, psems.at[b + n + s], True)
        done = lambda src, q: pltpu.make_async_copy(src, keep.at[0, pl.ds(0, src.shape[0])], psems.at[q]).wait()
        for s in range(n):
            done(dn.at[0, pl.ds(0, rf)], s)
            for c in range(nf):
                done(up.at[0, pl.ds(0, r)], n * (1 + c) + s)
            done(gwo.at[pl.ds(0, r)], b + s)
            done(vr, b + n + s)


def ffn(ln, me, tok, step, vec, upb, cot, mixed, mixedt, pieces, n):
    T, D = tok.shape
    FF = upb.shape[1]
    bm = min(512, T)
    nf = FF // D
    r = D // n
    meta = tuple((k, r0) for k, r0, _ in pieces)
    full = lambda a: pl.BlockSpec(a.shape, lambda i, l, m: (0,) * a.ndim)
    rows = pl.BlockSpec((bm, D), lambda i, l, m: (i, 0))
    B = S((n // 2, FF // n + (nf + 1) * r + VROWS, D), bf16)
    V = pltpu.VMEM
    return pl.pallas_call(
        functools.partial(ffn_body, n, meta, min(1024, FF)),
        grid_spec=pltpu.PrefetchScalarGridSpec(
            num_scalar_prefetch=2, grid=(T // bm,),
            in_specs=[rows, full(step), full(vec), full(upb), rows, rows, ANY] + [ANY] * len(pieces),
            out_specs=[rows, rows, pl.BlockSpec((D, bm), lambda i, l, m: (0, i)), ANY, ANY],
            scratch_shapes=[V((D, D), bf16), V((D, FF), bf16), V((FF, D), bf16), V((T, FF), bf16), V((T, FF), bf16), V((D, T), bf16), V((D, T), bf16), V((T, D), bf16), V((8, D), f32), V((1, FF), f32), V((nf, D, D), bf16), V((nf, D, D), bf16), V((D, D), bf16), V((VROWS, D), bf16), V((D, T), bf16), pltpu.SemaphoreType.DMA((16 * len(pieces),)), pltpu.SemaphoreType.DMA((n * (nf + 3) + 1,))]),
        out_shape=[S((T, D), bf16), S((T, D), f32), S((D, T), bf16), B, B],
        compiler_params=cp(), name="ffn", cost_estimate=cost(2 * T * D * (6 * FF + 3 * D), 16 * T * D, T * FF),
    )(ln, me, tok, step, vec, upb, cot, mixed, mixedt, *[a for _, _, a in pieces])


def attn_bwd_body(HD, scale, CR, v, kt, qt, gt, mt, linv, et, *refs):
    gq, ds = refs[-2:]
    T = v.shape[0]
    rid = lax.broadcasted_iota(jnp.int32, gt.shape, 0) // HD
    g = gt[...].astype(f32)
    q = qt[...]
    gv = gk = None
    for h in range(2):
        hs = slice(h * HD, (h + 1) * HD)
        gs = (g * linv[h : h + 1, :]).astype(bf16)
        gm = jnp.where(rid == h, gs, jnp.zeros_like(gs))
        dl = jnp.sum(gs[hs, :].astype(f32) * mt[hs, :], axis=0, keepdims=True)
        for c in range(T // CR):
            cs = slice(c * CR, (c + 1) * CR)
            ds[h, cs, :] = (et[h, cs, :].astype(f32) * (dot(v[cs, :], gm) - dl)).astype(bf16)
        a = dot(et[h], gm.T)
        b = dot(ds[h], jnp.where(rid == h, q, jnp.zeros_like(q)).T)
        gv = a if gv is None else gv + a
        gk = b if gk is None else gk + b
        gq[0, hs, :] = (dot(kt[hs, :], ds[h]) * scale).astype(bf16)
    gq[2] = gv.astype(bf16).T
    gq[1] = gk.astype(bf16).T


def attn_bwd(kv, qkvt, gmt, mixedf, linv, et, p0, cnt, prev):
    _, T, D = kv.shape
    HD = D // HEADS
    PW = 2 * HD
    NP = D // PW
    prev = list(prev)
    pr = pl.BlockSpec((PW, T), lambda p: (p0 + p, 0))
    of = lambda j: pl.BlockSpec((None, PW, T), lambda p: (j, p0 + p, 0))
    return pl.pallas_call(
        functools.partial(attn_bwd_body, HD, 1.0 / math.sqrt(HD), min(256, T)),
        grid=(cnt,),
        scratch_shapes=[pltpu.VMEM((2, T, T), bf16)],
        in_specs=[pl.BlockSpec((None, T, PW), lambda p: (1, 0, p0 + p)), of(1), of(0), pr, pr, pl.BlockSpec((None, 8, T), lambda p: (p0 + p, 0, 0)), pl.BlockSpec((2, T, T), lambda p: (p0 + p, 0, 0))] + [ANY] * len(prev),
        out_specs=pl.BlockSpec((3, PW, T), lambda p: (0, p0 + p, 0)),
        out_shape=S((3, D, T), bf16),
        input_output_aliases={7: 0} if prev else {},
        compiler_params=cp(), name="attn_bwd", cost_estimate=cost(cnt * 2 * 16 * T * T * 128, cnt * 2 * T * T * 2),
    )(kv, qkvt, qkvt, gmt, mixedf, linv, et, *prev)


def wqkv_body(n, me, xht, g, keep, send, res, vr, sems):
    j = pl.program_id(0)
    D = g.shape[0]
    r = D // n
    i0 = me[0]
    x = jnp.concatenate([xht[...], jnp.ones((16, xht.shape[1]), bf16)], axis=0)
    y = dot_t(x, g[...]).astype(bf16)
    res[j] = y[:D]
    vr[...] = jnp.where(lax.broadcasted_iota(jnp.int32, vr.shape, 0) == j, y[D:], jnp.where(j == 0, jnp.zeros_like(y[D:]), vr[...]))
    for s in range(n):
        push(i0, n, s, res.at[j, pl.ds(s * r, r)], keep, send, mult(j * r, 16), sems.at[j * n + s])

    @pl.when(j == 2)
    def _():
        for s in range(n):
            push(i0, n, s, vr, keep, send, 3 * r, sems.at[3 * n + s])
        for s in range(n):
            for q in range(3):
                pltpu.make_async_copy(res.at[0, pl.ds(0, r)], keep.at[0, pl.ds(0, r)], sems.at[q * n + s]).wait()
            pltpu.make_async_copy(vr, keep.at[0, pl.ds(0, VROWS)], sems.at[3 * n + s]).wait()


def wqkv(me, xht, g, n):
    D, T = xht.shape
    A = S((n // 2, 3 * (D // n) + VROWS, D), bf16)
    return pl.pallas_call(
        functools.partial(wqkv_body, n),
        grid_spec=pltpu.PrefetchScalarGridSpec(
            num_scalar_prefetch=1, grid=(3,),
            in_specs=[pl.BlockSpec((D, T), lambda j, m: (0, 0)), pl.BlockSpec((None, D, T), lambda j, m: (j, 0, 0))],
            out_specs=[ANY] * 2,
            scratch_shapes=[pltpu.VMEM((3, D, D), bf16), pltpu.VMEM((VROWS, D), bf16), pltpu.SemaphoreType.DMA((4 * n,))]),
        out_shape=[A, A],
        compiler_params=cp(), name="wqkv", cost_estimate=cost(6 * T * D * D, 10 * T * D),
    )(me, xht, g)


def back_body(tok, step, vec, g, gx1, *refs):
    ws, tg = refs[:-1], refs[-1]
    D = tok.shape[1]
    gw = D
    x = tok[...].astype(f32) + step[...].astype(f32)
    nx, rr = norm(x)
    gt = sum(dot(w[:, j * gw : (j + 1) * gw], g[j, q * gw : (q + 1) * gw, :]) for q, w in enumerate(ws) for j in range(3))
    gn = gt.T * row(vec[...], 0)
    tg[...] = gx1[...] + rr * (gn - jnp.mean(gn, axis=-1, keepdims=True) - nx * jnp.mean(gn * nx, axis=-1, keepdims=True))


def back(tok, step, vec, ws, g, gx1, bm=512):
    T, D = tok.shape
    full = lambda a: pl.BlockSpec(a.shape, lambda i: (0,) * a.ndim)
    rows = pl.BlockSpec((bm, D), lambda i: (i, 0))
    return pl.pallas_call(
        back_body, grid=(T // bm,),
        in_specs=[rows, full(step), full(vec), pl.BlockSpec((3, D, bm), lambda i: (0, 0, i)), rows] + [full(w) for w in ws],
        out_specs=rows, out_shape=S((T, D), f32), compiler_params=cp(), name="back", cost_estimate=cost(6 * T * D * D, 14 * T * D),
    )(tok, step, vec, g, gx1, *ws)


def shards(tokens, step_embed, lengths, cotangent, ln1_gain, ln1_bias, qkv_weight, q_bias, v_bias, out_weight, out_bias, ln2_gain, ln2_bias, up_weight, up_bias, down_weight, down_bias):
    n = lax.axis_size("shard")
    me = lax.axis_index("shard").astype(jnp.int32)
    mes = me[None]
    tok, cot, step = tokens[0], cotangent[0], step_embed
    T, D = tok.shape
    r = D // n
    FF = up_bias.shape[0] * n
    nc = FF // D
    rf = FF // n
    vblock, pack2 = pack(mes, [ln1_gain, ln1_bias, q_bias, v_bias, out_bias, ln2_gain, ln2_bias, down_bias], up_bias, out_weight, up_weight, down_weight)
    NP = HEADS // 2
    nx, xht = start(tok, step)
    vpieces = gather_direct(vblock, n, xht)
    pieces = gather_direct(qkv_weight, n, xht, *[a for _, _, a in vpieces[1:]])
    kv, qkvt, w, vec, upb = front(mes, nx, pieces, vpieces, n, FF)
    fw = attn_fwd(lengths, kv, qkvt, 0, NP // 2, [])
    fw2 = attn_fwd(lengths, kv, qkvt, NP // 2, NP // 2, fw)
    et, mixed, mixedt, mixedf, linv = fw2
    pieces2 = gather_forward(after(pack2, *[a for _, _, a in pieces[1:]]), n, fw[4], linv)
    out, gx1, gmt, keep, send = ffn(lengths, mes, tok, step, vec, upb, cot, mixed, mixedt, pieces2, n)
    bwd = lambda p, c, g, *deps: attn_bwd(kv, qkvt, after(gmt, *deps) if deps else gmt, mixedf, linv, et, p, c, g)
    ra = rf + r
    got = swap(send, 1)
    g = bwd(0, 1, [])
    got = after(got, g)
    h = n // 4
    add = lambda a, b, k: add16(a[k], b[k])
    rows_a, rows_b = slice(0, ra), slice(ra, None)
    lo, hi = slice(0, h), slice(h, None)
    ka, xa, kb, xb = [add(keep, got, k) for k in ((lo, rows_a), (hi, rows_a), (lo, rows_b), (hi, rows_b))]
    g = bwd(1, NP - 1, [g], ka, xa, kb, xb)
    m = (n // 2).bit_length() - 1
    ga, gb = swap(xa, 2 << (m - 1)), swap(xb, 2)
    for t in range(1, m):
        dep = g if t == 1 else keep
        ga, gb, _ = lax.optimization_barrier((ga, gb, dep))
        h //= 2
        lo, hi = slice(0, h), slice(h, None)
        ka, xa = add(ka, ga, lo), add(ka, ga, hi)
        kb, xb = add(kb, gb, lo), add(kb, gb, hi)
        ga, gb = swap(xa, 2 << (m - 1 - t)), swap(xb, 2 << t)
        if t == 1:
            keep, send = wqkv(mes, after(xht, ka, xa, kb, xb), g, n)
    got = swap(send, 1)
    p2 = [add16(keep[k], got[k]) for k in range(n // 2)]
    far2 = spread(p2)
    ga, gb, _ = lax.optimization_barrier((ga, gb, keep))
    got = swap(send, 1)
    p2 = [add16(keep[k], got[k]) for k in range(n // 2)]
    far2 = spread(p2)
    own1 = jnp.concatenate([add16(ka, ga)[0], add16(kb, gb)[0]], axis=0)
    m1, o1, x1 = rep_half(own1)
    z1 = add16(m1, after(o1, *p2[1:]))
    tg = back(tok, after(step, z1, *p2[1:]), vec, [w], g, gx1)
    own2 = total(p2[0], [after(a, tg) for a in far2])
    m2, o2, x2 = rep_half(own2)
    steps = rep_steps()
    z2 = None if steps else add16(m2, o2)
    for b in steps:
        z1 = add16(z1, after(rep_perm(z1, b), x2))
        if z2 is None:
            z2 = add16(m2, after(o2, z1))
        pz = rep_perm(z2, b)
        z2 = add16(z2, after(pz, z1))
    o1, o2 = rep_perm(z1, 1), rep_perm(z2, 1)
    ids = jnp.stack([me, (lax.axis_index("rep") % 2).astype(jnp.int32)])
    g_down, g_up, g_out, g_upb, g_ob, g_g2, g_b2, g_db = finish_rest(ids, z1, o1, r, rf, nc, n)
    g_qkv, g_g1, g_b1, g_q, g_v = finish_first(ids, z2, after(o2, g_out), qkv_weight, ln1_gain, ln1_bias)
    flat = lambda a: a.reshape(-1)
    return (out[None], tg[None], flat(g_g1), flat(g_b1), g_qkv, flat(g_q), flat(g_v), g_out, flat(g_ob), flat(g_g2), flat(g_b2), g_up, flat(g_upb), g_down, flat(g_db))


def solution(mesh):
    from jax.sharding import PartitionSpec as P

    in_specs = (
        P(("rep", "shard"), None, None),
        P(("rep", "shard"), None),
        P(("rep", "shard")),
        P(("rep", "shard"), None, None),
        P("shard"),
        P("shard"),
        P("shard", None),
        P("shard"),
        P("shard"),
        P("shard", None),
        P("shard"),
        P("shard"),
        P("shard"),
        P("shard", None),
        P("shard"),
        P("shard", None),
        P("shard"),
    )
    out_specs = (
        P(("rep", "shard"), None, None),
        P(("rep", "shard"), None, None),
        P("shard"),
        P("shard"),
        P("shard", None),
        P("shard"),
        P("shard"),
        P("shard", None),
        P("shard"),
        P("shard"),
        P("shard"),
        P("shard", None),
        P("shard"),
        P("shard", None),
        P("shard"),
    )
    return jax.shard_map(shards, mesh=mesh, in_specs=in_specs, out_specs=out_specs, check_vma=False)
```

```python
import functools, math
import jax, jax.numpy as jnp
from jax import lax
from jax.experimental import pallas as pl
from jax.experimental.pallas import tpu as pltpu

f32 = jnp.float32
bf16 = jnp.bfloat16
EPS = 1e-05
HEADS = 8

def dot(a, b):
    return jnp.dot(a, b, preferred_element_type=f32)

def dot_t(a, b):
    return lax.dot_general(a, b, (((1,), (1,)), ((), ())), preferred_element_type=f32)

def cp(n=1, vmem=100):
    return pltpu.CompilerParams(dimension_semantics=("arbitrary",) * n, vmem_limit_bytes=60 * 1024 * 1024)

def norm(x):
    c = x - jnp.mean(x, axis=-1, keepdims=True)
    r = lax.rsqrt(jnp.mean(c * c, axis=-1, keepdims=True) + EPS)
    return c * r, r

def row(v, i):
    return v[i : i + 1, :].astype(f32)


VROWS = 16
LANES = 128


def xor_perm(n, k):
    return [(i, i ^ k) for i in range(n)]


def rep_perm(x, b):
    return lax.ppermute(x, "rep", xor_perm(lax.axis_size("rep"), b))


def swap(x, k):
    return lax.ppermute(x, "shard", xor_perm(lax.axis_size("shard"), k))


def after(x, *deps):
    return lax.optimization_barrier((x,) + deps)[0]


def gather_direct(x, n, *gate):
    out = [(0, 0, x)]
    far = [(k, swap(x, k)) for k in range(2, n, 2)]
    out += [(k, 0, after(y, *gate) if gate else y) for k, y in far]
    return out + [(k ^ 1, 0, swap(y, 1)) for k, _, y in out]


def gather_forward(x, n, gate1, gate2):
    R = x.shape[0]
    cut = R // 2 // 16 * 16
    near = []
    far = []
    halves = {}
    for k in sorted(range(2, n, 2), key=lambda k: (bin(k).count("1"), k)):
        if bin(k).count("1") == 1:
            y = after(swap(x, k), gate1)
            near.append((k, 0, y))
            halves[k] = (y[:cut], y[cut:])
        else:
            low = k & -k
            high = 1 << (k.bit_length() - 1)
            a = swap(halves[k ^ low][0], low)
            b = swap(halves[k ^ high][1], high)
            far += [(k, 0, a), (k, cut, b)]
            halves[k] = (a, b)
    near = [(0, 0, x)] + near
    late = [(k, r0, after(a, gate2)) for k, r0, a in far]
    out = near + [(k ^ 1, r0, swap(a, 1)) for k, r0, a in near]
    return out + late + [(k ^ 1, r0, swap(a, 1)) for k, r0, a in late]


def add16(a, b):
    return a + b


def spread(parts):
    return [swap(parts[k], 2 * k) for k in range(len(parts) - 1, 0, -1)]


def total(own, got):
    t = own.astype(f32)
    for a in got:
        t = t + a.astype(f32)
    return t.astype(bf16)


def rep_half(x):
    h = x.shape[0] // 2
    odd = lax.axis_index("rep") % 2
    mine = lax.dynamic_slice_in_dim(x, odd * h, h, 0)
    other = lax.dynamic_slice_in_dim(x, (1 - odd) * h, h, 0)
    return mine, rep_perm(other, 1), other


def rep_steps():
    nr = lax.axis_size("rep")
    return [b for b in (2 << i for i in range(16)) if b < nr]


GROUPS = 1


def pack_first_body(me, w, upb, *refs):
    vecs = refs[:-GROUPS]
    outs = refs[-GROUPS:]
    r, W = w.shape
    D = W // 3
    gw = D // GROUPS
    for g, out in enumerate(outs):
        for j in range(3):
            out[j * r : (j + 1) * r, :] = w[:, j * D + g * gw : j * D + (g + 1) * gw]

    def spot(v):
        w_ = v.shape[1]
        if w_ >= LANES:
            return [v[q : q + 1, :] for q in range(v.shape[0])]
        t = LANES // w_
        lane = lax.broadcasted_iota(jnp.int32, (1, LANES), 1)
        return [jnp.where(lane // w_ == me[0] % t, jnp.concatenate([v] * t, axis=1), jnp.zeros((1, LANES), f32))]

    rows = [a for v in vecs for a in spot(v[...].astype(f32))] + spot(upb[...].astype(f32))
    b = jnp.concatenate(rows + [jnp.zeros((VROWS - len(rows), LANES), f32)], axis=0).astype(bf16)
    outs[0][3 * r :, :] = jnp.concatenate([b, jnp.zeros((VROWS, gw - LANES), bf16)], axis=1) if gw > LANES else b


def whole(n):
    return [pl.BlockSpec(memory_space=pltpu.VMEM)] * n


def once(*arrays):
    return [pl.BlockSpec(a.shape, lambda i, *m, nd=len(a.shape): (0,) * nd) for a in arrays]


def pack_first(me, w, vecs, upb):
    r, W = w.shape
    gw = W // 3 // GROUPS
    lanes = lambda v: v.reshape(-1, min(LANES, v.shape[0]))
    args = [w] + [lanes(v) for v in [upb] + vecs]
    outs = [S((3 * r + (VROWS if g == 0 else 0), gw), bf16) for g in range(GROUPS)]
    return pl.pallas_call(
        pack_first_body,
        grid_spec=pltpu.PrefetchScalarGridSpec(num_scalar_prefetch=1, grid=(1,), in_specs=once(*args), out_specs=once(*outs)),
        out_shape=outs, compiler_params=cp(), name="pack_first", cost_estimate=cost(0, 4 * w.size),
    )(me, *args)


def pack_rest_body(wo, wu, wd, out):
    r, D = wo.shape
    out[:r, :] = wo[...]
    for j in range(wu.shape[1] // D):
        out[(1 + j) * r : (2 + j) * r, :] = wu[:, j * D : (j + 1) * D]
    out[(1 + wu.shape[1] // D) * r :, :] = wd[...]


def pack_rest(wo, wu, wd):
    D = wo.shape[1]
    out = S(((wo.size + wu.size + wd.size) // D, D), bf16)
    return pl.pallas_call(
        pack_rest_body, grid=(1,), in_specs=once(wo, wu, wd), out_specs=once(out)[0],
        out_shape=out, compiler_params=cp(), name="pack_rest", cost_estimate=cost(0, 4 * wu.size),
    )(wo, wu, wd)


def own_lanes(tiles, me, w):
    pick = lambda i: sum(jnp.where(i == t, a, jnp.zeros_like(a)) for t, a in enumerate(tiles))
    if w >= LANES:
        q = w // LANES
        return jnp.concatenate([pick(me * q + c) for c in range(q)], axis=1)
    per = LANES // w
    x = pick(me // per)
    off = me % per
    return sum(jnp.where(off == o, x[:, o * w : (o + 1) * w], 0.0) for o in range(per))


def rows_of(lo, hi, a, b):
    h = lo.shape[0]
    if b <= h:
        return lo[a:b, :]
    if a >= h:
        return hi[a - h : b - h, :]
    return jnp.concatenate([lo[a:h, :], hi[: b - h, :]], axis=0)


def finish_rest_body(r, rf, n, ids, s, o, down, up, out, upb, *vecs):
    D = out.shape[1]
    nf = up.shape[1] // D

    def run(lo, hi):
        f = lambda a, b: rows_of(lo, hi, a, b).astype(f32)
        down[...] = f(0, rf)
        out[...] = f(rf, rf + r)
        for j in range(nf):
            up[:, j * D : (j + 1) * D] = f(rf + (j + 1) * r, rf + (j + 2) * r)
        b = rf + (nf + 1) * r
        v = f(b, b + VROWS)
        me = ids[0]
        tiles = [v[0:8, t * LANES : (t + 1) * LANES] for t in range(D // LANES)]
        x = own_lanes(tiles, me, r)
        for q, ref in enumerate(vecs):
            ref[...] = x[q : q + 1, :]
        tiles = [v[4 + q : 5 + q, t * LANES : (t + 1) * LANES] for q in range(nf) for t in range(D // LANES)]
        upb[...] = own_lanes(tiles, me, nf * D // n)

    @pl.when(ids[1] == 0)
    def _():
        run(s, o)

    @pl.when(ids[1] == 1)
    def _():
        run(o, s)


def finish_rest(ids, s, o, r, rf, nf, n):
    D = s.shape[1]
    row1 = lambda w: S((1, w), f32)
    return pl.pallas_call(
        functools.partial(finish_rest_body, r, rf, n),
        in_specs=[pl.BlockSpec(memory_space=pltpu.SMEM)] + whole(2), out_specs=whole(8),
        out_shape=[S((rf, D), f32), S((r, nf * D), f32), S((r, D), f32), row1(nf * D // n)] + [row1(r)] * 4,
        compiler_params=pltpu.CompilerParams(vmem_limit_bytes=16 << 20), name="finish_rest", cost_estimate=cost(0, 8 * s.size),
    )(ids, s, o)


def finish_first_body(ids, s, o, w, gain, bias, qkv, gg, gb, qb, vb):
    r, W = w.shape
    D = s.shape[1]

    def run(lo, hi):
        f = lambda a, b: rows_of(lo, hi, a, b).astype(f32)
        v = f(3 * r, 3 * r + VROWS)
        nt = D // LANES
        accg = accb = jnp.zeros((r, LANES), f32)
        col = lambda g: jnp.concatenate([g[...].astype(f32), jnp.zeros((7, r), f32)], axis=0).T[:, 0:1]
        cg, cb = col(gain), col(bias)
        for j in range(3):
            m = f(j * r, (j + 1) * r)
            sq = v[j : j + 1, :]
            ww = w[:, j * D : (j + 1) * D].astype(f32)
            qkv[:, j * D : (j + 1) * D] = cg * m + cb * sq
            pg, pb = ww * m, ww * sq
            accg = accg + sum(pg[:, t * LANES : (t + 1) * LANES] for t in range(nt))
            accb = accb + sum(pb[:, t * LANES : (t + 1) * LANES] for t in range(nt))
        gg[...] = jnp.sum(accg.T, axis=0, keepdims=True)
        gb[...] = jnp.sum(accb.T, axis=0, keepdims=True)
        x = own_lanes([v[0:8, t * LANES : (t + 1) * LANES] for t in range(nt)], ids[0], r)
        qb[...] = x[0:1, :]
        vb[...] = x[2:3, :]

    @pl.when(ids[1] == 0)
    def _():
        run(s, o)

    @pl.when(ids[1] == 1)
    def _():
        run(o, s)


def finish_first(ids, s, o, w, gain, bias):
    r, W = w.shape
    return pl.pallas_call(
        finish_first_body,
        in_specs=[pl.BlockSpec(memory_space=pltpu.SMEM)] + whole(5), out_specs=whole(5),
        out_shape=[S((r, W), f32)] + [S((1, r), f32)] * 4,
        compiler_params=pltpu.CompilerParams(vmem_limit_bytes=16 << 20), name="finish_first", cost_estimate=cost(0, 8 * w.size),
    )(ids, s, o, w, gain[None], bias[None])


def pull(me, refs, meta, segs, sems):
    copies = []
    for ref, (k, r0) in zip(refs, meta):
        s = jnp.bitwise_xor(me, k)
        r1 = r0 + ref.shape[0]
        for a, c, dst, lanes in segs:
            lo, hi = max(a, r0), min(a + c, r1)
            if lo < hi:
                src = ref.at[pl.ds(lo - r0, hi - lo), pl.ds(0, lanes)]
                copies.append(pltpu.make_async_copy(src, dst(s, lo - a, hi - lo), sems.at[len(copies)]))
    return copies


def mult(x, m):
    return pl.multiple_of(x, m)


def weight_segs(w, r):
    gw = w.shape[1] // 3
    seg = lambda j: (j * r, r, lambda s, o, c: w.at[pl.ds(mult(s * r + o, 16), c), pl.ds(j * gw, gw)], gw)
    return [seg(j) for j in range(3)]


def start_body(tok, step, nx, xht):
    n, _ = norm(tok[...].astype(f32) + step[...].astype(f32))
    nx[...] = n
    xht[...] = n.astype(bf16).T


def start(tok, step, bm=256):
    T, D = tok.shape
    rows = pl.BlockSpec((bm, D), lambda i: (i, 0))
    return pl.pallas_call(
        start_body, grid=(T // bm,),
        in_specs=[rows, pl.BlockSpec((1, D), lambda i: (0, 0))], out_specs=[rows, pl.BlockSpec((D, bm), lambda i: (0, i))],
        out_shape=[S((T, D), f32), S((D, T), bf16)], compiler_params=cp(), name="start", cost_estimate=cost(20 * T * D, 8 * T * D),
    )(tok, step)


def front_body(scale, n, meta, me, nx, *refs):
    np_ = len(meta)
    pieces = refs[:np_]
    kv, qkvt, wout, vec, upb, nv, h, w, vbuf, sems, own = refs[np_:]
    T, D = nv.shape
    r = D // n
    FF = upb.shape[1]
    i = pl.program_id(0)
    cw = kv.shape[2]
    per_j = D // cw
    segs = [(3 * r, VROWS, lambda s, o, c: vbuf.at[s, pl.ds(o, c)], LANES)] + weight_segs(w, r)
    load = pltpu.make_async_copy(nx, nv, own.at[0])
    save = pltpu.make_async_copy(w, wout, own.at[1])

    @pl.when(i == 0)
    def _():
        cs = pull(me[0], pieces, meta, segs, sems)
        for c in cs:
            c.start()
        load.start()
        for c in cs:
            c.wait()
        save.start()
        per = LANES // r
        tiles = [sum(vbuf[s, 0:8, :].astype(f32) for s in range(t * per, (t + 1) * per)) for t in range(D // LANES)]
        vec[...] = jnp.concatenate(tiles, axis=1)
        wu = FF // n
        if wu >= LANES:
            rows = [vbuf[s, 8 + q : 9 + q, :].astype(f32) for s in range(n) for q in range(wu // LANES)]
        else:
            per = LANES // wu
            rows = [sum(vbuf[s, 8:9, :].astype(f32) for s in range(t * per, (t + 1) * per)) for t in range(FF // LANES)]
        upb[...] = jnp.concatenate(rows, axis=1)
        load.wait()
        v = vec[...]
        h[...] = (nv[...] * row(v, 0) + row(v, 1)).astype(bf16)

    cols = pl.ds(mult(i * cw, 128), cw)
    y = dot(h[...], w[:, cols])
    here = pl.ds(mult((i % per_j) * cw, 128), cw)
    kind = i // per_j
    y = (y + jnp.where(kind == 0, vec[2:3, here], jnp.where(kind == 2, vec[3:4, here], 0.0))).astype(bf16)
    kv[0] = y
    qkvt[0] = jnp.where(kind == 0, y * bf16(scale), y).T

    @pl.when(i == pl.num_programs(0) - 1)
    def _():
        save.wait()


S = jax.ShapeDtypeStruct
ANY = pl.BlockSpec(memory_space=pl.ANY)


def cost(flops, nbytes, tr=0):
    return pl.CostEstimate(flops=int(flops), bytes_accessed=int(nbytes), transcendentals=int(tr))


def front(me, nx, pieces, n, FF, cw=512):
    T, D = nx.shape
    scale = 1.0 / math.sqrt(D // HEADS)
    meta = tuple((k, r0) for k, r0, _ in pieces)
    q = D // cw
    keep = lambda *sh: pl.BlockSpec(sh, lambda i, m: (0,) * len(sh))
    rest = lambda i: jnp.maximum(i - q, 0)
    V = pltpu.VMEM
    return pl.pallas_call(
        functools.partial(front_body, scale, n, meta),
        grid_spec=pltpu.PrefetchScalarGridSpec(
            num_scalar_prefetch=1, grid=(3 * q,),
            in_specs=[ANY] * (1 + len(pieces)),
            out_specs=[pl.BlockSpec((1, T, cw), lambda i, m: (rest(i) // q, 0, rest(i) % q)), pl.BlockSpec((1, cw, T), lambda i, m: (i // q, i % q, 0)), ANY, keep(8, D), keep(1, FF)],
            scratch_shapes=[V((T, D), f32), V((T, D), bf16), V((D, 3 * D), bf16), V((n, VROWS, LANES), bf16), pltpu.SemaphoreType.DMA((8 * len(pieces),)), pltpu.SemaphoreType.DMA((2,))]),
        out_shape=[S((2, T, D), bf16), S((3, D, T), bf16), S((D, 3 * D), bf16), S((8, D), f32), S((1, FF), f32)],
        compiler_params=cp(), name="front", cost_estimate=cost(6 * T * D * D, 12 * T * D),
    )(me, nx, *[a for _, _, a in pieces])


def attn_fwd_body(HD, bi, CR, p0, ln, k, qt, vt, *refs):
    et, mixed, mixedt, mixedf, linv, scr, ka, eb, esem = refs[-9:]
    T, PW = k.shape
    n = ln[0]
    p = pl.program_id(0)
    last = p == pl.num_programs(0) - 1
    rid = lax.broadcasted_iota(jnp.int32, (PW, bi), 0)
    lane = lax.broadcasted_iota(jnp.int32, (T, PW), 1)
    rows = lax.broadcasted_iota(jnp.int32, (T, PW), 0)
    ka[:, :PW] = k[...]
    ka[:, PW:] = jnp.where((lane == 0) & (rows >= n), f32(-1e30), f32(0)).astype(bf16)
    ones = jnp.where(rid == 0, f32(1), f32(0)).astype(bf16)
    va = [jnp.concatenate([vt[h * HD : (h + 1) * HD, :], jnp.ones((16, T), bf16)], axis=0) for h in range(2)]
    tasks = [(b, h) for b in range(T // bi) for h in range(2)]
    nch = T // CR

    def query(t):
        b, h = tasks[t]
        q = qt[:, b * bi : (b + 1) * bi]
        return jnp.concatenate([jnp.where(rid // HD == h, q, jnp.zeros_like(q)), ones], axis=0)

    def score(t, c, q):
        s = dot(ka[c * CR : (c + 1) * CR, :], q)
        scr[t % 2, c * CR : (c + 1) * CR, :] = s
        return jnp.max(s, axis=0, keepdims=True)

    q = query(0)
    m = functools.reduce(jnp.maximum, [score(0, c, q) for c in range(nch)])
    half = None
    for t, (b, h) in enumerate(tasks):
        sl = slice(b * bi, (b + 1) * bi)
        more = t + 1 < len(tasks)
        put = pltpu.make_async_copy(eb.at[t % 2], et.at[2 * (p0 + p) + h, :, pl.ds(b * bi, bi)], esem.at[t % 2])
        if t < 2:

            @pl.when(p > 0)
            def _():
                put.wait()

        else:
            put.wait()
        if more:
            q = query(t + 1)
        nxt = []
        for c in range(nch):
            cs = slice(c * CR, (c + 1) * CR)
            if more:
                nxt.append(score(t + 1, c, q))
            eb[t % 2, cs, :] = jnp.exp(scr[t % 2, cs, :] - m).astype(bf16)
        put.start()
        o = dot(va[h], eb[t % 2])
        if more:
            m = functools.reduce(jnp.maximum, nxt)
        inv = 1.0 / o[HD : HD + 1, :]
        linv[h : h + 1, sl] = inv
        o = o[:HD, :] * inv
        if h == 0:
            half = o
        else:
            mt = jnp.concatenate([half, o], axis=0)
            mixedf[:, sl] = mt
            mt = mt.astype(bf16)
            mixedt[:, sl] = mt
            mixed[sl, :] = mt.T

    @pl.when(last)
    def _():
        for q in range(2):
            pltpu.make_async_copy(eb.at[q], et.at[0, :, pl.ds(0, bi)], esem.at[q]).wait()


def attn_fwd(ln, kv, qkvt, p0, cnt, prev):
    _, T, D = kv.shape
    HD = D // HEADS
    PW = 2 * HD
    NP = D // PW
    bi = min(512, T)
    prev = list(prev)
    return pl.pallas_call(
        functools.partial(attn_fwd_body, HD, bi, min(256, T), p0),
        grid_spec=pltpu.PrefetchScalarGridSpec(
            num_scalar_prefetch=1, grid=(cnt,),
            in_specs=[pl.BlockSpec((None, T, PW), lambda p, r: (0, 0, p0 + p)), pl.BlockSpec((None, PW, T), lambda p, r: (0, p0 + p, 0)), pl.BlockSpec((None, PW, T), lambda p, r: (2, p0 + p, 0))] + [ANY] * len(prev),
            out_specs=[ANY, pl.BlockSpec((T, PW), lambda p, r: (0, p0 + p)), pl.BlockSpec((PW, T), lambda p, r: (p0 + p, 0)), pl.BlockSpec((PW, T), lambda p, r: (p0 + p, 0)), pl.BlockSpec((None, 8, T), lambda p, r: (p0 + p, 0, 0))],
            scratch_shapes=[pltpu.VMEM((2, T, bi), f32), pltpu.VMEM((T, 2 * PW), bf16), pltpu.VMEM((2, T, bi), bf16), pltpu.SemaphoreType.DMA((2,))]),
        out_shape=[S((HEADS, T, T), bf16), S((T, D), bf16), S((D, T), bf16), S((D, T), f32), S((NP, 8, T), f32)],
        input_output_aliases={4 + i: i for i in range(len(prev))},
        compiler_params=cp(), name="attn_fwd", cost_estimate=cost(cnt * 2 * 8 * T * T * 128, cnt * 2 * T * T * 2, cnt * 2 * T * T),
    )(ln, kv, qkvt, qkvt, *prev)


G0 = math.sqrt(2 / math.pi)


def bit_reverse(x, m):
    y = jnp.zeros_like(x)
    for t in range(m):
        y = y | (((x >> t) & 1) << (m - 1 - t))
    return y


def push(me, n, s, src, keep, send, row0, sem, reverse=False):
    k = jnp.bitwise_xor(me, s)
    p = k >> 1
    if reverse:
        p = bit_reverse(p, (n // 2).bit_length() - 1)
    put = lambda dst: pltpu.make_async_copy(src, dst.at[p, pl.ds(row0, src.shape[0])], sem)

    @pl.when(k & 1 == 0)
    def _():
        put(keep).start()

    @pl.when(k & 1 == 1)
    def _():
        put(send).start()


def ffn_body(n, meta, ch, ln, me, tok, step, vec, upb, cot, mixed, mixedt, *refs):
    np_ = len(meta)
    pieces = refs[:np_]
    out, gx1, gmt, keep, send, wo, wu, wd, act, gup, h2t, gdt, gattn, sums, upsum, dn, up, gwo, vr, mtv, sems, psems = refs[np_:]
    i = pl.program_id(0)
    bm, D = tok.shape
    FF = wu.shape[1]
    r = D // n
    rf = FF // n
    nf = FF // D
    i0 = me[0]
    ro = pl.ds(mult(i * bm, 128), bm)
    first = i == 0
    seg = lambda j: (r + j * r, r, lambda s, o, c: wu.at[pl.ds(mult(s * r + o, 16), c), pl.ds(j * D, D)], D)
    seg_o = [(0, r, lambda s, o, c: wo.at[pl.ds(mult(s * r + o, 16), c)], D)]
    seg_u = [seg(j) for j in range(nf)]
    seg_d = [(r + r * nf, rf, lambda s, o, c: wd.at[pl.ds(mult(s * rf + o, 16), c)], D)]
    q = sems.shape[0] // 4
    parts = [(seg_o, sems.at[pl.ds(0, q)]), (seg_d, sems.at[pl.ds(q, q)]), (seg_u, sems.at[pl.ds(2 * q, 2 * q)])]
    load = pltpu.make_async_copy(mixedt, mtv, psems.at[psems.shape[0] - 1])

    @pl.when(first)
    def _():
        for sg, sm in parts:
            for c in pull(i0, pieces, meta, sg, sm):
                c.start()
        load.start()
        sums[...] = jnp.zeros_like(sums)
        upsum[...] = jnp.zeros_like(upsum)
        for c in pull(i0, pieces, meta, *parts[0]):
            c.wait()

    v = vec[...]
    x1 = tok[...].astype(f32) + step[...].astype(f32) + dot(mixed[...], wo[...]) + row(v, 4)
    nx, rr = norm(x1)
    h2 = (nx * row(v, 5) + row(v, 6)).astype(bf16)
    live = (lax.broadcasted_iota(jnp.int32, (bm, 1), 0) + i * bm) < ln[0]
    gd = jnp.where(live, cot[...], jnp.zeros_like(cot))
    acc = x1 + row(v, 7)
    gh = None
    nc = FF // ch
    sl = [slice(c * ch, (c + 1) * ch) for c in range(nc)]
    lead = lambda c: (dot(h2, wu[:, sl[c]]), dot_t(gd, wd[sl[c], :]))
    h2t[:, ro] = h2.T
    gdt[:, ro] = gd.T

    @pl.when(first)
    def _():
        for sg, sm in parts[1:]:
            for c in pull(i0, pieces, meta, sg, sm):
                c.wait()

    nxt = lead(0)
    for c in range(nc):
        u, ga = nxt
        nxt = lead(c + 1) if c + 1 < nc else None
        u = u + upb[:, sl[c]]
        u2 = u * u
        t = jnp.tanh(u * (f32(G0) + f32(G0 * 0.044715) * u2))
        half = 0.5 + 0.5 * t
        a = (u * half).astype(bf16)
        act[ro, sl[c]] = a
        dg = half + u * (half * (1.0 - half)) * (f32(2 * G0) + f32(6 * 0.044715 * G0) * u2)
        gu = (ga * dg).astype(bf16)
        gup[ro, sl[c]] = gu
        upsum[:, sl[c]] += jnp.sum(gu.astype(f32), axis=0, keepdims=True)
        acc = acc + dot(a, wd[sl[c], :])
        p = dot_t(gu, wu[:, sl[c]])
        gh = p if gh is None else gh + p
    out[...] = jnp.where(live, acc, 0.0).astype(bf16)
    gn = gh * row(v, 5)
    gx = gd.astype(f32) + rr * (gn - jnp.mean(gn, axis=-1, keepdims=True) - nx * jnp.mean(gn * nx, axis=-1, keepdims=True))
    gx1[...] = gx
    gab = gx.astype(bf16)
    gattn[ro, :] = gab
    gmt[...] = dot_t(gab, wo[...]).astype(bf16).T
    s_ = lambda a: jnp.sum(a.astype(f32), axis=0, keepdims=True)
    sums[...] += jnp.concatenate([s_(gab), s_(gh * nx), s_(gh), s_(gd), jnp.zeros((4, D), f32)], axis=0)

    @pl.when(i == pl.num_programs(0) - 1)
    def _():
        per = D // rf
        o_out, o_up, o_vec = rf, rf + r, rf + (nf + 1) * r
        for j in range(nf):
            dn[j] = dot(gdt[...], act[:, j * D : (j + 1) * D]).astype(bf16).T
            for t in range(per):
                push(i0, n, j * per + t, dn.at[j, pl.ds(t * rf, rf)], keep, send, 0, psems.at[j * per + t])
            up[j] = dot(h2t[...], gup[:, j * D : (j + 1) * D]).astype(bf16)
            for s in range(n):
                push(i0, n, s, up.at[j, pl.ds(s * r, r)], keep, send, o_up + j * r, psems.at[n * (1 + j) + s], True)
        load.wait()
        gwo[...] = dot(mtv[...], gattn[...]).astype(bf16)
        vr[...] = jnp.concatenate([sums[0:4, :]] + [upsum[:, c * D : (c + 1) * D] for c in range(nf)] + [jnp.zeros((VROWS - 4 - nf, D), f32)], axis=0).astype(bf16)
        b = n * (1 + nf)
        for s in range(n):
            push(i0, n, s, gwo.at[pl.ds(s * r, r)], keep, send, o_out, psems.at[b + s])
            push(i0, n, s, vr, keep, send, o_vec, psems.at[b + n + s], True)
        done = lambda src, q: pltpu.make_async_copy(src, keep.at[0, pl.ds(0, src.shape[0])], psems.at[q]).wait()
        for s in range(n):
            done(dn.at[0, pl.ds(0, rf)], s)
            for c in range(nf):
                done(up.at[0, pl.ds(0, r)], n * (1 + c) + s)
            done(gwo.at[pl.ds(0, r)], b + s)
            done(vr, b + n + s)


def ffn(ln, me, tok, step, vec, upb, cot, mixed, mixedt, pieces, n):
    T, D = tok.shape
    FF = upb.shape[1]
    bm = min(512, T)
    nf = FF // D
    r = D // n
    meta = tuple((k, r0) for k, r0, _ in pieces)
    full = lambda a: pl.BlockSpec(a.shape, lambda i, l, m: (0,) * a.ndim)
    rows = pl.BlockSpec((bm, D), lambda i, l, m: (i, 0))
    B = S((n // 2, FF // n + (nf + 1) * r + VROWS, D), bf16)
    V = pltpu.VMEM
    return pl.pallas_call(
        functools.partial(ffn_body, n, meta, min(1024, FF)),
        grid_spec=pltpu.PrefetchScalarGridSpec(
            num_scalar_prefetch=2, grid=(T // bm,),
            in_specs=[rows, full(step), full(vec), full(upb), rows, rows, ANY] + [ANY] * len(pieces),
            out_specs=[rows, rows, pl.BlockSpec((D, bm), lambda i, l, m: (0, i)), ANY, ANY],
            scratch_shapes=[V((D, D), bf16), V((D, FF), bf16), V((FF, D), bf16), V((T, FF), bf16), V((T, FF), bf16), V((D, T), bf16), V((D, T), bf16), V((T, D), bf16), V((8, D), f32), V((1, FF), f32), V((nf, D, D), bf16), V((nf, D, D), bf16), V((D, D), bf16), V((VROWS, D), bf16), V((D, T), bf16), pltpu.SemaphoreType.DMA((16 * len(pieces),)), pltpu.SemaphoreType.DMA((n * (nf + 3) + 1,))]),
        out_shape=[S((T, D), bf16), S((T, D), f32), S((D, T), bf16), B, B],
        compiler_params=cp(), name="ffn", cost_estimate=cost(2 * T * D * (6 * FF + 3 * D), 16 * T * D, T * FF),
    )(ln, me, tok, step, vec, upb, cot, mixed, mixedt, *[a for _, _, a in pieces])


def attn_bwd_body(HD, scale, CR, v, kt, qt, gt, mt, linv, et, *refs):
    gq, ds = refs[-2:]
    T = v.shape[0]
    rid = lax.broadcasted_iota(jnp.int32, gt.shape, 0) // HD
    g = gt[...].astype(f32)
    q = qt[...]
    gv = gk = None
    for h in range(2):
        hs = slice(h * HD, (h + 1) * HD)
        gs = (g * linv[h : h + 1, :]).astype(bf16)
        gm = jnp.where(rid == h, gs, jnp.zeros_like(gs))
        dl = jnp.sum(gs[hs, :].astype(f32) * mt[hs, :], axis=0, keepdims=True)
        for c in range(T // CR):
            cs = slice(c * CR, (c + 1) * CR)
            ds[h, cs, :] = (et[h, cs, :].astype(f32) * (dot(v[cs, :], gm) - dl)).astype(bf16)
        a = dot(et[h], gm.T)
        b = dot(ds[h], jnp.where(rid == h, q, jnp.zeros_like(q)).T)
        gv = a if gv is None else gv + a
        gk = b if gk is None else gk + b
        gq[0, hs, :] = (dot(kt[hs, :], ds[h]) * scale).astype(bf16)
    gq[2] = gv.astype(bf16).T
    gq[1] = gk.astype(bf16).T


def attn_bwd(kv, qkvt, gmt, mixedf, linv, et, p0, cnt, prev):
    _, T, D = kv.shape
    HD = D // HEADS
    PW = 2 * HD
    NP = D // PW
    prev = list(prev)
    pr = pl.BlockSpec((PW, T), lambda p: (p0 + p, 0))
    of = lambda j: pl.BlockSpec((None, PW, T), lambda p: (j, p0 + p, 0))
    return pl.pallas_call(
        functools.partial(attn_bwd_body, HD, 1.0 / math.sqrt(HD), min(256, T)),
        grid=(cnt,),
        scratch_shapes=[pltpu.VMEM((2, T, T), bf16)],
        in_specs=[pl.BlockSpec((None, T, PW), lambda p: (1, 0, p0 + p)), of(1), of(0), pr, pr, pl.BlockSpec((None, 8, T), lambda p: (p0 + p, 0, 0)), pl.BlockSpec((2, T, T), lambda p: (p0 + p, 0, 0))] + [ANY] * len(prev),
        out_specs=pl.BlockSpec((3, PW, T), lambda p: (0, p0 + p, 0)),
        out_shape=S((3, D, T), bf16),
        input_output_aliases={7: 0} if prev else {},
        compiler_params=cp(), name="attn_bwd", cost_estimate=cost(cnt * 2 * 16 * T * T * 128, cnt * 2 * T * T * 2),
    )(kv, qkvt, qkvt, gmt, mixedf, linv, et, *prev)


def wqkv_body(n, me, xht, g, keep, send, res, vr, sems):
    j = pl.program_id(0)
    D = g.shape[0]
    r = D // n
    i0 = me[0]
    x = jnp.concatenate([xht[...], jnp.ones((16, xht.shape[1]), bf16)], axis=0)
    y = dot_t(x, g[...]).astype(bf16)
    res[j] = y[:D]
    vr[...] = jnp.where(lax.broadcasted_iota(jnp.int32, vr.shape, 0) == j, y[D:], jnp.where(j == 0, jnp.zeros_like(y[D:]), vr[...]))
    for s in range(n):
        push(i0, n, s, res.at[j, pl.ds(s * r, r)], keep, send, mult(j * r, 16), sems.at[j * n + s])

    @pl.when(j == 2)
    def _():
        for s in range(n):
            push(i0, n, s, vr, keep, send, 3 * r, sems.at[3 * n + s])
        for s in range(n):
            for q in range(3):
                pltpu.make_async_copy(res.at[0, pl.ds(0, r)], keep.at[0, pl.ds(0, r)], sems.at[q * n + s]).wait()
            pltpu.make_async_copy(vr, keep.at[0, pl.ds(0, VROWS)], sems.at[3 * n + s]).wait()


def wqkv(me, xht, g, n):
    D, T = xht.shape
    A = S((n // 2, 3 * (D // n) + VROWS, D), bf16)
    return pl.pallas_call(
        functools.partial(wqkv_body, n),
        grid_spec=pltpu.PrefetchScalarGridSpec(
            num_scalar_prefetch=1, grid=(3,),
            in_specs=[pl.BlockSpec((D, T), lambda j, m: (0, 0)), pl.BlockSpec((None, D, T), lambda j, m: (j, 0, 0))],
            out_specs=[ANY] * 2,
            scratch_shapes=[pltpu.VMEM((3, D, D), bf16), pltpu.VMEM((VROWS, D), bf16), pltpu.SemaphoreType.DMA((4 * n,))]),
        out_shape=[A, A],
        compiler_params=cp(), name="wqkv", cost_estimate=cost(6 * T * D * D, 10 * T * D),
    )(me, xht, g)


def back_body(tok, step, vec, g, gx1, *refs):
    ws, tg = refs[:-1], refs[-1]
    D = tok.shape[1]
    gw = D // GROUPS
    x = tok[...].astype(f32) + step[...].astype(f32)
    nx, rr = norm(x)
    gt = sum(dot(w[:, j * gw : (j + 1) * gw], g[j, q * gw : (q + 1) * gw, :]) for q, w in enumerate(ws) for j in range(3))
    gn = gt.T * row(vec[...], 0)
    tg[...] = gx1[...] + rr * (gn - jnp.mean(gn, axis=-1, keepdims=True) - nx * jnp.mean(gn * nx, axis=-1, keepdims=True))


def back(tok, step, vec, ws, g, gx1, bm=512):
    T, D = tok.shape
    full = lambda a: pl.BlockSpec(a.shape, lambda i: (0,) * a.ndim)
    rows = pl.BlockSpec((bm, D), lambda i: (i, 0))
    return pl.pallas_call(
        back_body, grid=(T // bm,),
        in_specs=[rows, full(step), full(vec), pl.BlockSpec((3, D, bm), lambda i: (0, 0, i)), rows] + [full(w) for w in ws],
        out_specs=rows, out_shape=S((T, D), f32), compiler_params=cp(), name="back", cost_estimate=cost(6 * T * D * D, 14 * T * D),
    )(tok, step, vec, g, gx1, *ws)


def shards(tokens, step_embed, lengths, cotangent, ln1_gain, ln1_bias, qkv_weight, q_bias, v_bias, out_weight, out_bias, ln2_gain, ln2_bias, up_weight, up_bias, down_weight, down_bias):
    n = lax.axis_size("shard")
    me = lax.axis_index("shard").astype(jnp.int32)
    mes = me[None]
    tok, cot, step = tokens[0], cotangent[0], step_embed
    T, D = tok.shape
    r = D // n
    FF = up_bias.shape[0] * n
    nc = FF // D
    rf = FF // n
    packs = pack_first(mes, qkv_weight, [ln1_gain, ln1_bias, q_bias, v_bias, out_bias, ln2_gain, ln2_bias, down_bias], up_bias)
    pack2 = pack_rest(out_weight, up_weight, down_weight)
    NP = HEADS // 2
    nx, xht = start(tok, step)
    pieces = gather_direct(packs[0], n, xht, pack2)
    kv, qkvt, w, vec, upb = front(mes, nx, pieces, n, FF)
    fw = attn_fwd(lengths, kv, qkvt, 0, NP // 2, [])
    fw2 = attn_fwd(lengths, kv, qkvt, NP // 2, NP // 2, fw)
    et, mixed, mixedt, mixedf, linv = fw2
    pieces2 = gather_forward(after(pack2, *[a for _, _, a in pieces[1:]]), n, fw[4], linv)
    out, gx1, gmt, keep, send = ffn(lengths, mes, tok, step, vec, upb, cot, mixed, mixedt, pieces2, n)
    bwd = lambda p, c, g, *deps: attn_bwd(kv, qkvt, after(gmt, *deps) if deps else gmt, mixedf, linv, et, p, c, g)
    ra = rf + r
    got = swap(send, 1)
    g = bwd(0, 1, [])
    got = after(got, g)
    h = n // 4
    add = lambda a, b, k: add16(a[k], b[k])
    rows_a, rows_b = slice(0, ra), slice(ra, None)
    lo, hi = slice(0, h), slice(h, None)
    ka, xa, kb, xb = [add(keep, got, k) for k in ((lo, rows_a), (hi, rows_a), (lo, rows_b), (hi, rows_b))]
    g = bwd(1, NP - 1, [g], ka, xa, kb, xb)
    m = (n // 2).bit_length() - 1
    ga, gb = swap(xa, 2 << (m - 1)), swap(xb, 2)
    for t in range(1, m):
        dep = g if t == 1 else keep
        ga, gb, _ = lax.optimization_barrier((ga, gb, dep))
        h //= 2
        lo, hi = slice(0, h), slice(h, None)
        ka, xa = add(ka, ga, lo), add(ka, ga, hi)
        kb, xb = add(kb, gb, lo), add(kb, gb, hi)
        ga, gb = swap(xa, 2 << (m - 1 - t)), swap(xb, 2 << t)
        if t == 1:
            keep, send = wqkv(mes, after(xht, ka, xa, kb, xb), g, n)
    got = swap(send, 1)
    p2 = [add16(keep[k], got[k]) for k in range(n // 2)]
    far2 = spread(p2)
    ga, gb, _ = lax.optimization_barrier((ga, gb, keep))
    got = swap(send, 1)
    p2 = [add16(keep[k], got[k]) for k in range(n // 2)]
    far2 = spread(p2)
    own1 = jnp.concatenate([add16(ka, ga)[0], add16(kb, gb)[0]], axis=0)
    m1, o1, x1 = rep_half(own1)
    z1 = add16(m1, after(o1, *p2[1:]))
    tg = back(tok, after(step, z1, *p2[1:]), vec, [w], g, gx1)
    own2 = total(p2[0], [after(a, tg) for a in far2])
    m2, o2, x2 = rep_half(own2)
    steps = rep_steps()
    z2 = None if steps else add16(m2, o2)
    for b in steps:
        z1 = add16(z1, after(rep_perm(z1, b), x2))
        if z2 is None:
            z2 = add16(m2, after(o2, z1))
        pz = rep_perm(z2, b)
        z2 = add16(z2, after(pz, z1))
    o1, o2 = rep_perm(z1, 1), rep_perm(z2, 1)
    ids = jnp.stack([me, (lax.axis_index("rep") % 2).astype(jnp.int32)])
    g_down, g_up, g_out, g_upb, g_ob, g_g2, g_b2, g_db = finish_rest(ids, z1, o1, r, rf, nc, n)
    g_qkv, g_g1, g_b1, g_q, g_v = finish_first(ids, z2, after(o2, g_out), qkv_weight, ln1_gain, ln1_bias)
    flat = lambda a: a.reshape(-1)
    return (out[None], tg[None], flat(g_g1), flat(g_b1), g_qkv, flat(g_q), flat(g_v), g_out, flat(g_ob), flat(g_g2), flat(g_b2), g_up, flat(g_upb), g_down, flat(g_db))


def solution(mesh):
    from jax.sharding import PartitionSpec as P

    in_specs = (
        P(("rep", "shard"), None, None),
        P(("rep", "shard"), None),
        P(("rep", "shard")),
        P(("rep", "shard"), None, None),
        P("shard"),
        P("shard"),
        P("shard", None),
        P("shard"),
        P("shard"),
        P("shard", None),
        P("shard"),
        P("shard"),
        P("shard"),
        P("shard", None),
        P("shard"),
        P("shard", None),
        P("shard"),
    )
    out_specs = (
        P(("rep", "shard"), None, None),
        P(("rep", "shard"), None, None),
        P("shard"),
        P("shard"),
        P("shard", None),
        P("shard"),
        P("shard"),
        P("shard", None),
        P("shard"),
        P("shard"),
        P("shard"),
        P("shard", None),
        P("shard"),
        P("shard", None),
        P("shard"),
    )
    return jax.shard_map(shards, mesh=mesh, in_specs=in_specs, out_specs=out_specs, check_vma=False)
```

```python
import functools, math
import jax, jax.numpy as jnp
from jax import lax
from jax.experimental import pallas as pl
from jax.experimental.pallas import tpu as pltpu

f32 = jnp.float32
bf16 = jnp.bfloat16
EPS = 1e-05
HEADS = 8

def dot(a, b):
    return jnp.dot(a, b, preferred_element_type=f32)

def dot_t(a, b):
    return lax.dot_general(a, b, (((1,), (1,)), ((), ())), preferred_element_type=f32)

def cp(n=1, vmem=100):
    return pltpu.CompilerParams(dimension_semantics=("arbitrary",) * n, vmem_limit_bytes=60 * 1024 * 1024)

def norm(x):
    c = x - jnp.mean(x, axis=-1, keepdims=True)
    r = lax.rsqrt(jnp.mean(c * c, axis=-1, keepdims=True) + EPS)
    return c * r, r

def row(v, i):
    return v[i : i + 1, :].astype(f32)


VROWS = 16
LANES = 128


def xor_perm(n, k):
    return [(i, i ^ k) for i in range(n)]


def rep_perm(x, b):
    return lax.ppermute(x, "rep", xor_perm(lax.axis_size("rep"), b))


def swap(x, k):
    return lax.ppermute(x, "shard", xor_perm(lax.axis_size("shard"), k))


def after(x, *deps):
    return lax.optimization_barrier((x,) + deps)[0]


def gather_direct(x, n, *gate):
    out = [(0, 0, x)]
    far = [(k, swap(x, k)) for k in range(2, n, 2)]
    out += [(k, 0, after(y, *gate) if gate else y) for k, y in far]
    return out + [(k ^ 1, 0, swap(y, 1)) for k, _, y in out]


def gather_forward(x, n, gate1, gate2):
    R = x.shape[0]
    cut = R // 2 // 16 * 16
    near = []
    far = []
    halves = {}
    for k in sorted(range(2, n, 2), key=lambda k: (bin(k).count("1"), k)):
        if bin(k).count("1") == 1:
            y = after(swap(x, k), gate1)
            near.append((k, 0, y))
            halves[k] = (y[:cut], y[cut:])
        else:
            low = k & -k
            high = 1 << (k.bit_length() - 1)
            a = swap(halves[k ^ low][0], low)
            b = swap(halves[k ^ high][1], high)
            far += [(k, 0, a), (k, cut, b)]
            halves[k] = (a, b)
    near = [(0, 0, x)] + near
    late = [(k, r0, after(a, gate2)) for k, r0, a in far]
    out = near + [(k ^ 1, r0, swap(a, 1)) for k, r0, a in near]
    return out + late + [(k ^ 1, r0, swap(a, 1)) for k, r0, a in late]


def add16(a, b):
    return a + b


def spread(parts):
    return [swap(parts[k], 2 * k) for k in range(len(parts) - 1, 0, -1)]


def total(own, got):
    t = own.astype(f32)
    for a in got:
        t = t + a.astype(f32)
    return t.astype(bf16)


def rep_half(x):
    h = x.shape[0] // 2
    odd = lax.axis_index("rep") % 2
    mine = lax.dynamic_slice_in_dim(x, odd * h, h, 0)
    other = lax.dynamic_slice_in_dim(x, (1 - odd) * h, h, 0)
    return mine, rep_perm(other, 1), other


def rep_steps():
    nr = lax.axis_size("rep")
    return [b for b in (2 << i for i in range(16)) if b < nr]


GROUPS = 1


def pack_first_body(me, w, upb, *refs):
    vecs = refs[:-GROUPS]
    outs = refs[-GROUPS:]
    r, W = w.shape
    D = W // 3
    gw = D // GROUPS
    for g, out in enumerate(outs):
        for j in range(3):
            out[j * r : (j + 1) * r, :] = w[:, j * D + g * gw : j * D + (g + 1) * gw]

    def spot(v):
        w_ = v.shape[1]
        if w_ >= LANES:
            return [v[q : q + 1, :] for q in range(v.shape[0])]
        t = LANES // w_
        lane = lax.broadcasted_iota(jnp.int32, (1, LANES), 1)
        return [jnp.where(lane // w_ == me[0] % t, jnp.concatenate([v] * t, axis=1), jnp.zeros((1, LANES), f32))]

    rows = [a for v in vecs for a in spot(v[...].astype(f32))] + spot(upb[...].astype(f32))
    b = jnp.concatenate(rows + [jnp.zeros((VROWS - len(rows), LANES), f32)], axis=0).astype(bf16)
    outs[0][3 * r :, :] = jnp.concatenate([b, jnp.zeros((VROWS, gw - LANES), bf16)], axis=1) if gw > LANES else b


def whole(n):
    return [pl.BlockSpec(memory_space=pltpu.VMEM)] * n


def once(*arrays):
    return [pl.BlockSpec(a.shape, lambda i, *m, nd=len(a.shape): (0,) * nd) for a in arrays]


def pack_first(me, w, vecs, upb):
    r, W = w.shape
    gw = W // 3 // GROUPS
    lanes = lambda v: v.reshape(-1, min(LANES, v.shape[0]))
    args = [w] + [lanes(v) for v in [upb] + vecs]
    outs = [S((3 * r + (VROWS if g == 0 else 0), gw), bf16) for g in range(GROUPS)]
    return pl.pallas_call(
        pack_first_body,
        grid_spec=pltpu.PrefetchScalarGridSpec(num_scalar_prefetch=1, grid=(1,), in_specs=once(*args), out_specs=once(*outs)),
        out_shape=outs, compiler_params=cp(), name="pack_first", cost_estimate=cost(0, 4 * w.size),
    )(me, *args)


def pack_rest_body(wo, wu, wd, out):
    r, D = wo.shape
    out[:r, :] = wo[...]
    for j in range(wu.shape[1] // D):
        out[(1 + j) * r : (2 + j) * r, :] = wu[:, j * D : (j + 1) * D]
    out[(1 + wu.shape[1] // D) * r :, :] = wd[...]


def pack_rest(wo, wu, wd):
    D = wo.shape[1]
    out = S(((wo.size + wu.size + wd.size) // D, D), bf16)
    return pl.pallas_call(
        pack_rest_body, grid=(1,), in_specs=once(wo, wu, wd), out_specs=once(out)[0],
        out_shape=out, compiler_params=cp(), name="pack_rest", cost_estimate=cost(0, 4 * wu.size),
    )(wo, wu, wd)


def own_lanes(tiles, me, w):
    pick = lambda i: sum(jnp.where(i == t, a, jnp.zeros_like(a)) for t, a in enumerate(tiles))
    if w >= LANES:
        q = w // LANES
        return jnp.concatenate([pick(me * q + c) for c in range(q)], axis=1)
    per = LANES // w
    x = pick(me // per)
    off = me % per
    return sum(jnp.where(off == o, x[:, o * w : (o + 1) * w], 0.0) for o in range(per))


def rows_of(lo, hi, a, b):
    h = lo.shape[0]
    if b <= h:
        return lo[a:b, :]
    if a >= h:
        return hi[a - h : b - h, :]
    return jnp.concatenate([lo[a:h, :], hi[: b - h, :]], axis=0)


def finish_rest_body(r, rf, n, ids, s, o, down, up, out, upb, *vecs):
    D = out.shape[1]
    nf = up.shape[1] // D

    def run(lo, hi):
        f = lambda a, b: rows_of(lo, hi, a, b).astype(f32)
        down[...] = f(0, rf)
        out[...] = f(rf, rf + r)
        for j in range(nf):
            up[:, j * D : (j + 1) * D] = f(rf + (j + 1) * r, rf + (j + 2) * r)
        b = rf + (nf + 1) * r
        v = f(b, b + VROWS)
        me = ids[0]
        tiles = [v[0:8, t * LANES : (t + 1) * LANES] for t in range(D // LANES)]
        x = own_lanes(tiles, me, r)
        for q, ref in enumerate(vecs):
            ref[...] = x[q : q + 1, :]
        tiles = [v[4 + q : 5 + q, t * LANES : (t + 1) * LANES] for q in range(nf) for t in range(D // LANES)]
        upb[...] = own_lanes(tiles, me, nf * D // n)

    @pl.when(ids[1] == 0)
    def _():
        run(s, o)

    @pl.when(ids[1] == 1)
    def _():
        run(o, s)


def finish_rest(ids, s, o, r, rf, nf, n):
    D = s.shape[1]
    row1 = lambda w: S((1, w), f32)
    return pl.pallas_call(
        functools.partial(finish_rest_body, r, rf, n),
        in_specs=[pl.BlockSpec(memory_space=pltpu.SMEM)] + whole(2), out_specs=whole(8),
        out_shape=[S((rf, D), f32), S((r, nf * D), f32), S((r, D), f32), row1(nf * D // n)] + [row1(r)] * 4,
        compiler_params=pltpu.CompilerParams(vmem_limit_bytes=16 << 20), name="finish_rest", cost_estimate=cost(0, 8 * s.size),
    )(ids, s, o)


def finish_first_body(ids, s, o, w, gain, bias, qkv, gg, gb, qb, vb):
    r, W = w.shape
    D = s.shape[1]

    def run(lo, hi):
        f = lambda a, b: rows_of(lo, hi, a, b).astype(f32)
        v = f(3 * r, 3 * r + VROWS)
        nt = D // LANES
        accg = accb = jnp.zeros((r, LANES), f32)
        col = lambda g: jnp.concatenate([g[...].astype(f32), jnp.zeros((7, r), f32)], axis=0).T[:, 0:1]
        cg, cb = col(gain), col(bias)
        for j in range(3):
            m = f(j * r, (j + 1) * r)
            sq = v[j : j + 1, :]
            ww = w[:, j * D : (j + 1) * D].astype(f32)
            qkv[:, j * D : (j + 1) * D] = cg * m + cb * sq
            pg, pb = ww * m, ww * sq
            accg = accg + sum(pg[:, t * LANES : (t + 1) * LANES] for t in range(nt))
            accb = accb + sum(pb[:, t * LANES : (t + 1) * LANES] for t in range(nt))
        gg[...] = jnp.sum(accg.T, axis=0, keepdims=True)
        gb[...] = jnp.sum(accb.T, axis=0, keepdims=True)
        x = own_lanes([v[0:8, t * LANES : (t + 1) * LANES] for t in range(nt)], ids[0], r)
        qb[...] = x[0:1, :]
        vb[...] = x[2:3, :]

    @pl.when(ids[1] == 0)
    def _():
        run(s, o)

    @pl.when(ids[1] == 1)
    def _():
        run(o, s)


def finish_first(ids, s, o, w, gain, bias):
    r, W = w.shape
    return pl.pallas_call(
        finish_first_body,
        in_specs=[pl.BlockSpec(memory_space=pltpu.SMEM)] + whole(5), out_specs=whole(5),
        out_shape=[S((r, W), f32)] + [S((1, r), f32)] * 4,
        compiler_params=pltpu.CompilerParams(vmem_limit_bytes=16 << 20), name="finish_first", cost_estimate=cost(0, 8 * w.size),
    )(ids, s, o, w, gain[None], bias[None])


def pull(me, refs, meta, segs, sems):
    copies = []
    for ref, (k, r0) in zip(refs, meta):
        s = jnp.bitwise_xor(me, k)
        r1 = r0 + ref.shape[0]
        for a, c, dst, lanes in segs:
            lo, hi = max(a, r0), min(a + c, r1)
            if lo < hi:
                src = ref.at[pl.ds(lo - r0, hi - lo), pl.ds(0, lanes)]
                copies.append(pltpu.make_async_copy(src, dst(s, lo - a, hi - lo), sems.at[len(copies)]))
    return copies


def mult(x, m):
    return pl.multiple_of(x, m)


def weight_segs(w, r):
    gw = w.shape[1] // 3
    seg = lambda j: (j * r, r, lambda s, o, c: w.at[pl.ds(mult(s * r + o, 16), c), pl.ds(j * gw, gw)], gw)
    return [seg(j) for j in range(3)]


def start_body(tok, step, nx, xht):
    n, _ = norm(tok[...].astype(f32) + step[...].astype(f32))
    nx[...] = n
    xht[...] = n.astype(bf16).T


def start(tok, step, bm=256):
    T, D = tok.shape
    rows = pl.BlockSpec((bm, D), lambda i: (i, 0))
    return pl.pallas_call(
        start_body, grid=(T // bm,),
        in_specs=[rows, pl.BlockSpec((1, D), lambda i: (0, 0))], out_specs=[rows, pl.BlockSpec((D, bm), lambda i: (0, i))],
        out_shape=[S((T, D), f32), S((D, T), bf16)], compiler_params=cp(), name="start", cost_estimate=cost(20 * T * D, 8 * T * D),
    )(tok, step)


def front_body(scale, n, meta, me, nx, *refs):
    np_ = len(meta)
    pieces = refs[:np_]
    kv, qkvt, wout, vec, upb, nv, h, w, vbuf, sems, own = refs[np_:]
    T, D = nv.shape
    r = D // n
    FF = upb.shape[1]
    i = pl.program_id(0)
    cw = kv.shape[2]
    per_j = D // cw
    segs = [(3 * r, VROWS, lambda s, o, c: vbuf.at[s, pl.ds(o, c)], LANES)] + weight_segs(w, r)
    load = pltpu.make_async_copy(nx, nv, own.at[0])
    save = pltpu.make_async_copy(w, wout, own.at[1])

    @pl.when(i == 0)
    def _():
        cs = pull(me[0], pieces, meta, segs, sems)
        for c in cs:
            c.start()
        load.start()
        for c in cs:
            c.wait()
        save.start()
        per = LANES // r
        tiles = [sum(vbuf[s, 0:8, :].astype(f32) for s in range(t * per, (t + 1) * per)) for t in range(D // LANES)]
        vec[...] = jnp.concatenate(tiles, axis=1)
        wu = FF // n
        if wu >= LANES:
            rows = [vbuf[s, 8 + q : 9 + q, :].astype(f32) for s in range(n) for q in range(wu // LANES)]
        else:
            per = LANES // wu
            rows = [sum(vbuf[s, 8:9, :].astype(f32) for s in range(t * per, (t + 1) * per)) for t in range(FF // LANES)]
        upb[...] = jnp.concatenate(rows, axis=1)
        load.wait()
        v = vec[...]
        h[...] = (nv[...] * row(v, 0) + row(v, 1)).astype(bf16)

    cols = pl.ds(mult(i * cw, 128), cw)
    y = dot(h[...], w[:, cols])
    here = pl.ds(mult((i % per_j) * cw, 128), cw)
    kind = i // per_j
    y = (y + jnp.where(kind == 0, vec[2:3, here], jnp.where(kind == 2, vec[3:4, here], 0.0))).astype(bf16)
    kv[0] = y
    qkvt[0] = jnp.where(kind == 0, y * bf16(scale), y).T

    @pl.when(i == pl.num_programs(0) - 1)
    def _():
        save.wait()


S = jax.ShapeDtypeStruct
ANY = pl.BlockSpec(memory_space=pl.ANY)


def cost(flops, nbytes, tr=0):
    return pl.CostEstimate(flops=int(flops), bytes_accessed=int(nbytes), transcendentals=int(tr))


def front(me, nx, pieces, n, FF, cw=512):
    T, D = nx.shape
    scale = 1.0 / math.sqrt(D // HEADS)
    meta = tuple((k, r0) for k, r0, _ in pieces)
    q = D // cw
    keep = lambda *sh: pl.BlockSpec(sh, lambda i, m: (0,) * len(sh))
    rest = lambda i: jnp.maximum(i - q, 0)
    V = pltpu.VMEM
    return pl.pallas_call(
        functools.partial(front_body, scale, n, meta),
        grid_spec=pltpu.PrefetchScalarGridSpec(
            num_scalar_prefetch=1, grid=(3 * q,),
            in_specs=[ANY] * (1 + len(pieces)),
            out_specs=[pl.BlockSpec((1, T, cw), lambda i, m: (rest(i) // q, 0, rest(i) % q)), pl.BlockSpec((1, cw, T), lambda i, m: (i // q, i % q, 0)), ANY, keep(8, D), keep(1, FF)],
            scratch_shapes=[V((T, D), f32), V((T, D), bf16), V((D, 3 * D), bf16), V((n, VROWS, LANES), bf16), pltpu.SemaphoreType.DMA((8 * len(pieces),)), pltpu.SemaphoreType.DMA((2,))]),
        out_shape=[S((2, T, D), bf16), S((3, D, T), bf16), S((D, 3 * D), bf16), S((8, D), f32), S((1, FF), f32)],
        compiler_params=cp(), name="front", cost_estimate=cost(6 * T * D * D, 12 * T * D),
    )(me, nx, *[a for _, _, a in pieces])


def attn_fwd_body(HD, bi, CR, p0, ln, k, qt, vt, *refs):
    et, mixed, mixedt, mixedf, linv, scr, ka, eb, esem = refs[-9:]
    T, PW = k.shape
    n = ln[0]
    p = pl.program_id(0)
    last = p == pl.num_programs(0) - 1
    rid = lax.broadcasted_iota(jnp.int32, (PW, bi), 0)
    lane = lax.broadcasted_iota(jnp.int32, (T, PW), 1)
    rows = lax.broadcasted_iota(jnp.int32, (T, PW), 0)
    ka[:, :PW] = k[...]
    ka[:, PW:] = jnp.where((lane == 0) & (rows >= n), f32(-1e30), f32(0)).astype(bf16)
    ones = jnp.where(rid == 0, f32(1), f32(0)).astype(bf16)
    va = [jnp.concatenate([vt[h * HD : (h + 1) * HD, :], jnp.ones((16, T), bf16)], axis=0) for h in range(2)]
    tasks = [(b, h) for b in range(T // bi) for h in range(2)]
    nch = T // CR

    def query(t):
        b, h = tasks[t]
        q = qt[:, b * bi : (b + 1) * bi]
        return jnp.concatenate([jnp.where(rid // HD == h, q, jnp.zeros_like(q)), ones], axis=0)

    def score(t, c, q):
        s = dot(ka[c * CR : (c + 1) * CR, :], q)
        scr[t % 2, c * CR : (c + 1) * CR, :] = s
        return jnp.max(s, axis=0, keepdims=True)

    q = query(0)
    m = functools.reduce(jnp.maximum, [score(0, c, q) for c in range(nch)])
    half = None
    for t, (b, h) in enumerate(tasks):
        sl = slice(b * bi, (b + 1) * bi)
        more = t + 1 < len(tasks)
        put = pltpu.make_async_copy(eb.at[t % 2], et.at[2 * (p0 + p) + h, :, pl.ds(b * bi, bi)], esem.at[t % 2])
        if t < 2:

            @pl.when(p > 0)
            def _():
                put.wait()

        else:
            put.wait()
        if more:
            q = query(t + 1)
        nxt = []
        for c in range(nch):
            cs = slice(c * CR, (c + 1) * CR)
            if more:
                nxt.append(score(t + 1, c, q))
            eb[t % 2, cs, :] = jnp.exp(scr[t % 2, cs, :] - m).astype(bf16)
        put.start()
        o = dot(va[h], eb[t % 2])
        if more:
            m = functools.reduce(jnp.maximum, nxt)
        inv = 1.0 / o[HD : HD + 1, :]
        linv[h : h + 1, sl] = inv
        o = o[:HD, :] * inv
        if h == 0:
            half = o
        else:
            mt = jnp.concatenate([half, o], axis=0)
            mixedf[:, sl] = mt
            mt = mt.astype(bf16)
            mixedt[:, sl] = mt
            mixed[sl, :] = mt.T

    @pl.when(last)
    def _():
        for q in range(2):
            pltpu.make_async_copy(eb.at[q], et.at[0, :, pl.ds(0, bi)], esem.at[q]).wait()


def attn_fwd(ln, kv, qkvt, p0, cnt, prev):
    _, T, D = kv.shape
    HD = D // HEADS
    PW = 2 * HD
    NP = D // PW
    bi = min(512, T)
    prev = list(prev)
    return pl.pallas_call(
        functools.partial(attn_fwd_body, HD, bi, min(256, T), p0),
        grid_spec=pltpu.PrefetchScalarGridSpec(
            num_scalar_prefetch=1, grid=(cnt,),
            in_specs=[pl.BlockSpec((None, T, PW), lambda p, r: (0, 0, p0 + p)), pl.BlockSpec((None, PW, T), lambda p, r: (0, p0 + p, 0)), pl.BlockSpec((None, PW, T), lambda p, r: (2, p0 + p, 0))] + [ANY] * len(prev),
            out_specs=[ANY, pl.BlockSpec((T, PW), lambda p, r: (0, p0 + p)), pl.BlockSpec((PW, T), lambda p, r: (p0 + p, 0)), pl.BlockSpec((PW, T), lambda p, r: (p0 + p, 0)), pl.BlockSpec((None, 8, T), lambda p, r: (p0 + p, 0, 0))],
            scratch_shapes=[pltpu.VMEM((2, T, bi), f32), pltpu.VMEM((T, 2 * PW), bf16), pltpu.VMEM((2, T, bi), bf16), pltpu.SemaphoreType.DMA((2,))]),
        out_shape=[S((HEADS, T, T), bf16), S((T, D), bf16), S((D, T), bf16), S((D, T), f32), S((NP, 8, T), f32)],
        input_output_aliases={4 + i: i for i in range(len(prev))},
        compiler_params=cp(), name="attn_fwd", cost_estimate=cost(cnt * 2 * 8 * T * T * 128, cnt * 2 * T * T * 2, cnt * 2 * T * T),
    )(ln, kv, qkvt, qkvt, *prev)


G0 = math.sqrt(2 / math.pi)


def bit_reverse(x, m):
    y = jnp.zeros_like(x)
    for t in range(m):
        y = y | (((x >> t) & 1) << (m - 1 - t))
    return y


def push(me, n, s, src, keep, send, row0, sem, reverse=False):
    k = jnp.bitwise_xor(me, s)
    p = k >> 1
    if reverse:
        p = bit_reverse(p, (n // 2).bit_length() - 1)
    put = lambda dst: pltpu.make_async_copy(src, dst.at[p, pl.ds(row0, src.shape[0])], sem)

    @pl.when(k & 1 == 0)
    def _():
        put(keep).start()

    @pl.when(k & 1 == 1)
    def _():
        put(send).start()


def ffn_body(n, meta, ch, ln, me, tok, step, vec, upb, cot, mixed, mixedt, *refs):
    np_ = len(meta)
    pieces = refs[:np_]
    out, gx1, gmt, keep, send, wo, wu, wd, act, gup, h2t, gdt, gattn, sums, upsum, dn, up, gwo, vr, mtv, sems, psems = refs[np_:]
    i = pl.program_id(0)
    bm, D = tok.shape
    FF = wu.shape[1]
    r = D // n
    rf = FF // n
    nf = FF // D
    i0 = me[0]
    ro = pl.ds(mult(i * bm, 128), bm)
    first = i == 0
    seg = lambda j: (r + j * r, r, lambda s, o, c: wu.at[pl.ds(mult(s * r + o, 16), c), pl.ds(j * D, D)], D)
    seg_o = [(0, r, lambda s, o, c: wo.at[pl.ds(mult(s * r + o, 16), c)], D)]
    seg_u = [seg(j) for j in range(nf)]
    seg_d = [(r + r * nf, rf, lambda s, o, c: wd.at[pl.ds(mult(s * rf + o, 16), c)], D)]
    q = sems.shape[0] // 4
    parts = [(seg_o, sems.at[pl.ds(0, q)]), (seg_d, sems.at[pl.ds(q, q)]), (seg_u, sems.at[pl.ds(2 * q, 2 * q)])]
    load = pltpu.make_async_copy(mixedt, mtv, psems.at[psems.shape[0] - 1])

    @pl.when(first)
    def _():
        for sg, sm in parts:
            for c in pull(i0, pieces, meta, sg, sm):
                c.start()
        load.start()
        sums[...] = jnp.zeros_like(sums)
        upsum[...] = jnp.zeros_like(upsum)
        for c in pull(i0, pieces, meta, *parts[0]):
            c.wait()

    v = vec[...]
    x1 = tok[...].astype(f32) + step[...].astype(f32) + dot(mixed[...], wo[...]) + row(v, 4)
    nx, rr = norm(x1)
    h2 = (nx * row(v, 5) + row(v, 6)).astype(bf16)
    live = (lax.broadcasted_iota(jnp.int32, (bm, 1), 0) + i * bm) < ln[0]
    gd = jnp.where(live, cot[...], jnp.zeros_like(cot))
    acc = x1 + row(v, 7)
    gh = None
    nc = FF // ch
    sl = [slice(c * ch, (c + 1) * ch) for c in range(nc)]
    lead = lambda c: (dot(h2, wu[:, sl[c]]), dot_t(gd, wd[sl[c], :]))
    h2t[:, ro] = h2.T
    gdt[:, ro] = gd.T

    @pl.when(first)
    def _():
        for sg, sm in parts[1:]:
            for c in pull(i0, pieces, meta, sg, sm):
                c.wait()

    nxt = lead(0)
    for c in range(nc):
        u, ga = nxt
        nxt = lead(c + 1) if c + 1 < nc else None
        u = u + upb[:, sl[c]]
        u2 = u * u
        t = jnp.tanh(u * (f32(G0) + f32(G0 * 0.044715) * u2))
        half = 0.5 + 0.5 * t
        a = (u * half).astype(bf16)
        act[ro, sl[c]] = a
        dg = half + u * (half * (1.0 - half)) * (f32(2 * G0) + f32(6 * 0.044715 * G0) * u2)
        gu = (ga * dg).astype(bf16)
        gup[ro, sl[c]] = gu
        upsum[:, sl[c]] += jnp.sum(gu.astype(f32), axis=0, keepdims=True)
        acc = acc + dot(a, wd[sl[c], :])
        p = dot_t(gu, wu[:, sl[c]])
        gh = p if gh is None else gh + p
    out[...] = jnp.where(live, acc, 0.0).astype(bf16)
    gn = gh * row(v, 5)
    gx = gd.astype(f32) + rr * (gn - jnp.mean(gn, axis=-1, keepdims=True) - nx * jnp.mean(gn * nx, axis=-1, keepdims=True))
    gx1[...] = gx
    gab = gx.astype(bf16)
    gattn[ro, :] = gab
    gmt[...] = dot_t(gab, wo[...]).astype(bf16).T
    s_ = lambda a: jnp.sum(a.astype(f32), axis=0, keepdims=True)
    sums[...] += jnp.concatenate([s_(gab), s_(gh * nx), s_(gh), s_(gd), jnp.zeros((4, D), f32)], axis=0)

    @pl.when(i == pl.num_programs(0) - 1)
    def _():
        per = D // rf
        o_out, o_up, o_vec = rf, rf + r, rf + (nf + 1) * r
        for j in range(nf):
            dn[j] = dot(gdt[...], act[:, j * D : (j + 1) * D]).astype(bf16).T
            for t in range(per):
                push(i0, n, j * per + t, dn.at[j, pl.ds(t * rf, rf)], keep, send, 0, psems.at[j * per + t])
            up[j] = dot(h2t[...], gup[:, j * D : (j + 1) * D]).astype(bf16)
            for s in range(n):
                push(i0, n, s, up.at[j, pl.ds(s * r, r)], keep, send, o_up + j * r, psems.at[n * (1 + j) + s], True)
        load.wait()
        gwo[...] = dot(mtv[...], gattn[...]).astype(bf16)
        vr[...] = jnp.concatenate([sums[0:4, :]] + [upsum[:, c * D : (c + 1) * D] for c in range(nf)] + [jnp.zeros((VROWS - 4 - nf, D), f32)], axis=0).astype(bf16)
        b = n * (1 + nf)
        for s in range(n):
            push(i0, n, s, gwo.at[pl.ds(s * r, r)], keep, send, o_out, psems.at[b + s])
            push(i0, n, s, vr, keep, send, o_vec, psems.at[b + n + s], True)
        done = lambda src, q: pltpu.make_async_copy(src, keep.at[0, pl.ds(0, src.shape[0])], psems.at[q]).wait()
        for s in range(n):
            done(dn.at[0, pl.ds(0, rf)], s)
            for c in range(nf):
                done(up.at[0, pl.ds(0, r)], n * (1 + c) + s)
            done(gwo.at[pl.ds(0, r)], b + s)
            done(vr, b + n + s)


def ffn(ln, me, tok, step, vec, upb, cot, mixed, mixedt, pieces, n):
    T, D = tok.shape
    FF = upb.shape[1]
    bm = min(512, T)
    nf = FF // D
    r = D // n
    meta = tuple((k, r0) for k, r0, _ in pieces)
    full = lambda a: pl.BlockSpec(a.shape, lambda i, l, m: (0,) * a.ndim)
    rows = pl.BlockSpec((bm, D), lambda i, l, m: (i, 0))
    B = S((n // 2, FF // n + (nf + 1) * r + VROWS, D), bf16)
    V = pltpu.VMEM
    return pl.pallas_call(
        functools.partial(ffn_body, n, meta, min(1024, FF)),
        grid_spec=pltpu.PrefetchScalarGridSpec(
            num_scalar_prefetch=2, grid=(T // bm,),
            in_specs=[rows, full(step), full(vec), full(upb), rows, rows, ANY] + [ANY] * len(pieces),
            out_specs=[rows, rows, pl.BlockSpec((D, bm), lambda i, l, m: (0, i)), ANY, ANY],
            scratch_shapes=[V((D, D), bf16), V((D, FF), bf16), V((FF, D), bf16), V((T, FF), bf16), V((T, FF), bf16), V((D, T), bf16), V((D, T), bf16), V((T, D), bf16), V((8, D), f32), V((1, FF), f32), V((nf, D, D), bf16), V((nf, D, D), bf16), V((D, D), bf16), V((VROWS, D), bf16), V((D, T), bf16), pltpu.SemaphoreType.DMA((16 * len(pieces),)), pltpu.SemaphoreType.DMA((n * (nf + 3) + 1,))]),
        out_shape=[S((T, D), bf16), S((T, D), f32), S((D, T), bf16), B, B],
        compiler_params=cp(), name="ffn", cost_estimate=cost(2 * T * D * (6 * FF + 3 * D), 16 * T * D, T * FF),
    )(ln, me, tok, step, vec, upb, cot, mixed, mixedt, *[a for _, _, a in pieces])


def attn_bwd_body(HD, scale, CR, v, kt, qt, gt, mt, linv, et, *refs):
    gq, ds = refs[-2:]
    T = v.shape[0]
    rid = lax.broadcasted_iota(jnp.int32, gt.shape, 0) // HD
    g = gt[...].astype(f32)
    q = qt[...]
    gv = gk = None
    for h in range(2):
        hs = slice(h * HD, (h + 1) * HD)
        gs = (g * linv[h : h + 1, :]).astype(bf16)
        gm = jnp.where(rid == h, gs, jnp.zeros_like(gs))
        dl = jnp.sum(gs[hs, :].astype(f32) * mt[hs, :], axis=0, keepdims=True)
        for c in range(T // CR):
            cs = slice(c * CR, (c + 1) * CR)
            ds[h, cs, :] = (et[h, cs, :].astype(f32) * (dot(v[cs, :], gm) - dl)).astype(bf16)
        a = dot(et[h], gm.T)
        b = dot(ds[h], jnp.where(rid == h, q, jnp.zeros_like(q)).T)
        gv = a if gv is None else gv + a
        gk = b if gk is None else gk + b
        gq[0, hs, :] = (dot(kt[hs, :], ds[h]) * scale).astype(bf16)
    gq[2] = gv.astype(bf16).T
    gq[1] = gk.astype(bf16).T


def attn_bwd(kv, qkvt, gmt, mixedf, linv, et, p0, cnt, prev):
    _, T, D = kv.shape
    HD = D // HEADS
    PW = 2 * HD
    NP = D // PW
    prev = list(prev)
    pr = pl.BlockSpec((PW, T), lambda p: (p0 + p, 0))
    of = lambda j: pl.BlockSpec((None, PW, T), lambda p: (j, p0 + p, 0))
    return pl.pallas_call(
        functools.partial(attn_bwd_body, HD, 1.0 / math.sqrt(HD), min(256, T)),
        grid=(cnt,),
        scratch_shapes=[pltpu.VMEM((2, T, T), bf16)],
        in_specs=[pl.BlockSpec((None, T, PW), lambda p: (1, 0, p0 + p)), of(1), of(0), pr, pr, pl.BlockSpec((None, 8, T), lambda p: (p0 + p, 0, 0)), pl.BlockSpec((2, T, T), lambda p: (p0 + p, 0, 0))] + [ANY] * len(prev),
        out_specs=pl.BlockSpec((3, PW, T), lambda p: (0, p0 + p, 0)),
        out_shape=S((3, D, T), bf16),
        input_output_aliases={7: 0} if prev else {},
        compiler_params=cp(), name="attn_bwd", cost_estimate=cost(cnt * 2 * 16 * T * T * 128, cnt * 2 * T * T * 2),
    )(kv, qkvt, qkvt, gmt, mixedf, linv, et, *prev)


def wqkv_body(n, me, xht, g, keep, send, res, vr, sems):
    j = pl.program_id(0)
    D = g.shape[0]
    r = D // n
    i0 = me[0]
    x = jnp.concatenate([xht[...], jnp.ones((16, xht.shape[1]), bf16)], axis=0)
    y = dot_t(x, g[...]).astype(bf16)
    res[j] = y[:D]
    vr[...] = jnp.where(lax.broadcasted_iota(jnp.int32, vr.shape, 0) == j, y[D:], jnp.where(j == 0, jnp.zeros_like(y[D:]), vr[...]))
    for s in range(n):
        push(i0, n, s, res.at[j, pl.ds(s * r, r)], keep, send, mult(j * r, 16), sems.at[j * n + s])

    @pl.when(j == 2)
    def _():
        for s in range(n):
            push(i0, n, s, vr, keep, send, 3 * r, sems.at[3 * n + s])
        for s in range(n):
            for q in range(3):
                pltpu.make_async_copy(res.at[0, pl.ds(0, r)], keep.at[0, pl.ds(0, r)], sems.at[q * n + s]).wait()
            pltpu.make_async_copy(vr, keep.at[0, pl.ds(0, VROWS)], sems.at[3 * n + s]).wait()


def wqkv(me, xht, g, n):
    D, T = xht.shape
    A = S((n // 2, 3 * (D // n) + VROWS, D), bf16)
    return pl.pallas_call(
        functools.partial(wqkv_body, n),
        grid_spec=pltpu.PrefetchScalarGridSpec(
            num_scalar_prefetch=1, grid=(3,),
            in_specs=[pl.BlockSpec((D, T), lambda j, m: (0, 0)), pl.BlockSpec((None, D, T), lambda j, m: (j, 0, 0))],
            out_specs=[ANY] * 2,
            scratch_shapes=[pltpu.VMEM((3, D, D), bf16), pltpu.VMEM((VROWS, D), bf16), pltpu.SemaphoreType.DMA((4 * n,))]),
        out_shape=[A, A],
        compiler_params=cp(), name="wqkv", cost_estimate=cost(6 * T * D * D, 10 * T * D),
    )(me, xht, g)


def back_body(tok, step, vec, g, gx1, *refs):
    ws, tg = refs[:-1], refs[-1]
    D = tok.shape[1]
    gw = D // GROUPS
    x = tok[...].astype(f32) + step[...].astype(f32)
    nx, rr = norm(x)
    gt = sum(dot(w[:, j * gw : (j + 1) * gw], g[j, q * gw : (q + 1) * gw, :]) for q, w in enumerate(ws) for j in range(3))
    gn = gt.T * row(vec[...], 0)
    tg[...] = gx1[...] + rr * (gn - jnp.mean(gn, axis=-1, keepdims=True) - nx * jnp.mean(gn * nx, axis=-1, keepdims=True))


def back(tok, step, vec, ws, g, gx1, bm=512):
    T, D = tok.shape
    full = lambda a: pl.BlockSpec(a.shape, lambda i: (0,) * a.ndim)
    rows = pl.BlockSpec((bm, D), lambda i: (i, 0))
    return pl.pallas_call(
        back_body, grid=(T // bm,),
        in_specs=[rows, full(step), full(vec), pl.BlockSpec((3, D, bm), lambda i: (0, 0, i)), rows] + [full(w) for w in ws],
        out_specs=rows, out_shape=S((T, D), f32), compiler_params=cp(), name="back", cost_estimate=cost(6 * T * D * D, 14 * T * D),
    )(tok, step, vec, g, gx1, *ws)


def shards(tokens, step_embed, lengths, cotangent, ln1_gain, ln1_bias, qkv_weight, q_bias, v_bias, out_weight, out_bias, ln2_gain, ln2_bias, up_weight, up_bias, down_weight, down_bias):
    n = lax.axis_size("shard")
    me = lax.axis_index("shard").astype(jnp.int32)
    mes = me[None]
    tok, cot, step = tokens[0], cotangent[0], step_embed
    T, D = tok.shape
    r = D // n
    FF = up_bias.shape[0] * n
    nc = FF // D
    rf = FF // n
    packs = pack_first(mes, qkv_weight, [ln1_gain, ln1_bias, q_bias, v_bias, out_bias, ln2_gain, ln2_bias, down_bias], up_bias)
    pack2 = pack_rest(out_weight, up_weight, down_weight)
    NP = HEADS // 2
    nx, xht = start(tok, step)
    pieces = gather_direct(packs[0], n, xht, pack2)
    kv, qkvt, w, vec, upb = front(mes, nx, pieces, n, FF)
    fw = attn_fwd(lengths, kv, qkvt, 0, NP // 2, [])
    fw2 = attn_fwd(lengths, kv, qkvt, NP // 2, NP // 2, fw)
    et, mixed, mixedt, mixedf, linv = fw2
    pieces2 = gather_forward(after(pack2, xht), n, fw[4], linv)
    out, gx1, gmt, keep, send = ffn(lengths, mes, tok, step, vec, upb, cot, mixed, mixedt, pieces2, n)
    bwd = lambda p, c, g, *deps: attn_bwd(kv, qkvt, after(gmt, *deps) if deps else gmt, mixedf, linv, et, p, c, g)
    ra = rf + r
    got = swap(send, 1)
    g = bwd(0, 1, [])
    got = after(got, g)
    h = n // 4
    add = lambda a, b, k: add16(a[k], b[k])
    rows_a, rows_b = slice(0, ra), slice(ra, None)
    lo, hi = slice(0, h), slice(h, None)
    xa, xb = add(keep, got, (hi, rows_a)), add(keep, got, (hi, rows_b))
    g = bwd(1, NP - 1, [g], xa, xb)
    mine, got, _ = lax.optimization_barrier((keep, got, g))
    ka, kb = add(mine, got, (lo, rows_a)), add(mine, got, (lo, rows_b))
    m = (n // 2).bit_length() - 1
    ga, gb = swap(xa, 2 << (m - 1)), swap(xb, 2)
    for t in range(1, m):
        dep = g if t == 1 else keep
        ga, gb, _ = lax.optimization_barrier((ga, gb, dep))
        h //= 2
        lo, hi = slice(0, h), slice(h, None)
        ka, xa = add(ka, ga, lo), add(ka, ga, hi)
        kb, xb = add(kb, gb, lo), add(kb, gb, hi)
        ga, gb = swap(xa, 2 << (m - 1 - t)), swap(xb, 2 << t)
        if t == 1:
            keep, send = wqkv(mes, after(xht, ka, xa, kb, xb), g, n)
    got = swap(send, 1)
    p2 = [add16(keep[k], got[k]) for k in range(n // 2)]
    far2 = spread(p2)
    ga, gb, _ = lax.optimization_barrier((ga, gb, keep))
    got = swap(send, 1)
    p2 = [add16(keep[k], got[k]) for k in range(n // 2)]
    far2 = spread(p2)
    own1 = jnp.concatenate([add16(ka, ga)[0], add16(kb, gb)[0]], axis=0)
    m1, o1, x1 = rep_half(own1)
    z1 = add16(m1, after(o1, *p2[1:]))
    tg = back(tok, after(step, z1, *p2[1:]), vec, [w], g, gx1)
    own2 = total(p2[0], [after(a, tg) for a in far2])
    m2, o2, x2 = rep_half(own2)
    steps = rep_steps()
    z2 = None if steps else add16(m2, o2)
    for b in steps:
        z1 = add16(z1, after(rep_perm(z1, b), x2))
        if z2 is None:
            z2 = add16(m2, after(o2, z1))
        pz = rep_perm(z2, b)
        z2 = add16(z2, after(pz, z1))
    o1, o2 = rep_perm(z1, 1), rep_perm(z2, 1)
    ids = jnp.stack([me, (lax.axis_index("rep") % 2).astype(jnp.int32)])
    g_down, g_up, g_out, g_upb, g_ob, g_g2, g_b2, g_db = finish_rest(ids, z1, o1, r, rf, nc, n)
    g_qkv, g_g1, g_b1, g_q, g_v = finish_first(ids, z2, after(o2, g_out), qkv_weight, ln1_gain, ln1_bias)
    flat = lambda a: a.reshape(-1)
    return (out[None], tg[None], flat(g_g1), flat(g_b1), g_qkv, flat(g_q), flat(g_v), g_out, flat(g_ob), flat(g_g2), flat(g_b2), g_up, flat(g_upb), g_down, flat(g_db))


def solution(mesh):
    from jax.sharding import PartitionSpec as P

    in_specs = (
        P(("rep", "shard"), None, None),
        P(("rep", "shard"), None),
        P(("rep", "shard")),
        P(("rep", "shard"), None, None),
        P("shard"),
        P("shard"),
        P("shard", None),
        P("shard"),
        P("shard"),
        P("shard", None),
        P("shard"),
        P("shard"),
        P("shard"),
        P("shard", None),
        P("shard"),
        P("shard", None),
        P("shard"),
    )
    out_specs = (
        P(("rep", "shard"), None, None),
        P(("rep", "shard"), None, None),
        P("shard"),
        P("shard"),
        P("shard", None),
        P("shard"),
        P("shard"),
        P("shard", None),
        P("shard"),
        P("shard"),
        P("shard"),
        P("shard", None),
        P("shard"),
        P("shard", None),
        P("shard"),
    )
    return jax.shard_map(shards, mesh=mesh, in_specs=in_specs, out_specs=out_specs, check_vma=False)
```

```python
import functools, math
import jax, jax.numpy as jnp
from jax import lax
from jax.experimental import pallas as pl
from jax.experimental.pallas import tpu as pltpu

f32 = jnp.float32
bf16 = jnp.bfloat16
EPS = 1e-05
HEADS = 8

def dot(a, b):
    return jnp.dot(a, b, preferred_element_type=f32)

def dot_t(a, b):
    return lax.dot_general(a, b, (((1,), (1,)), ((), ())), preferred_element_type=f32)

def cp(n=1, vmem=100):
    return pltpu.CompilerParams(dimension_semantics=("arbitrary",) * n, vmem_limit_bytes=60 * 1024 * 1024)

def norm(x):
    c = x - jnp.mean(x, axis=-1, keepdims=True)
    r = lax.rsqrt(jnp.mean(c * c, axis=-1, keepdims=True) + EPS)
    return c * r, r

def row(v, i):
    return v[i : i + 1, :].astype(f32)


VROWS = 16
LANES = 128


def xor_perm(n, k):
    return [(i, i ^ k) for i in range(n)]


def rep_perm(x, b):
    return lax.ppermute(x, "rep", xor_perm(lax.axis_size("rep"), b))


def swap(x, k):
    return lax.ppermute(x, "shard", xor_perm(lax.axis_size("shard"), k))


def after(x, *deps):
    return lax.optimization_barrier((x,) + deps)[0]


def gather_direct(x, n, *gate):
    out = [(0, 0, x)]
    far = [(k, swap(x, k)) for k in range(2, n, 2)]
    out += [(k, 0, after(y, *gate) if gate else y) for k, y in far]
    return out + [(k ^ 1, 0, swap(y, 1)) for k, _, y in out]


def gather_forward(x, n, gate1, gate2):
    R = x.shape[0]
    cut = R // 2 // 16 * 16
    near = []
    far = []
    halves = {}
    for k in sorted(range(2, n, 2), key=lambda k: (bin(k).count("1"), k)):
        if bin(k).count("1") == 1:
            y = after(swap(x, k), gate1)
            near.append((k, 0, y))
            halves[k] = (y[:cut], y[cut:])
        else:
            low = k & -k
            high = 1 << (k.bit_length() - 1)
            a = swap(halves[k ^ low][0], low)
            b = swap(halves[k ^ high][1], high)
            far += [(k, 0, a), (k, cut, b)]
            halves[k] = (a, b)
    near = [(0, 0, x)] + near
    late = [(k, r0, after(a, gate2)) for k, r0, a in far]
    out = near + [(k ^ 1, r0, swap(a, 1)) for k, r0, a in near]
    return out + late + [(k ^ 1, r0, swap(a, 1)) for k, r0, a in late]


def add16(a, b):
    return a + b


def spread(parts):
    return [swap(parts[k], 2 * k) for k in range(len(parts) - 1, 0, -1)]


def total(own, got):
    t = own.astype(f32)
    for a in got:
        t = t + a.astype(f32)
    return t.astype(bf16)


def rep_half(x):
    h = x.shape[0] // 2
    odd = lax.axis_index("rep") % 2
    mine = lax.dynamic_slice_in_dim(x, odd * h, h, 0)
    other = lax.dynamic_slice_in_dim(x, (1 - odd) * h, h, 0)
    return mine, rep_perm(other, 1), other


def rep_steps():
    nr = lax.axis_size("rep")
    return [b for b in (2 << i for i in range(16)) if b < nr]


GROUPS = 1


def pack_first_body(me, w, upb, *refs):
    vecs = refs[:-GROUPS]
    outs = refs[-GROUPS:]
    r, W = w.shape
    D = W // 3
    gw = D // GROUPS
    for g, out in enumerate(outs):
        for j in range(3):
            out[j * r : (j + 1) * r, :] = w[:, j * D + g * gw : j * D + (g + 1) * gw]

    def spot(v):
        w_ = v.shape[1]
        if w_ >= LANES:
            return [v[q : q + 1, :] for q in range(v.shape[0])]
        t = LANES // w_
        lane = lax.broadcasted_iota(jnp.int32, (1, LANES), 1)
        return [jnp.where(lane // w_ == me[0] % t, jnp.concatenate([v] * t, axis=1), jnp.zeros((1, LANES), f32))]

    rows = [a for v in vecs for a in spot(v[...].astype(f32))] + spot(upb[...].astype(f32))
    b = jnp.concatenate(rows + [jnp.zeros((VROWS - len(rows), LANES), f32)], axis=0).astype(bf16)
    outs[0][3 * r :, :] = jnp.concatenate([b, jnp.zeros((VROWS, gw - LANES), bf16)], axis=1) if gw > LANES else b


def whole(n):
    return [pl.BlockSpec(memory_space=pltpu.VMEM)] * n


def once(*arrays):
    return [pl.BlockSpec(a.shape, lambda i, *m, nd=len(a.shape): (0,) * nd) for a in arrays]


def pack_first(me, w, vecs, upb):
    r, W = w.shape
    gw = W // 3 // GROUPS
    lanes = lambda v: v.reshape(-1, min(LANES, v.shape[0]))
    args = [w] + [lanes(v) for v in [upb] + vecs]
    outs = [S((3 * r + (VROWS if g == 0 else 0), gw), bf16) for g in range(GROUPS)]
    return pl.pallas_call(
        pack_first_body,
        grid_spec=pltpu.PrefetchScalarGridSpec(num_scalar_prefetch=1, grid=(1,), in_specs=once(*args), out_specs=once(*outs)),
        out_shape=outs, compiler_params=cp(), name="pack_first", cost_estimate=cost(0, 4 * w.size),
    )(me, *args)


def pack_rest_body(wo, wu, wd, out):
    r, D = wo.shape
    out[:r, :] = wo[...]
    for j in range(wu.shape[1] // D):
        out[(1 + j) * r : (2 + j) * r, :] = wu[:, j * D : (j + 1) * D]
    out[(1 + wu.shape[1] // D) * r :, :] = wd[...]


def pack_rest(wo, wu, wd):
    D = wo.shape[1]
    out = S(((wo.size + wu.size + wd.size) // D, D), bf16)
    return pl.pallas_call(
        pack_rest_body, grid=(1,), in_specs=once(wo, wu, wd), out_specs=once(out)[0],
        out_shape=out, compiler_params=cp(), name="pack_rest", cost_estimate=cost(0, 4 * wu.size),
    )(wo, wu, wd)


def own_lanes(tiles, me, w):
    pick = lambda i: sum(jnp.where(i == t, a, jnp.zeros_like(a)) for t, a in enumerate(tiles))
    if w >= LANES:
        q = w // LANES
        return jnp.concatenate([pick(me * q + c) for c in range(q)], axis=1)
    per = LANES // w
    x = pick(me // per)
    off = me % per
    return sum(jnp.where(off == o, x[:, o * w : (o + 1) * w], 0.0) for o in range(per))


def rows_of(lo, hi, a, b):
    h = lo.shape[0]
    if b <= h:
        return lo[a:b, :]
    if a >= h:
        return hi[a - h : b - h, :]
    return jnp.concatenate([lo[a:h, :], hi[: b - h, :]], axis=0)


def finish_rest_body(r, rf, n, ids, s, o, down, up, out, upb, *vecs):
    D = out.shape[1]
    nf = up.shape[1] // D

    def run(lo, hi):
        f = lambda a, b: rows_of(lo, hi, a, b).astype(f32)
        down[...] = f(0, rf)
        out[...] = f(rf, rf + r)
        for j in range(nf):
            up[:, j * D : (j + 1) * D] = f(rf + (j + 1) * r, rf + (j + 2) * r)
        b = rf + (nf + 1) * r
        v = f(b, b + VROWS)
        me = ids[0]
        tiles = [v[0:8, t * LANES : (t + 1) * LANES] for t in range(D // LANES)]
        x = own_lanes(tiles, me, r)
        for q, ref in enumerate(vecs):
            ref[...] = x[q : q + 1, :]
        tiles = [v[4 + q : 5 + q, t * LANES : (t + 1) * LANES] for q in range(nf) for t in range(D // LANES)]
        upb[...] = own_lanes(tiles, me, nf * D // n)

    @pl.when(ids[1] == 0)
    def _():
        run(s, o)

    @pl.when(ids[1] == 1)
    def _():
        run(o, s)


def finish_rest(ids, s, o, r, rf, nf, n):
    D = s.shape[1]
    row1 = lambda w: S((1, w), f32)
    return pl.pallas_call(
        functools.partial(finish_rest_body, r, rf, n),
        in_specs=[pl.BlockSpec(memory_space=pltpu.SMEM)] + whole(2), out_specs=whole(8),
        out_shape=[S((rf, D), f32), S((r, nf * D), f32), S((r, D), f32), row1(nf * D // n)] + [row1(r)] * 4,
        compiler_params=pltpu.CompilerParams(vmem_limit_bytes=16 << 20), name="finish_rest", cost_estimate=cost(0, 8 * s.size),
    )(ids, s, o)


def finish_first_body(ids, s, o, w, gain, bias, qkv, gg, gb, qb, vb):
    r, W = w.shape
    D = s.shape[1]

    def run(lo, hi):
        f = lambda a, b: rows_of(lo, hi, a, b).astype(f32)
        v = f(3 * r, 3 * r + VROWS)
        nt = D // LANES
        accg = accb = jnp.zeros((r, LANES), f32)
        col = lambda g: jnp.concatenate([g[...].astype(f32), jnp.zeros((7, r), f32)], axis=0).T[:, 0:1]
        cg, cb = col(gain), col(bias)
        for j in range(3):
            m = f(j * r, (j + 1) * r)
            sq = v[j : j + 1, :]
            ww = w[:, j * D : (j + 1) * D].astype(f32)
            qkv[:, j * D : (j + 1) * D] = cg * m + cb * sq
            pg, pb = ww * m, ww * sq
            accg = accg + sum(pg[:, t * LANES : (t + 1) * LANES] for t in range(nt))
            accb = accb + sum(pb[:, t * LANES : (t + 1) * LANES] for t in range(nt))
        gg[...] = jnp.sum(accg.T, axis=0, keepdims=True)
        gb[...] = jnp.sum(accb.T, axis=0, keepdims=True)
        x = own_lanes([v[0:8, t * LANES : (t + 1) * LANES] for t in range(nt)], ids[0], r)
        qb[...] = x[0:1, :]
        vb[...] = x[2:3, :]

    @pl.when(ids[1] == 0)
    def _():
        run(s, o)

    @pl.when(ids[1] == 1)
    def _():
        run(o, s)


def finish_first(ids, s, o, w, gain, bias):
    r, W = w.shape
    return pl.pallas_call(
        finish_first_body,
        in_specs=[pl.BlockSpec(memory_space=pltpu.SMEM)] + whole(5), out_specs=whole(5),
        out_shape=[S((r, W), f32)] + [S((1, r), f32)] * 4,
        compiler_params=pltpu.CompilerParams(vmem_limit_bytes=16 << 20), name="finish_first", cost_estimate=cost(0, 8 * w.size),
    )(ids, s, o, w, gain[None], bias[None])


def pull(me, refs, meta, segs, sems):
    copies = []
    for ref, (k, r0) in zip(refs, meta):
        s = jnp.bitwise_xor(me, k)
        r1 = r0 + ref.shape[0]
        for a, c, dst, lanes in segs:
            lo, hi = max(a, r0), min(a + c, r1)
            if lo < hi:
                src = ref.at[pl.ds(lo - r0, hi - lo), pl.ds(0, lanes)]
                copies.append(pltpu.make_async_copy(src, dst(s, lo - a, hi - lo), sems.at[len(copies)]))
    return copies


def mult(x, m):
    return pl.multiple_of(x, m)


def weight_segs(w, r):
    gw = w.shape[1] // 3
    seg = lambda j: (j * r, r, lambda s, o, c: w.at[pl.ds(mult(s * r + o, 16), c), pl.ds(j * gw, gw)], gw)
    return [seg(j) for j in range(3)]


def start_body(tok, step, nx, xht):
    n, _ = norm(tok[...].astype(f32) + step[...].astype(f32))
    nx[...] = n
    xht[...] = n.astype(bf16).T


def start(tok, step, bm=256):
    T, D = tok.shape
    rows = pl.BlockSpec((bm, D), lambda i: (i, 0))
    return pl.pallas_call(
        start_body, grid=(T // bm,),
        in_specs=[rows, pl.BlockSpec((1, D), lambda i: (0, 0))], out_specs=[rows, pl.BlockSpec((D, bm), lambda i: (0, i))],
        out_shape=[S((T, D), f32), S((D, T), bf16)], compiler_params=cp(), name="start", cost_estimate=cost(20 * T * D, 8 * T * D),
    )(tok, step)


def front_body(scale, n, meta, me, nx, *refs):
    np_ = len(meta)
    pieces = refs[:np_]
    kv, qkvt, wout, vec, upb, nv, h, w, vbuf, sems, own = refs[np_:]
    T, D = nv.shape
    r = D // n
    FF = upb.shape[1]
    i = pl.program_id(0)
    cw = kv.shape[2]
    per_j = D // cw
    segs = [(3 * r, VROWS, lambda s, o, c: vbuf.at[s, pl.ds(o, c)], LANES)] + weight_segs(w, r)
    load = pltpu.make_async_copy(nx, nv, own.at[0])
    save = pltpu.make_async_copy(w, wout, own.at[1])

    @pl.when(i == 0)
    def _():
        cs = pull(me[0], pieces, meta, segs, sems)
        for c in cs:
            c.start()
        load.start()
        for c in cs:
            c.wait()
        save.start()
        per = LANES // r
        tiles = [sum(vbuf[s, 0:8, :].astype(f32) for s in range(t * per, (t + 1) * per)) for t in range(D // LANES)]
        vec[...] = jnp.concatenate(tiles, axis=1)
        wu = FF // n
        if wu >= LANES:
            rows = [vbuf[s, 8 + q : 9 + q, :].astype(f32) for s in range(n) for q in range(wu // LANES)]
        else:
            per = LANES // wu
            rows = [sum(vbuf[s, 8:9, :].astype(f32) for s in range(t * per, (t + 1) * per)) for t in range(FF // LANES)]
        upb[...] = jnp.concatenate(rows, axis=1)
        load.wait()
        v = vec[...]
        h[...] = (nv[...] * row(v, 0) + row(v, 1)).astype(bf16)

    cols = pl.ds(mult(i * cw, 128), cw)
    y = dot(h[...], w[:, cols])
    here = pl.ds(mult((i % per_j) * cw, 128), cw)
    kind = i // per_j
    y = (y + jnp.where(kind == 0, vec[2:3, here], jnp.where(kind == 2, vec[3:4, here], 0.0))).astype(bf16)
    kv[0] = y
    qkvt[0] = jnp.where(kind == 0, y * bf16(scale), y).T

    @pl.when(i == pl.num_programs(0) - 1)
    def _():
        save.wait()


S = jax.ShapeDtypeStruct
ANY = pl.BlockSpec(memory_space=pl.ANY)


def cost(flops, nbytes, tr=0):
    return pl.CostEstimate(flops=int(flops), bytes_accessed=int(nbytes), transcendentals=int(tr))


def front(me, nx, pieces, n, FF, cw=512):
    T, D = nx.shape
    scale = 1.0 / math.sqrt(D // HEADS)
    meta = tuple((k, r0) for k, r0, _ in pieces)
    q = D // cw
    keep = lambda *sh: pl.BlockSpec(sh, lambda i, m: (0,) * len(sh))
    rest = lambda i: jnp.maximum(i - q, 0)
    V = pltpu.VMEM
    return pl.pallas_call(
        functools.partial(front_body, scale, n, meta),
        grid_spec=pltpu.PrefetchScalarGridSpec(
            num_scalar_prefetch=1, grid=(3 * q,),
            in_specs=[ANY] * (1 + len(pieces)),
            out_specs=[pl.BlockSpec((1, T, cw), lambda i, m: (rest(i) // q, 0, rest(i) % q)), pl.BlockSpec((1, cw, T), lambda i, m: (i // q, i % q, 0)), ANY, keep(8, D), keep(1, FF)],
            scratch_shapes=[V((T, D), f32), V((T, D), bf16), V((D, 3 * D), bf16), V((n, VROWS, LANES), bf16), pltpu.SemaphoreType.DMA((8 * len(pieces),)), pltpu.SemaphoreType.DMA((2,))]),
        out_shape=[S((2, T, D), bf16), S((3, D, T), bf16), S((D, 3 * D), bf16), S((8, D), f32), S((1, FF), f32)],
        compiler_params=cp(), name="front", cost_estimate=cost(6 * T * D * D, 12 * T * D),
    )(me, nx, *[a for _, _, a in pieces])


def attn_fwd_body(HD, bi, CR, p0, ln, k, qt, vt, *refs):
    et, mixed, mixedt, mixedf, linv, scr, ka, eb, esem = refs[-9:]
    T, PW = k.shape
    n = ln[0]
    p = pl.program_id(0)
    last = p == pl.num_programs(0) - 1
    rid = lax.broadcasted_iota(jnp.int32, (PW, bi), 0)
    lane = lax.broadcasted_iota(jnp.int32, (T, PW), 1)
    rows = lax.broadcasted_iota(jnp.int32, (T, PW), 0)
    ka[:, :PW] = k[...]
    ka[:, PW:] = jnp.where((lane == 0) & (rows >= n), f32(-1e30), f32(0)).astype(bf16)
    ones = jnp.where(rid == 0, f32(1), f32(0)).astype(bf16)
    va = [jnp.concatenate([vt[h * HD : (h + 1) * HD, :], jnp.ones((16, T), bf16)], axis=0) for h in range(2)]
    tasks = [(b, h) for b in range(T // bi) for h in range(2)]
    nch = T // CR

    def query(t):
        b, h = tasks[t]
        q = qt[:, b * bi : (b + 1) * bi]
        return jnp.concatenate([jnp.where(rid // HD == h, q, jnp.zeros_like(q)), ones], axis=0)

    def score(t, c, q):
        s = dot(ka[c * CR : (c + 1) * CR, :], q)
        scr[t % 2, c * CR : (c + 1) * CR, :] = s
        return jnp.max(s, axis=0, keepdims=True)

    q = query(0)
    m = functools.reduce(jnp.maximum, [score(0, c, q) for c in range(nch)])
    half = None
    for t, (b, h) in enumerate(tasks):
        sl = slice(b * bi, (b + 1) * bi)
        more = t + 1 < len(tasks)
        put = pltpu.make_async_copy(eb.at[t % 2], et.at[2 * (p0 + p) + h, :, pl.ds(b * bi, bi)], esem.at[t % 2])
        if t < 2:

            @pl.when(p > 0)
            def _():
                put.wait()

        else:
            put.wait()
        if more:
            q = query(t + 1)
        nxt = []
        for c in range(nch):
            cs = slice(c * CR, (c + 1) * CR)
            if more:
                nxt.append(score(t + 1, c, q))
            eb[t % 2, cs, :] = jnp.exp(scr[t % 2, cs, :] - m).astype(bf16)
        put.start()
        o = dot(va[h], eb[t % 2])
        if more:
            m = functools.reduce(jnp.maximum, nxt)
        inv = 1.0 / o[HD : HD + 1, :]
        linv[h : h + 1, sl] = inv
        o = o[:HD, :] * inv
        if h == 0:
            half = o
        else:
            mt = jnp.concatenate([half, o], axis=0)
            mixedf[:, sl] = mt
            mt = mt.astype(bf16)
            mixedt[:, sl] = mt
            mixed[sl, :] = mt.T

    @pl.when(last)
    def _():
        for q in range(2):
            pltpu.make_async_copy(eb.at[q], et.at[0, :, pl.ds(0, bi)], esem.at[q]).wait()


def attn_fwd(ln, kv, qkvt, p0, cnt, prev):
    _, T, D = kv.shape
    HD = D // HEADS
    PW = 2 * HD
    NP = D // PW
    bi = min(512, T)
    prev = list(prev)
    return pl.pallas_call(
        functools.partial(attn_fwd_body, HD, bi, min(256, T), p0),
        grid_spec=pltpu.PrefetchScalarGridSpec(
            num_scalar_prefetch=1, grid=(cnt,),
            in_specs=[pl.BlockSpec((None, T, PW), lambda p, r: (0, 0, p0 + p)), pl.BlockSpec((None, PW, T), lambda p, r: (0, p0 + p, 0)), pl.BlockSpec((None, PW, T), lambda p, r: (2, p0 + p, 0))] + [ANY] * len(prev),
            out_specs=[ANY, pl.BlockSpec((T, PW), lambda p, r: (0, p0 + p)), pl.BlockSpec((PW, T), lambda p, r: (p0 + p, 0)), pl.BlockSpec((PW, T), lambda p, r: (p0 + p, 0)), pl.BlockSpec((None, 8, T), lambda p, r: (p0 + p, 0, 0))],
            scratch_shapes=[pltpu.VMEM((2, T, bi), f32), pltpu.VMEM((T, 2 * PW), bf16), pltpu.VMEM((2, T, bi), bf16), pltpu.SemaphoreType.DMA((2,))]),
        out_shape=[S((HEADS, T, T), bf16), S((T, D), bf16), S((D, T), bf16), S((D, T), f32), S((NP, 8, T), f32)],
        input_output_aliases={4 + i: i for i in range(len(prev))},
        compiler_params=cp(), name="attn_fwd", cost_estimate=cost(cnt * 2 * 8 * T * T * 128, cnt * 2 * T * T * 2, cnt * 2 * T * T),
    )(ln, kv, qkvt, qkvt, *prev)


G0 = math.sqrt(2 / math.pi)


def bit_reverse(x, m):
    y = jnp.zeros_like(x)
    for t in range(m):
        y = y | (((x >> t) & 1) << (m - 1 - t))
    return y


def push(me, n, s, src, keep, send, row0, sem, reverse=False):
    k = jnp.bitwise_xor(me, s)
    p = k >> 1
    if reverse:
        p = bit_reverse(p, (n // 2).bit_length() - 1)
    put = lambda dst: pltpu.make_async_copy(src, dst.at[p, pl.ds(row0, src.shape[0])], sem)

    @pl.when(k & 1 == 0)
    def _():
        put(keep).start()

    @pl.when(k & 1 == 1)
    def _():
        put(send).start()


def ffn_body(n, meta, ch, ln, me, tok, step, vec, upb, cot, mixed, mixedt, *refs):
    np_ = len(meta)
    pieces = refs[:np_]
    out, gx1, gmt, keep, send, wo, wu, wd, act, gup, h2t, gdt, gattn, sums, upsum, dn, up, gwo, vr, mtv, sems, psems = refs[np_:]
    i = pl.program_id(0)
    bm, D = tok.shape
    FF = wu.shape[1]
    r = D // n
    rf = FF // n
    nf = FF // D
    i0 = me[0]
    ro = pl.ds(mult(i * bm, 128), bm)
    first = i == 0
    seg = lambda j: (r + j * r, r, lambda s, o, c: wu.at[pl.ds(mult(s * r + o, 16), c), pl.ds(j * D, D)], D)
    seg_o = [(0, r, lambda s, o, c: wo.at[pl.ds(mult(s * r + o, 16), c)], D)]
    seg_u = [seg(j) for j in range(nf)]
    seg_d = [(r + r * nf, rf, lambda s, o, c: wd.at[pl.ds(mult(s * rf + o, 16), c)], D)]
    q = sems.shape[0] // 4
    parts = [(seg_o, sems.at[pl.ds(0, q)]), (seg_d, sems.at[pl.ds(q, q)]), (seg_u, sems.at[pl.ds(2 * q, 2 * q)])]
    load = pltpu.make_async_copy(mixedt, mtv, psems.at[psems.shape[0] - 1])

    @pl.when(first)
    def _():
        for sg, sm in parts:
            for c in pull(i0, pieces, meta, sg, sm):
                c.start()
        load.start()
        sums[...] = jnp.zeros_like(sums)
        upsum[...] = jnp.zeros_like(upsum)
        for c in pull(i0, pieces, meta, *parts[0]):
            c.wait()

    v = vec[...]
    x1 = tok[...].astype(f32) + step[...].astype(f32) + dot(mixed[...], wo[...]) + row(v, 4)
    nx, rr = norm(x1)
    h2 = (nx * row(v, 5) + row(v, 6)).astype(bf16)
    live = (lax.broadcasted_iota(jnp.int32, (bm, 1), 0) + i * bm) < ln[0]
    gd = jnp.where(live, cot[...], jnp.zeros_like(cot))
    acc = x1 + row(v, 7)
    gh = None
    nc = FF // ch
    sl = [slice(c * ch, (c + 1) * ch) for c in range(nc)]
    lead = lambda c: (dot(h2, wu[:, sl[c]]), dot_t(gd, wd[sl[c], :]))
    h2t[:, ro] = h2.T
    gdt[:, ro] = gd.T

    @pl.when(first)
    def _():
        for sg, sm in parts[1:]:
            for c in pull(i0, pieces, meta, sg, sm):
                c.wait()

    nxt = lead(0)
    for c in range(nc):
        u, ga = nxt
        nxt = lead(c + 1) if c + 1 < nc else None
        u = u + upb[:, sl[c]]
        u2 = u * u
        t = jnp.tanh(u * (f32(G0) + f32(G0 * 0.044715) * u2))
        half = 0.5 + 0.5 * t
        a = (u * half).astype(bf16)
        act[ro, sl[c]] = a
        dg = half + u * (half * (1.0 - half)) * (f32(2 * G0) + f32(6 * 0.044715 * G0) * u2)
        gu = (ga * dg).astype(bf16)
        gup[ro, sl[c]] = gu
        upsum[:, sl[c]] += jnp.sum(gu.astype(f32), axis=0, keepdims=True)
        acc = acc + dot(a, wd[sl[c], :])
        p = dot_t(gu, wu[:, sl[c]])
        gh = p if gh is None else gh + p
    out[...] = jnp.where(live, acc, 0.0).astype(bf16)
    gn = gh * row(v, 5)
    gx = gd.astype(f32) + rr * (gn - jnp.mean(gn, axis=-1, keepdims=True) - nx * jnp.mean(gn * nx, axis=-1, keepdims=True))
    gx1[...] = gx
    gab = gx.astype(bf16)
    gattn[ro, :] = gab
    gmt[...] = dot_t(gab, wo[...]).astype(bf16).T
    s_ = lambda a: jnp.sum(a.astype(f32), axis=0, keepdims=True)
    sums[...] += jnp.concatenate([s_(gab), s_(gh * nx), s_(gh), s_(gd), jnp.zeros((4, D), f32)], axis=0)

    @pl.when(i == pl.num_programs(0) - 1)
    def _():
        per = D // rf
        o_out, o_up, o_vec = rf, rf + r, rf + (nf + 1) * r
        for j in range(nf):
            dn[j] = dot(gdt[...], act[:, j * D : (j + 1) * D]).astype(bf16).T
            for t in range(per):
                push(i0, n, j * per + t, dn.at[j, pl.ds(t * rf, rf)], keep, send, 0, psems.at[j * per + t])
            up[j] = dot(h2t[...], gup[:, j * D : (j + 1) * D]).astype(bf16)
            for s in range(n):
                push(i0, n, s, up.at[j, pl.ds(s * r, r)], keep, send, o_up + j * r, psems.at[n * (1 + j) + s], True)
        load.wait()
        gwo[...] = dot(mtv[...], gattn[...]).astype(bf16)
        vr[...] = jnp.concatenate([sums[0:4, :]] + [upsum[:, c * D : (c + 1) * D] for c in range(nf)] + [jnp.zeros((VROWS - 4 - nf, D), f32)], axis=0).astype(bf16)
        b = n * (1 + nf)
        for s in range(n):
            push(i0, n, s, gwo.at[pl.ds(s * r, r)], keep, send, o_out, psems.at[b + s])
            push(i0, n, s, vr, keep, send, o_vec, psems.at[b + n + s], True)
        done = lambda src, q: pltpu.make_async_copy(src, keep.at[0, pl.ds(0, src.shape[0])], psems.at[q]).wait()
        for s in range(n):
            done(dn.at[0, pl.ds(0, rf)], s)
            for c in range(nf):
                done(up.at[0, pl.ds(0, r)], n * (1 + c) + s)
            done(gwo.at[pl.ds(0, r)], b + s)
            done(vr, b + n + s)


def ffn(ln, me, tok, step, vec, upb, cot, mixed, mixedt, pieces, n):
    T, D = tok.shape
    FF = upb.shape[1]
    bm = min(512, T)
    nf = FF // D
    r = D // n
    meta = tuple((k, r0) for k, r0, _ in pieces)
    full = lambda a: pl.BlockSpec(a.shape, lambda i, l, m: (0,) * a.ndim)
    rows = pl.BlockSpec((bm, D), lambda i, l, m: (i, 0))
    B = S((n // 2, FF // n + (nf + 1) * r + VROWS, D), bf16)
    V = pltpu.VMEM
    return pl.pallas_call(
        functools.partial(ffn_body, n, meta, min(1024, FF)),
        grid_spec=pltpu.PrefetchScalarGridSpec(
            num_scalar_prefetch=2, grid=(T // bm,),
            in_specs=[rows, full(step), full(vec), full(upb), rows, rows, ANY] + [ANY] * len(pieces),
            out_specs=[rows, rows, pl.BlockSpec((D, bm), lambda i, l, m: (0, i)), ANY, ANY],
            scratch_shapes=[V((D, D), bf16), V((D, FF), bf16), V((FF, D), bf16), V((T, FF), bf16), V((T, FF), bf16), V((D, T), bf16), V((D, T), bf16), V((T, D), bf16), V((8, D), f32), V((1, FF), f32), V((nf, D, D), bf16), V((nf, D, D), bf16), V((D, D), bf16), V((VROWS, D), bf16), V((D, T), bf16), pltpu.SemaphoreType.DMA((16 * len(pieces),)), pltpu.SemaphoreType.DMA((n * (nf + 3) + 1,))]),
        out_shape=[S((T, D), bf16), S((T, D), f32), S((D, T), bf16), B, B],
        compiler_params=cp(), name="ffn", cost_estimate=cost(2 * T * D * (6 * FF + 3 * D), 16 * T * D, T * FF),
    )(ln, me, tok, step, vec, upb, cot, mixed, mixedt, *[a for _, _, a in pieces])


def attn_bwd_body(HD, scale, CR, v, kt, qt, gt, mt, linv, et, *refs):
    gq, ds = refs[-2:]
    T = v.shape[0]
    rid = lax.broadcasted_iota(jnp.int32, gt.shape, 0) // HD
    g = gt[...].astype(f32)
    q = qt[...]
    gv = gk = None
    for h in range(2):
        hs = slice(h * HD, (h + 1) * HD)
        gs = (g * linv[h : h + 1, :]).astype(bf16)
        gm = jnp.where(rid == h, gs, jnp.zeros_like(gs))
        dl = jnp.sum(gs[hs, :].astype(f32) * mt[hs, :], axis=0, keepdims=True)
        for c in range(T // CR):
            cs = slice(c * CR, (c + 1) * CR)
            ds[h, cs, :] = (et[h, cs, :].astype(f32) * (dot(v[cs, :], gm) - dl)).astype(bf16)
        a = dot(et[h], gm.T)
        b = dot(ds[h], jnp.where(rid == h, q, jnp.zeros_like(q)).T)
        gv = a if gv is None else gv + a
        gk = b if gk is None else gk + b
        gq[0, hs, :] = (dot(kt[hs, :], ds[h]) * scale).astype(bf16)
    gq[2] = gv.astype(bf16).T
    gq[1] = gk.astype(bf16).T


def attn_bwd(kv, qkvt, gmt, mixedf, linv, et, p0, cnt, prev):
    _, T, D = kv.shape
    HD = D // HEADS
    PW = 2 * HD
    NP = D // PW
    prev = list(prev)
    pr = pl.BlockSpec((PW, T), lambda p: (p0 + p, 0))
    of = lambda j: pl.BlockSpec((None, PW, T), lambda p: (j, p0 + p, 0))
    return pl.pallas_call(
        functools.partial(attn_bwd_body, HD, 1.0 / math.sqrt(HD), min(256, T)),
        grid=(cnt,),
        scratch_shapes=[pltpu.VMEM((2, T, T), bf16)],
        in_specs=[pl.BlockSpec((None, T, PW), lambda p: (1, 0, p0 + p)), of(1), of(0), pr, pr, pl.BlockSpec((None, 8, T), lambda p: (p0 + p, 0, 0)), pl.BlockSpec((2, T, T), lambda p: (p0 + p, 0, 0))] + [ANY] * len(prev),
        out_specs=pl.BlockSpec((3, PW, T), lambda p: (0, p0 + p, 0)),
        out_shape=S((3, D, T), bf16),
        input_output_aliases={7: 0} if prev else {},
        compiler_params=cp(), name="attn_bwd", cost_estimate=cost(cnt * 2 * 16 * T * T * 128, cnt * 2 * T * T * 2),
    )(kv, qkvt, qkvt, gmt, mixedf, linv, et, *prev)


def wqkv_body(n, me, xht, g, keep, send, res, vr, sems):
    j = pl.program_id(0)
    D = g.shape[0]
    r = D // n
    i0 = me[0]
    x = jnp.concatenate([xht[...], jnp.ones((16, xht.shape[1]), bf16)], axis=0)
    y = dot_t(x, g[...]).astype(bf16)
    res[j] = y[:D]
    vr[...] = jnp.where(lax.broadcasted_iota(jnp.int32, vr.shape, 0) == j, y[D:], jnp.where(j == 0, jnp.zeros_like(y[D:]), vr[...]))
    for s in range(n):
        push(i0, n, s, res.at[j, pl.ds(s * r, r)], keep, send, mult(j * r, 16), sems.at[j * n + s])

    @pl.when(j == 2)
    def _():
        for s in range(n):
            push(i0, n, s, vr, keep, send, 3 * r, sems.at[3 * n + s])
        for s in range(n):
            for q in range(3):
                pltpu.make_async_copy(res.at[0, pl.ds(0, r)], keep.at[0, pl.ds(0, r)], sems.at[q * n + s]).wait()
            pltpu.make_async_copy(vr, keep.at[0, pl.ds(0, VROWS)], sems.at[3 * n + s]).wait()


def wqkv(me, xht, g, n):
    D, T = xht.shape
    A = S((n // 2, 3 * (D // n) + VROWS, D), bf16)
    return pl.pallas_call(
        functools.partial(wqkv_body, n),
        grid_spec=pltpu.PrefetchScalarGridSpec(
            num_scalar_prefetch=1, grid=(3,),
            in_specs=[pl.BlockSpec((D, T), lambda j, m: (0, 0)), pl.BlockSpec((None, D, T), lambda j, m: (j, 0, 0))],
            out_specs=[ANY] * 2,
            scratch_shapes=[pltpu.VMEM((3, D, D), bf16), pltpu.VMEM((VROWS, D), bf16), pltpu.SemaphoreType.DMA((4 * n,))]),
        out_shape=[A, A],
        compiler_params=cp(), name="wqkv", cost_estimate=cost(6 * T * D * D, 10 * T * D),
    )(me, xht, g)


def back_body(tok, step, vec, g, gx1, *refs):
    ws, tg = refs[:-1], refs[-1]
    D = tok.shape[1]
    gw = D // GROUPS
    x = tok[...].astype(f32) + step[...].astype(f32)
    nx, rr = norm(x)
    gt = sum(dot(w[:, j * gw : (j + 1) * gw], g[j, q * gw : (q + 1) * gw, :]) for q, w in enumerate(ws) for j in range(3))
    gn = gt.T * row(vec[...], 0)
    tg[...] = gx1[...] + rr * (gn - jnp.mean(gn, axis=-1, keepdims=True) - nx * jnp.mean(gn * nx, axis=-1, keepdims=True))


def back(tok, step, vec, ws, g, gx1, bm=512):
    T, D = tok.shape
    full = lambda a: pl.BlockSpec(a.shape, lambda i: (0,) * a.ndim)
    rows = pl.BlockSpec((bm, D), lambda i: (i, 0))
    return pl.pallas_call(
        back_body, grid=(T // bm,),
        in_specs=[rows, full(step), full(vec), pl.BlockSpec((3, D, bm), lambda i: (0, 0, i)), rows] + [full(w) for w in ws],
        out_specs=rows, out_shape=S((T, D), f32), compiler_params=cp(), name="back", cost_estimate=cost(6 * T * D * D, 14 * T * D),
    )(tok, step, vec, g, gx1, *ws)


def shards(tokens, step_embed, lengths, cotangent, ln1_gain, ln1_bias, qkv_weight, q_bias, v_bias, out_weight, out_bias, ln2_gain, ln2_bias, up_weight, up_bias, down_weight, down_bias):
    n = lax.axis_size("shard")
    me = lax.axis_index("shard").astype(jnp.int32)
    mes = me[None]
    tok, cot, step = tokens[0], cotangent[0], step_embed
    T, D = tok.shape
    r = D // n
    FF = up_bias.shape[0] * n
    nc = FF // D
    rf = FF // n
    packs = pack_first(mes, qkv_weight, [ln1_gain, ln1_bias, q_bias, v_bias, out_bias, ln2_gain, ln2_bias, down_bias], up_bias)
    pack2 = pack_rest(out_weight, up_weight, down_weight)
    NP = HEADS // 2
    nx, xht = start(tok, step)
    pieces = gather_direct(packs[0], n, xht, pack2)
    kv, qkvt, w, vec, upb = front(mes, nx, pieces, n, FF)
    fw = attn_fwd(lengths, kv, qkvt, 0, NP // 2, [])
    fw2 = attn_fwd(lengths, kv, qkvt, NP // 2, NP // 2, fw)
    et, mixed, mixedt, mixedf, linv = fw2
    pieces2 = gather_forward(after(pack2, xht), n, fw[4], linv)
    out, gx1, gmt, keep, send = ffn(lengths, mes, tok, step, vec, upb, cot, mixed, mixedt, pieces2, n)
    bwd = lambda p, c, g, *deps: attn_bwd(kv, qkvt, after(gmt, *deps) if deps else gmt, mixedf, linv, et, p, c, g)
    ra = rf + r
    got = swap(send, 1)
    g = bwd(0, 1, [])
    got = after(got, g)
    pick = lambda terms, s: [t[s] for t in terms]
    sum_of = lambda terms: total(terms[0], terms[1:])
    h = n // 4
    lo, hi = slice(0, h), slice(h, None)
    of = lambda s, rows: [keep[s, rows], got[s, rows]]
    rows_a, rows_b = slice(0, ra), slice(ra, None)
    xa, xb = sum_of(of(hi, rows_a)), sum_of(of(hi, rows_b))
    g = bwd(1, NP - 1, [g], xa, xb)
    m = (n // 2).bit_length() - 1
    ga, gb = swap(xa, 2 << (m - 1)), swap(xb, 2)
    keep, got, ga, gb, _ = lax.optimization_barrier((keep, got, ga, gb, g))
    ta, tb = of(lo, rows_a) + [ga], of(lo, rows_b) + [gb]
    for t in range(1, m):
        h //= 2
        lo, hi = slice(0, h), slice(h, None)
        xa, xb = sum_of(pick(ta, hi)), sum_of(pick(tb, hi))
        ta, tb = pick(ta, lo), pick(tb, lo)
        ga, gb = swap(xa, 2 << (m - 1 - t)), swap(xb, 2 << t)
        if t == 1:
            keep, send = wqkv(mes, after(xht, xa, xb), g, n)
        ga, gb, *rest, _ = lax.optimization_barrier((ga, gb, *ta, *tb, keep))
        ta, tb = rest[: len(ta)] + [ga], rest[len(ta) :] + [gb]
    ga, gb = sum_of(ta), sum_of(tb)
    got = swap(send, 1)
    p2 = [add16(keep[k], got[k]) for k in range(n // 2)]
    far2 = spread(p2)
    ga, gb, _ = lax.optimization_barrier((ga, gb, keep))
    got = swap(send, 1)
    p2 = [add16(keep[k], got[k]) for k in range(n // 2)]
    far2 = spread(p2)
    own1 = jnp.concatenate([ga[0], gb[0]], axis=0)
    m1, o1, x1 = rep_half(own1)
    z1 = add16(m1, after(o1, *p2[1:]))
    tg = back(tok, after(step, z1, *p2[1:]), vec, [w], g, gx1)
    own2 = total(p2[0], [after(a, tg) for a in far2])
    m2, o2, x2 = rep_half(own2)
    steps = rep_steps()
    z2 = None if steps else add16(m2, o2)
    for b in steps:
        z1 = add16(z1, after(rep_perm(z1, b), x2))
        if z2 is None:
            z2 = add16(m2, after(o2, z1))
        pz = rep_perm(z2, b)
        z2 = add16(z2, after(pz, z1))
    o1, o2 = rep_perm(z1, 1), rep_perm(z2, 1)
    ids = jnp.stack([me, (lax.axis_index("rep") % 2).astype(jnp.int32)])
    g_down, g_up, g_out, g_upb, g_ob, g_g2, g_b2, g_db = finish_rest(ids, z1, o1, r, rf, nc, n)
    g_qkv, g_g1, g_b1, g_q, g_v = finish_first(ids, z2, after(o2, g_out), qkv_weight, ln1_gain, ln1_bias)
    flat = lambda a: a.reshape(-1)
    return (out[None], tg[None], flat(g_g1), flat(g_b1), g_qkv, flat(g_q), flat(g_v), g_out, flat(g_ob), flat(g_g2), flat(g_b2), g_up, flat(g_upb), g_down, flat(g_db))


def solution(mesh):
    from jax.sharding import PartitionSpec as P

    in_specs = (
        P(("rep", "shard"), None, None),
        P(("rep", "shard"), None),
        P(("rep", "shard")),
        P(("rep", "shard"), None, None),
        P("shard"),
        P("shard"),
        P("shard", None),
        P("shard"),
        P("shard"),
        P("shard", None),
        P("shard"),
        P("shard"),
        P("shard"),
        P("shard", None),
        P("shard"),
        P("shard", None),
        P("shard"),
    )
    out_specs = (
        P(("rep", "shard"), None, None),
        P(("rep", "shard"), None, None),
        P("shard"),
        P("shard"),
        P("shard", None),
        P("shard"),
        P("shard"),
        P("shard", None),
        P("shard"),
        P("shard"),
        P("shard"),
        P("shard", None),
        P("shard"),
        P("shard", None),
        P("shard"),
    )
    return jax.shard_map(shards, mesh=mesh, in_specs=in_specs, out_specs=out_specs, check_vma=False)
```

```python
import functools, math
import jax, jax.numpy as jnp
from jax import lax
from jax.experimental import pallas as pl
from jax.experimental.pallas import tpu as pltpu

f32 = jnp.float32
bf16 = jnp.bfloat16
EPS = 1e-05
HEADS = 8

def dot(a, b):
    return jnp.dot(a, b, preferred_element_type=f32)

def dot_t(a, b):
    return lax.dot_general(a, b, (((1,), (1,)), ((), ())), preferred_element_type=f32)

def cp(n=1, vmem=100):
    return pltpu.CompilerParams(dimension_semantics=("arbitrary",) * n, vmem_limit_bytes=60 * 1024 * 1024)

def norm(x):
    c = x - jnp.mean(x, axis=-1, keepdims=True)
    r = lax.rsqrt(jnp.mean(c * c, axis=-1, keepdims=True) + EPS)
    return c * r, r

def row(v, i):
    return v[i : i + 1, :].astype(f32)


VROWS = 16
LANES = 128


def xor_perm(n, k):
    return [(i, i ^ k) for i in range(n)]


def rep_perm(x, b):
    return lax.ppermute(x, "rep", xor_perm(lax.axis_size("rep"), b))


def swap(x, k):
    return lax.ppermute(x, "shard", xor_perm(lax.axis_size("shard"), k))


def after(x, *deps):
    return lax.optimization_barrier((x,) + deps)[0]


def gather_direct(x, n, *gate):
    out = [(0, 0, x)]
    far = [(k, swap(x, k)) for k in range(2, n, 2)]
    out += [(k, 0, after(y, *gate) if gate else y) for k, y in far]
    return out + [(k ^ 1, 0, swap(y, 1)) for k, _, y in out]


def add16(a, b):
    return a + b


def spread(parts):
    return [swap(parts[k], 2 * k) for k in range(len(parts) - 1, 0, -1)]


def total(own, got):
    t = own.astype(f32)
    for a in got:
        t = t + a.astype(f32)
    return t.astype(bf16)


def rep_half(x):
    h = x.shape[0] // 2
    odd = lax.axis_index("rep") % 2
    mine = lax.dynamic_slice_in_dim(x, odd * h, h, 0)
    other = lax.dynamic_slice_in_dim(x, (1 - odd) * h, h, 0)
    return mine, rep_perm(other, 1), other


def rep_steps():
    nr = lax.axis_size("rep")
    return [b for b in (2 << i for i in range(16)) if b < nr]


GROUPS = 1


def pack_first_body(me, w, upb, *refs):
    vecs = refs[:-GROUPS]
    outs = refs[-GROUPS:]
    r, W = w.shape
    D = W // 3
    gw = D // GROUPS
    for g, out in enumerate(outs):
        for j in range(3):
            out[j * r : (j + 1) * r, :] = w[:, j * D + g * gw : j * D + (g + 1) * gw]

    def spot(v):
        w_ = v.shape[1]
        if w_ >= LANES:
            return [v[q : q + 1, :] for q in range(v.shape[0])]
        t = LANES // w_
        lane = lax.broadcasted_iota(jnp.int32, (1, LANES), 1)
        return [jnp.where(lane // w_ == me[0] % t, jnp.concatenate([v] * t, axis=1), jnp.zeros((1, LANES), f32))]

    rows = [a for v in vecs for a in spot(v[...].astype(f32))] + spot(upb[...].astype(f32))
    b = jnp.concatenate(rows + [jnp.zeros((VROWS - len(rows), LANES), f32)], axis=0).astype(bf16)
    outs[0][3 * r :, :] = jnp.concatenate([b, jnp.zeros((VROWS, gw - LANES), bf16)], axis=1) if gw > LANES else b


def whole(n):
    return [pl.BlockSpec(memory_space=pltpu.VMEM)] * n


def once(*arrays):
    return [pl.BlockSpec(a.shape, lambda i, *m, nd=len(a.shape): (0,) * nd) for a in arrays]


def pack_first(me, w, vecs, upb):
    r, W = w.shape
    gw = W // 3 // GROUPS
    lanes = lambda v: v.reshape(-1, min(LANES, v.shape[0]))
    args = [w] + [lanes(v) for v in [upb] + vecs]
    outs = [S((3 * r + (VROWS if g == 0 else 0), gw), bf16) for g in range(GROUPS)]
    return pl.pallas_call(
        pack_first_body,
        grid_spec=pltpu.PrefetchScalarGridSpec(num_scalar_prefetch=1, grid=(1,), in_specs=once(*args), out_specs=once(*outs)),
        out_shape=outs, compiler_params=cp(), name="pack_first", cost_estimate=cost(0, 4 * w.size),
    )(me, *args)


def pack_rest_body(wo, wu, wd, out):
    r, D = wo.shape
    out[:r, :] = wo[...]
    for j in range(wu.shape[1] // D):
        out[(1 + j) * r : (2 + j) * r, :] = wu[:, j * D : (j + 1) * D]
    out[(1 + wu.shape[1] // D) * r :, :] = wd[...]


def pack_rest(wo, wu, wd):
    D = wo.shape[1]
    out = S(((wo.size + wu.size + wd.size) // D, D), bf16)
    return pl.pallas_call(
        pack_rest_body, grid=(1,), in_specs=once(wo, wu, wd), out_specs=once(out)[0],
        out_shape=out, compiler_params=cp(), name="pack_rest", cost_estimate=cost(0, 4 * wu.size),
    )(wo, wu, wd)


def own_lanes(tiles, me, w):
    pick = lambda i: sum(jnp.where(i == t, a, jnp.zeros_like(a)) for t, a in enumerate(tiles))
    if w >= LANES:
        q = w // LANES
        return jnp.concatenate([pick(me * q + c) for c in range(q)], axis=1)
    per = LANES // w
    x = pick(me // per)
    off = me % per
    return sum(jnp.where(off == o, x[:, o * w : (o + 1) * w], 0.0) for o in range(per))


def rows_of(lo, hi, a, b):
    h = lo.shape[0]
    if b <= h:
        return lo[a:b, :]
    if a >= h:
        return hi[a - h : b - h, :]
    return jnp.concatenate([lo[a:h, :], hi[: b - h, :]], axis=0)


def finish_rest_body(r, rf, n, ids, s, o, down, up, out, upb, *vecs):
    D = out.shape[1]
    nf = up.shape[1] // D

    def run(lo, hi):
        f = lambda a, b: rows_of(lo, hi, a, b).astype(f32)
        down[...] = f(0, rf)
        out[...] = f(rf, rf + r)
        for j in range(nf):
            up[:, j * D : (j + 1) * D] = f(rf + (j + 1) * r, rf + (j + 2) * r)
        b = rf + (nf + 1) * r
        v = f(b, b + VROWS)
        me = ids[0]
        tiles = [v[0:8, t * LANES : (t + 1) * LANES] for t in range(D // LANES)]
        x = own_lanes(tiles, me, r)
        for q, ref in enumerate(vecs):
            ref[...] = x[q : q + 1, :]
        tiles = [v[4 + q : 5 + q, t * LANES : (t + 1) * LANES] for q in range(nf) for t in range(D // LANES)]
        upb[...] = own_lanes(tiles, me, nf * D // n)

    @pl.when(ids[1] == 0)
    def _():
        run(s, o)

    @pl.when(ids[1] == 1)
    def _():
        run(o, s)


def finish_rest(ids, s, o, r, rf, nf, n):
    D = s.shape[1]
    row1 = lambda w: S((1, w), f32)
    return pl.pallas_call(
        functools.partial(finish_rest_body, r, rf, n),
        in_specs=[pl.BlockSpec(memory_space=pltpu.SMEM)] + whole(2), out_specs=whole(8),
        out_shape=[S((rf, D), f32), S((r, nf * D), f32), S((r, D), f32), row1(nf * D // n)] + [row1(r)] * 4,
        compiler_params=pltpu.CompilerParams(vmem_limit_bytes=16 << 20), name="finish_rest", cost_estimate=cost(0, 8 * s.size),
    )(ids, s, o)


def finish_first_body(ids, s, o, w, gain, bias, qkv, gg, gb, qb, vb):
    r, W = w.shape
    D = s.shape[1]

    def run(lo, hi):
        f = lambda a, b: rows_of(lo, hi, a, b).astype(f32)
        v = f(3 * r, 3 * r + VROWS)
        nt = D // LANES
        accg = accb = jnp.zeros((r, LANES), f32)
        col = lambda g: jnp.concatenate([g[...].astype(f32), jnp.zeros((7, r), f32)], axis=0).T[:, 0:1]
        cg, cb = col(gain), col(bias)
        for j in range(3):
            m = f(j * r, (j + 1) * r)
            sq = v[j : j + 1, :]
            ww = w[:, j * D : (j + 1) * D].astype(f32)
            qkv[:, j * D : (j + 1) * D] = cg * m + cb * sq
            pg, pb = ww * m, ww * sq
            accg = accg + sum(pg[:, t * LANES : (t + 1) * LANES] for t in range(nt))
            accb = accb + sum(pb[:, t * LANES : (t + 1) * LANES] for t in range(nt))
        gg[...] = jnp.sum(accg.T, axis=0, keepdims=True)
        gb[...] = jnp.sum(accb.T, axis=0, keepdims=True)
        x = own_lanes([v[0:8, t * LANES : (t + 1) * LANES] for t in range(nt)], ids[0], r)
        qb[...] = x[0:1, :]
        vb[...] = x[2:3, :]

    @pl.when(ids[1] == 0)
    def _():
        run(s, o)

    @pl.when(ids[1] == 1)
    def _():
        run(o, s)


def finish_first(ids, s, o, w, gain, bias):
    r, W = w.shape
    return pl.pallas_call(
        finish_first_body,
        in_specs=[pl.BlockSpec(memory_space=pltpu.SMEM)] + whole(5), out_specs=whole(5),
        out_shape=[S((r, W), f32)] + [S((1, r), f32)] * 4,
        compiler_params=pltpu.CompilerParams(vmem_limit_bytes=16 << 20), name="finish_first", cost_estimate=cost(0, 8 * w.size),
    )(ids, s, o, w, gain[None], bias[None])


def pull(me, refs, meta, segs, sems):
    copies = []
    for ref, (k, r0) in zip(refs, meta):
        s = jnp.bitwise_xor(me, k)
        r1 = r0 + ref.shape[0]
        for a, c, dst, lanes in segs:
            lo, hi = max(a, r0), min(a + c, r1)
            if lo < hi:
                src = ref.at[pl.ds(lo - r0, hi - lo), pl.ds(0, lanes)]
                copies.append(pltpu.make_async_copy(src, dst(s, lo - a, hi - lo), sems.at[len(copies)]))
    return copies


def mult(x, m):
    return pl.multiple_of(x, m)


def weight_segs(w, r):
    gw = w.shape[1] // 3
    seg = lambda j: (j * r, r, lambda s, o, c: w.at[pl.ds(mult(s * r + o, 16), c), pl.ds(j * gw, gw)], gw)
    return [seg(j) for j in range(3)]


def start_body(tok, step, nx, xht):
    n, _ = norm(tok[...].astype(f32) + step[...].astype(f32))
    nx[...] = n
    xht[...] = n.astype(bf16).T


def start(tok, step, bm=256):
    T, D = tok.shape
    rows = pl.BlockSpec((bm, D), lambda i: (i, 0))
    return pl.pallas_call(
        start_body, grid=(T // bm,),
        in_specs=[rows, pl.BlockSpec((1, D), lambda i: (0, 0))], out_specs=[rows, pl.BlockSpec((D, bm), lambda i: (0, i))],
        out_shape=[S((T, D), f32), S((D, T), bf16)], compiler_params=cp(), name="start", cost_estimate=cost(20 * T * D, 8 * T * D),
    )(tok, step)


def front_body(scale, n, meta, me, nx, *refs):
    np_ = len(meta)
    pieces = refs[:np_]
    kv, qkvt, wout, vec, upb, nv, h, w, vbuf, sems, own = refs[np_:]
    T, D = nv.shape
    r = D // n
    FF = upb.shape[1]
    i = pl.program_id(0)
    cw = kv.shape[2]
    per_j = D // cw
    segs = [(3 * r, VROWS, lambda s, o, c: vbuf.at[s, pl.ds(o, c)], LANES)] + weight_segs(w, r)
    load = pltpu.make_async_copy(nx, nv, own.at[0])
    save = pltpu.make_async_copy(w, wout, own.at[1])

    @pl.when(i == 0)
    def _():
        cs = pull(me[0], pieces, meta, segs, sems)
        for c in cs:
            c.start()
        load.start()
        for c in cs:
            c.wait()
        save.start()
        per = LANES // r
        tiles = [sum(vbuf[s, 0:8, :].astype(f32) for s in range(t * per, (t + 1) * per)) for t in range(D // LANES)]
        vec[...] = jnp.concatenate(tiles, axis=1)
        wu = FF // n
        if wu >= LANES:
            rows = [vbuf[s, 8 + q : 9 + q, :].astype(f32) for s in range(n) for q in range(wu // LANES)]
        else:
            per = LANES // wu
            rows = [sum(vbuf[s, 8:9, :].astype(f32) for s in range(t * per, (t + 1) * per)) for t in range(FF // LANES)]
        upb[...] = jnp.concatenate(rows, axis=1)
        load.wait()
        v = vec[...]
        h[...] = (nv[...] * row(v, 0) + row(v, 1)).astype(bf16)

    cols = pl.ds(mult(i * cw, 128), cw)
    y = dot(h[...], w[:, cols])
    here = pl.ds(mult((i % per_j) * cw, 128), cw)
    kind = i // per_j
    y = (y + jnp.where(kind == 0, vec[2:3, here], jnp.where(kind == 2, vec[3:4, here], 0.0))).astype(bf16)
    kv[0] = y
    qkvt[0] = jnp.where(kind == 0, y * bf16(scale), y).T

    @pl.when(i == pl.num_programs(0) - 1)
    def _():
        save.wait()


S = jax.ShapeDtypeStruct
ANY = pl.BlockSpec(memory_space=pl.ANY)


def cost(flops, nbytes, tr=0):
    return pl.CostEstimate(flops=int(flops), bytes_accessed=int(nbytes), transcendentals=int(tr))


def front(me, nx, pieces, n, FF, cw=512):
    T, D = nx.shape
    scale = 1.0 / math.sqrt(D // HEADS)
    meta = tuple((k, r0) for k, r0, _ in pieces)
    q = D // cw
    keep = lambda *sh: pl.BlockSpec(sh, lambda i, m: (0,) * len(sh))
    rest = lambda i: jnp.maximum(i - q, 0)
    V = pltpu.VMEM
    return pl.pallas_call(
        functools.partial(front_body, scale, n, meta),
        grid_spec=pltpu.PrefetchScalarGridSpec(
            num_scalar_prefetch=1, grid=(3 * q,),
            in_specs=[ANY] * (1 + len(pieces)),
            out_specs=[pl.BlockSpec((1, T, cw), lambda i, m: (rest(i) // q, 0, rest(i) % q)), pl.BlockSpec((1, cw, T), lambda i, m: (i // q, i % q, 0)), ANY, keep(8, D), keep(1, FF)],
            scratch_shapes=[V((T, D), f32), V((T, D), bf16), V((D, 3 * D), bf16), V((n, VROWS, LANES), bf16), pltpu.SemaphoreType.DMA((8 * len(pieces),)), pltpu.SemaphoreType.DMA((2,))]),
        out_shape=[S((2, T, D), bf16), S((3, D, T), bf16), S((D, 3 * D), bf16), S((8, D), f32), S((1, FF), f32)],
        compiler_params=cp(), name="front", cost_estimate=cost(6 * T * D * D, 12 * T * D),
    )(me, nx, *[a for _, _, a in pieces])


def attn_fwd_body(HD, bi, CR, p0, ln, k, qt, vt, *refs):
    et, mixed, mixedt, mixedf, linv, scr, ka, eb, esem = refs[-9:]
    T, PW = k.shape
    n = ln[0]
    p = pl.program_id(0)
    last = p == pl.num_programs(0) - 1
    rid = lax.broadcasted_iota(jnp.int32, (PW, bi), 0)
    lane = lax.broadcasted_iota(jnp.int32, (T, PW), 1)
    rows = lax.broadcasted_iota(jnp.int32, (T, PW), 0)
    ka[:, :PW] = k[...]
    ka[:, PW:] = jnp.where((lane == 0) & (rows >= n), f32(-1e30), f32(0)).astype(bf16)
    ones = jnp.where(rid == 0, f32(1), f32(0)).astype(bf16)
    va = [jnp.concatenate([vt[h * HD : (h + 1) * HD, :], jnp.ones((16, T), bf16)], axis=0) for h in range(2)]
    tasks = [(b, h) for b in range(T // bi) for h in range(2)]
    nch = T // CR

    def query(t):
        b, h = tasks[t]
        q = qt[:, b * bi : (b + 1) * bi]
        return jnp.concatenate([jnp.where(rid // HD == h, q, jnp.zeros_like(q)), ones], axis=0)

    def score(t, c, q):
        s = dot(ka[c * CR : (c + 1) * CR, :], q)
        scr[t % 2, c * CR : (c + 1) * CR, :] = s
        return jnp.max(s, axis=0, keepdims=True)

    q = query(0)
    m = functools.reduce(jnp.maximum, [score(0, c, q) for c in range(nch)])
    half = None
    for t, (b, h) in enumerate(tasks):
        sl = slice(b * bi, (b + 1) * bi)
        more = t + 1 < len(tasks)
        put = pltpu.make_async_copy(eb.at[t % 2], et.at[2 * (p0 + p) + h, :, pl.ds(b * bi, bi)], esem.at[t % 2])
        if t < 2:

            @pl.when(p > 0)
            def _():
                put.wait()

        else:
            put.wait()
        if more:
            q = query(t + 1)
        nxt = []
        for c in range(nch):
            cs = slice(c * CR, (c + 1) * CR)
            if more:
                nxt.append(score(t + 1, c, q))
            eb[t % 2, cs, :] = jnp.exp(scr[t % 2, cs, :] - m).astype(bf16)
        put.start()
        o = dot(va[h], eb[t % 2])
        if more:
            m = functools.reduce(jnp.maximum, nxt)
        inv = 1.0 / o[HD : HD + 1, :]
        linv[h : h + 1, sl] = inv
        o = o[:HD, :] * inv
        if h == 0:
            half = o
        else:
            mt = jnp.concatenate([half, o], axis=0)
            mixedf[:, sl] = mt
            mt = mt.astype(bf16)
            mixedt[:, sl] = mt
            mixed[sl, :] = mt.T

    @pl.when(last)
    def _():
        for q in range(2):
            pltpu.make_async_copy(eb.at[q], et.at[0, :, pl.ds(0, bi)], esem.at[q]).wait()


def attn_fwd(ln, kv, qkvt, p0, cnt, prev):
    _, T, D = kv.shape
    HD = D // HEADS
    PW = 2 * HD
    NP = D // PW
    bi = min(512, T)
    prev = list(prev)
    return pl.pallas_call(
        functools.partial(attn_fwd_body, HD, bi, min(256, T), p0),
        grid_spec=pltpu.PrefetchScalarGridSpec(
            num_scalar_prefetch=1, grid=(cnt,),
            in_specs=[pl.BlockSpec((None, T, PW), lambda p, r: (0, 0, p0 + p)), pl.BlockSpec((None, PW, T), lambda p, r: (0, p0 + p, 0)), pl.BlockSpec((None, PW, T), lambda p, r: (2, p0 + p, 0))] + [ANY] * len(prev),
            out_specs=[ANY, pl.BlockSpec((T, PW), lambda p, r: (0, p0 + p)), pl.BlockSpec((PW, T), lambda p, r: (p0 + p, 0)), pl.BlockSpec((PW, T), lambda p, r: (p0 + p, 0)), pl.BlockSpec((None, 8, T), lambda p, r: (p0 + p, 0, 0))],
            scratch_shapes=[pltpu.VMEM((2, T, bi), f32), pltpu.VMEM((T, 2 * PW), bf16), pltpu.VMEM((2, T, bi), bf16), pltpu.SemaphoreType.DMA((2,))]),
        out_shape=[S((HEADS, T, T), bf16), S((T, D), bf16), S((D, T), bf16), S((D, T), f32), S((NP, 8, T), f32)],
        input_output_aliases={4 + i: i for i in range(len(prev))},
        compiler_params=cp(), name="attn_fwd", cost_estimate=cost(cnt * 2 * 8 * T * T * 128, cnt * 2 * T * T * 2, cnt * 2 * T * T),
    )(ln, kv, qkvt, qkvt, *prev)


G0 = math.sqrt(2 / math.pi)


def bit_reverse(x, m):
    y = jnp.zeros_like(x)
    for t in range(m):
        y = y | (((x >> t) & 1) << (m - 1 - t))
    return y


def push(me, n, s, src, keep, send, row0, sem, reverse=False):
    k = jnp.bitwise_xor(me, s)
    p = k >> 1
    if reverse:
        p = bit_reverse(p, (n // 2).bit_length() - 1)
    put = lambda dst: pltpu.make_async_copy(src, dst.at[p, pl.ds(row0, src.shape[0])], sem)

    @pl.when(k & 1 == 0)
    def _():
        put(keep).start()

    @pl.when(k & 1 == 1)
    def _():
        put(send).start()


def ffn_body(n, meta, ch, ln, me, tok, step, vec, upb, cot, mixed, mixedt, *refs):
    np_ = len(meta)
    pieces = refs[:np_]
    out, gx1, gmt, keep, send, wo, wu, wd, act, gup, h2t, gdt, gattn, sums, upsum, dn, up, gwo, vr, mtv, sems, psems = refs[np_:]
    i = pl.program_id(0)
    bm, D = tok.shape
    FF = wu.shape[1]
    r = D // n
    rf = FF // n
    nf = FF // D
    i0 = me[0]
    ro = pl.ds(mult(i * bm, 128), bm)
    first = i == 0
    seg = lambda j: (r + j * r, r, lambda s, o, c: wu.at[pl.ds(mult(s * r + o, 16), c), pl.ds(j * D, D)], D)
    seg_o = [(0, r, lambda s, o, c: wo.at[pl.ds(mult(s * r + o, 16), c)], D)]
    seg_u = [seg(j) for j in range(nf)]
    seg_d = [(r + r * nf, rf, lambda s, o, c: wd.at[pl.ds(mult(s * rf + o, 16), c)], D)]
    q = sems.shape[0] // 4
    parts = [(seg_o, sems.at[pl.ds(0, q)]), (seg_d, sems.at[pl.ds(q, q)]), (seg_u, sems.at[pl.ds(2 * q, 2 * q)])]
    load = pltpu.make_async_copy(mixedt, mtv, psems.at[psems.shape[0] - 1])

    @pl.when(first)
    def _():
        for sg, sm in parts:
            for c in pull(i0, pieces, meta, sg, sm):
                c.start()
        load.start()
        sums[...] = jnp.zeros_like(sums)
        upsum[...] = jnp.zeros_like(upsum)
        for c in pull(i0, pieces, meta, *parts[0]):
            c.wait()

    v = vec[...]
    x1 = tok[...].astype(f32) + step[...].astype(f32) + dot(mixed[...], wo[...]) + row(v, 4)
    nx, rr = norm(x1)
    h2 = (nx * row(v, 5) + row(v, 6)).astype(bf16)
    live = (lax.broadcasted_iota(jnp.int32, (bm, 1), 0) + i * bm) < ln[0]
    gd = jnp.where(live, cot[...], jnp.zeros_like(cot))
    acc = x1 + row(v, 7)
    gh = None
    nc = FF // ch
    sl = [slice(c * ch, (c + 1) * ch) for c in range(nc)]
    lead = lambda c: (dot(h2, wu[:, sl[c]]), dot_t(gd, wd[sl[c], :]))
    h2t[:, ro] = h2.T
    gdt[:, ro] = gd.T

    @pl.when(first)
    def _():
        for sg, sm in parts[1:]:
            for c in pull(i0, pieces, meta, sg, sm):
                c.wait()

    nxt = lead(0)
    for c in range(nc):
        u, ga = nxt
        nxt = lead(c + 1) if c + 1 < nc else None
        u = u + upb[:, sl[c]]
        u2 = u * u
        t = jnp.tanh(u * (f32(G0) + f32(G0 * 0.044715) * u2))
        half = 0.5 + 0.5 * t
        a = (u * half).astype(bf16)
        act[ro, sl[c]] = a
        dg = half + u * (half * (1.0 - half)) * (f32(2 * G0) + f32(6 * 0.044715 * G0) * u2)
        gu = (ga * dg).astype(bf16)
        gup[ro, sl[c]] = gu
        upsum[:, sl[c]] += jnp.sum(gu.astype(f32), axis=0, keepdims=True)
        acc = acc + dot(a, wd[sl[c], :])
        p = dot_t(gu, wu[:, sl[c]])
        gh = p if gh is None else gh + p
    out[...] = jnp.where(live, acc, 0.0).astype(bf16)
    gn = gh * row(v, 5)
    gx = gd.astype(f32) + rr * (gn - jnp.mean(gn, axis=-1, keepdims=True) - nx * jnp.mean(gn * nx, axis=-1, keepdims=True))
    gx1[...] = gx
    gab = gx.astype(bf16)
    gattn[ro, :] = gab
    gmt[...] = dot_t(gab, wo[...]).astype(bf16).T
    s_ = lambda a: jnp.sum(a.astype(f32), axis=0, keepdims=True)
    sums[...] += jnp.concatenate([s_(gab), s_(gh * nx), s_(gh), s_(gd), jnp.zeros((4, D), f32)], axis=0)

    @pl.when(i == pl.num_programs(0) - 1)
    def _():
        per = D // rf
        o_out, o_up, o_vec = rf, rf + r, rf + (nf + 1) * r
        for j in range(nf):
            dn[j] = dot(gdt[...], act[:, j * D : (j + 1) * D]).astype(bf16).T
            for t in range(per):
                push(i0, n, j * per + t, dn.at[j, pl.ds(t * rf, rf)], keep, send, 0, psems.at[j * per + t])
            up[j] = dot(h2t[...], gup[:, j * D : (j + 1) * D]).astype(bf16)
            for s in range(n):
                push(i0, n, s, up.at[j, pl.ds(s * r, r)], keep, send, o_up + j * r, psems.at[n * (1 + j) + s], True)
        load.wait()
        gwo[...] = dot(mtv[...], gattn[...]).astype(bf16)
        vr[...] = jnp.concatenate([sums[0:4, :]] + [upsum[:, c * D : (c + 1) * D] for c in range(nf)] + [jnp.zeros((VROWS - 4 - nf, D), f32)], axis=0).astype(bf16)
        b = n * (1 + nf)
        for s in range(n):
            push(i0, n, s, gwo.at[pl.ds(s * r, r)], keep, send, o_out, psems.at[b + s])
            push(i0, n, s, vr, keep, send, o_vec, psems.at[b + n + s], True)
        done = lambda src, q: pltpu.make_async_copy(src, keep.at[0, pl.ds(0, src.shape[0])], psems.at[q]).wait()
        for s in range(n):
            done(dn.at[0, pl.ds(0, rf)], s)
            for c in range(nf):
                done(up.at[0, pl.ds(0, r)], n * (1 + c) + s)
            done(gwo.at[pl.ds(0, r)], b + s)
            done(vr, b + n + s)


def ffn(ln, me, tok, step, vec, upb, cot, mixed, mixedt, pieces, n):
    T, D = tok.shape
    FF = upb.shape[1]
    bm = min(512, T)
    nf = FF // D
    r = D // n
    meta = tuple((k, r0) for k, r0, _ in pieces)
    full = lambda a: pl.BlockSpec(a.shape, lambda i, l, m: (0,) * a.ndim)
    rows = pl.BlockSpec((bm, D), lambda i, l, m: (i, 0))
    B = S((n // 2, FF // n + (nf + 1) * r + VROWS, D), bf16)
    V = pltpu.VMEM
    return pl.pallas_call(
        functools.partial(ffn_body, n, meta, min(1024, FF)),
        grid_spec=pltpu.PrefetchScalarGridSpec(
            num_scalar_prefetch=2, grid=(T // bm,),
            in_specs=[rows, full(step), full(vec), full(upb), rows, rows, ANY] + [ANY] * len(pieces),
            out_specs=[rows, rows, pl.BlockSpec((D, bm), lambda i, l, m: (0, i)), ANY, ANY],
            scratch_shapes=[V((D, D), bf16), V((D, FF), bf16), V((FF, D), bf16), V((T, FF), bf16), V((T, FF), bf16), V((D, T), bf16), V((D, T), bf16), V((T, D), bf16), V((8, D), f32), V((1, FF), f32), V((nf, D, D), bf16), V((nf, D, D), bf16), V((D, D), bf16), V((VROWS, D), bf16), V((D, T), bf16), pltpu.SemaphoreType.DMA((16 * len(pieces),)), pltpu.SemaphoreType.DMA((n * (nf + 3) + 1,))]),
        out_shape=[S((T, D), bf16), S((T, D), f32), S((D, T), bf16), B, B],
        compiler_params=cp(), name="ffn", cost_estimate=cost(2 * T * D * (6 * FF + 3 * D), 16 * T * D, T * FF),
    )(ln, me, tok, step, vec, upb, cot, mixed, mixedt, *[a for _, _, a in pieces])


def attn_bwd_body(HD, scale, CR, v, kt, qt, gt, mt, linv, et, *refs):
    gq, ds = refs[-2:]
    T = v.shape[0]
    rid = lax.broadcasted_iota(jnp.int32, gt.shape, 0) // HD
    g = gt[...].astype(f32)
    q = qt[...]
    gv = gk = None
    for h in range(2):
        hs = slice(h * HD, (h + 1) * HD)
        gs = (g * linv[h : h + 1, :]).astype(bf16)
        gm = jnp.where(rid == h, gs, jnp.zeros_like(gs))
        dl = jnp.sum(gs[hs, :].astype(f32) * mt[hs, :], axis=0, keepdims=True)
        for c in range(T // CR):
            cs = slice(c * CR, (c + 1) * CR)
            ds[h, cs, :] = (et[h, cs, :].astype(f32) * (dot(v[cs, :], gm) - dl)).astype(bf16)
        a = dot(et[h], gm.T)
        b = dot(ds[h], jnp.where(rid == h, q, jnp.zeros_like(q)).T)
        gv = a if gv is None else gv + a
        gk = b if gk is None else gk + b
        gq[0, hs, :] = (dot(kt[hs, :], ds[h]) * scale).astype(bf16)
    gq[2] = gv.astype(bf16).T
    gq[1] = gk.astype(bf16).T


def attn_bwd(kv, qkvt, gmt, mixedf, linv, et, p0, cnt, prev):
    _, T, D = kv.shape
    HD = D // HEADS
    PW = 2 * HD
    NP = D // PW
    prev = list(prev)
    pr = pl.BlockSpec((PW, T), lambda p: (p0 + p, 0))
    of = lambda j: pl.BlockSpec((None, PW, T), lambda p: (j, p0 + p, 0))
    return pl.pallas_call(
        functools.partial(attn_bwd_body, HD, 1.0 / math.sqrt(HD), min(256, T)),
        grid=(cnt,),
        scratch_shapes=[pltpu.VMEM((2, T, T), bf16)],
        in_specs=[pl.BlockSpec((None, T, PW), lambda p: (1, 0, p0 + p)), of(1), of(0), pr, pr, pl.BlockSpec((None, 8, T), lambda p: (p0 + p, 0, 0)), pl.BlockSpec((2, T, T), lambda p: (p0 + p, 0, 0))] + [ANY] * len(prev),
        out_specs=pl.BlockSpec((3, PW, T), lambda p: (0, p0 + p, 0)),
        out_shape=S((3, D, T), bf16),
        input_output_aliases={7: 0} if prev else {},
        compiler_params=cp(), name="attn_bwd", cost_estimate=cost(cnt * 2 * 16 * T * T * 128, cnt * 2 * T * T * 2),
    )(kv, qkvt, qkvt, gmt, mixedf, linv, et, *prev)


def wqkv_body(n, me, xht, g, keep, send, res, vr, sems):
    j = pl.program_id(0)
    D = g.shape[0]
    r = D // n
    i0 = me[0]
    x = jnp.concatenate([xht[...], jnp.ones((16, xht.shape[1]), bf16)], axis=0)
    y = dot_t(x, g[...]).astype(bf16)
    res[j] = y[:D]
    vr[...] = jnp.where(lax.broadcasted_iota(jnp.int32, vr.shape, 0) == j, y[D:], jnp.where(j == 0, jnp.zeros_like(y[D:]), vr[...]))
    for s in range(n):
        push(i0, n, s, res.at[j, pl.ds(s * r, r)], keep, send, mult(j * r, 16), sems.at[j * n + s])

    @pl.when(j == 2)
    def _():
        for s in range(n):
            push(i0, n, s, vr, keep, send, 3 * r, sems.at[3 * n + s])
        for s in range(n):
            for q in range(3):
                pltpu.make_async_copy(res.at[0, pl.ds(0, r)], keep.at[0, pl.ds(0, r)], sems.at[q * n + s]).wait()
            pltpu.make_async_copy(vr, keep.at[0, pl.ds(0, VROWS)], sems.at[3 * n + s]).wait()


def wqkv(me, xht, g, n):
    D, T = xht.shape
    A = S((n // 2, 3 * (D // n) + VROWS, D), bf16)
    return pl.pallas_call(
        functools.partial(wqkv_body, n),
        grid_spec=pltpu.PrefetchScalarGridSpec(
            num_scalar_prefetch=1, grid=(3,),
            in_specs=[pl.BlockSpec((D, T), lambda j, m: (0, 0)), pl.BlockSpec((None, D, T), lambda j, m: (j, 0, 0))],
            out_specs=[ANY] * 2,
            scratch_shapes=[pltpu.VMEM((3, D, D), bf16), pltpu.VMEM((VROWS, D), bf16), pltpu.SemaphoreType.DMA((4 * n,))]),
        out_shape=[A, A],
        compiler_params=cp(), name="wqkv", cost_estimate=cost(6 * T * D * D, 10 * T * D),
    )(me, xht, g)


def back_body(tok, step, vec, g, gx1, *refs):
    ws, tg = refs[:-1], refs[-1]
    D = tok.shape[1]
    gw = D // GROUPS
    x = tok[...].astype(f32) + step[...].astype(f32)
    nx, rr = norm(x)
    gt = sum(dot(w[:, j * gw : (j + 1) * gw], g[j, q * gw : (q + 1) * gw, :]) for q, w in enumerate(ws) for j in range(3))
    gn = gt.T * row(vec[...], 0)
    tg[...] = gx1[...] + rr * (gn - jnp.mean(gn, axis=-1, keepdims=True) - nx * jnp.mean(gn * nx, axis=-1, keepdims=True))


def back(tok, step, vec, ws, g, gx1, bm=512):
    T, D = tok.shape
    full = lambda a: pl.BlockSpec(a.shape, lambda i: (0,) * a.ndim)
    rows = pl.BlockSpec((bm, D), lambda i: (i, 0))
    return pl.pallas_call(
        back_body, grid=(T // bm,),
        in_specs=[rows, full(step), full(vec), pl.BlockSpec((3, D, bm), lambda i: (0, 0, i)), rows] + [full(w) for w in ws],
        out_specs=rows, out_shape=S((T, D), f32), compiler_params=cp(), name="back", cost_estimate=cost(6 * T * D * D, 14 * T * D),
    )(tok, step, vec, g, gx1, *ws)


def shards(tokens, step_embed, lengths, cotangent, ln1_gain, ln1_bias, qkv_weight, q_bias, v_bias, out_weight, out_bias, ln2_gain, ln2_bias, up_weight, up_bias, down_weight, down_bias):
    n = lax.axis_size("shard")
    me = lax.axis_index("shard").astype(jnp.int32)
    mes = me[None]
    tok, cot, step = tokens[0], cotangent[0], step_embed
    T, D = tok.shape
    r = D // n
    FF = up_bias.shape[0] * n
    nc = FF // D
    rf = FF // n
    packs = pack_first(mes, qkv_weight, [ln1_gain, ln1_bias, q_bias, v_bias, out_bias, ln2_gain, ln2_bias, down_bias], up_bias)
    pack2 = pack_rest(out_weight, up_weight, down_weight)
    NP = HEADS // 2
    nx, xht = start(tok, step)
    pieces = gather_direct(packs[0], n, xht, pack2)
    kv, qkvt, w, vec, upb = front(mes, nx, pieces, n, FF)
    et, mixed, mixedt, mixedf, linv = attn_fwd(lengths, kv, qkvt, 0, NP, [])
    pieces2 = gather_direct(after(pack2, xht), n, linv)
    out, gx1, gmt, keep, send = ffn(lengths, mes, tok, step, vec, upb, cot, mixed, mixedt, pieces2, n)
    bwd = lambda p, c, g, *deps: attn_bwd(kv, qkvt, after(gmt, *deps) if deps else gmt, mixedf, linv, et, p, c, g)
    ra = rf + r
    got = swap(send, 1)
    g = bwd(0, 1, [])
    got = after(got, g)
    h = n // 4
    add = lambda a, b, k: add16(a[k], b[k])
    rows_a, rows_b = slice(0, ra), slice(ra, None)
    lo, hi = slice(0, h), slice(h, None)
    ka, xa, kb, xb = [add(keep, got, k) for k in ((lo, rows_a), (hi, rows_a), (lo, rows_b), (hi, rows_b))]
    g = bwd(1, NP - 1, [g], ka, xa, kb, xb)
    m = (n // 2).bit_length() - 1
    ga, gb = swap(xa, 2 << (m - 1)), swap(xb, 2)
    for t in range(1, m):
        dep = g if t == 1 else keep
        ga, gb, _ = lax.optimization_barrier((ga, gb, dep))
        h //= 2
        lo, hi = slice(0, h), slice(h, None)
        ka, xa = add(ka, ga, lo), add(ka, ga, hi)
        kb, xb = add(kb, gb, lo), add(kb, gb, hi)
        ga, gb = swap(xa, 2 << (m - 1 - t)), swap(xb, 2 << t)
        if t == 1:
            keep, send = wqkv(mes, after(xht, ka, xa, kb, xb), g, n)
    got = swap(send, 1)
    p2 = [add16(keep[k], got[k]) for k in range(n // 2)]
    far2 = spread(p2)
    ga, gb, _ = lax.optimization_barrier((ga, gb, keep))
    got = swap(send, 1)
    p2 = [add16(keep[k], got[k]) for k in range(n // 2)]
    far2 = spread(p2)
    own1 = jnp.concatenate([add16(ka, ga)[0], add16(kb, gb)[0]], axis=0)
    m1, o1, x1 = rep_half(own1)
    z1 = add16(m1, after(o1, *p2[1:]))
    tg = back(tok, after(step, z1, *p2[1:]), vec, [w], g, gx1)
    own2 = total(p2[0], [after(a, tg) for a in far2])
    m2, o2, x2 = rep_half(own2)
    steps = rep_steps()
    z2 = None if steps else add16(m2, o2)
    for b in steps:
        z1 = add16(z1, after(rep_perm(z1, b), x2))
        if z2 is None:
            z2 = add16(m2, after(o2, z1))
        pz = rep_perm(z2, b)
        z2 = add16(z2, after(pz, z1))
    o1, o2 = rep_perm(z1, 1), rep_perm(z2, 1)
    ids = jnp.stack([me, (lax.axis_index("rep") % 2).astype(jnp.int32)])
    g_down, g_up, g_out, g_upb, g_ob, g_g2, g_b2, g_db = finish_rest(ids, z1, o1, r, rf, nc, n)
    g_qkv, g_g1, g_b1, g_q, g_v = finish_first(ids, z2, after(o2, g_out), qkv_weight, ln1_gain, ln1_bias)
    flat = lambda a: a.reshape(-1)
    return (out[None], tg[None], flat(g_g1), flat(g_b1), g_qkv, flat(g_q), flat(g_v), g_out, flat(g_ob), flat(g_g2), flat(g_b2), g_up, flat(g_upb), g_down, flat(g_db))


def solution(mesh):
    from jax.sharding import PartitionSpec as P

    in_specs = (
        P(("rep", "shard"), None, None),
        P(("rep", "shard"), None),
        P(("rep", "shard")),
        P(("rep", "shard"), None, None),
        P("shard"),
        P("shard"),
        P("shard", None),
        P("shard"),
        P("shard"),
        P("shard", None),
        P("shard"),
        P("shard"),
        P("shard"),
        P("shard", None),
        P("shard"),
        P("shard", None),
        P("shard"),
    )
    out_specs = (
        P(("rep", "shard"), None, None),
        P(("rep", "shard"), None, None),
        P("shard"),
        P("shard"),
        P("shard", None),
        P("shard"),
        P("shard"),
        P("shard", None),
        P("shard"),
        P("shard"),
        P("shard"),
        P("shard", None),
        P("shard"),
        P("shard", None),
        P("shard"),
    )
    return jax.shard_map(shards, mesh=mesh, in_specs=in_specs, out_specs=out_specs, check_vma=False)
```

```python
import functools, math
import jax, jax.numpy as jnp
from jax import lax
from jax.experimental import pallas as pl
from jax.experimental.pallas import tpu as pltpu

f32 = jnp.float32
bf16 = jnp.bfloat16
EPS = 1e-05
HEADS = 8

def dot(a, b):
    return jnp.dot(a, b, preferred_element_type=f32)

def dot_t(a, b):
    return lax.dot_general(a, b, (((1,), (1,)), ((), ())), preferred_element_type=f32)

def cp(mib=60):
    return pltpu.CompilerParams(dimension_semantics=("arbitrary",), vmem_limit_bytes=mib << 20)

def norm(x):
    c = x - jnp.mean(x, axis=-1, keepdims=True)
    r = lax.rsqrt(jnp.mean(c * c, axis=-1, keepdims=True) + EPS)
    return c * r, r

def row(v, i):
    return v[i : i + 1, :].astype(f32)


VROWS = 16
LANES = 128


def xor_perm(n, k):
    return [(i, i ^ k) for i in range(n)]


def rep_perm(x, b):
    return lax.ppermute(x, "rep", xor_perm(lax.axis_size("rep"), b))


def swap(x, k):
    return lax.ppermute(x, "shard", xor_perm(lax.axis_size("shard"), k))


def after(x, *deps):
    return lax.optimization_barrier((x,) + deps)[0]


def gather_direct(x, n, *gate):
    out = [(0, 0, x)]
    far = [(k, swap(x, k)) for k in range(2, n, 2)]
    out += [(k, 0, after(y, *gate) if gate else y) for k, y in far]
    return out + [(k ^ 1, 0, swap(y, 1)) for k, _, y in out]


def add16(a, b):
    return a + b


def spread(parts):
    return [swap(parts[k], 2 * k) for k in range(len(parts) - 1, 0, -1)]


def total(own, got):
    t = own.astype(f32)
    for a in got:
        t = t + a.astype(f32)
    return t.astype(bf16)


def rep_half(x):
    h = x.shape[0] // 2
    odd = lax.axis_index("rep") % 2
    mine = lax.dynamic_slice_in_dim(x, odd * h, h, 0)
    other = lax.dynamic_slice_in_dim(x, (1 - odd) * h, h, 0)
    return mine, rep_perm(other, 1), other


def rep_steps():
    nr = lax.axis_size("rep")
    return [b for b in (2 << i for i in range(16)) if b < nr]


GROUPS = 1


def pack_first_body(me, w, upb, *refs):
    vecs = refs[:-GROUPS]
    outs = refs[-GROUPS:]
    r, W = w.shape
    D = W // 3
    gw = D // GROUPS
    for g, out in enumerate(outs):
        for j in range(3):
            out[j * r : (j + 1) * r, :] = w[:, j * D + g * gw : j * D + (g + 1) * gw]

    def spot(v):
        w_ = v.shape[1]
        if w_ >= LANES:
            return [v[q : q + 1, :] for q in range(v.shape[0])]
        t = LANES // w_
        lane = lax.broadcasted_iota(jnp.int32, (1, LANES), 1)
        return [jnp.where(lane // w_ == me[0] % t, jnp.concatenate([v] * t, axis=1), jnp.zeros((1, LANES), f32))]

    rows = [a for v in vecs for a in spot(v[...].astype(f32))] + spot(upb[...].astype(f32))
    b = jnp.concatenate(rows + [jnp.zeros((VROWS - len(rows), LANES), f32)], axis=0).astype(bf16)
    outs[0][3 * r :, :] = jnp.concatenate([b, jnp.zeros((VROWS, gw - LANES), bf16)], axis=1) if gw > LANES else b


def whole(n):
    return [pl.BlockSpec(memory_space=pltpu.VMEM)] * n


def once(*arrays):
    return [pl.BlockSpec(a.shape, lambda i, *m, nd=len(a.shape): (0,) * nd) for a in arrays]


def pack_first(me, w, vecs, upb):
    r, W = w.shape
    gw = W // 3 // GROUPS
    lanes = lambda v: v.reshape(-1, min(LANES, v.shape[0]))
    args = [w] + [lanes(v) for v in [upb] + vecs]
    outs = [S((3 * r + (VROWS if g == 0 else 0), gw), bf16) for g in range(GROUPS)]
    return pl.pallas_call(
        pack_first_body,
        grid_spec=pltpu.PrefetchScalarGridSpec(num_scalar_prefetch=1, grid=(1,), in_specs=once(*args), out_specs=once(*outs)),
        out_shape=outs, compiler_params=cp(), name="pack_first", cost_estimate=cost(0, 4 * w.size),
    )(me, *args)


def pack_rest_body(wo, wu, wd, out):
    r, D = wo.shape
    out[:r, :] = wo[...]
    for j in range(wu.shape[1] // D):
        out[(1 + j) * r : (2 + j) * r, :] = wu[:, j * D : (j + 1) * D]
    out[(1 + wu.shape[1] // D) * r :, :] = wd[...]


def pack_rest(wo, wu, wd):
    D = wo.shape[1]
    out = S(((wo.size + wu.size + wd.size) // D, D), bf16)
    return pl.pallas_call(
        pack_rest_body, grid=(1,), in_specs=once(wo, wu, wd), out_specs=once(out)[0],
        out_shape=out, compiler_params=cp(), name="pack_rest", cost_estimate=cost(0, 4 * wu.size),
    )(wo, wu, wd)


def own_lanes(tiles, me, w):
    pick = lambda i: sum(jnp.where(i == t, a, jnp.zeros_like(a)) for t, a in enumerate(tiles))
    if w >= LANES:
        q = w // LANES
        return jnp.concatenate([pick(me * q + c) for c in range(q)], axis=1)
    per = LANES // w
    x = pick(me // per)
    off = me % per
    return sum(jnp.where(off == o, x[:, o * w : (o + 1) * w], 0.0) for o in range(per))


def rows_of(lo, hi, a, b):
    h = lo.shape[0]
    if b <= h:
        return lo[a:b, :]
    if a >= h:
        return hi[a - h : b - h, :]
    return jnp.concatenate([lo[a:h, :], hi[: b - h, :]], axis=0)


def finish_rest_body(r, rf, n, ids, s, o, down, up, out, upb, *vecs):
    D = out.shape[1]
    nf = up.shape[1] // D

    def run(lo, hi):
        f = lambda a, b: rows_of(lo, hi, a, b).astype(f32)
        down[...] = f(0, rf)
        out[...] = f(rf, rf + r)
        for j in range(nf):
            up[:, j * D : (j + 1) * D] = f(rf + (j + 1) * r, rf + (j + 2) * r)
        b = rf + (nf + 1) * r
        v = f(b, b + VROWS)
        me = ids[0]
        tiles = [v[0:8, t * LANES : (t + 1) * LANES] for t in range(D // LANES)]
        x = own_lanes(tiles, me, r)
        for q, ref in enumerate(vecs):
            ref[...] = x[q : q + 1, :]
        tiles = [v[4 + q : 5 + q, t * LANES : (t + 1) * LANES] for q in range(nf) for t in range(D // LANES)]
        upb[...] = own_lanes(tiles, me, nf * D // n)

    @pl.when(ids[1] == 0)
    def _():
        run(s, o)

    @pl.when(ids[1] == 1)
    def _():
        run(o, s)


def finish_rest(ids, s, o, r, rf, nf, n):
    D = s.shape[1]
    row1 = lambda w: S((1, w), f32)
    return pl.pallas_call(
        functools.partial(finish_rest_body, r, rf, n),
        in_specs=[pl.BlockSpec(memory_space=pltpu.SMEM)] + whole(2), out_specs=whole(8),
        out_shape=[S((rf, D), f32), S((r, nf * D), f32), S((r, D), f32), row1(nf * D // n)] + [row1(r)] * 4,
        compiler_params=pltpu.CompilerParams(vmem_limit_bytes=16 << 20), name="finish_rest", cost_estimate=cost(0, 8 * s.size),
    )(ids, s, o)


def finish_first_body(ids, s, o, w, gain, bias, qkv, gg, gb, qb, vb):
    r, W = w.shape
    D = s.shape[1]

    def run(lo, hi):
        f = lambda a, b: rows_of(lo, hi, a, b).astype(f32)
        v = f(3 * r, 3 * r + VROWS)
        nt = D // LANES
        accg = accb = jnp.zeros((r, LANES), f32)
        col = lambda g: jnp.concatenate([g[...].astype(f32), jnp.zeros((7, r), f32)], axis=0).T[:, 0:1]
        cg, cb = col(gain), col(bias)
        for j in range(3):
            m = f(j * r, (j + 1) * r)
            sq = v[j : j + 1, :]
            ww = w[:, j * D : (j + 1) * D].astype(f32)
            qkv[:, j * D : (j + 1) * D] = cg * m + cb * sq
            pg, pb = ww * m, ww * sq
            accg = accg + sum(pg[:, t * LANES : (t + 1) * LANES] for t in range(nt))
            accb = accb + sum(pb[:, t * LANES : (t + 1) * LANES] for t in range(nt))
        gg[...] = jnp.sum(accg.T, axis=0, keepdims=True)
        gb[...] = jnp.sum(accb.T, axis=0, keepdims=True)
        x = own_lanes([v[0:8, t * LANES : (t + 1) * LANES] for t in range(nt)], ids[0], r)
        qb[...] = x[0:1, :]
        vb[...] = x[2:3, :]

    @pl.when(ids[1] == 0)
    def _():
        run(s, o)

    @pl.when(ids[1] == 1)
    def _():
        run(o, s)


def finish_first(ids, s, o, w, gain, bias):
    r, W = w.shape
    return pl.pallas_call(
        finish_first_body,
        in_specs=[pl.BlockSpec(memory_space=pltpu.SMEM)] + whole(5), out_specs=whole(5),
        out_shape=[S((r, W), f32)] + [S((1, r), f32)] * 4,
        compiler_params=pltpu.CompilerParams(vmem_limit_bytes=16 << 20), name="finish_first", cost_estimate=cost(0, 8 * w.size),
    )(ids, s, o, w, gain[None], bias[None])


def pull(me, refs, meta, segs, sems):
    copies = []
    for ref, (k, r0) in zip(refs, meta):
        s = jnp.bitwise_xor(me, k)
        r1 = r0 + ref.shape[0]
        for a, c, dst, lanes in segs:
            lo, hi = max(a, r0), min(a + c, r1)
            if lo < hi:
                src = ref.at[pl.ds(lo - r0, hi - lo), pl.ds(0, lanes)]
                copies.append(pltpu.make_async_copy(src, dst(s, lo - a, hi - lo), sems.at[len(copies)]))
    return copies


def mult(x, m):
    return pl.multiple_of(x, m)


def weight_segs(w, r):
    gw = w.shape[1] // 3
    seg = lambda j: (j * r, r, lambda s, o, c: w.at[pl.ds(mult(s * r + o, 16), c), pl.ds(j * gw, gw)], gw)
    return [seg(j) for j in range(3)]


def start_body(tok, step, nx, xht):
    n, _ = norm(tok[...].astype(f32) + step[...].astype(f32))
    nx[...] = n
    xht[...] = n.astype(bf16).T


def start(tok, step, bm=256):
    T, D = tok.shape
    rows = pl.BlockSpec((bm, D), lambda i: (i, 0))
    return pl.pallas_call(
        start_body, grid=(T // bm,),
        in_specs=[rows, pl.BlockSpec((1, D), lambda i: (0, 0))], out_specs=[rows, pl.BlockSpec((D, bm), lambda i: (0, i))],
        out_shape=[S((T, D), f32), S((D, T), bf16)], compiler_params=cp(), name="start", cost_estimate=cost(20 * T * D, 8 * T * D),
    )(tok, step)


def front_body(scale, n, meta, me, nx, *refs):
    np_ = len(meta)
    pieces = refs[:np_]
    kv, qkvt, wout, vec, upb, nv, h, w, vbuf, sems, own = refs[np_:]
    T, D = nv.shape
    r = D // n
    FF = upb.shape[1]
    i = pl.program_id(0)
    cw = kv.shape[2]
    per_j = D // cw
    segs = [(3 * r, VROWS, lambda s, o, c: vbuf.at[s, pl.ds(o, c)], LANES)] + weight_segs(w, r)
    load = pltpu.make_async_copy(nx, nv, own.at[0])
    save = pltpu.make_async_copy(w, wout, own.at[1])

    @pl.when(i == 0)
    def _():
        cs = pull(me[0], pieces, meta, segs, sems)
        for c in cs:
            c.start()
        load.start()
        for c in cs:
            c.wait()
        save.start()
        per = LANES // r
        tiles = [sum(vbuf[s, 0:8, :].astype(f32) for s in range(t * per, (t + 1) * per)) for t in range(D // LANES)]
        vec[...] = jnp.concatenate(tiles, axis=1)
        wu = FF // n
        if wu >= LANES:
            rows = [vbuf[s, 8 + q : 9 + q, :].astype(f32) for s in range(n) for q in range(wu // LANES)]
        else:
            per = LANES // wu
            rows = [sum(vbuf[s, 8:9, :].astype(f32) for s in range(t * per, (t + 1) * per)) for t in range(FF // LANES)]
        upb[...] = jnp.concatenate(rows, axis=1)
        load.wait()
        v = vec[...]
        h[...] = (nv[...] * row(v, 0) + row(v, 1)).astype(bf16)

    cols = pl.ds(mult(i * cw, 128), cw)
    y = dot(h[...], w[:, cols])
    here = pl.ds(mult((i % per_j) * cw, 128), cw)
    kind = i // per_j
    y = (y + jnp.where(kind == 0, vec[2:3, here], jnp.where(kind == 2, vec[3:4, here], 0.0))).astype(bf16)
    kv[0] = y
    qkvt[0] = jnp.where(kind == 0, y * bf16(scale), y).T

    @pl.when(i == pl.num_programs(0) - 1)
    def _():
        save.wait()


S = jax.ShapeDtypeStruct
ANY = pl.BlockSpec(memory_space=pl.ANY)


def cost(flops, nbytes, tr=0):
    return pl.CostEstimate(flops=int(flops), bytes_accessed=int(nbytes), transcendentals=int(tr))


def front(me, nx, pieces, n, FF, cw=512):
    T, D = nx.shape
    scale = 1.0 / math.sqrt(D // HEADS)
    meta = tuple((k, r0) for k, r0, _ in pieces)
    q = D // cw
    keep = lambda *sh: pl.BlockSpec(sh, lambda i, m: (0,) * len(sh))
    rest = lambda i: jnp.maximum(i - q, 0)
    V = pltpu.VMEM
    return pl.pallas_call(
        functools.partial(front_body, scale, n, meta),
        grid_spec=pltpu.PrefetchScalarGridSpec(
            num_scalar_prefetch=1, grid=(3 * q,),
            in_specs=[ANY] * (1 + len(pieces)),
            out_specs=[pl.BlockSpec((1, T, cw), lambda i, m: (rest(i) // q, 0, rest(i) % q)), pl.BlockSpec((1, cw, T), lambda i, m: (i // q, i % q, 0)), ANY, keep(8, D), keep(1, FF)],
            scratch_shapes=[V((T, D), f32), V((T, D), bf16), V((D, 3 * D), bf16), V((n, VROWS, LANES), bf16), pltpu.SemaphoreType.DMA((8 * len(pieces),)), pltpu.SemaphoreType.DMA((2,))]),
        out_shape=[S((2, T, D), bf16), S((3, D, T), bf16), S((D, 3 * D), bf16), S((8, D), f32), S((1, FF), f32)],
        compiler_params=cp(), name="front", cost_estimate=cost(6 * T * D * D, 12 * T * D),
    )(me, nx, *[a for _, _, a in pieces])


def attn_fwd_body(HD, bi, CR, p0, ln, k, qt, vt, *refs):
    et, mixed, mixedt, mixedf, linv, scr, ka, eb, esem = refs[-9:]
    T, PW = k.shape
    n = ln[0]
    p = pl.program_id(0)
    last = p == pl.num_programs(0) - 1
    rid = lax.broadcasted_iota(jnp.int32, (PW, bi), 0)
    lane = lax.broadcasted_iota(jnp.int32, (T, PW), 1)
    rows = lax.broadcasted_iota(jnp.int32, (T, PW), 0)
    ka[:, :PW] = k[...]
    ka[:, PW:] = jnp.where((lane == 0) & (rows >= n), f32(-1e30), f32(0)).astype(bf16)
    ones = jnp.where(rid == 0, f32(1), f32(0)).astype(bf16)
    va = [jnp.concatenate([vt[h * HD : (h + 1) * HD, :], jnp.ones((16, T), bf16)], axis=0) for h in range(2)]
    tasks = [(b, h) for b in range(T // bi) for h in range(2)]
    nch = T // CR

    def query(t):
        b, h = tasks[t]
        q = qt[:, b * bi : (b + 1) * bi]
        return jnp.concatenate([jnp.where(rid // HD == h, q, jnp.zeros_like(q)), ones], axis=0)

    def score(t, c, q):
        s = dot(ka[c * CR : (c + 1) * CR, :], q)
        scr[t % 2, c * CR : (c + 1) * CR, :] = s
        return jnp.max(s, axis=0, keepdims=True)

    q = query(0)
    m = functools.reduce(jnp.maximum, [score(0, c, q) for c in range(nch)])
    half = None
    for t, (b, h) in enumerate(tasks):
        sl = slice(b * bi, (b + 1) * bi)
        more = t + 1 < len(tasks)
        put = pltpu.make_async_copy(eb.at[t % 2], et.at[2 * (p0 + p) + h, :, pl.ds(b * bi, bi)], esem.at[t % 2])
        if t < 2:

            @pl.when(p > 0)
            def _():
                put.wait()

        else:
            put.wait()
        if more:
            q = query(t + 1)
        nxt = []
        for c in range(nch):
            cs = slice(c * CR, (c + 1) * CR)
            if more:
                nxt.append(score(t + 1, c, q))
            eb[t % 2, cs, :] = jnp.exp(scr[t % 2, cs, :] - m).astype(bf16)
        put.start()
        o = dot(va[h], eb[t % 2])
        if more:
            m = functools.reduce(jnp.maximum, nxt)
        inv = 1.0 / o[HD : HD + 1, :]
        linv[h : h + 1, sl] = inv
        o = o[:HD, :] * inv
        if h == 0:
            half = o
        else:
            mt = jnp.concatenate([half, o], axis=0)
            mixedf[:, sl] = mt
            mt = mt.astype(bf16)
            mixedt[:, sl] = mt
            mixed[sl, :] = mt.T

    @pl.when(last)
    def _():
        for q in range(2):
            pltpu.make_async_copy(eb.at[q], et.at[0, :, pl.ds(0, bi)], esem.at[q]).wait()


def attn_fwd(ln, kv, qkvt, p0, cnt, prev):
    _, T, D = kv.shape
    HD = D // HEADS
    PW = 2 * HD
    NP = D // PW
    bi = T
    prev = list(prev)
    return pl.pallas_call(
        functools.partial(attn_fwd_body, HD, bi, min(512, T), p0),
        grid_spec=pltpu.PrefetchScalarGridSpec(
            num_scalar_prefetch=1, grid=(cnt,),
            in_specs=[pl.BlockSpec((None, T, PW), lambda p, r: (0, 0, p0 + p)), pl.BlockSpec((None, PW, T), lambda p, r: (0, p0 + p, 0)), pl.BlockSpec((None, PW, T), lambda p, r: (2, p0 + p, 0))] + [ANY] * len(prev),
            out_specs=[ANY, pl.BlockSpec((T, PW), lambda p, r: (0, p0 + p)), pl.BlockSpec((PW, T), lambda p, r: (p0 + p, 0)), pl.BlockSpec((PW, T), lambda p, r: (p0 + p, 0)), pl.BlockSpec((None, 8, T), lambda p, r: (p0 + p, 0, 0))],
            scratch_shapes=[pltpu.VMEM((2, T, bi), f32), pltpu.VMEM((T, 2 * PW), bf16), pltpu.VMEM((2, T, bi), bf16), pltpu.SemaphoreType.DMA((2,))]),
        out_shape=[S((HEADS, T, T), bf16), S((T, D), bf16), S((D, T), bf16), S((D, T), f32), S((NP, 8, T), f32)],
        input_output_aliases={4 + i: i for i in range(len(prev))},
        compiler_params=cp(), name="attn_fwd", cost_estimate=cost(cnt * 2 * 8 * T * T * 128, cnt * 2 * T * T * 2, cnt * 2 * T * T),
    )(ln, kv, qkvt, qkvt, *prev)


G0 = math.sqrt(2 / math.pi)


def bit_reverse(x, m):
    y = jnp.zeros_like(x)
    for t in range(m):
        y = y | (((x >> t) & 1) << (m - 1 - t))
    return y


def push(me, n, s, src, keep, send, row0, sem, reverse=False):
    k = jnp.bitwise_xor(me, s)
    p = k >> 1
    if reverse:
        p = bit_reverse(p, (n // 2).bit_length() - 1)
    put = lambda dst: pltpu.make_async_copy(src, dst.at[p, pl.ds(row0, src.shape[0])], sem)

    @pl.when(k & 1 == 0)
    def _():
        put(keep).start()

    @pl.when(k & 1 == 1)
    def _():
        put(send).start()


def ffn_body(n, meta, ch, ln, me, tok, step, vec, upb, cot, mixed, mixedt, *refs):
    np_ = len(meta)
    pieces = refs[:np_]
    out, gx1, gmt, keep, send, wo, wu, wd, act, gup, h2t, gdt, gattn, sums, upsum, dn, up, gwo, vr, mtv, sems, psems = refs[np_:]
    i = pl.program_id(0)
    bm, D = tok.shape
    FF = wu.shape[1]
    r = D // n
    rf = FF // n
    nf = FF // D
    i0 = me[0]
    ro = pl.ds(mult(i * bm, 128), bm)
    first = i == 0
    seg = lambda j: (r + j * r, r, lambda s, o, c: wu.at[pl.ds(mult(s * r + o, 16), c), pl.ds(j * D, D)], D)
    seg_o = [(0, r, lambda s, o, c: wo.at[pl.ds(mult(s * r + o, 16), c)], D)]
    seg_u = [seg(j) for j in range(nf)]
    seg_d = [(r + r * nf, rf, lambda s, o, c: wd.at[pl.ds(mult(s * rf + o, 16), c)], D)]
    q = sems.shape[0] // 4
    parts = [(seg_o, sems.at[pl.ds(0, q)]), (seg_d, sems.at[pl.ds(q, q)]), (seg_u, sems.at[pl.ds(2 * q, 2 * q)])]
    load = pltpu.make_async_copy(mixedt, mtv, psems.at[psems.shape[0] - 1])

    @pl.when(first)
    def _():
        for sg, sm in parts:
            for c in pull(i0, pieces, meta, sg, sm):
                c.start()
        load.start()
        sums[...] = jnp.zeros_like(sums)
        upsum[...] = jnp.zeros_like(upsum)
        for c in pull(i0, pieces, meta, *parts[0]):
            c.wait()

    v = vec[...]
    x1 = tok[...].astype(f32) + step[...].astype(f32) + dot(mixed[...], wo[...]) + row(v, 4)
    nx, rr = norm(x1)
    h2 = (nx * row(v, 5) + row(v, 6)).astype(bf16)
    live = (lax.broadcasted_iota(jnp.int32, (bm, 1), 0) + i * bm) < ln[0]
    gd = jnp.where(live, cot[...], jnp.zeros_like(cot))
    acc = x1 + row(v, 7)
    gh = None
    nc = FF // ch
    sl = [slice(c * ch, (c + 1) * ch) for c in range(nc)]
    lead = lambda c: (dot(h2, wu[:, sl[c]]), dot_t(gd, wd[sl[c], :]))
    h2t[:, ro] = h2.T
    gdt[:, ro] = gd.T

    @pl.when(first)
    def _():
        for sg, sm in parts[1:]:
            for c in pull(i0, pieces, meta, sg, sm):
                c.wait()

    nxt = lead(0)
    for c in range(nc):
        u, ga = nxt
        nxt = lead(c + 1) if c + 1 < nc else None
        u = u + upb[:, sl[c]]
        u2 = u * u
        t = jnp.tanh(u * (f32(G0) + f32(G0 * 0.044715) * u2))
        half = 0.5 + 0.5 * t
        a = (u * half).astype(bf16)
        act[ro, sl[c]] = a
        dg = half + u * (half * (1.0 - half)) * (f32(2 * G0) + f32(6 * 0.044715 * G0) * u2)
        gu = (ga * dg).astype(bf16)
        gup[ro, sl[c]] = gu
        upsum[:, sl[c]] += jnp.sum(gu.astype(f32), axis=0, keepdims=True)
        acc = acc + dot(a, wd[sl[c], :])
        p = dot_t(gu, wu[:, sl[c]])
        gh = p if gh is None else gh + p
    out[...] = jnp.where(live, acc, 0.0).astype(bf16)
    gn = gh * row(v, 5)
    gx = gd.astype(f32) + rr * (gn - jnp.mean(gn, axis=-1, keepdims=True) - nx * jnp.mean(gn * nx, axis=-1, keepdims=True))
    gx1[...] = gx
    gab = gx.astype(bf16)
    gattn[ro, :] = gab
    gmt[...] = dot_t(gab, wo[...]).astype(bf16).T
    s_ = lambda a: jnp.sum(a.astype(f32), axis=0, keepdims=True)
    sums[...] += jnp.concatenate([s_(gab), s_(gh * nx), s_(gh), s_(gd), jnp.zeros((4, D), f32)], axis=0)

    @pl.when(i == pl.num_programs(0) - 1)
    def _():
        per = D // rf
        o_out, o_up, o_vec = rf, rf + r, rf + (nf + 1) * r
        for j in range(nf):
            dn[j] = dot(gdt[...], act[:, j * D : (j + 1) * D]).astype(bf16).T
            for t in range(per):
                push(i0, n, j * per + t, dn.at[j, pl.ds(t * rf, rf)], keep, send, 0, psems.at[j * per + t])
            up[j] = dot(h2t[...], gup[:, j * D : (j + 1) * D]).astype(bf16)
            for s in range(n):
                push(i0, n, s, up.at[j, pl.ds(s * r, r)], keep, send, o_up + j * r, psems.at[n * (1 + j) + s], True)
        load.wait()
        gwo[...] = dot(mtv[...], gattn[...]).astype(bf16)
        vr[...] = jnp.concatenate([sums[0:4, :]] + [upsum[:, c * D : (c + 1) * D] for c in range(nf)] + [jnp.zeros((VROWS - 4 - nf, D), f32)], axis=0).astype(bf16)
        b = n * (1 + nf)
        for s in range(n):
            push(i0, n, s, gwo.at[pl.ds(s * r, r)], keep, send, o_out, psems.at[b + s])
            push(i0, n, s, vr, keep, send, o_vec, psems.at[b + n + s], True)
        done = lambda src, q: pltpu.make_async_copy(src, keep.at[0, pl.ds(0, src.shape[0])], psems.at[q]).wait()
        for s in range(n):
            done(dn.at[0, pl.ds(0, rf)], s)
            for c in range(nf):
                done(up.at[0, pl.ds(0, r)], n * (1 + c) + s)
            done(gwo.at[pl.ds(0, r)], b + s)
            done(vr, b + n + s)


def ffn(ln, me, tok, step, vec, upb, cot, mixed, mixedt, pieces, n):
    T, D = tok.shape
    FF = upb.shape[1]
    bm = min(512, T)
    nf = FF // D
    r = D // n
    meta = tuple((k, r0) for k, r0, _ in pieces)
    full = lambda a: pl.BlockSpec(a.shape, lambda i, l, m: (0,) * a.ndim)
    rows = pl.BlockSpec((bm, D), lambda i, l, m: (i, 0))
    B = S((n // 2, FF // n + (nf + 1) * r + VROWS, D), bf16)
    V = pltpu.VMEM
    return pl.pallas_call(
        functools.partial(ffn_body, n, meta, min(1024, FF)),
        grid_spec=pltpu.PrefetchScalarGridSpec(
            num_scalar_prefetch=2, grid=(T // bm,),
            in_specs=[rows, full(step), full(vec), full(upb), rows, rows, ANY] + [ANY] * len(pieces),
            out_specs=[rows, rows, pl.BlockSpec((D, bm), lambda i, l, m: (0, i)), ANY, ANY],
            scratch_shapes=[V((D, D), bf16), V((D, FF), bf16), V((FF, D), bf16), V((T, FF), bf16), V((T, FF), bf16), V((D, T), bf16), V((D, T), bf16), V((T, D), bf16), V((8, D), f32), V((1, FF), f32), V((nf, D, D), bf16), V((nf, D, D), bf16), V((D, D), bf16), V((VROWS, D), bf16), V((D, T), bf16), pltpu.SemaphoreType.DMA((16 * len(pieces),)), pltpu.SemaphoreType.DMA((n * (nf + 3) + 1,))]),
        out_shape=[S((T, D), bf16), S((T, D), f32), S((D, T), bf16), B, B],
        compiler_params=cp(48), name="ffn", cost_estimate=cost(2 * T * D * (6 * FF + 3 * D), 16 * T * D, T * FF),
    )(ln, me, tok, step, vec, upb, cot, mixed, mixedt, *[a for _, _, a in pieces])


def attn_bwd_body(HD, scale, CR, v, kt, qt, gt, mt, linv, et, *refs):
    gq, ds = refs[-2:]
    T = v.shape[0]
    rid = lax.broadcasted_iota(jnp.int32, gt.shape, 0) // HD
    g = gt[...].astype(f32)
    q = qt[...]
    gv = gk = None
    for h in range(2):
        hs = slice(h * HD, (h + 1) * HD)
        gs = (g * linv[h : h + 1, :]).astype(bf16)
        gm = jnp.where(rid == h, gs, jnp.zeros_like(gs))
        dl = jnp.sum(gs[hs, :].astype(f32) * mt[hs, :], axis=0, keepdims=True)
        for c in range(T // CR):
            cs = slice(c * CR, (c + 1) * CR)
            ds[h, cs, :] = (et[h, cs, :].astype(f32) * (dot(v[cs, :], gm) - dl)).astype(bf16)
        a = dot(et[h], gm.T)
        b = dot(ds[h], jnp.where(rid == h, q, jnp.zeros_like(q)).T)
        gv = a if gv is None else gv + a
        gk = b if gk is None else gk + b
        gq[0, hs, :] = (dot(kt[hs, :], ds[h]) * scale).astype(bf16)
    gq[2] = gv.astype(bf16).T
    gq[1] = gk.astype(bf16).T


def attn_bwd(kv, qkvt, gmt, mixedf, linv, et, p0, cnt, prev):
    _, T, D = kv.shape
    HD = D // HEADS
    PW = 2 * HD
    NP = D // PW
    prev = list(prev)
    pr = pl.BlockSpec((PW, T), lambda p: (p0 + p, 0))
    of = lambda j: pl.BlockSpec((None, PW, T), lambda p: (j, p0 + p, 0))
    return pl.pallas_call(
        functools.partial(attn_bwd_body, HD, 1.0 / math.sqrt(HD), min(256, T)),
        grid=(cnt,),
        scratch_shapes=[pltpu.VMEM((2, T, T), bf16)],
        in_specs=[pl.BlockSpec((None, T, PW), lambda p: (1, 0, p0 + p)), of(1), of(0), pr, pr, pl.BlockSpec((None, 8, T), lambda p: (p0 + p, 0, 0)), pl.BlockSpec((2, T, T), lambda p: (p0 + p, 0, 0))] + [ANY] * len(prev),
        out_specs=pl.BlockSpec((3, PW, T), lambda p: (0, p0 + p, 0)),
        out_shape=S((3, D, T), bf16),
        input_output_aliases={7: 0} if prev else {},
        compiler_params=cp(), name="attn_bwd", cost_estimate=cost(cnt * 2 * 16 * T * T * 128, cnt * 2 * T * T * 2),
    )(kv, qkvt, qkvt, gmt, mixedf, linv, et, *prev)


def wqkv_body(n, me, xht, g, keep, send, res, vr, sems):
    j = pl.program_id(0)
    D = g.shape[0]
    r = D // n
    i0 = me[0]
    x = jnp.concatenate([xht[...], jnp.ones((16, xht.shape[1]), bf16)], axis=0)
    y = dot_t(x, g[...]).astype(bf16)
    res[j] = y[:D]
    vr[...] = jnp.where(lax.broadcasted_iota(jnp.int32, vr.shape, 0) == j, y[D:], jnp.where(j == 0, jnp.zeros_like(y[D:]), vr[...]))
    for s in range(n):
        push(i0, n, s, res.at[j, pl.ds(s * r, r)], keep, send, mult(j * r, 16), sems.at[j * n + s])

    @pl.when(j == 2)
    def _():
        for s in range(n):
            push(i0, n, s, vr, keep, send, 3 * r, sems.at[3 * n + s])
        for s in range(n):
            for q in range(3):
                pltpu.make_async_copy(res.at[0, pl.ds(0, r)], keep.at[0, pl.ds(0, r)], sems.at[q * n + s]).wait()
            pltpu.make_async_copy(vr, keep.at[0, pl.ds(0, VROWS)], sems.at[3 * n + s]).wait()


def wqkv(me, xht, g, n):
    D, T = xht.shape
    A = S((n // 2, 3 * (D // n) + VROWS, D), bf16)
    return pl.pallas_call(
        functools.partial(wqkv_body, n),
        grid_spec=pltpu.PrefetchScalarGridSpec(
            num_scalar_prefetch=1, grid=(3,),
            in_specs=[pl.BlockSpec((D, T), lambda j, m: (0, 0)), pl.BlockSpec((None, D, T), lambda j, m: (j, 0, 0))],
            out_specs=[ANY] * 2,
            scratch_shapes=[pltpu.VMEM((3, D, D), bf16), pltpu.VMEM((VROWS, D), bf16), pltpu.SemaphoreType.DMA((4 * n,))]),
        out_shape=[A, A],
        compiler_params=cp(), name="wqkv", cost_estimate=cost(6 * T * D * D, 10 * T * D),
    )(me, xht, g)


def back_body(tok, step, vec, g, gx1, *refs):
    ws, tg = refs[:-1], refs[-1]
    D = tok.shape[1]
    gw = D // GROUPS
    x = tok[...].astype(f32) + step[...].astype(f32)
    nx, rr = norm(x)
    gt = sum(dot(w[:, j * gw : (j + 1) * gw], g[j, q * gw : (q + 1) * gw, :]) for q, w in enumerate(ws) for j in range(3))
    gn = gt.T * row(vec[...], 0)
    tg[...] = gx1[...] + rr * (gn - jnp.mean(gn, axis=-1, keepdims=True) - nx * jnp.mean(gn * nx, axis=-1, keepdims=True))


def back(tok, step, vec, ws, g, gx1, bm=512):
    T, D = tok.shape
    full = lambda a: pl.BlockSpec(a.shape, lambda i: (0,) * a.ndim)
    rows = pl.BlockSpec((bm, D), lambda i: (i, 0))
    return pl.pallas_call(
        back_body, grid=(T // bm,),
        in_specs=[rows, full(step), full(vec), pl.BlockSpec((3, D, bm), lambda i: (0, 0, i)), rows] + [full(w) for w in ws],
        out_specs=rows, out_shape=S((T, D), f32), compiler_params=cp(), name="back", cost_estimate=cost(6 * T * D * D, 14 * T * D),
    )(tok, step, vec, g, gx1, *ws)


def shards(tokens, step_embed, lengths, cotangent, ln1_gain, ln1_bias, qkv_weight, q_bias, v_bias, out_weight, out_bias, ln2_gain, ln2_bias, up_weight, up_bias, down_weight, down_bias):
    n = lax.axis_size("shard")
    me = lax.axis_index("shard").astype(jnp.int32)
    mes = me[None]
    tok, cot, step = tokens[0], cotangent[0], step_embed
    T, D = tok.shape
    r = D // n
    FF = up_bias.shape[0] * n
    nc = FF // D
    rf = FF // n
    packs = pack_first(mes, qkv_weight, [ln1_gain, ln1_bias, q_bias, v_bias, out_bias, ln2_gain, ln2_bias, down_bias], up_bias)
    pack2 = pack_rest(out_weight, up_weight, down_weight)
    NP = HEADS // 2
    nx, xht = start(tok, step)
    pieces = gather_direct(packs[0], n, xht, pack2)
    kv, qkvt, w, vec, upb = front(mes, nx, pieces, n, FF)
    et, mixed, mixedt, mixedf, linv = attn_fwd(lengths, kv, qkvt, 0, NP, [])
    pieces2 = gather_direct(after(pack2, xht), n, linv)
    out, gx1, gmt, keep, send = ffn(lengths, mes, tok, step, vec, upb, cot, mixed, mixedt, pieces2, n)
    bwd = lambda p, c, g, *deps: attn_bwd(kv, qkvt, after(gmt, *deps) if deps else gmt, mixedf, linv, et, p, c, g)
    ra = rf + r
    got = swap(send, 1)
    g = bwd(0, 1, [])
    got = after(got, g)
    h = n // 4
    add = lambda a, b, k: add16(a[k], b[k])
    rows_a, rows_b = slice(0, ra), slice(ra, None)
    lo, hi = slice(0, h), slice(h, None)
    ka, xa, kb, xb = [add(keep, got, k) for k in ((lo, rows_a), (hi, rows_a), (lo, rows_b), (hi, rows_b))]
    g = bwd(1, NP - 1, [g], ka, xa, kb, xb)
    m = (n // 2).bit_length() - 1
    ga, gb = swap(xa, 2 << (m - 1)), swap(xb, 2)
    for t in range(1, m):
        dep = g if t == 1 else keep
        ga, gb, _ = lax.optimization_barrier((ga, gb, dep))
        h //= 2
        lo, hi = slice(0, h), slice(h, None)
        ka, xa = add(ka, ga, lo), add(ka, ga, hi)
        kb, xb = add(kb, gb, lo), add(kb, gb, hi)
        ga, gb = swap(xa, 2 << (m - 1 - t)), swap(xb, 2 << t)
        if t == 1:
            keep, send = wqkv(mes, after(xht, ka, xa, kb, xb), g, n)
    got = swap(send, 1)
    p2 = [add16(keep[k], got[k]) for k in range(n // 2)]
    far2 = spread(p2)
    ga, gb, _ = lax.optimization_barrier((ga, gb, keep))
    got = swap(send, 1)
    p2 = [add16(keep[k], got[k]) for k in range(n // 2)]
    far2 = spread(p2)
    own1 = jnp.concatenate([add16(ka, ga)[0], add16(kb, gb)[0]], axis=0)
    m1, o1, x1 = rep_half(own1)
    z1 = add16(m1, after(o1, *p2[1:]))
    tg = back(tok, after(step, z1, *p2[1:]), vec, [w], g, gx1)
    own2 = total(p2[0], [after(a, tg) for a in far2])
    m2, o2, x2 = rep_half(own2)
    steps = rep_steps()
    z2 = None if steps else add16(m2, o2)
    for b in steps:
        z1 = add16(z1, after(rep_perm(z1, b), x2))
        if z2 is None:
            z2 = add16(m2, after(o2, z1))
        pz = rep_perm(z2, b)
        z2 = add16(z2, after(pz, z1))
    o1, o2 = rep_perm(z1, 1), rep_perm(z2, 1)
    ids = jnp.stack([me, (lax.axis_index("rep") % 2).astype(jnp.int32)])
    g_down, g_up, g_out, g_upb, g_ob, g_g2, g_b2, g_db = finish_rest(ids, z1, o1, r, rf, nc, n)
    g_qkv, g_g1, g_b1, g_q, g_v = finish_first(ids, z2, after(o2, g_out), qkv_weight, ln1_gain, ln1_bias)
    flat = lambda a: a.reshape(-1)
    return (out[None], tg[None], flat(g_g1), flat(g_b1), g_qkv, flat(g_q), flat(g_v), g_out, flat(g_ob), flat(g_g2), flat(g_b2), g_up, flat(g_upb), g_down, flat(g_db))


def solution(mesh):
    from jax.sharding import PartitionSpec as P

    in_specs = (
        P(("rep", "shard"), None, None),
        P(("rep", "shard"), None),
        P(("rep", "shard")),
        P(("rep", "shard"), None, None),
        P("shard"),
        P("shard"),
        P("shard", None),
        P("shard"),
        P("shard"),
        P("shard", None),
        P("shard"),
        P("shard"),
        P("shard"),
        P("shard", None),
        P("shard"),
        P("shard", None),
        P("shard"),
    )
    out_specs = (
        P(("rep", "shard"), None, None),
        P(("rep", "shard"), None, None),
        P("shard"),
        P("shard"),
        P("shard", None),
        P("shard"),
        P("shard"),
        P("shard", None),
        P("shard"),
        P("shard"),
        P("shard"),
        P("shard", None),
        P("shard"),
        P("shard", None),
        P("shard"),
    )
    return jax.shard_map(shards, mesh=mesh, in_specs=in_specs, out_specs=out_specs, check_vma=False)
```

```python
import functools, math
import jax, jax.numpy as jnp
from jax import lax
from jax.experimental import pallas as pl
from jax.experimental.pallas import tpu as pltpu

f32 = jnp.float32
bf16 = jnp.bfloat16
EPS = 1e-05
HEADS = 8

def dot(a, b):
    return jnp.dot(a, b, preferred_element_type=f32)

def dot_t(a, b):
    return lax.dot_general(a, b, (((1,), (1,)), ((), ())), preferred_element_type=f32)

def cp(mib=60):
    return pltpu.CompilerParams(dimension_semantics=("arbitrary",), vmem_limit_bytes=mib << 20)

def norm(x):
    c = x - jnp.mean(x, axis=-1, keepdims=True)
    r = lax.rsqrt(jnp.mean(c * c, axis=-1, keepdims=True) + EPS)
    return c * r, r

def row(v, i):
    return v[i : i + 1, :].astype(f32)


VROWS = 16
LANES = 128


def xor_perm(n, k):
    return [(i, i ^ k) for i in range(n)]


def rep_perm(x, b):
    return lax.ppermute(x, "rep", xor_perm(lax.axis_size("rep"), b))


def swap(x, k):
    return lax.ppermute(x, "shard", xor_perm(lax.axis_size("shard"), k))


def after(x, *deps):
    return lax.optimization_barrier((x,) + deps)[0]


def gather_direct(x, n, *gate):
    out = [(0, 0, x)]
    far = [(k, swap(x, k)) for k in range(2, n, 2)]
    out += [(k, 0, after(y, *gate) if gate else y) for k, y in far]
    return out + [(k ^ 1, 0, swap(y, 1)) for k, _, y in out]


def add16(a, b):
    return a + b


def spread(parts):
    return [swap(parts[k], 2 * k) for k in range(len(parts) - 1, 0, -1)]


def total(own, got):
    t = own.astype(f32)
    for a in got:
        t = t + a.astype(f32)
    return t.astype(bf16)


def rep_half(x):
    h = x.shape[0] // 2
    odd = lax.axis_index("rep") % 2
    mine = lax.dynamic_slice_in_dim(x, odd * h, h, 0)
    other = lax.dynamic_slice_in_dim(x, (1 - odd) * h, h, 0)
    return mine, rep_perm(other, 1), other


def rep_steps():
    nr = lax.axis_size("rep")
    return [b for b in (2 << i for i in range(16)) if b < nr]


GROUPS = 1


def pack_first_body(me, w, upb, *refs):
    vecs = refs[:-GROUPS]
    outs = refs[-GROUPS:]
    r, W = w.shape
    D = W // 3
    gw = D // GROUPS
    for g, out in enumerate(outs):
        for j in range(3):
            out[j * r : (j + 1) * r, :] = w[:, j * D + g * gw : j * D + (g + 1) * gw]

    def spot(v):
        w_ = v.shape[1]
        if w_ >= LANES:
            return [v[q : q + 1, :] for q in range(v.shape[0])]
        t = LANES // w_
        lane = lax.broadcasted_iota(jnp.int32, (1, LANES), 1)
        return [jnp.where(lane // w_ == me[0] % t, jnp.concatenate([v] * t, axis=1), jnp.zeros((1, LANES), f32))]

    rows = [a for v in vecs for a in spot(v[...].astype(f32))] + spot(upb[...].astype(f32))
    b = jnp.concatenate(rows + [jnp.zeros((VROWS - len(rows), LANES), f32)], axis=0).astype(bf16)
    outs[0][3 * r :, :] = jnp.concatenate([b, jnp.zeros((VROWS, gw - LANES), bf16)], axis=1) if gw > LANES else b


def whole(n):
    return [pl.BlockSpec(memory_space=pltpu.VMEM)] * n


def once(*arrays):
    return [pl.BlockSpec(a.shape, lambda i, *m, nd=len(a.shape): (0,) * nd) for a in arrays]


def pack_first(me, w, vecs, upb):
    r, W = w.shape
    gw = W // 3 // GROUPS
    lanes = lambda v: v.reshape(-1, min(LANES, v.shape[0]))
    args = [w] + [lanes(v) for v in [upb] + vecs]
    outs = [S((3 * r + (VROWS if g == 0 else 0), gw), bf16) for g in range(GROUPS)]
    return pl.pallas_call(
        pack_first_body,
        grid_spec=pltpu.PrefetchScalarGridSpec(num_scalar_prefetch=1, grid=(1,), in_specs=once(*args), out_specs=once(*outs)),
        out_shape=outs, compiler_params=cp(), name="pack_first", cost_estimate=cost(0, 4 * w.size),
    )(me, *args)


def pack_rest_body(wo, wu, wd, out):
    r, D = wo.shape
    out[:r, :] = wo[...]
    for j in range(wu.shape[1] // D):
        out[(1 + j) * r : (2 + j) * r, :] = wu[:, j * D : (j + 1) * D]
    out[(1 + wu.shape[1] // D) * r :, :] = wd[...]


def pack_rest(wo, wu, wd):
    D = wo.shape[1]
    out = S(((wo.size + wu.size + wd.size) // D, D), bf16)
    return pl.pallas_call(
        pack_rest_body, grid=(1,), in_specs=once(wo, wu, wd), out_specs=once(out)[0],
        out_shape=out, compiler_params=cp(), name="pack_rest", cost_estimate=cost(0, 4 * wu.size),
    )(wo, wu, wd)


def own_lanes(tiles, me, w):
    pick = lambda i: sum(jnp.where(i == t, a, jnp.zeros_like(a)) for t, a in enumerate(tiles))
    if w >= LANES:
        q = w // LANES
        return jnp.concatenate([pick(me * q + c) for c in range(q)], axis=1)
    per = LANES // w
    x = pick(me // per)
    off = me % per
    return sum(jnp.where(off == o, x[:, o * w : (o + 1) * w], 0.0) for o in range(per))


def rows_of(lo, hi, a, b):
    h = lo.shape[0]
    if b <= h:
        return lo[a:b, :]
    if a >= h:
        return hi[a - h : b - h, :]
    return jnp.concatenate([lo[a:h, :], hi[: b - h, :]], axis=0)


def finish_rest_body(r, rf, n, ids, s, o, down, up, out, upb, *vecs):
    D = out.shape[1]
    nf = up.shape[1] // D

    def run(lo, hi):
        f = lambda a, b: rows_of(lo, hi, a, b).astype(f32)
        down[...] = f(0, rf)
        out[...] = f(rf, rf + r)
        for j in range(nf):
            up[:, j * D : (j + 1) * D] = f(rf + (j + 1) * r, rf + (j + 2) * r)
        b = rf + (nf + 1) * r
        v = f(b, b + VROWS)
        me = ids[0]
        tiles = [v[0:8, t * LANES : (t + 1) * LANES] for t in range(D // LANES)]
        x = own_lanes(tiles, me, r)
        for q, ref in enumerate(vecs):
            ref[...] = x[q : q + 1, :]
        tiles = [v[4 + q : 5 + q, t * LANES : (t + 1) * LANES] for q in range(nf) for t in range(D // LANES)]
        upb[...] = own_lanes(tiles, me, nf * D // n)

    @pl.when(ids[1] == 0)
    def _():
        run(s, o)

    @pl.when(ids[1] == 1)
    def _():
        run(o, s)


def finish_rest(ids, s, o, r, rf, nf, n):
    D = s.shape[1]
    row1 = lambda w: S((1, w), f32)
    return pl.pallas_call(
        functools.partial(finish_rest_body, r, rf, n),
        in_specs=[pl.BlockSpec(memory_space=pltpu.SMEM)] + whole(2), out_specs=whole(8),
        out_shape=[S((rf, D), f32), S((r, nf * D), f32), S((r, D), f32), row1(nf * D // n)] + [row1(r)] * 4,
        compiler_params=pltpu.CompilerParams(vmem_limit_bytes=16 << 20), name="finish_rest", cost_estimate=cost(0, 8 * s.size),
    )(ids, s, o)


def finish_first_body(ids, s, o, w, gain, bias, qkv, gg, gb, qb, vb):
    r, W = w.shape
    D = s.shape[1]

    def run(lo, hi):
        f = lambda a, b: rows_of(lo, hi, a, b).astype(f32)
        v = f(3 * r, 3 * r + VROWS)
        nt = D // LANES
        accg = accb = jnp.zeros((r, LANES), f32)
        col = lambda g: jnp.concatenate([g[...].astype(f32), jnp.zeros((7, r), f32)], axis=0).T[:, 0:1]
        cg, cb = col(gain), col(bias)
        for j in range(3):
            m = f(j * r, (j + 1) * r)
            sq = v[j : j + 1, :]
            ww = w[:, j * D : (j + 1) * D].astype(f32)
            qkv[:, j * D : (j + 1) * D] = cg * m + cb * sq
            pg, pb = ww * m, ww * sq
            accg = accg + sum(pg[:, t * LANES : (t + 1) * LANES] for t in range(nt))
            accb = accb + sum(pb[:, t * LANES : (t + 1) * LANES] for t in range(nt))
        gg[...] = jnp.sum(accg.T, axis=0, keepdims=True)
        gb[...] = jnp.sum(accb.T, axis=0, keepdims=True)
        x = own_lanes([v[0:8, t * LANES : (t + 1) * LANES] for t in range(nt)], ids[0], r)
        qb[...] = x[0:1, :]
        vb[...] = x[2:3, :]

    @pl.when(ids[1] == 0)
    def _():
        run(s, o)

    @pl.when(ids[1] == 1)
    def _():
        run(o, s)


def finish_first(ids, s, o, w, gain, bias):
    r, W = w.shape
    return pl.pallas_call(
        finish_first_body,
        in_specs=[pl.BlockSpec(memory_space=pltpu.SMEM)] + whole(5), out_specs=whole(5),
        out_shape=[S((r, W), f32)] + [S((1, r), f32)] * 4,
        compiler_params=pltpu.CompilerParams(vmem_limit_bytes=16 << 20), name="finish_first", cost_estimate=cost(0, 8 * w.size),
    )(ids, s, o, w, gain[None], bias[None])


def pull(me, refs, meta, segs, sems):
    copies = []
    for ref, (k, r0) in zip(refs, meta):
        s = jnp.bitwise_xor(me, k)
        r1 = r0 + ref.shape[0]
        for a, c, dst, lanes in segs:
            lo, hi = max(a, r0), min(a + c, r1)
            if lo < hi:
                src = ref.at[pl.ds(lo - r0, hi - lo), pl.ds(0, lanes)]
                copies.append(pltpu.make_async_copy(src, dst(s, lo - a, hi - lo), sems.at[len(copies)]))
    return copies


def mult(x, m):
    return pl.multiple_of(x, m)


def weight_segs(w, r):
    gw = w.shape[1] // 3
    seg = lambda j: (j * r, r, lambda s, o, c: w.at[pl.ds(mult(s * r + o, 16), c), pl.ds(j * gw, gw)], gw)
    return [seg(j) for j in range(3)]


def start_body(tok, step, nx, xht):
    n, _ = norm(tok[...].astype(f32) + step[...].astype(f32))
    D = tok.shape[1]
    nx[...] = n
    xht[:D, :] = n.astype(bf16).T
    xht[D:, :] = jnp.ones((16, tok.shape[0]), bf16)


def start(tok, step, bm=256):
    T, D = tok.shape
    rows = pl.BlockSpec((bm, D), lambda i: (i, 0))
    return pl.pallas_call(
        start_body, grid=(T // bm,),
        in_specs=[rows, pl.BlockSpec((1, D), lambda i: (0, 0))], out_specs=[rows, pl.BlockSpec((D + 16, bm), lambda i: (0, i))],
        out_shape=[S((T, D), f32), S((D + 16, T), bf16)], compiler_params=cp(), name="start", cost_estimate=cost(20 * T * D, 8 * T * D),
    )(tok, step)


def front_body(scale, n, meta, me, nx, *refs):
    np_ = len(meta)
    pieces = refs[:np_]
    kv, qkvt, wout, vec, upb, nv, h, w, vbuf, sems, own = refs[np_:]
    T, D = nv.shape
    r = D // n
    FF = upb.shape[1]
    i = pl.program_id(0)
    cw = kv.shape[2]
    per_j = D // cw
    segs = [(3 * r, VROWS, lambda s, o, c: vbuf.at[s, pl.ds(o, c)], LANES)] + weight_segs(w, r)
    load = pltpu.make_async_copy(nx, nv, own.at[0])
    save = pltpu.make_async_copy(w, wout, own.at[1])

    @pl.when(i == 0)
    def _():
        cs = pull(me[0], pieces, meta, segs, sems)
        for c in cs:
            c.start()
        load.start()
        for c in cs:
            c.wait()
        save.start()
        per = LANES // r
        tiles = [sum(vbuf[s, 0:8, :].astype(f32) for s in range(t * per, (t + 1) * per)) for t in range(D // LANES)]
        vec[...] = jnp.concatenate(tiles, axis=1)
        wu = FF // n
        if wu >= LANES:
            rows = [vbuf[s, 8 + q : 9 + q, :].astype(f32) for s in range(n) for q in range(wu // LANES)]
        else:
            per = LANES // wu
            rows = [sum(vbuf[s, 8:9, :].astype(f32) for s in range(t * per, (t + 1) * per)) for t in range(FF // LANES)]
        upb[...] = jnp.concatenate(rows, axis=1)
        load.wait()
        v = vec[...]
        h[...] = (nv[...] * row(v, 0) + row(v, 1)).astype(bf16)

    cols = pl.ds(mult(i * cw, 128), cw)
    y = dot(h[...], w[:, cols])
    here = pl.ds(mult((i % per_j) * cw, 128), cw)
    kind = i // per_j
    y = (y + jnp.where(kind == 0, vec[2:3, here], jnp.where(kind == 2, vec[3:4, here], 0.0))).astype(bf16)
    kv[0] = y
    qkvt[0] = jnp.where(kind == 0, y * bf16(scale), y).T

    @pl.when(i == pl.num_programs(0) - 1)
    def _():
        save.wait()


S = jax.ShapeDtypeStruct
ANY = pl.BlockSpec(memory_space=pl.ANY)


def cost(flops, nbytes, tr=0):
    return pl.CostEstimate(flops=int(flops), bytes_accessed=int(nbytes), transcendentals=int(tr))


def front(me, nx, pieces, n, FF, cw=512):
    T, D = nx.shape
    scale = 1.0 / math.sqrt(D // HEADS)
    meta = tuple((k, r0) for k, r0, _ in pieces)
    q = D // cw
    keep = lambda *sh: pl.BlockSpec(sh, lambda i, m: (0,) * len(sh))
    rest = lambda i: jnp.maximum(i - q, 0)
    V = pltpu.VMEM
    return pl.pallas_call(
        functools.partial(front_body, scale, n, meta),
        grid_spec=pltpu.PrefetchScalarGridSpec(
            num_scalar_prefetch=1, grid=(3 * q,),
            in_specs=[ANY] * (1 + len(pieces)),
            out_specs=[pl.BlockSpec((1, T, cw), lambda i, m: (rest(i) // q, 0, rest(i) % q)), pl.BlockSpec((1, cw, T), lambda i, m: (i // q, i % q, 0)), ANY, keep(8, D), keep(1, FF)],
            scratch_shapes=[V((T, D), f32), V((T, D), bf16), V((D, 3 * D), bf16), V((n, VROWS, LANES), bf16), pltpu.SemaphoreType.DMA((8 * len(pieces),)), pltpu.SemaphoreType.DMA((2,))]),
        out_shape=[S((2, T, D), bf16), S((3, D, T), bf16), S((D, 3 * D), bf16), S((8, D), f32), S((1, FF), f32)],
        compiler_params=cp(), name="front", cost_estimate=cost(6 * T * D * D, 12 * T * D),
    )(me, nx, *[a for _, _, a in pieces])


def attn_fwd_body(HD, bi, CR, p0, ln, k, qt, vt, *refs):
    et, mixed, mixedt, mixedf, linv, scr, ka, eb, esem = refs[-9:]
    T, PW = k.shape
    n = ln[0]
    p = pl.program_id(0)
    last = p == pl.num_programs(0) - 1
    rid = lax.broadcasted_iota(jnp.int32, (PW, bi), 0)
    lane = lax.broadcasted_iota(jnp.int32, (T, PW), 1)
    rows = lax.broadcasted_iota(jnp.int32, (T, PW), 0)
    ka[:, :PW] = k[...]
    ka[:, PW:] = jnp.where((lane == 0) & (rows >= n), f32(-1e30), f32(0)).astype(bf16)
    ones = jnp.where(rid == 0, f32(1), f32(0)).astype(bf16)
    va = [jnp.concatenate([vt[h * HD : (h + 1) * HD, :], jnp.ones((16, T), bf16)], axis=0) for h in range(2)]
    tasks = [(b, h) for b in range(T // bi) for h in range(2)]
    nch = T // CR

    def query(t):
        b, h = tasks[t]
        q = qt[:, b * bi : (b + 1) * bi]
        return jnp.concatenate([jnp.where(rid // HD == h, q, jnp.zeros_like(q)), ones], axis=0)

    def score(t, c, q):
        s = dot(ka[c * CR : (c + 1) * CR, :], q)
        scr[t % 2, c * CR : (c + 1) * CR, :] = s
        return jnp.max(s, axis=0, keepdims=True)

    q = query(0)
    m = functools.reduce(jnp.maximum, [score(0, c, q) for c in range(nch)])
    half = None
    for t, (b, h) in enumerate(tasks):
        sl = slice(b * bi, (b + 1) * bi)
        more = t + 1 < len(tasks)
        put = pltpu.make_async_copy(eb.at[t % 2], et.at[2 * (p0 + p) + h, :, pl.ds(b * bi, bi)], esem.at[t % 2])
        if t < 2:

            @pl.when(p > 0)
            def _():
                put.wait()

        else:
            put.wait()
        if more:
            q = query(t + 1)
        nxt = []
        for c in range(nch):
            cs = slice(c * CR, (c + 1) * CR)
            if more:
                nxt.append(score(t + 1, c, q))
            eb[t % 2, cs, :] = jnp.exp(scr[t % 2, cs, :] - m).astype(bf16)
        put.start()
        o = dot(va[h], eb[t % 2])
        if more:
            m = functools.reduce(jnp.maximum, nxt)
        inv = 1.0 / o[HD : HD + 1, :]
        linv[h : h + 1, sl] = inv
        o = o[:HD, :] * inv
        if h == 0:
            half = o
        else:
            mt = jnp.concatenate([half, o], axis=0)
            mixedf[:, sl] = mt
            mt = mt.astype(bf16)
            mixedt[:, sl] = mt
            mixed[sl, :] = mt.T

    @pl.when(last)
    def _():
        for q in range(2):
            pltpu.make_async_copy(eb.at[q], et.at[0, :, pl.ds(0, bi)], esem.at[q]).wait()


def attn_fwd(ln, kv, qkvt, p0, cnt, prev):
    _, T, D = kv.shape
    HD = D // HEADS
    PW = 2 * HD
    NP = D // PW
    bi = T
    prev = list(prev)
    return pl.pallas_call(
        functools.partial(attn_fwd_body, HD, bi, min(512, T), p0),
        grid_spec=pltpu.PrefetchScalarGridSpec(
            num_scalar_prefetch=1, grid=(cnt,),
            in_specs=[pl.BlockSpec((None, T, PW), lambda p, r: (0, 0, p0 + p)), pl.BlockSpec((None, PW, T), lambda p, r: (0, p0 + p, 0)), pl.BlockSpec((None, PW, T), lambda p, r: (2, p0 + p, 0))] + [ANY] * len(prev),
            out_specs=[ANY, pl.BlockSpec((T, PW), lambda p, r: (0, p0 + p)), pl.BlockSpec((PW, T), lambda p, r: (p0 + p, 0)), pl.BlockSpec((PW, T), lambda p, r: (p0 + p, 0)), pl.BlockSpec((None, 8, T), lambda p, r: (p0 + p, 0, 0))],
            scratch_shapes=[pltpu.VMEM((2, T, bi), f32), pltpu.VMEM((T, 2 * PW), bf16), pltpu.VMEM((2, T, bi), bf16), pltpu.SemaphoreType.DMA((2,))]),
        out_shape=[S((HEADS, T, T), bf16), S((T, D), bf16), S((D, T), bf16), S((D, T), f32), S((NP, 8, T), f32)],
        input_output_aliases={4 + i: i for i in range(len(prev))},
        compiler_params=cp(), name="attn_fwd", cost_estimate=cost(cnt * 2 * 8 * T * T * 128, cnt * 2 * T * T * 2, cnt * 2 * T * T),
    )(ln, kv, qkvt, qkvt, *prev)


G0 = math.sqrt(2 / math.pi)


def bit_reverse(x, m):
    y = jnp.zeros_like(x)
    for t in range(m):
        y = y | (((x >> t) & 1) << (m - 1 - t))
    return y


def push(me, n, s, src, keep, send, row0, sem, reverse=False):
    k = jnp.bitwise_xor(me, s)
    p = k >> 1
    if reverse:
        p = bit_reverse(p, (n // 2).bit_length() - 1)
    put = lambda dst: pltpu.make_async_copy(src, dst.at[p, pl.ds(row0, src.shape[0])], sem)

    @pl.when(k & 1 == 0)
    def _():
        put(keep).start()

    @pl.when(k & 1 == 1)
    def _():
        put(send).start()


def ffn_body(n, meta, ch, ln, me, tok, step, vec, upb, cot, mixed, mixedt, *refs):
    np_ = len(meta)
    pieces = refs[:np_]
    out, gx1, gmt, keep, send, wo, wu, wd, act, gup, h2t, gdt, gattn, sums, upsum, dn, up, gwo, vr, mtv, sems, psems = refs[np_:]
    i = pl.program_id(0)
    bm, D = tok.shape
    FF = wu.shape[1]
    r = D // n
    rf = FF // n
    nf = FF // D
    i0 = me[0]
    ro = pl.ds(mult(i * bm, 128), bm)
    first = i == 0
    seg = lambda j: (r + j * r, r, lambda s, o, c: wu.at[pl.ds(mult(s * r + o, 16), c), pl.ds(j * D, D)], D)
    seg_o = [(0, r, lambda s, o, c: wo.at[pl.ds(mult(s * r + o, 16), c)], D)]
    seg_u = [seg(j) for j in range(nf)]
    seg_d = [(r + r * nf, rf, lambda s, o, c: wd.at[pl.ds(mult(s * rf + o, 16), c)], D)]
    q = sems.shape[0] // 4
    parts = [(seg_o, sems.at[pl.ds(0, q)]), (seg_d, sems.at[pl.ds(q, q)]), (seg_u, sems.at[pl.ds(2 * q, 2 * q)])]
    load = pltpu.make_async_copy(mixedt, mtv, psems.at[psems.shape[0] - 1])

    @pl.when(first)
    def _():
        for sg, sm in parts:
            for c in pull(i0, pieces, meta, sg, sm):
                c.start()
        load.start()
        sums[...] = jnp.zeros_like(sums)
        upsum[...] = jnp.zeros_like(upsum)
        for c in pull(i0, pieces, meta, *parts[0]):
            c.wait()

    v = vec[...]
    x1 = tok[...].astype(f32) + step[...].astype(f32) + dot(mixed[...], wo[...]) + row(v, 4)
    nx, rr = norm(x1)
    h2 = (nx * row(v, 5) + row(v, 6)).astype(bf16)
    live = (lax.broadcasted_iota(jnp.int32, (bm, 1), 0) + i * bm) < ln[0]
    gd = jnp.where(live, cot[...], jnp.zeros_like(cot))
    acc = x1 + row(v, 7)
    gh = None
    nc = FF // ch
    sl = [slice(c * ch, (c + 1) * ch) for c in range(nc)]
    lead = lambda c: (dot(h2, wu[:, sl[c]]), dot_t(gd, wd[sl[c], :]))
    h2t[:, ro] = h2.T
    gdt[:, ro] = gd.T

    @pl.when(first)
    def _():
        for sg, sm in parts[1:]:
            for c in pull(i0, pieces, meta, sg, sm):
                c.wait()

    nxt = lead(0)
    for c in range(nc):
        u, ga = nxt
        nxt = lead(c + 1) if c + 1 < nc else None
        u = u + upb[:, sl[c]]
        u2 = u * u
        t = jnp.tanh(u * (f32(G0) + f32(G0 * 0.044715) * u2))
        half = 0.5 + 0.5 * t
        a = (u * half).astype(bf16)
        act[ro, sl[c]] = a
        dg = half + u * (half * (1.0 - half)) * (f32(2 * G0) + f32(6 * 0.044715 * G0) * u2)
        gu = (ga * dg).astype(bf16)
        gup[ro, sl[c]] = gu
        upsum[:, sl[c]] += jnp.sum(gu.astype(f32), axis=0, keepdims=True)
        acc = acc + dot(a, wd[sl[c], :])
        p = dot_t(gu, wu[:, sl[c]])
        gh = p if gh is None else gh + p
    out[...] = jnp.where(live, acc, 0.0).astype(bf16)
    gn = gh * row(v, 5)
    gx = gd.astype(f32) + rr * (gn - jnp.mean(gn, axis=-1, keepdims=True) - nx * jnp.mean(gn * nx, axis=-1, keepdims=True))
    gab = gx.astype(bf16)
    gx1[...] = gab
    gattn[ro, :] = gab
    gmt[...] = dot_t(gab, wo[...]).astype(bf16).T
    s_ = lambda a: jnp.sum(a.astype(f32), axis=0, keepdims=True)
    sums[...] += jnp.concatenate([s_(gab), s_(gh * nx), s_(gh), s_(gd), jnp.zeros((4, D), f32)], axis=0)

    @pl.when(i == pl.num_programs(0) - 1)
    def _():
        per = D // rf
        o_out, o_up, o_vec = rf, rf + r, rf + (nf + 1) * r
        for j in range(nf):
            dn[j] = dot(gdt[...], act[:, j * D : (j + 1) * D]).astype(bf16).T
            for t in range(per):
                push(i0, n, j * per + t, dn.at[j, pl.ds(t * rf, rf)], keep, send, 0, psems.at[j * per + t])
            up[j] = dot(h2t[...], gup[:, j * D : (j + 1) * D]).astype(bf16)
            for s in range(n):
                push(i0, n, s, up.at[j, pl.ds(s * r, r)], keep, send, o_up + j * r, psems.at[n * (1 + j) + s], True)
        load.wait()
        gwo[...] = dot(mtv[...], gattn[...]).astype(bf16)
        vr[...] = jnp.concatenate([sums[0:4, :]] + [upsum[:, c * D : (c + 1) * D] for c in range(nf)] + [jnp.zeros((VROWS - 4 - nf, D), f32)], axis=0).astype(bf16)
        b = n * (1 + nf)
        for s in range(n):
            push(i0, n, s, gwo.at[pl.ds(s * r, r)], keep, send, o_out, psems.at[b + s])
            push(i0, n, s, vr, keep, send, o_vec, psems.at[b + n + s], True)
        done = lambda src, q: pltpu.make_async_copy(src, keep.at[0, pl.ds(0, src.shape[0])], psems.at[q]).wait()
        for s in range(n):
            done(dn.at[0, pl.ds(0, rf)], s)
            for c in range(nf):
                done(up.at[0, pl.ds(0, r)], n * (1 + c) + s)
            done(gwo.at[pl.ds(0, r)], b + s)
            done(vr, b + n + s)


def ffn(ln, me, tok, step, vec, upb, cot, mixed, mixedt, pieces, n):
    T, D = tok.shape
    FF = upb.shape[1]
    bm = min(512, T)
    nf = FF // D
    r = D // n
    meta = tuple((k, r0) for k, r0, _ in pieces)
    full = lambda a: pl.BlockSpec(a.shape, lambda i, l, m: (0,) * a.ndim)
    rows = pl.BlockSpec((bm, D), lambda i, l, m: (i, 0))
    B = S((n // 2, FF // n + (nf + 1) * r + VROWS, D), bf16)
    V = pltpu.VMEM
    return pl.pallas_call(
        functools.partial(ffn_body, n, meta, min(1024, FF)),
        grid_spec=pltpu.PrefetchScalarGridSpec(
            num_scalar_prefetch=2, grid=(T // bm,),
            in_specs=[rows, full(step), full(vec), full(upb), rows, rows, ANY] + [ANY] * len(pieces),
            out_specs=[rows, rows, pl.BlockSpec((D, bm), lambda i, l, m: (0, i)), ANY, ANY],
            scratch_shapes=[V((D, D), bf16), V((D, FF), bf16), V((FF, D), bf16), V((T, FF), bf16), V((T, FF), bf16), V((D, T), bf16), V((D, T), bf16), V((T, D), bf16), V((8, D), f32), V((1, FF), f32), V((nf, D, D), bf16), V((nf, D, D), bf16), V((D, D), bf16), V((VROWS, D), bf16), V((D, T), bf16), pltpu.SemaphoreType.DMA((16 * len(pieces),)), pltpu.SemaphoreType.DMA((n * (nf + 3) + 1,))]),
        out_shape=[S((T, D), bf16), S((T, D), bf16), S((D, T), bf16), B, B],
        compiler_params=cp(49), name="ffn", cost_estimate=cost(2 * T * D * (6 * FF + 3 * D), 16 * T * D, T * FF),
    )(ln, me, tok, step, vec, upb, cot, mixed, mixedt, *[a for _, _, a in pieces])


def attn_bwd_body(HD, scale, CR, v, kt, qt, gt, mt, linv, et, *refs):
    gq, ds = refs[-2:]
    T = v.shape[0]
    rid = lax.broadcasted_iota(jnp.int32, gt.shape, 0) // HD
    g = gt[...].astype(f32)
    q = qt[...]
    gv = gk = None
    for h in range(2):
        hs = slice(h * HD, (h + 1) * HD)
        gs = (g * linv[h : h + 1, :]).astype(bf16)
        gm = jnp.where(rid == h, gs, jnp.zeros_like(gs))
        dl = jnp.sum(gs[hs, :].astype(f32) * mt[hs, :], axis=0, keepdims=True)
        for c in range(T // CR):
            cs = slice(c * CR, (c + 1) * CR)
            ds[h, cs, :] = (et[h, cs, :].astype(f32) * (dot(v[cs, :], gm) - dl)).astype(bf16)
        a = dot(et[h], gm.T)
        b = dot(ds[h], jnp.where(rid == h, q, jnp.zeros_like(q)).T)
        gv = a if gv is None else gv + a
        gk = b if gk is None else gk + b
        gq[0, hs, :] = (dot(kt[hs, :], ds[h]) * scale).astype(bf16)
    gq[2] = gv.astype(bf16).T
    gq[1] = gk.astype(bf16).T


def attn_bwd(kv, qkvt, gmt, mixedf, linv, et, p0, cnt, prev):
    _, T, D = kv.shape
    HD = D // HEADS
    PW = 2 * HD
    NP = D // PW
    prev = list(prev)
    pr = pl.BlockSpec((PW, T), lambda p: (p0 + p, 0))
    of = lambda j: pl.BlockSpec((None, PW, T), lambda p: (j, p0 + p, 0))
    return pl.pallas_call(
        functools.partial(attn_bwd_body, HD, 1.0 / math.sqrt(HD), min(256, T)),
        grid=(cnt,),
        scratch_shapes=[pltpu.VMEM((2, T, T), bf16)],
        in_specs=[pl.BlockSpec((None, T, PW), lambda p: (1, 0, p0 + p)), of(1), of(0), pr, pr, pl.BlockSpec((None, 8, T), lambda p: (p0 + p, 0, 0)), pl.BlockSpec((2, T, T), lambda p: (p0 + p, 0, 0))] + [ANY] * len(prev),
        out_specs=pl.BlockSpec((3, PW, T), lambda p: (0, p0 + p, 0)),
        out_shape=S((3, D, T), bf16),
        input_output_aliases={7: 0} if prev else {},
        compiler_params=cp(), name="attn_bwd", cost_estimate=cost(cnt * 2 * 16 * T * T * 128, cnt * 2 * T * T * 2),
    )(kv, qkvt, qkvt, gmt, mixedf, linv, et, *prev)


def wqkv_body(n, me, xht, g, keep, send, res, vr, sems):
    j = pl.program_id(0)
    D = g.shape[0]
    r = D // n
    i0 = me[0]
    y = dot_t(xht[...], g[...]).astype(bf16)
    res[j] = y[:D]
    vr[...] = jnp.where(lax.broadcasted_iota(jnp.int32, vr.shape, 0) == j, y[D:], jnp.where(j == 0, jnp.zeros_like(y[D:]), vr[...]))
    for s in range(n):
        push(i0, n, s, res.at[j, pl.ds(s * r, r)], keep, send, mult(j * r, 16), sems.at[j * n + s])

    @pl.when(j == 2)
    def _():
        for s in range(n):
            push(i0, n, s, vr, keep, send, 3 * r, sems.at[3 * n + s])
        for s in range(n):
            for q in range(3):
                pltpu.make_async_copy(res.at[0, pl.ds(0, r)], keep.at[0, pl.ds(0, r)], sems.at[q * n + s]).wait()
            pltpu.make_async_copy(vr, keep.at[0, pl.ds(0, VROWS)], sems.at[3 * n + s]).wait()


def wqkv(me, xht, g, n):
    _, D, T = g.shape
    A = S((n // 2, 3 * (D // n) + VROWS, D), bf16)
    return pl.pallas_call(
        functools.partial(wqkv_body, n),
        grid_spec=pltpu.PrefetchScalarGridSpec(
            num_scalar_prefetch=1, grid=(3,),
            in_specs=[pl.BlockSpec((D + 16, T), lambda j, m: (0, 0)), pl.BlockSpec((None, D, T), lambda j, m: (j, 0, 0))],
            out_specs=[ANY] * 2,
            scratch_shapes=[pltpu.VMEM((3, D, D), bf16), pltpu.VMEM((VROWS, D), bf16), pltpu.SemaphoreType.DMA((4 * n,))]),
        out_shape=[A, A],
        compiler_params=cp(), name="wqkv", cost_estimate=cost(6 * T * D * D, 10 * T * D),
    )(me, xht, g)


def back_body(tok, step, vec, g, gx1, *refs):
    ws, tg = refs[:-1], refs[-1]
    D = tok.shape[1]
    gw = D // GROUPS
    x = tok[...].astype(f32) + step[...].astype(f32)
    nx, rr = norm(x)
    gt = sum(dot(w[:, j * gw : (j + 1) * gw], g[j, q * gw : (q + 1) * gw, :]) for q, w in enumerate(ws) for j in range(3))
    gn = gt.T * row(vec[...], 0)
    tg[...] = gx1[...].astype(f32) + rr * (gn - jnp.mean(gn, axis=-1, keepdims=True) - nx * jnp.mean(gn * nx, axis=-1, keepdims=True))


def back(tok, step, vec, ws, g, gx1, bm=512):
    T, D = tok.shape
    full = lambda a: pl.BlockSpec(a.shape, lambda i: (0,) * a.ndim)
    rows = pl.BlockSpec((bm, D), lambda i: (i, 0))
    return pl.pallas_call(
        back_body, grid=(T // bm,),
        in_specs=[rows, full(step), full(vec), pl.BlockSpec((3, D, bm), lambda i: (0, 0, i)), rows] + [full(w) for w in ws],
        out_specs=rows, out_shape=S((T, D), f32), compiler_params=cp(), name="back", cost_estimate=cost(6 * T * D * D, 14 * T * D),
    )(tok, step, vec, g, gx1, *ws)


def shards(tokens, step_embed, lengths, cotangent, ln1_gain, ln1_bias, qkv_weight, q_bias, v_bias, out_weight, out_bias, ln2_gain, ln2_bias, up_weight, up_bias, down_weight, down_bias):
    n = lax.axis_size("shard")
    me = lax.axis_index("shard").astype(jnp.int32)
    mes = me[None]
    tok, cot, step = tokens[0], cotangent[0], step_embed
    T, D = tok.shape
    r = D // n
    FF = up_bias.shape[0] * n
    nc = FF // D
    rf = FF // n
    packs = pack_first(mes, qkv_weight, [ln1_gain, ln1_bias, q_bias, v_bias, out_bias, ln2_gain, ln2_bias, down_bias], up_bias)
    pack2 = pack_rest(out_weight, up_weight, down_weight)
    NP = HEADS // 2
    nx, xht = start(tok, step)
    pieces = gather_direct(packs[0], n, xht, pack2)
    kv, qkvt, w, vec, upb = front(mes, nx, pieces, n, FF)
    et, mixed, mixedt, mixedf, linv = attn_fwd(lengths, kv, qkvt, 0, NP, [])
    pieces2 = gather_direct(after(pack2, xht), n, linv)
    out, gx1, gmt, keep, send = ffn(lengths, mes, tok, step, vec, upb, cot, mixed, mixedt, pieces2, n)
    bwd = lambda p, c, g, *deps: attn_bwd(kv, qkvt, after(gmt, *deps) if deps else gmt, mixedf, linv, et, p, c, g)
    ra = rf + r
    got = swap(send, 1)
    g = bwd(0, 1, [])
    got = after(got, g)
    h = n // 4
    add = lambda a, b, k: add16(a[k], b[k])
    rows_a, rows_b = slice(0, ra), slice(ra, None)
    lo, hi = slice(0, h), slice(h, None)
    ka, xa, kb, xb = [add(keep, got, k) for k in ((lo, rows_a), (hi, rows_a), (lo, rows_b), (hi, rows_b))]
    g = bwd(1, NP - 1, [g], ka, xa, kb, xb)
    m = (n // 2).bit_length() - 1
    ga, gb = swap(xa, 2 << (m - 1)), swap(xb, 2)
    for t in range(1, m):
        dep = g if t == 1 else keep
        ga, gb, _ = lax.optimization_barrier((ga, gb, dep))
        h //= 2
        lo, hi = slice(0, h), slice(h, None)
        ka, xa = add(ka, ga, lo), add(ka, ga, hi)
        kb, xb = add(kb, gb, lo), add(kb, gb, hi)
        ga, gb = swap(xa, 2 << (m - 1 - t)), swap(xb, 2 << t)
        if t == 1:
            keep, send = wqkv(mes, after(xht, ka, xa, kb, xb), g, n)
    got = swap(send, 1)
    p2 = [add16(keep[k], got[k]) for k in range(n // 2)]
    far2 = spread(p2)
    ga, gb, _ = lax.optimization_barrier((ga, gb, keep))
    got = swap(send, 1)
    p2 = [add16(keep[k], got[k]) for k in range(n // 2)]
    far2 = spread(p2)
    own1 = jnp.concatenate([add16(ka, ga)[0], add16(kb, gb)[0]], axis=0)
    m1, o1, x1 = rep_half(own1)
    z1 = add16(m1, after(o1, *p2[1:]))
    tg = back(tok, after(step, z1, *p2[1:]), vec, [w], g, gx1)
    own2 = total(p2[0], [after(a, tg) for a in far2])
    m2, o2, x2 = rep_half(own2)
    steps = rep_steps()
    z2 = None if steps else add16(m2, o2)
    for b in steps:
        z1 = add16(z1, after(rep_perm(z1, b), x2))
        if z2 is None:
            z2 = add16(m2, after(o2, z1))
        pz = rep_perm(z2, b)
        z2 = add16(z2, after(pz, z1))
    o1, o2 = rep_perm(z1, 1), rep_perm(z2, 1)
    ids = jnp.stack([me, (lax.axis_index("rep") % 2).astype(jnp.int32)])
    g_down, g_up, g_out, g_upb, g_ob, g_g2, g_b2, g_db = finish_rest(ids, z1, o1, r, rf, nc, n)
    g_qkv, g_g1, g_b1, g_q, g_v = finish_first(ids, z2, after(o2, g_out), qkv_weight, ln1_gain, ln1_bias)
    flat = lambda a: a.reshape(-1)
    return (out[None], tg[None], flat(g_g1), flat(g_b1), g_qkv, flat(g_q), flat(g_v), g_out, flat(g_ob), flat(g_g2), flat(g_b2), g_up, flat(g_upb), g_down, flat(g_db))


def solution(mesh):
    from jax.sharding import PartitionSpec as P

    in_specs = (
        P(("rep", "shard"), None, None),
        P(("rep", "shard"), None),
        P(("rep", "shard")),
        P(("rep", "shard"), None, None),
        P("shard"),
        P("shard"),
        P("shard", None),
        P("shard"),
        P("shard"),
        P("shard", None),
        P("shard"),
        P("shard"),
        P("shard"),
        P("shard", None),
        P("shard"),
        P("shard", None),
        P("shard"),
    )
    out_specs = (
        P(("rep", "shard"), None, None),
        P(("rep", "shard"), None, None),
        P("shard"),
        P("shard"),
        P("shard", None),
        P("shard"),
        P("shard"),
        P("shard", None),
        P("shard"),
        P("shard"),
        P("shard"),
        P("shard", None),
        P("shard"),
        P("shard", None),
        P("shard"),
    )
    return jax.shard_map(shards, mesh=mesh, in_specs=in_specs, out_specs=out_specs, check_vma=False)
```

```python
import functools, math
import jax, jax.numpy as jnp
from jax import lax
from jax.experimental import pallas as pl
from jax.experimental.pallas import tpu as pltpu

f32 = jnp.float32
bf16 = jnp.bfloat16
EPS = 1e-05
HEADS = 8

def dot(a, b):
    return jnp.dot(a, b, preferred_element_type=f32)

def dot_t(a, b):
    return lax.dot_general(a, b, (((1,), (1,)), ((), ())), preferred_element_type=f32)

def cp(mib=60):
    return pltpu.CompilerParams(dimension_semantics=("arbitrary",), vmem_limit_bytes=mib << 20)

def norm(x):
    c = x - jnp.mean(x, axis=-1, keepdims=True)
    r = lax.rsqrt(jnp.mean(c * c, axis=-1, keepdims=True) + EPS)
    return c * r, r

def row(v, i):
    return v[i : i + 1, :].astype(f32)


VROWS = 16
LANES = 128


def xor_perm(n, k):
    return [(i, i ^ k) for i in range(n)]


def rep_perm(x, b):
    return lax.ppermute(x, "rep", xor_perm(lax.axis_size("rep"), b))


def swap(x, k):
    return lax.ppermute(x, "shard", xor_perm(lax.axis_size("shard"), k))


def after(x, *deps):
    return lax.optimization_barrier((x,) + deps)[0]


def gather_direct(x, n, *gate):
    out = [(0, 0, x)]
    far = [(k, swap(x, k)) for k in range(2, n, 2)]
    out += [(k, 0, after(y, *gate) if gate else y) for k, y in far]
    return out + [(k ^ 1, 0, swap(y, 1)) for k, _, y in out]


def add16(a, b):
    return a + b


def spread(parts):
    return [swap(parts[k], 2 * k) for k in range(len(parts) - 1, 0, -1)]


def total(own, got):
    t = own.astype(f32)
    for a in got:
        t = t + a.astype(f32)
    return t.astype(bf16)


def rep_half(x):
    h = x.shape[0] // 2
    odd = lax.axis_index("rep") % 2
    mine = lax.dynamic_slice_in_dim(x, odd * h, h, 0)
    other = lax.dynamic_slice_in_dim(x, (1 - odd) * h, h, 0)
    return mine, rep_perm(other, 1), other


def rep_steps():
    nr = lax.axis_size("rep")
    return [b for b in (2 << i for i in range(16)) if b < nr]


GROUPS = 1


def pack_first_body(me, w, upb, *refs):
    vecs = refs[:-GROUPS]
    outs = refs[-GROUPS:]
    r, W = w.shape
    D = W // 3
    gw = D // GROUPS
    for g, out in enumerate(outs):
        for j in range(3):
            out[j * r : (j + 1) * r, :] = w[:, j * D + g * gw : j * D + (g + 1) * gw]

    def spot(v):
        w_ = v.shape[1]
        if w_ >= LANES:
            return [v[q : q + 1, :] for q in range(v.shape[0])]
        t = LANES // w_
        lane = lax.broadcasted_iota(jnp.int32, (1, LANES), 1)
        return [jnp.where(lane // w_ == me[0] % t, jnp.concatenate([v] * t, axis=1), jnp.zeros((1, LANES), f32))]

    rows = [a for v in vecs for a in spot(v[...].astype(f32))] + spot(upb[...].astype(f32))
    b = jnp.concatenate(rows + [jnp.zeros((VROWS - len(rows), LANES), f32)], axis=0).astype(bf16)
    outs[0][3 * r :, :] = jnp.concatenate([b, jnp.zeros((VROWS, gw - LANES), bf16)], axis=1) if gw > LANES else b


def whole(n):
    return [pl.BlockSpec(memory_space=pltpu.VMEM)] * n


def once(*arrays):
    return [pl.BlockSpec(a.shape, lambda i, *m, nd=len(a.shape): (0,) * nd) for a in arrays]


def pack_first(me, w, vecs, upb):
    r, W = w.shape
    gw = W // 3 // GROUPS
    lanes = lambda v: v.reshape(-1, min(LANES, v.shape[0]))
    args = [w] + [lanes(v) for v in [upb] + vecs]
    outs = [S((3 * r + (VROWS if g == 0 else 0), gw), bf16) for g in range(GROUPS)]
    return pl.pallas_call(
        pack_first_body,
        grid_spec=pltpu.PrefetchScalarGridSpec(num_scalar_prefetch=1, grid=(1,), in_specs=once(*args), out_specs=once(*outs)),
        out_shape=outs, compiler_params=cp(), name="pack_first", cost_estimate=cost(0, 4 * w.size),
    )(me, *args)


def pack_rest_body(wo, wu, wd, out):
    r, D = wo.shape
    out[:r, :] = wo[...]
    for j in range(wu.shape[1] // D):
        out[(1 + j) * r : (2 + j) * r, :] = wu[:, j * D : (j + 1) * D]
    out[(1 + wu.shape[1] // D) * r :, :] = wd[...]


def pack_rest(wo, wu, wd):
    D = wo.shape[1]
    out = S(((wo.size + wu.size + wd.size) // D, D), bf16)
    return pl.pallas_call(
        pack_rest_body, grid=(1,), in_specs=once(wo, wu, wd), out_specs=once(out)[0],
        out_shape=out, compiler_params=cp(), name="pack_rest", cost_estimate=cost(0, 4 * wu.size),
    )(wo, wu, wd)


def own_lanes(tiles, me, w):
    pick = lambda i: sum(jnp.where(i == t, a, jnp.zeros_like(a)) for t, a in enumerate(tiles))
    if w >= LANES:
        q = w // LANES
        return jnp.concatenate([pick(me * q + c) for c in range(q)], axis=1)
    per = LANES // w
    x = pick(me // per)
    off = me % per
    return sum(jnp.where(off == o, x[:, o * w : (o + 1) * w], 0.0) for o in range(per))


def rows_of(lo, hi, a, b):
    h = lo.shape[0]
    if b <= h:
        return lo[a:b, :]
    if a >= h:
        return hi[a - h : b - h, :]
    return jnp.concatenate([lo[a:h, :], hi[: b - h, :]], axis=0)


def finish_rest_body(r, rf, n, ids, s, o, down, up, out, upb, *vecs):
    D = out.shape[1]
    nf = up.shape[1] // D

    def run(lo, hi):
        f = lambda a, b: rows_of(lo, hi, a, b).astype(f32)
        down[...] = f(0, rf)
        out[...] = f(rf, rf + r)
        for j in range(nf):
            up[:, j * D : (j + 1) * D] = f(rf + (j + 1) * r, rf + (j + 2) * r)
        b = rf + (nf + 1) * r
        v = f(b, b + VROWS)
        me = ids[0]
        tiles = [v[0:8, t * LANES : (t + 1) * LANES] for t in range(D // LANES)]
        x = own_lanes(tiles, me, r)
        for q, ref in enumerate(vecs):
            ref[...] = x[q : q + 1, :]
        tiles = [v[4 + q : 5 + q, t * LANES : (t + 1) * LANES] for q in range(nf) for t in range(D // LANES)]
        upb[...] = own_lanes(tiles, me, nf * D // n)

    @pl.when(ids[1] == 0)
    def _():
        run(s, o)

    @pl.when(ids[1] == 1)
    def _():
        run(o, s)


def finish_rest(ids, s, o, r, rf, nf, n):
    D = s.shape[1]
    row1 = lambda w: S((1, w), f32)
    return pl.pallas_call(
        functools.partial(finish_rest_body, r, rf, n),
        in_specs=[pl.BlockSpec(memory_space=pltpu.SMEM)] + whole(2), out_specs=whole(8),
        out_shape=[S((rf, D), f32), S((r, nf * D), f32), S((r, D), f32), row1(nf * D // n)] + [row1(r)] * 4,
        compiler_params=pltpu.CompilerParams(vmem_limit_bytes=16 << 20), name="finish_rest", cost_estimate=cost(0, 8 * s.size),
    )(ids, s, o)


def finish_first_body(ids, s, o, w, gain, bias, qkv, gg, gb, qb, vb):
    r, W = w.shape
    D = s.shape[1]

    def run(lo, hi):
        f = lambda a, b: rows_of(lo, hi, a, b).astype(f32)
        v = f(3 * r, 3 * r + VROWS)
        nt = D // LANES
        accg = accb = jnp.zeros((r, LANES), f32)
        col = lambda g: jnp.concatenate([g[...].astype(f32), jnp.zeros((7, r), f32)], axis=0).T[:, 0:1]
        cg, cb = col(gain), col(bias)
        for j in range(3):
            m = f(j * r, (j + 1) * r)
            sq = v[j : j + 1, :]
            ww = w[:, j * D : (j + 1) * D].astype(f32)
            qkv[:, j * D : (j + 1) * D] = cg * m + cb * sq
            pg, pb = ww * m, ww * sq
            accg = accg + sum(pg[:, t * LANES : (t + 1) * LANES] for t in range(nt))
            accb = accb + sum(pb[:, t * LANES : (t + 1) * LANES] for t in range(nt))
        gg[...] = jnp.sum(accg.T, axis=0, keepdims=True)
        gb[...] = jnp.sum(accb.T, axis=0, keepdims=True)
        x = own_lanes([v[0:8, t * LANES : (t + 1) * LANES] for t in range(nt)], ids[0], r)
        qb[...] = x[0:1, :]
        vb[...] = x[2:3, :]

    @pl.when(ids[1] == 0)
    def _():
        run(s, o)

    @pl.when(ids[1] == 1)
    def _():
        run(o, s)


def finish_first(ids, s, o, w, gain, bias):
    r, W = w.shape
    return pl.pallas_call(
        finish_first_body,
        in_specs=[pl.BlockSpec(memory_space=pltpu.SMEM)] + whole(5), out_specs=whole(5),
        out_shape=[S((r, W), f32)] + [S((1, r), f32)] * 4,
        compiler_params=pltpu.CompilerParams(vmem_limit_bytes=16 << 20), name="finish_first", cost_estimate=cost(0, 8 * w.size),
    )(ids, s, o, w, gain[None], bias[None])


def pull(me, refs, meta, segs, sems):
    copies = []
    for ref, (k, r0) in zip(refs, meta):
        s = jnp.bitwise_xor(me, k)
        r1 = r0 + ref.shape[0]
        for a, c, dst, lanes in segs:
            lo, hi = max(a, r0), min(a + c, r1)
            if lo < hi:
                src = ref.at[pl.ds(lo - r0, hi - lo), pl.ds(0, lanes)]
                copies.append(pltpu.make_async_copy(src, dst(s, lo - a, hi - lo), sems.at[len(copies)]))
    return copies


def mult(x, m):
    return pl.multiple_of(x, m)


def weight_segs(w, r):
    gw = w.shape[1] // 3
    seg = lambda j: (j * r, r, lambda s, o, c: w.at[pl.ds(mult(s * r + o, 16), c), pl.ds(j * gw, gw)], gw)
    return [seg(j) for j in range(3)]


def start_body(tok, step, nx, xht):
    n, _ = norm(tok[...].astype(f32) + step[...].astype(f32))
    D = tok.shape[1]
    nx[...] = n
    xht[:D, :] = n.astype(bf16).T
    xht[D:, :] = jnp.ones((16, tok.shape[0]), bf16)


def start(tok, step, bm=256):
    T, D = tok.shape
    rows = pl.BlockSpec((bm, D), lambda i: (i, 0))
    return pl.pallas_call(
        start_body, grid=(T // bm,),
        in_specs=[rows, pl.BlockSpec((1, D), lambda i: (0, 0))], out_specs=[rows, pl.BlockSpec((D + 16, bm), lambda i: (0, i))],
        out_shape=[S((T, D), f32), S((D + 16, T), bf16)], compiler_params=cp(), name="start", cost_estimate=cost(20 * T * D, 8 * T * D),
    )(tok, step)


def front_body(scale, n, meta, me, nx, *refs):
    np_ = len(meta)
    pieces = refs[:np_]
    kv, qkvt, wout, vec, upb, nv, h, w, vbuf, sems, own = refs[np_:]
    T, D = nv.shape
    r = D // n
    FF = upb.shape[1]
    i = pl.program_id(0)
    cw = kv.shape[2]
    per_j = D // cw
    segs = [(3 * r, VROWS, lambda s, o, c: vbuf.at[s, pl.ds(o, c)], LANES)] + weight_segs(w, r)
    load = pltpu.make_async_copy(nx, nv, own.at[0])
    save = pltpu.make_async_copy(w, wout, own.at[1])

    @pl.when(i == 0)
    def _():
        cs = pull(me[0], pieces, meta, segs, sems)
        for c in cs:
            c.start()
        load.start()
        for c in cs:
            c.wait()
        save.start()
        per = LANES // r
        tiles = [sum(vbuf[s, 0:8, :].astype(f32) for s in range(t * per, (t + 1) * per)) for t in range(D // LANES)]
        vec[...] = jnp.concatenate(tiles, axis=1)
        wu = FF // n
        if wu >= LANES:
            rows = [vbuf[s, 8 + q : 9 + q, :].astype(f32) for s in range(n) for q in range(wu // LANES)]
        else:
            per = LANES // wu
            rows = [sum(vbuf[s, 8:9, :].astype(f32) for s in range(t * per, (t + 1) * per)) for t in range(FF // LANES)]
        upb[...] = jnp.concatenate(rows, axis=1)
        load.wait()
        v = vec[...]
        h[...] = (nv[...] * row(v, 0) + row(v, 1)).astype(bf16)

    cols = pl.ds(mult(i * cw, 128), cw)
    y = dot(h[...], w[:, cols])
    here = pl.ds(mult((i % per_j) * cw, 128), cw)
    kind = i // per_j
    y = (y + jnp.where(kind == 0, vec[2:3, here], jnp.where(kind == 2, vec[3:4, here], 0.0))).astype(bf16)
    kv[0] = y
    qkvt[0] = jnp.where(kind == 0, y * bf16(scale), y).T

    @pl.when(i == pl.num_programs(0) - 1)
    def _():
        save.wait()


S = jax.ShapeDtypeStruct
ANY = pl.BlockSpec(memory_space=pl.ANY)


def cost(flops, nbytes, tr=0):
    return pl.CostEstimate(flops=int(flops), bytes_accessed=int(nbytes), transcendentals=int(tr))


def front(me, nx, pieces, n, FF, cw=512):
    T, D = nx.shape
    scale = 1.0 / math.sqrt(D // HEADS)
    meta = tuple((k, r0) for k, r0, _ in pieces)
    q = D // cw
    keep = lambda *sh: pl.BlockSpec(sh, lambda i, m: (0,) * len(sh))
    rest = lambda i: jnp.maximum(i - q, 0)
    V = pltpu.VMEM
    return pl.pallas_call(
        functools.partial(front_body, scale, n, meta),
        grid_spec=pltpu.PrefetchScalarGridSpec(
            num_scalar_prefetch=1, grid=(3 * q,),
            in_specs=[ANY] * (1 + len(pieces)),
            out_specs=[pl.BlockSpec((1, T, cw), lambda i, m: (rest(i) // q, 0, rest(i) % q)), pl.BlockSpec((1, cw, T), lambda i, m: (i // q, i % q, 0)), ANY, keep(8, D), keep(1, FF)],
            scratch_shapes=[V((T, D), f32), V((T, D), bf16), V((D, 3 * D), bf16), V((n, VROWS, LANES), bf16), pltpu.SemaphoreType.DMA((8 * len(pieces),)), pltpu.SemaphoreType.DMA((2,))]),
        out_shape=[S((2, T, D), bf16), S((3, D, T), bf16), S((D, 3 * D), bf16), S((8, D), f32), S((1, FF), f32)],
        compiler_params=cp(), name="front", cost_estimate=cost(6 * T * D * D, 12 * T * D),
    )(me, nx, *[a for _, _, a in pieces])


def attn_fwd_body(HD, bi, CR, p0, ln, k, qt, vt, *refs):
    et, mixed, mixedt, mixedf, linv, scr, ka, eb, esem = refs[-9:]
    T, PW = k.shape
    n = ln[0]
    p = pl.program_id(0)
    last = p == pl.num_programs(0) - 1
    rid = lax.broadcasted_iota(jnp.int32, (PW, bi), 0)
    lane = lax.broadcasted_iota(jnp.int32, (T, PW), 1)
    rows = lax.broadcasted_iota(jnp.int32, (T, PW), 0)
    ka[:, :PW] = k[...]
    ka[:, PW:] = jnp.where((lane == 0) & (rows >= n), f32(-1e30), f32(0)).astype(bf16)
    ones = jnp.where(rid == 0, f32(1), f32(0)).astype(bf16)
    va = [jnp.concatenate([vt[h * HD : (h + 1) * HD, :], jnp.ones((16, T), bf16)], axis=0) for h in range(2)]
    tasks = [(b, h) for b in range(T // bi) for h in range(2)]
    nch = T // CR

    def query(t):
        b, h = tasks[t]
        q = qt[:, b * bi : (b + 1) * bi]
        return jnp.concatenate([jnp.where(rid // HD == h, q, jnp.zeros_like(q)), ones], axis=0)

    def score(t, c, q):
        s = dot(ka[c * CR : (c + 1) * CR, :], q)
        scr[t % 2, c * CR : (c + 1) * CR, :] = s
        return jnp.max(s, axis=0, keepdims=True)

    q = query(0)
    m = functools.reduce(jnp.maximum, [score(0, c, q) for c in range(nch)])
    half = None
    for t, (b, h) in enumerate(tasks):
        sl = slice(b * bi, (b + 1) * bi)
        more = t + 1 < len(tasks)
        put = pltpu.make_async_copy(eb.at[t % 2], et.at[2 * (p0 + p) + h, :, pl.ds(b * bi, bi)], esem.at[t % 2])
        if t < 2:

            @pl.when(p > 0)
            def _():
                put.wait()

        else:
            put.wait()
        if more:
            q = query(t + 1)
        nxt = []
        for c in range(nch):
            cs = slice(c * CR, (c + 1) * CR)
            if more:
                nxt.append(score(t + 1, c, q))
            eb[t % 2, cs, :] = jnp.exp(scr[t % 2, cs, :] - m).astype(bf16)
        put.start()
        o = dot(va[h], eb[t % 2])
        if more:
            m = functools.reduce(jnp.maximum, nxt)
        inv = 1.0 / o[HD : HD + 1, :]
        linv[h : h + 1, sl] = inv
        o = o[:HD, :] * inv
        if h == 0:
            half = o
        else:
            mt = jnp.concatenate([half, o], axis=0)
            mixedf[:, sl] = mt
            mt = mt.astype(bf16)
            mixedt[:, sl] = mt
            mixed[sl, :] = mt.T

    @pl.when(last)
    def _():
        for q in range(2):
            pltpu.make_async_copy(eb.at[q], et.at[0, :, pl.ds(0, bi)], esem.at[q]).wait()


def attn_fwd(ln, kv, qkvt, p0, cnt, prev):
    _, T, D = kv.shape
    HD = D // HEADS
    PW = 2 * HD
    NP = D // PW
    bi = T
    prev = list(prev)
    return pl.pallas_call(
        functools.partial(attn_fwd_body, HD, bi, min(512, T), p0),
        grid_spec=pltpu.PrefetchScalarGridSpec(
            num_scalar_prefetch=1, grid=(cnt,),
            in_specs=[pl.BlockSpec((None, T, PW), lambda p, r: (0, 0, p0 + p)), pl.BlockSpec((None, PW, T), lambda p, r: (0, p0 + p, 0)), pl.BlockSpec((None, PW, T), lambda p, r: (2, p0 + p, 0))] + [ANY] * len(prev),
            out_specs=[ANY, pl.BlockSpec((T, PW), lambda p, r: (0, p0 + p)), pl.BlockSpec((PW, T), lambda p, r: (p0 + p, 0)), pl.BlockSpec((PW, T), lambda p, r: (p0 + p, 0)), pl.BlockSpec((None, 8, T), lambda p, r: (p0 + p, 0, 0))],
            scratch_shapes=[pltpu.VMEM((2, T, bi), f32), pltpu.VMEM((T, 2 * PW), bf16), pltpu.VMEM((2, T, bi), bf16), pltpu.SemaphoreType.DMA((2,))]),
        out_shape=[S((HEADS, T, T), bf16), S((T, D), bf16), S((D, T), bf16), S((D, T), f32), S((NP, 8, T), f32)],
        input_output_aliases={4 + i: i for i in range(len(prev))},
        compiler_params=cp(), name="attn_fwd", cost_estimate=cost(cnt * 2 * 8 * T * T * 128, cnt * 2 * T * T * 2, cnt * 2 * T * T),
    )(ln, kv, qkvt, qkvt, *prev)


G0 = math.sqrt(2 / math.pi)


def bit_reverse(x, m):
    y = jnp.zeros_like(x)
    for t in range(m):
        y = y | (((x >> t) & 1) << (m - 1 - t))
    return y


def push(me, n, s, src, keep, send, row0, sem, reverse=False):
    k = jnp.bitwise_xor(me, s)
    p = k >> 1
    if reverse:
        p = bit_reverse(p, (n // 2).bit_length() - 1)
    put = lambda dst: pltpu.make_async_copy(src, dst.at[p, pl.ds(row0, src.shape[0])], sem)

    @pl.when(k & 1 == 0)
    def _():
        put(keep).start()

    @pl.when(k & 1 == 1)
    def _():
        put(send).start()


def ffn_body(n, meta, ch, ln, me, tok, step, vec, upb, cot, mixed, mixedt, *refs):
    np_ = len(meta)
    pieces = refs[:np_]
    out, gx1, gmt, ka, sa, kb, sb, wo, wu, wd, act, gup, h2t, gdt, gattn, sums, upsum, dn, up, gwo, vr, mtv, sems, psems = refs[np_:]
    i = pl.program_id(0)
    bm, D = tok.shape
    FF = wu.shape[1]
    r = D // n
    rf = FF // n
    nf = FF // D
    i0 = me[0]
    ro = pl.ds(mult(i * bm, 128), bm)
    first = i == 0
    seg = lambda j: (r + j * r, r, lambda s, o, c: wu.at[pl.ds(mult(s * r + o, 16), c), pl.ds(j * D, D)], D)
    seg_o = [(0, r, lambda s, o, c: wo.at[pl.ds(mult(s * r + o, 16), c)], D)]
    seg_u = [seg(j) for j in range(nf)]
    seg_d = [(r + r * nf, rf, lambda s, o, c: wd.at[pl.ds(mult(s * rf + o, 16), c)], D)]
    q = sems.shape[0] // 4
    parts = [(seg_o, sems.at[pl.ds(0, q)]), (seg_d, sems.at[pl.ds(q, q)]), (seg_u, sems.at[pl.ds(2 * q, 2 * q)])]
    load = pltpu.make_async_copy(mixedt, mtv, psems.at[psems.shape[0] - 1])

    @pl.when(first)
    def _():
        for sg, sm in parts:
            for c in pull(i0, pieces, meta, sg, sm):
                c.start()
        load.start()
        sums[...] = jnp.zeros_like(sums)
        upsum[...] = jnp.zeros_like(upsum)
        for c in pull(i0, pieces, meta, *parts[0]):
            c.wait()

    v = vec[...]
    x1 = tok[...].astype(f32) + step[...].astype(f32) + dot(mixed[...], wo[...]) + row(v, 4)
    nx, rr = norm(x1)
    h2 = (nx * row(v, 5) + row(v, 6)).astype(bf16)
    live = (lax.broadcasted_iota(jnp.int32, (bm, 1), 0) + i * bm) < ln[0]
    gd = jnp.where(live, cot[...], jnp.zeros_like(cot))
    acc = x1 + row(v, 7)
    gh = None
    nc = FF // ch
    sl = [slice(c * ch, (c + 1) * ch) for c in range(nc)]
    lead = lambda c: (dot(h2, wu[:, sl[c]]), dot_t(gd, wd[sl[c], :]))
    h2t[:, ro] = h2.T
    gdt[:, ro] = gd.T

    @pl.when(first)
    def _():
        for sg, sm in parts[1:]:
            for c in pull(i0, pieces, meta, sg, sm):
                c.wait()

    nxt = lead(0)
    for c in range(nc):
        u, ga = nxt
        nxt = lead(c + 1) if c + 1 < nc else None
        u = u + upb[:, sl[c]]
        u2 = u * u
        t = jnp.tanh(u * (f32(G0) + f32(G0 * 0.044715) * u2))
        half = 0.5 + 0.5 * t
        a = (u * half).astype(bf16)
        act[ro, sl[c]] = a
        dg = half + u * (half * (1.0 - half)) * (f32(2 * G0) + f32(6 * 0.044715 * G0) * u2)
        gu = (ga * dg).astype(bf16)
        gup[ro, sl[c]] = gu
        upsum[:, sl[c]] += jnp.sum(gu.astype(f32), axis=0, keepdims=True)
        acc = acc + dot(a, wd[sl[c], :])
        p = dot_t(gu, wu[:, sl[c]])
        gh = p if gh is None else gh + p
    out[...] = jnp.where(live, acc, 0.0).astype(bf16)
    gn = gh * row(v, 5)
    gx = gd.astype(f32) + rr * (gn - jnp.mean(gn, axis=-1, keepdims=True) - nx * jnp.mean(gn * nx, axis=-1, keepdims=True))
    gab = gx.astype(bf16)
    gx1[...] = gab
    gattn[ro, :] = gab
    gmt[...] = dot_t(gab, wo[...]).astype(bf16).T
    s_ = lambda a: jnp.sum(a.astype(f32), axis=0, keepdims=True)
    sums[...] += jnp.concatenate([s_(gab), s_(gh * nx), s_(gh), s_(gd), jnp.zeros((4, D), f32)], axis=0)

    @pl.when(i == pl.num_programs(0) - 1)
    def _():
        per = D // rf
        for j in range(nf):
            dn[j] = dot(gdt[...], act[:, j * D : (j + 1) * D]).astype(bf16).T
            for t in range(per):
                push(i0, n, j * per + t, dn.at[j, pl.ds(t * rf, rf)], ka, sa, 0, psems.at[j * per + t])
            up[j] = dot(h2t[...], gup[:, j * D : (j + 1) * D]).astype(bf16)
            for s in range(n):
                push(i0, n, s, up.at[j, pl.ds(s * r, r)], kb, sb, j * r, psems.at[n * (1 + j) + s], True)
        load.wait()
        gwo[...] = dot(mtv[...], gattn[...]).astype(bf16)
        vr[...] = jnp.concatenate([sums[0:4, :]] + [upsum[:, c * D : (c + 1) * D] for c in range(nf)] + [jnp.zeros((VROWS - 4 - nf, D), f32)], axis=0).astype(bf16)
        b = n * (1 + nf)
        for s in range(n):
            push(i0, n, s, gwo.at[pl.ds(s * r, r)], ka, sa, rf, psems.at[b + s])
            push(i0, n, s, vr, kb, sb, nf * r, psems.at[b + n + s], True)
        done = lambda src, q: pltpu.make_async_copy(src, (ka if src.shape[0] == rf else kb).at[0, pl.ds(0, src.shape[0])], psems.at[q]).wait()
        for s in range(n):
            done(dn.at[0, pl.ds(0, rf)], s)
            for c in range(nf):
                done(up.at[0, pl.ds(0, r)], n * (1 + c) + s)
            done(gwo.at[pl.ds(0, r)], b + s)
            done(vr, b + n + s)


def ffn(ln, me, tok, step, vec, upb, cot, mixed, mixedt, pieces, n):
    T, D = tok.shape
    FF = upb.shape[1]
    bm = min(512, T)
    nf = FF // D
    r = D // n
    meta = tuple((k, r0) for k, r0, _ in pieces)
    full = lambda a: pl.BlockSpec(a.shape, lambda i, l, m: (0,) * a.ndim)
    rows = pl.BlockSpec((bm, D), lambda i, l, m: (i, 0))
    A = S((n // 2, FF // n + r, D), bf16)
    B = S((n // 2, nf * r + VROWS, D), bf16)
    V = pltpu.VMEM
    return pl.pallas_call(
        functools.partial(ffn_body, n, meta, min(1024, FF)),
        grid_spec=pltpu.PrefetchScalarGridSpec(
            num_scalar_prefetch=2, grid=(T // bm,),
            in_specs=[rows, full(step), full(vec), full(upb), rows, rows, ANY] + [ANY] * len(pieces),
            out_specs=[rows, rows, pl.BlockSpec((D, bm), lambda i, l, m: (0, i))] + [ANY] * 4,
            scratch_shapes=[V((D, D), bf16), V((D, FF), bf16), V((FF, D), bf16), V((T, FF), bf16), V((T, FF), bf16), V((D, T), bf16), V((D, T), bf16), V((T, D), bf16), V((8, D), f32), V((1, FF), f32), V((nf, D, D), bf16), V((nf, D, D), bf16), V((D, D), bf16), V((VROWS, D), bf16), V((D, T), bf16), pltpu.SemaphoreType.DMA((16 * len(pieces),)), pltpu.SemaphoreType.DMA((n * (nf + 3) + 1,))]),
        out_shape=[S((T, D), bf16), S((T, D), bf16), S((D, T), bf16), A, A, B, B],
        compiler_params=cp(49), name="ffn", cost_estimate=cost(2 * T * D * (6 * FF + 3 * D), 16 * T * D, T * FF),
    )(ln, me, tok, step, vec, upb, cot, mixed, mixedt, *[a for _, _, a in pieces])


def attn_bwd_body(HD, scale, CR, v, kt, qt, gt, mt, linv, et, *refs):
    gq, ds = refs[-2:]
    T = v.shape[0]
    rid = lax.broadcasted_iota(jnp.int32, gt.shape, 0) // HD
    g = gt[...].astype(f32)
    q = qt[...]
    gv = gk = None
    for h in range(2):
        hs = slice(h * HD, (h + 1) * HD)
        gs = (g * linv[h : h + 1, :]).astype(bf16)
        gm = jnp.where(rid == h, gs, jnp.zeros_like(gs))
        dl = jnp.sum(gs[hs, :].astype(f32) * mt[hs, :], axis=0, keepdims=True)
        for c in range(T // CR):
            cs = slice(c * CR, (c + 1) * CR)
            ds[h, cs, :] = (et[h, cs, :].astype(f32) * (dot(v[cs, :], gm) - dl)).astype(bf16)
        a = dot(et[h], gm.T)
        b = dot(ds[h], jnp.where(rid == h, q, jnp.zeros_like(q)).T)
        gv = a if gv is None else gv + a
        gk = b if gk is None else gk + b
        gq[0, hs, :] = (dot(kt[hs, :], ds[h]) * scale).astype(bf16)
    gq[2] = gv.astype(bf16).T
    gq[1] = gk.astype(bf16).T


def attn_bwd(kv, qkvt, gmt, mixedf, linv, et, p0, cnt, prev):
    _, T, D = kv.shape
    HD = D // HEADS
    PW = 2 * HD
    NP = D // PW
    prev = list(prev)
    pr = pl.BlockSpec((PW, T), lambda p: (p0 + p, 0))
    of = lambda j: pl.BlockSpec((None, PW, T), lambda p: (j, p0 + p, 0))
    return pl.pallas_call(
        functools.partial(attn_bwd_body, HD, 1.0 / math.sqrt(HD), min(256, T)),
        grid=(cnt,),
        scratch_shapes=[pltpu.VMEM((2, T, T), bf16)],
        in_specs=[pl.BlockSpec((None, T, PW), lambda p: (1, 0, p0 + p)), of(1), of(0), pr, pr, pl.BlockSpec((None, 8, T), lambda p: (p0 + p, 0, 0)), pl.BlockSpec((2, T, T), lambda p: (p0 + p, 0, 0))] + [ANY] * len(prev),
        out_specs=pl.BlockSpec((3, PW, T), lambda p: (0, p0 + p, 0)),
        out_shape=S((3, D, T), bf16),
        input_output_aliases={7: 0} if prev else {},
        compiler_params=cp(), name="attn_bwd", cost_estimate=cost(cnt * 2 * 16 * T * T * 128, cnt * 2 * T * T * 2),
    )(kv, qkvt, qkvt, gmt, mixedf, linv, et, *prev)


def wqkv_body(n, me, xht, g, keep, send, res, vr, sems):
    j = pl.program_id(0)
    D = g.shape[0]
    r = D // n
    i0 = me[0]
    y = dot_t(xht[...], g[...]).astype(bf16)
    res[j] = y[:D]
    vr[...] = jnp.where(lax.broadcasted_iota(jnp.int32, vr.shape, 0) == j, y[D:], jnp.where(j == 0, jnp.zeros_like(y[D:]), vr[...]))
    for s in range(n):
        push(i0, n, s, res.at[j, pl.ds(s * r, r)], keep, send, mult(j * r, 16), sems.at[j * n + s])

    @pl.when(j == 2)
    def _():
        for s in range(n):
            push(i0, n, s, vr, keep, send, 3 * r, sems.at[3 * n + s])
        for s in range(n):
            for q in range(3):
                pltpu.make_async_copy(res.at[0, pl.ds(0, r)], keep.at[0, pl.ds(0, r)], sems.at[q * n + s]).wait()
            pltpu.make_async_copy(vr, keep.at[0, pl.ds(0, VROWS)], sems.at[3 * n + s]).wait()


def wqkv(me, xht, g, n):
    _, D, T = g.shape
    A = S((n // 2, 3 * (D // n) + VROWS, D), bf16)
    return pl.pallas_call(
        functools.partial(wqkv_body, n),
        grid_spec=pltpu.PrefetchScalarGridSpec(
            num_scalar_prefetch=1, grid=(3,),
            in_specs=[pl.BlockSpec((D + 16, T), lambda j, m: (0, 0)), pl.BlockSpec((None, D, T), lambda j, m: (j, 0, 0))],
            out_specs=[ANY] * 2,
            scratch_shapes=[pltpu.VMEM((3, D, D), bf16), pltpu.VMEM((VROWS, D), bf16), pltpu.SemaphoreType.DMA((4 * n,))]),
        out_shape=[A, A],
        compiler_params=cp(), name="wqkv", cost_estimate=cost(6 * T * D * D, 10 * T * D),
    )(me, xht, g)


def back_body(tok, step, vec, g, gx1, *refs):
    ws, tg = refs[:-1], refs[-1]
    D = tok.shape[1]
    gw = D // GROUPS
    x = tok[...].astype(f32) + step[...].astype(f32)
    nx, rr = norm(x)
    gt = sum(dot(w[:, j * gw : (j + 1) * gw], g[j, q * gw : (q + 1) * gw, :]) for q, w in enumerate(ws) for j in range(3))
    gn = gt.T * row(vec[...], 0)
    tg[...] = gx1[...].astype(f32) + rr * (gn - jnp.mean(gn, axis=-1, keepdims=True) - nx * jnp.mean(gn * nx, axis=-1, keepdims=True))


def back(tok, step, vec, ws, g, gx1, bm=512):
    T, D = tok.shape
    full = lambda a: pl.BlockSpec(a.shape, lambda i: (0,) * a.ndim)
    rows = pl.BlockSpec((bm, D), lambda i: (i, 0))
    return pl.pallas_call(
        back_body, grid=(T // bm,),
        in_specs=[rows, full(step), full(vec), pl.BlockSpec((3, D, bm), lambda i: (0, 0, i)), rows] + [full(w) for w in ws],
        out_specs=rows, out_shape=S((T, D), f32), compiler_params=cp(), name="back", cost_estimate=cost(6 * T * D * D, 14 * T * D),
    )(tok, step, vec, g, gx1, *ws)


def shards(tokens, step_embed, lengths, cotangent, ln1_gain, ln1_bias, qkv_weight, q_bias, v_bias, out_weight, out_bias, ln2_gain, ln2_bias, up_weight, up_bias, down_weight, down_bias):
    n = lax.axis_size("shard")
    me = lax.axis_index("shard").astype(jnp.int32)
    mes = me[None]
    tok, cot, step = tokens[0], cotangent[0], step_embed
    T, D = tok.shape
    r = D // n
    FF = up_bias.shape[0] * n
    nc = FF // D
    rf = FF // n
    packs = pack_first(mes, qkv_weight, [ln1_gain, ln1_bias, q_bias, v_bias, out_bias, ln2_gain, ln2_bias, down_bias], up_bias)
    pack2 = pack_rest(out_weight, up_weight, down_weight)
    NP = HEADS // 2
    nx, xht = start(tok, step)
    pieces = gather_direct(packs[0], n, xht, pack2)
    kv, qkvt, w, vec, upb = front(mes, nx, pieces, n, FF)
    et, mixed, mixedt, mixedf, linv = attn_fwd(lengths, kv, qkvt, 0, NP, [])
    pieces2 = gather_direct(after(pack2, xht), n, linv)
    out, gx1, gmt, ka, sa, kb, sb = ffn(lengths, mes, tok, step, vec, upb, cot, mixed, mixedt, pieces2, n)
    bwd = lambda p, c, g, *deps: attn_bwd(kv, qkvt, after(gmt, *deps) if deps else gmt, mixedf, linv, et, p, c, g)
    ga, gb = swap(sa, 1), swap(sb, 1)
    g = bwd(0, 1, [])
    ga, gb, _ = lax.optimization_barrier((ga, gb, g))
    h = n // 4
    lo, hi = slice(0, h), slice(h, None)
    add = lambda a, b, s: add16(a[s], b[s])
    ka, xa, kb, xb = add(ka, ga, lo), add(ka, ga, hi), add(kb, gb, lo), add(kb, gb, hi)
    g = bwd(1, NP - 1, [g], ka, xa, kb, xb)
    m = (n // 2).bit_length() - 1
    ga, gb = swap(xa, 2 << (m - 1)), swap(xb, 2)
    for t in range(1, m):
        dep = g if t == 1 else keep
        ga, gb, _ = lax.optimization_barrier((ga, gb, dep))
        h //= 2
        lo, hi = slice(0, h), slice(h, None)
        ka, xa = add(ka, ga, lo), add(ka, ga, hi)
        kb, xb = add(kb, gb, lo), add(kb, gb, hi)
        ga, gb = swap(xa, 2 << (m - 1 - t)), swap(xb, 2 << t)
        if t == 1:
            keep, send = wqkv(mes, after(xht, ka, xa, kb, xb), g, n)
    got = swap(send, 1)
    p2 = [add16(keep[k], got[k]) for k in range(n // 2)]
    far2 = spread(p2)
    ga, gb, _ = lax.optimization_barrier((ga, gb, keep))
    got = swap(send, 1)
    p2 = [add16(keep[k], got[k]) for k in range(n // 2)]
    far2 = spread(p2)
    own1 = jnp.concatenate([add16(ka, ga)[0], add16(kb, gb)[0]], axis=0)
    m1, o1, x1 = rep_half(own1)
    z1 = add16(m1, after(o1, *p2[1:]))
    tg = back(tok, after(step, z1, *p2[1:]), vec, [w], g, gx1)
    own2 = total(p2[0], [after(a, tg) for a in far2])
    m2, o2, x2 = rep_half(own2)
    steps = rep_steps()
    z2 = None if steps else add16(m2, o2)
    for b in steps:
        z1 = add16(z1, after(rep_perm(z1, b), x2))
        if z2 is None:
            z2 = add16(m2, after(o2, z1))
        pz = rep_perm(z2, b)
        z2 = add16(z2, after(pz, z1))
    o1, o2 = rep_perm(z1, 1), rep_perm(z2, 1)
    ids = jnp.stack([me, (lax.axis_index("rep") % 2).astype(jnp.int32)])
    g_down, g_up, g_out, g_upb, g_ob, g_g2, g_b2, g_db = finish_rest(ids, z1, o1, r, rf, nc, n)
    g_qkv, g_g1, g_b1, g_q, g_v = finish_first(ids, z2, after(o2, g_out), qkv_weight, ln1_gain, ln1_bias)
    flat = lambda a: a.reshape(-1)
    return (out[None], tg[None], flat(g_g1), flat(g_b1), g_qkv, flat(g_q), flat(g_v), g_out, flat(g_ob), flat(g_g2), flat(g_b2), g_up, flat(g_upb), g_down, flat(g_db))


def solution(mesh):
    from jax.sharding import PartitionSpec as P

    in_specs = (
        P(("rep", "shard"), None, None),
        P(("rep", "shard"), None),
        P(("rep", "shard")),
        P(("rep", "shard"), None, None),
        P("shard"),
        P("shard"),
        P("shard", None),
        P("shard"),
        P("shard"),
        P("shard", None),
        P("shard"),
        P("shard"),
        P("shard"),
        P("shard", None),
        P("shard"),
        P("shard", None),
        P("shard"),
    )
    out_specs = (
        P(("rep", "shard"), None, None),
        P(("rep", "shard"), None, None),
        P("shard"),
        P("shard"),
        P("shard", None),
        P("shard"),
        P("shard"),
        P("shard", None),
        P("shard"),
        P("shard"),
        P("shard"),
        P("shard", None),
        P("shard"),
        P("shard", None),
        P("shard"),
    )
    return jax.shard_map(shards, mesh=mesh, in_specs=in_specs, out_specs=out_specs, check_vma=False)
```

```python
import functools, math
import jax, jax.numpy as jnp
from jax import lax
from jax.experimental import pallas as pl
from jax.experimental.pallas import tpu as pltpu

f32 = jnp.float32
bf16 = jnp.bfloat16
EPS = 1e-05
HEADS = 8

def dot(a, b):
    return jnp.dot(a, b, preferred_element_type=f32)

def dot_t(a, b):
    return lax.dot_general(a, b, (((1,), (1,)), ((), ())), preferred_element_type=f32)

def cp(mib=60):
    return pltpu.CompilerParams(dimension_semantics=("arbitrary",), vmem_limit_bytes=mib << 20)

def norm(x):
    c = x - jnp.mean(x, axis=-1, keepdims=True)
    r = lax.rsqrt(jnp.mean(c * c, axis=-1, keepdims=True) + EPS)
    return c * r, r

def row(v, i):
    return v[i : i + 1, :].astype(f32)


VROWS = 16
LANES = 128


def xor_perm(n, k):
    return [(i, i ^ k) for i in range(n)]


def rep_perm(x, b):
    return lax.ppermute(x, "rep", xor_perm(lax.axis_size("rep"), b))


def swap(x, k):
    return lax.ppermute(x, "shard", xor_perm(lax.axis_size("shard"), k))


def after(x, *deps):
    return lax.optimization_barrier((x,) + deps)[0]


def gather_direct(x, n, *gate):
    out = [(0, 0, x)]
    far = [(k, swap(x, k)) for k in range(2, n, 2)]
    out += [(k, 0, after(y, *gate) if gate else y) for k, y in far]
    return out + [(k ^ 1, 0, swap(y, 1)) for k, _, y in out]


def add16(a, b):
    return a + b


def spread(parts):
    return [swap(parts[k], 2 * k) for k in range(len(parts) - 1, 0, -1)]


def total(own, got):
    t = own.astype(f32)
    for a in got:
        t = t + a.astype(f32)
    return t.astype(bf16)


def rep_half(x):
    h = x.shape[0] // 2
    odd = lax.axis_index("rep") % 2
    mine = lax.dynamic_slice_in_dim(x, odd * h, h, 0)
    other = lax.dynamic_slice_in_dim(x, (1 - odd) * h, h, 0)
    return mine, rep_perm(other, 1), other


def rep_steps():
    nr = lax.axis_size("rep")
    return [b for b in (2 << i for i in range(16)) if b < nr]


GROUPS = 1


def pack_first_body(me, w, upb, *refs):
    vecs = refs[:-GROUPS]
    outs = refs[-GROUPS:]
    r, W = w.shape
    D = W // 3
    gw = D // GROUPS
    for g, out in enumerate(outs):
        for j in range(3):
            out[j * r : (j + 1) * r, :] = w[:, j * D + g * gw : j * D + (g + 1) * gw]

    def spot(v):
        w_ = v.shape[1]
        if w_ >= LANES:
            return [v[q : q + 1, :] for q in range(v.shape[0])]
        t = LANES // w_
        lane = lax.broadcasted_iota(jnp.int32, (1, LANES), 1)
        return [jnp.where(lane // w_ == me[0] % t, jnp.concatenate([v] * t, axis=1), jnp.zeros((1, LANES), f32))]

    rows = [a for v in vecs for a in spot(v[...].astype(f32))] + spot(upb[...].astype(f32))
    b = jnp.concatenate(rows + [jnp.zeros((VROWS - len(rows), LANES), f32)], axis=0).astype(bf16)
    outs[0][3 * r :, :] = jnp.concatenate([b, jnp.zeros((VROWS, gw - LANES), bf16)], axis=1) if gw > LANES else b


def whole(n):
    return [pl.BlockSpec(memory_space=pltpu.VMEM)] * n


def once(*arrays):
    return [pl.BlockSpec(a.shape, lambda i, *m, nd=len(a.shape): (0,) * nd) for a in arrays]


def pack_first(me, w, vecs, upb):
    r, W = w.shape
    gw = W // 3 // GROUPS
    lanes = lambda v: v.reshape(-1, min(LANES, v.shape[0]))
    args = [w] + [lanes(v) for v in [upb] + vecs]
    outs = [S((3 * r + (VROWS if g == 0 else 0), gw), bf16) for g in range(GROUPS)]
    return pl.pallas_call(
        pack_first_body,
        grid_spec=pltpu.PrefetchScalarGridSpec(num_scalar_prefetch=1, grid=(1,), in_specs=once(*args), out_specs=once(*outs)),
        out_shape=outs, compiler_params=cp(), name="pack_first", cost_estimate=cost(0, 4 * w.size),
    )(me, *args)


def pack_rest_body(wo, wu, wd, out):
    r, D = wo.shape
    out[:r, :] = wo[...]
    for j in range(wu.shape[1] // D):
        out[(1 + j) * r : (2 + j) * r, :] = wu[:, j * D : (j + 1) * D]
    out[(1 + wu.shape[1] // D) * r :, :] = wd[...]


def pack_rest(wo, wu, wd):
    D = wo.shape[1]
    out = S(((wo.size + wu.size + wd.size) // D, D), bf16)
    return pl.pallas_call(
        pack_rest_body, grid=(1,), in_specs=once(wo, wu, wd), out_specs=once(out)[0],
        out_shape=out, compiler_params=cp(), name="pack_rest", cost_estimate=cost(0, 4 * wu.size),
    )(wo, wu, wd)


def own_lanes(tiles, me, w):
    pick = lambda i: sum(jnp.where(i == t, a, jnp.zeros_like(a)) for t, a in enumerate(tiles))
    if w >= LANES:
        q = w // LANES
        return jnp.concatenate([pick(me * q + c) for c in range(q)], axis=1)
    per = LANES // w
    x = pick(me // per)
    off = me % per
    return sum(jnp.where(off == o, x[:, o * w : (o + 1) * w], 0.0) for o in range(per))


def rows_of(lo, hi, a, b):
    h = lo.shape[0]
    if b <= h:
        return lo[a:b, :]
    if a >= h:
        return hi[a - h : b - h, :]
    return jnp.concatenate([lo[a:h, :], hi[: b - h, :]], axis=0)


def finish_rest_body(r, rf, n, ids, s, o, down, up, out, upb, *vecs):
    D = out.shape[1]
    nf = up.shape[1] // D

    def run(lo, hi):
        f = lambda a, b: rows_of(lo, hi, a, b).astype(f32)
        down[...] = f(0, rf)
        out[...] = f(rf, rf + r)
        for j in range(nf):
            up[:, j * D : (j + 1) * D] = f(rf + (j + 1) * r, rf + (j + 2) * r)
        b = rf + (nf + 1) * r
        v = f(b, b + VROWS)
        me = ids[0]
        tiles = [v[0:8, t * LANES : (t + 1) * LANES] for t in range(D // LANES)]
        x = own_lanes(tiles, me, r)
        for q, ref in enumerate(vecs):
            ref[...] = x[q : q + 1, :]
        tiles = [v[4 + q : 5 + q, t * LANES : (t + 1) * LANES] for q in range(nf) for t in range(D // LANES)]
        upb[...] = own_lanes(tiles, me, nf * D // n)

    @pl.when(ids[1] == 0)
    def _():
        run(s, o)

    @pl.when(ids[1] == 1)
    def _():
        run(o, s)


def finish_rest(ids, s, o, r, rf, nf, n):
    D = s.shape[1]
    row1 = lambda w: S((1, w), f32)
    return pl.pallas_call(
        functools.partial(finish_rest_body, r, rf, n),
        in_specs=[pl.BlockSpec(memory_space=pltpu.SMEM)] + whole(2), out_specs=whole(8),
        out_shape=[S((rf, D), f32), S((r, nf * D), f32), S((r, D), f32), row1(nf * D // n)] + [row1(r)] * 4,
        compiler_params=pltpu.CompilerParams(vmem_limit_bytes=16 << 20), name="finish_rest", cost_estimate=cost(0, 8 * s.size),
    )(ids, s, o)


def finish_first_body(ids, s, o, w, gain, bias, qkv, gg, gb, qb, vb):
    r, W = w.shape
    D = s.shape[1]

    def run(lo, hi):
        f = lambda a, b: rows_of(lo, hi, a, b).astype(f32)
        v = f(3 * r, 3 * r + VROWS)
        nt = D // LANES
        accg = accb = jnp.zeros((r, LANES), f32)
        col = lambda g: jnp.concatenate([g[...].astype(f32), jnp.zeros((7, r), f32)], axis=0).T[:, 0:1]
        cg, cb = col(gain), col(bias)
        for j in range(3):
            m = f(j * r, (j + 1) * r)
            sq = v[j : j + 1, :]
            ww = w[:, j * D : (j + 1) * D].astype(f32)
            qkv[:, j * D : (j + 1) * D] = cg * m + cb * sq
            pg, pb = ww * m, ww * sq
            accg = accg + sum(pg[:, t * LANES : (t + 1) * LANES] for t in range(nt))
            accb = accb + sum(pb[:, t * LANES : (t + 1) * LANES] for t in range(nt))
        gg[...] = jnp.sum(accg.T, axis=0, keepdims=True)
        gb[...] = jnp.sum(accb.T, axis=0, keepdims=True)
        x = own_lanes([v[0:8, t * LANES : (t + 1) * LANES] for t in range(nt)], ids[0], r)
        qb[...] = x[0:1, :]
        vb[...] = x[2:3, :]

    @pl.when(ids[1] == 0)
    def _():
        run(s, o)

    @pl.when(ids[1] == 1)
    def _():
        run(o, s)


def finish_first(ids, s, o, w, gain, bias):
    r, W = w.shape
    return pl.pallas_call(
        finish_first_body,
        in_specs=[pl.BlockSpec(memory_space=pltpu.SMEM)] + whole(5), out_specs=whole(5),
        out_shape=[S((r, W), f32)] + [S((1, r), f32)] * 4,
        compiler_params=pltpu.CompilerParams(vmem_limit_bytes=16 << 20), name="finish_first", cost_estimate=cost(0, 8 * w.size),
    )(ids, s, o, w, gain[None], bias[None])


def pull(me, refs, meta, segs, sems):
    copies = []
    for ref, (k, r0) in zip(refs, meta):
        s = jnp.bitwise_xor(me, k)
        r1 = r0 + ref.shape[0]
        for a, c, dst, lanes in segs:
            lo, hi = max(a, r0), min(a + c, r1)
            if lo < hi:
                src = ref.at[pl.ds(lo - r0, hi - lo), pl.ds(0, lanes)]
                copies.append(pltpu.make_async_copy(src, dst(s, lo - a, hi - lo), sems.at[len(copies)]))
    return copies


def mult(x, m):
    return pl.multiple_of(x, m)


def weight_segs(w, r):
    gw = w.shape[1] // 3
    seg = lambda j: (j * r, r, lambda s, o, c: w.at[pl.ds(mult(s * r + o, 16), c), pl.ds(j * gw, gw)], gw)
    return [seg(j) for j in range(3)]


def start_body(tok, step, nx, xht):
    n, _ = norm(tok[...].astype(f32) + step[...].astype(f32))
    D = tok.shape[1]
    nx[...] = n
    xht[:D, :] = n.astype(bf16).T
    xht[D:, :] = jnp.ones((16, tok.shape[0]), bf16)


def start(tok, step, bm=256):
    T, D = tok.shape
    rows = pl.BlockSpec((bm, D), lambda i: (i, 0))
    return pl.pallas_call(
        start_body, grid=(T // bm,),
        in_specs=[rows, pl.BlockSpec((1, D), lambda i: (0, 0))], out_specs=[rows, pl.BlockSpec((D + 16, bm), lambda i: (0, i))],
        out_shape=[S((T, D), f32), S((D + 16, T), bf16)], compiler_params=cp(), name="start", cost_estimate=cost(20 * T * D, 8 * T * D),
    )(tok, step)


def front_body(scale, n, meta, me, nx, *refs):
    np_ = len(meta)
    pieces = refs[:np_]
    kv, qkvt, wout, vec, upb, nv, h, w, vbuf, sems, own = refs[np_:]
    T, D = nv.shape
    r = D // n
    FF = upb.shape[1]
    i = pl.program_id(0)
    cw = kv.shape[2]
    per_j = D // cw
    segs = [(3 * r, VROWS, lambda s, o, c: vbuf.at[s, pl.ds(o, c)], LANES)] + weight_segs(w, r)
    load = pltpu.make_async_copy(nx, nv, own.at[0])
    save = pltpu.make_async_copy(w, wout, own.at[1])

    @pl.when(i == 0)
    def _():
        cs = pull(me[0], pieces, meta, segs, sems)
        for c in cs:
            c.start()
        load.start()
        for c in cs:
            c.wait()
        save.start()
        per = LANES // r
        tiles = [sum(vbuf[s, 0:8, :].astype(f32) for s in range(t * per, (t + 1) * per)) for t in range(D // LANES)]
        vec[...] = jnp.concatenate(tiles, axis=1)
        wu = FF // n
        if wu >= LANES:
            rows = [vbuf[s, 8 + q : 9 + q, :].astype(f32) for s in range(n) for q in range(wu // LANES)]
        else:
            per = LANES // wu
            rows = [sum(vbuf[s, 8:9, :].astype(f32) for s in range(t * per, (t + 1) * per)) for t in range(FF // LANES)]
        upb[...] = jnp.concatenate(rows, axis=1)
        load.wait()
        v = vec[...]
        h[...] = (nv[...] * row(v, 0) + row(v, 1)).astype(bf16)

    cols = pl.ds(mult(i * cw, 128), cw)
    y = dot(h[...], w[:, cols])
    here = pl.ds(mult((i % per_j) * cw, 128), cw)
    kind = i // per_j
    y = (y + jnp.where(kind == 0, vec[2:3, here], jnp.where(kind == 2, vec[3:4, here], 0.0))).astype(bf16)
    kv[0] = y
    qkvt[0] = jnp.where(kind == 0, y * bf16(scale), y).T

    @pl.when(i == pl.num_programs(0) - 1)
    def _():
        save.wait()


S = jax.ShapeDtypeStruct
ANY = pl.BlockSpec(memory_space=pl.ANY)


def cost(flops, nbytes, tr=0):
    return pl.CostEstimate(flops=int(flops), bytes_accessed=int(nbytes), transcendentals=int(tr))


def front(me, nx, pieces, n, FF, cw=512):
    T, D = nx.shape
    scale = 1.0 / math.sqrt(D // HEADS)
    meta = tuple((k, r0) for k, r0, _ in pieces)
    q = D // cw
    keep = lambda *sh: pl.BlockSpec(sh, lambda i, m: (0,) * len(sh))
    rest = lambda i: jnp.maximum(i - q, 0)
    V = pltpu.VMEM
    return pl.pallas_call(
        functools.partial(front_body, scale, n, meta),
        grid_spec=pltpu.PrefetchScalarGridSpec(
            num_scalar_prefetch=1, grid=(3 * q,),
            in_specs=[ANY] * (1 + len(pieces)),
            out_specs=[pl.BlockSpec((1, T, cw), lambda i, m: (rest(i) // q, 0, rest(i) % q)), pl.BlockSpec((1, cw, T), lambda i, m: (i // q, i % q, 0)), ANY, keep(8, D), keep(1, FF)],
            scratch_shapes=[V((T, D), f32), V((T, D), bf16), V((D, 3 * D), bf16), V((n, VROWS, LANES), bf16), pltpu.SemaphoreType.DMA((8 * len(pieces),)), pltpu.SemaphoreType.DMA((2,))]),
        out_shape=[S((2, T, D), bf16), S((3, D, T), bf16), S((D, 3 * D), bf16), S((8, D), f32), S((1, FF), f32)],
        compiler_params=cp(), name="front", cost_estimate=cost(6 * T * D * D, 12 * T * D),
    )(me, nx, *[a for _, _, a in pieces])


def attn_fwd_body(HD, bi, CR, p0, ln, k, qt, vt, *refs):
    et, mixed, mixedt, mixedf, linv, scr, ka, eb, esem = refs[-9:]
    T, PW = k.shape
    n = ln[0]
    p = pl.program_id(0)
    last = p == pl.num_programs(0) - 1
    rid = lax.broadcasted_iota(jnp.int32, (PW, bi), 0)
    lane = lax.broadcasted_iota(jnp.int32, (T, PW), 1)
    rows = lax.broadcasted_iota(jnp.int32, (T, PW), 0)
    ka[:, :PW] = k[...]
    ka[:, PW:] = jnp.where((lane == 0) & (rows >= n), f32(-1e30), f32(0)).astype(bf16)
    ones = jnp.where(rid == 0, f32(1), f32(0)).astype(bf16)
    va = [jnp.concatenate([vt[h * HD : (h + 1) * HD, :], jnp.ones((16, T), bf16)], axis=0) for h in range(2)]
    tasks = [(b, h) for b in range(T // bi) for h in range(2)]
    nch = T // CR

    def query(t):
        b, h = tasks[t]
        q = qt[:, b * bi : (b + 1) * bi]
        return jnp.concatenate([jnp.where(rid // HD == h, q, jnp.zeros_like(q)), ones], axis=0)

    def score(t, c, q):
        s = dot(ka[c * CR : (c + 1) * CR, :], q)
        scr[t % 2, c * CR : (c + 1) * CR, :] = s
        return jnp.max(s, axis=0, keepdims=True)

    q = query(0)
    m = functools.reduce(jnp.maximum, [score(0, c, q) for c in range(nch)])
    half = None
    for t, (b, h) in enumerate(tasks):
        sl = slice(b * bi, (b + 1) * bi)
        more = t + 1 < len(tasks)
        put = pltpu.make_async_copy(eb.at[t % 2], et.at[2 * (p0 + p) + h, :, pl.ds(b * bi, bi)], esem.at[t % 2])
        if t < 2:

            @pl.when(p > 0)
            def _():
                put.wait()

        else:
            put.wait()
        if more:
            q = query(t + 1)
        nxt = []
        for c in range(nch):
            cs = slice(c * CR, (c + 1) * CR)
            if more:
                nxt.append(score(t + 1, c, q))
            eb[t % 2, cs, :] = jnp.exp(scr[t % 2, cs, :] - m).astype(bf16)
        put.start()
        o = dot(va[h], eb[t % 2])
        if more:
            m = functools.reduce(jnp.maximum, nxt)
        inv = 1.0 / o[HD : HD + 1, :]
        linv[h : h + 1, sl] = inv
        o = o[:HD, :] * inv
        if h == 0:
            half = o
        else:
            mt = jnp.concatenate([half, o], axis=0)
            mixedf[:, sl] = mt
            mt = mt.astype(bf16)
            mixedt[:, sl] = mt
            mixed[sl, :] = mt.T

    @pl.when(last)
    def _():
        for q in range(2):
            pltpu.make_async_copy(eb.at[q], et.at[0, :, pl.ds(0, bi)], esem.at[q]).wait()


def attn_fwd(ln, kv, qkvt, p0, cnt, prev):
    _, T, D = kv.shape
    HD = D // HEADS
    PW = 2 * HD
    NP = D // PW
    bi = T
    prev = list(prev)
    return pl.pallas_call(
        functools.partial(attn_fwd_body, HD, bi, min(512, T), p0),
        grid_spec=pltpu.PrefetchScalarGridSpec(
            num_scalar_prefetch=1, grid=(cnt,),
            in_specs=[pl.BlockSpec((None, T, PW), lambda p, r: (0, 0, p0 + p)), pl.BlockSpec((None, PW, T), lambda p, r: (0, p0 + p, 0)), pl.BlockSpec((None, PW, T), lambda p, r: (2, p0 + p, 0))] + [ANY] * len(prev),
            out_specs=[ANY, pl.BlockSpec((T, PW), lambda p, r: (0, p0 + p)), pl.BlockSpec((PW, T), lambda p, r: (p0 + p, 0)), pl.BlockSpec((PW, T), lambda p, r: (p0 + p, 0)), pl.BlockSpec((None, 8, T), lambda p, r: (p0 + p, 0, 0))],
            scratch_shapes=[pltpu.VMEM((2, T, bi), f32), pltpu.VMEM((T, 2 * PW), bf16), pltpu.VMEM((2, T, bi), bf16), pltpu.SemaphoreType.DMA((2,))]),
        out_shape=[S((HEADS, T, T), bf16), S((T, D), bf16), S((D, T), bf16), S((D, T), f32), S((NP, 8, T), f32)],
        input_output_aliases={4 + i: i for i in range(len(prev))},
        compiler_params=cp(), name="attn_fwd", cost_estimate=cost(cnt * 2 * 8 * T * T * 128, cnt * 2 * T * T * 2, cnt * 2 * T * T),
    )(ln, kv, qkvt, qkvt, *prev)


G0 = math.sqrt(2 / math.pi)


def bit_reverse(x, m):
    y = jnp.zeros_like(x)
    for t in range(m):
        y = y | (((x >> t) & 1) << (m - 1 - t))
    return y


def push(me, n, s, src, keep, send, row0, sem, reverse=False):
    k = jnp.bitwise_xor(me, s)
    p = k >> 1
    if reverse:
        p = bit_reverse(p, (n // 2).bit_length() - 1)
    put = lambda dst: pltpu.make_async_copy(src, dst.at[p, pl.ds(row0, src.shape[0])], sem)

    @pl.when(k & 1 == 0)
    def _():
        put(keep).start()

    @pl.when(k & 1 == 1)
    def _():
        put(send).start()


def ffn_body(n, meta, ch, ln, me, tok, step, vec, upb, cot, mixed, mixedt, *refs):
    np_ = len(meta)
    pieces = refs[:np_]
    out, gx1, gmt, ka, sa, kb, sb, wo, wu, wd, act, gup, h2t, gdt, gattn, sums, upsum, dn, up, gwo, vr, mtv, sems, psems = refs[np_:]
    i = pl.program_id(0)
    bm, D = tok.shape
    FF = wu.shape[1]
    r = D // n
    rf = FF // n
    nf = FF // D
    i0 = me[0]
    ro = pl.ds(mult(i * bm, 128), bm)
    first = i == 0
    seg = lambda j: (r + j * r, r, lambda s, o, c: wu.at[pl.ds(mult(s * r + o, 16), c), pl.ds(j * D, D)], D)
    seg_o = [(0, r, lambda s, o, c: wo.at[pl.ds(mult(s * r + o, 16), c)], D)]
    seg_u = [seg(j) for j in range(nf)]
    seg_d = [(r + r * nf, rf, lambda s, o, c: wd.at[pl.ds(mult(s * rf + o, 16), c)], D)]
    q = sems.shape[0] // 4
    parts = [(seg_o, sems.at[pl.ds(0, q)]), (seg_d, sems.at[pl.ds(q, q)]), (seg_u, sems.at[pl.ds(2 * q, 2 * q)])]
    load = pltpu.make_async_copy(mixedt, mtv, psems.at[psems.shape[0] - 1])

    @pl.when(first)
    def _():
        for sg, sm in parts:
            for c in pull(i0, pieces, meta, sg, sm):
                c.start()
        load.start()
        sums[...] = jnp.zeros_like(sums)
        upsum[...] = jnp.zeros_like(upsum)
        for c in pull(i0, pieces, meta, *parts[0]):
            c.wait()

    v = vec[...]
    x1 = tok[...].astype(f32) + step[...].astype(f32) + dot(mixed[...], wo[...]) + row(v, 4)
    nx, rr = norm(x1)
    h2 = (nx * row(v, 5) + row(v, 6)).astype(bf16)
    live = (lax.broadcasted_iota(jnp.int32, (bm, 1), 0) + i * bm) < ln[0]
    gd = jnp.where(live, cot[...], jnp.zeros_like(cot))
    acc = x1 + row(v, 7)
    gh = None
    nc = FF // ch
    sl = [slice(c * ch, (c + 1) * ch) for c in range(nc)]
    lead = lambda c: (dot(h2, wu[:, sl[c]]), dot_t(gd, wd[sl[c], :]))
    h2t[:, ro] = h2.T
    gdt[:, ro] = gd.T

    @pl.when(first)
    def _():
        for sg, sm in parts[1:]:
            for c in pull(i0, pieces, meta, sg, sm):
                c.wait()

    nxt = lead(0)
    for c in range(nc):
        u, ga = nxt
        nxt = lead(c + 1) if c + 1 < nc else None
        u = u + upb[:, sl[c]]
        u2 = u * u
        t = jnp.tanh(u * (f32(G0) + f32(G0 * 0.044715) * u2))
        half = 0.5 + 0.5 * t
        a = (u * half).astype(bf16)
        act[ro, sl[c]] = a
        dg = half + u * (half * (1.0 - half)) * (f32(2 * G0) + f32(6 * 0.044715 * G0) * u2)
        gu = (ga * dg).astype(bf16)
        gup[ro, sl[c]] = gu
        upsum[:, sl[c]] += jnp.sum(gu.astype(f32), axis=0, keepdims=True)
        acc = acc + dot(a, wd[sl[c], :])
        p = dot_t(gu, wu[:, sl[c]])
        gh = p if gh is None else gh + p
    out[...] = jnp.where(live, acc, 0.0).astype(bf16)
    gn = gh * row(v, 5)
    gx = gd.astype(f32) + rr * (gn - jnp.mean(gn, axis=-1, keepdims=True) - nx * jnp.mean(gn * nx, axis=-1, keepdims=True))
    gab = gx.astype(bf16)
    gx1[...] = gab
    gattn[ro, :] = gab
    gmt[...] = dot_t(gab, wo[...]).astype(bf16).T
    s_ = lambda a: jnp.sum(a.astype(f32), axis=0, keepdims=True)
    sums[...] += jnp.concatenate([s_(gab), s_(gh * nx), s_(gh), s_(gd), jnp.zeros((4, D), f32)], axis=0)

    @pl.when(i == pl.num_programs(0) - 1)
    def _():
        per = D // rf
        for j in range(nf):
            dn[j] = dot(gdt[...], act[:, j * D : (j + 1) * D]).astype(bf16).T
            for t in range(per):
                push(i0, n, j * per + t, dn.at[j, pl.ds(t * rf, rf)], ka, sa, 0, psems.at[j * per + t])
            up[j] = dot(h2t[...], gup[:, j * D : (j + 1) * D]).astype(bf16)
            for s in range(n):
                push(i0, n, s, up.at[j, pl.ds(s * r, r)], kb, sb, j * r, psems.at[n * (1 + j) + s], True)
        load.wait()
        gwo[...] = dot(mtv[...], gattn[...]).astype(bf16)
        vr[...] = jnp.concatenate([sums[0:4, :]] + [upsum[:, c * D : (c + 1) * D] for c in range(nf)] + [jnp.zeros((VROWS - 4 - nf, D), f32)], axis=0).astype(bf16)
        b = n * (1 + nf)
        for s in range(n):
            push(i0, n, s, gwo.at[pl.ds(s * r, r)], ka, sa, rf, psems.at[b + s])
            push(i0, n, s, vr, kb, sb, nf * r, psems.at[b + n + s], True)
        done = lambda src, q: pltpu.make_async_copy(src, (ka if src.shape[0] == rf else kb).at[0, pl.ds(0, src.shape[0])], psems.at[q]).wait()
        for s in range(n):
            done(dn.at[0, pl.ds(0, rf)], s)
            for c in range(nf):
                done(up.at[0, pl.ds(0, r)], n * (1 + c) + s)
            done(gwo.at[pl.ds(0, r)], b + s)
            done(vr, b + n + s)


def ffn(ln, me, tok, step, vec, upb, cot, mixed, mixedt, pieces, n):
    T, D = tok.shape
    FF = upb.shape[1]
    bm = min(512, T)
    nf = FF // D
    r = D // n
    meta = tuple((k, r0) for k, r0, _ in pieces)
    full = lambda a: pl.BlockSpec(a.shape, lambda i, l, m: (0,) * a.ndim)
    rows = pl.BlockSpec((bm, D), lambda i, l, m: (i, 0))
    A = S((n // 2, FF // n + r, D), bf16)
    B = S((n // 2, nf * r + VROWS, D), bf16)
    V = pltpu.VMEM
    return pl.pallas_call(
        functools.partial(ffn_body, n, meta, min(1024, FF)),
        grid_spec=pltpu.PrefetchScalarGridSpec(
            num_scalar_prefetch=2, grid=(T // bm,),
            in_specs=[rows, full(step), full(vec), full(upb), rows, rows, ANY] + [ANY] * len(pieces),
            out_specs=[rows, rows, pl.BlockSpec((D, bm), lambda i, l, m: (0, i))] + [ANY] * 4,
            scratch_shapes=[V((D, D), bf16), V((D, FF), bf16), V((FF, D), bf16), V((T, FF), bf16), V((T, FF), bf16), V((D, T), bf16), V((D, T), bf16), V((T, D), bf16), V((8, D), f32), V((1, FF), f32), V((nf, D, D), bf16), V((nf, D, D), bf16), V((D, D), bf16), V((VROWS, D), bf16), V((D, T), bf16), pltpu.SemaphoreType.DMA((16 * len(pieces),)), pltpu.SemaphoreType.DMA((n * (nf + 3) + 1,))]),
        out_shape=[S((T, D), bf16), S((T, D), bf16), S((D, T), bf16), A, A, B, B],
        compiler_params=cp(49), name="ffn", cost_estimate=cost(2 * T * D * (6 * FF + 3 * D), 16 * T * D, T * FF),
    )(ln, me, tok, step, vec, upb, cot, mixed, mixedt, *[a for _, _, a in pieces])


def attn_bwd_body(HD, scale, CR, v, kt, qt, gt, mt, linv, et, *refs):
    gq, ds = refs[-2:]
    T = v.shape[0]
    rid = lax.broadcasted_iota(jnp.int32, gt.shape, 0) // HD
    g = gt[...].astype(f32)
    q = qt[...]
    gv = gk = None
    for h in range(2):
        hs = slice(h * HD, (h + 1) * HD)
        gs = (g * linv[h : h + 1, :]).astype(bf16)
        gm = jnp.where(rid == h, gs, jnp.zeros_like(gs))
        dl = jnp.sum(gs[hs, :].astype(f32) * mt[hs, :], axis=0, keepdims=True)
        for c in range(T // CR):
            cs = slice(c * CR, (c + 1) * CR)
            ds[h, cs, :] = (et[h, cs, :].astype(f32) * (dot(v[cs, :], gm) - dl)).astype(bf16)
        a = dot(et[h], gm.T)
        b = dot(ds[h], jnp.where(rid == h, q, jnp.zeros_like(q)).T)
        gv = a if gv is None else gv + a
        gk = b if gk is None else gk + b
        gq[0, hs, :] = (dot(kt[hs, :], ds[h]) * scale).astype(bf16)
    gq[2] = gv.astype(bf16).T
    gq[1] = gk.astype(bf16).T


def attn_bwd(kv, qkvt, gmt, mixedf, linv, et, p0, cnt, prev):
    _, T, D = kv.shape
    HD = D // HEADS
    PW = 2 * HD
    NP = D // PW
    prev = list(prev)
    pr = pl.BlockSpec((PW, T), lambda p: (p0 + p, 0))
    of = lambda j: pl.BlockSpec((None, PW, T), lambda p: (j, p0 + p, 0))
    return pl.pallas_call(
        functools.partial(attn_bwd_body, HD, 1.0 / math.sqrt(HD), min(256, T)),
        grid=(cnt,),
        scratch_shapes=[pltpu.VMEM((2, T, T), bf16)],
        in_specs=[pl.BlockSpec((None, T, PW), lambda p: (1, 0, p0 + p)), of(1), of(0), pr, pr, pl.BlockSpec((None, 8, T), lambda p: (p0 + p, 0, 0)), pl.BlockSpec((2, T, T), lambda p: (p0 + p, 0, 0))] + [ANY] * len(prev),
        out_specs=pl.BlockSpec((3, PW, T), lambda p: (0, p0 + p, 0)),
        out_shape=S((3, D, T), bf16),
        input_output_aliases={7: 0} if prev else {},
        compiler_params=cp(), name="attn_bwd", cost_estimate=cost(cnt * 2 * 16 * T * T * 128, cnt * 2 * T * T * 2),
    )(kv, qkvt, qkvt, gmt, mixedf, linv, et, *prev)


def wqkv_body(n, me, xht, g, keep, send, res, vr, sems):
    j = pl.program_id(0)
    D = g.shape[0]
    r = D // n
    i0 = me[0]
    y = dot_t(xht[...], g[...]).astype(bf16)
    res[j] = y[:D]
    vr[...] = jnp.where(lax.broadcasted_iota(jnp.int32, vr.shape, 0) == j, y[D:], jnp.where(j == 0, jnp.zeros_like(y[D:]), vr[...]))
    for s in range(n):
        push(i0, n, s, res.at[j, pl.ds(s * r, r)], keep, send, mult(j * r, 16), sems.at[j * n + s])

    @pl.when(j == 2)
    def _():
        for s in range(n):
            push(i0, n, s, vr, keep, send, 3 * r, sems.at[3 * n + s])
        for s in range(n):
            for q in range(3):
                pltpu.make_async_copy(res.at[0, pl.ds(0, r)], keep.at[0, pl.ds(0, r)], sems.at[q * n + s]).wait()
            pltpu.make_async_copy(vr, keep.at[0, pl.ds(0, VROWS)], sems.at[3 * n + s]).wait()


def wqkv(me, xht, g, n):
    _, D, T = g.shape
    A = S((n // 2, 3 * (D // n) + VROWS, D), bf16)
    return pl.pallas_call(
        functools.partial(wqkv_body, n),
        grid_spec=pltpu.PrefetchScalarGridSpec(
            num_scalar_prefetch=1, grid=(3,),
            in_specs=[pl.BlockSpec((D + 16, T), lambda j, m: (0, 0)), pl.BlockSpec((None, D, T), lambda j, m: (j, 0, 0))],
            out_specs=[ANY] * 2,
            scratch_shapes=[pltpu.VMEM((3, D, D), bf16), pltpu.VMEM((VROWS, D), bf16), pltpu.SemaphoreType.DMA((4 * n,))]),
        out_shape=[A, A],
        compiler_params=cp(), name="wqkv", cost_estimate=cost(6 * T * D * D, 10 * T * D),
    )(me, xht, g)


def back_body(tok, step, vec, g, gx1, *refs):
    ws, tg = refs[:-1], refs[-1]
    D = tok.shape[1]
    gw = D // GROUPS
    x = tok[...].astype(f32) + step[...].astype(f32)
    nx, rr = norm(x)
    gt = sum(dot(w[:, j * gw : (j + 1) * gw], g[j, q * gw : (q + 1) * gw, :]) for q, w in enumerate(ws) for j in range(3))
    gn = gt.T * row(vec[...], 0)
    tg[...] = gx1[...].astype(f32) + rr * (gn - jnp.mean(gn, axis=-1, keepdims=True) - nx * jnp.mean(gn * nx, axis=-1, keepdims=True))


def back(tok, step, vec, ws, g, gx1, bm=512):
    T, D = tok.shape
    full = lambda a: pl.BlockSpec(a.shape, lambda i: (0,) * a.ndim)
    rows = pl.BlockSpec((bm, D), lambda i: (i, 0))
    return pl.pallas_call(
        back_body, grid=(T // bm,),
        in_specs=[rows, full(step), full(vec), pl.BlockSpec((3, D, bm), lambda i: (0, 0, i)), rows] + [full(w) for w in ws],
        out_specs=rows, out_shape=S((T, D), f32), compiler_params=cp(), name="back", cost_estimate=cost(6 * T * D * D, 14 * T * D),
    )(tok, step, vec, g, gx1, *ws)


def shards(tokens, step_embed, lengths, cotangent, ln1_gain, ln1_bias, qkv_weight, q_bias, v_bias, out_weight, out_bias, ln2_gain, ln2_bias, up_weight, up_bias, down_weight, down_bias):
    n = lax.axis_size("shard")
    me = lax.axis_index("shard").astype(jnp.int32)
    mes = me[None]
    tok, cot, step = tokens[0], cotangent[0], step_embed
    T, D = tok.shape
    r = D // n
    FF = up_bias.shape[0] * n
    nc = FF // D
    rf = FF // n
    packs = pack_first(mes, qkv_weight, [ln1_gain, ln1_bias, q_bias, v_bias, out_bias, ln2_gain, ln2_bias, down_bias], up_bias)
    pack2 = pack_rest(out_weight, up_weight, down_weight)
    NP = HEADS // 2
    nx, xht = start(tok, step)
    pieces = gather_direct(packs[0], n, xht, pack2)
    kv, qkvt, w, vec, upb = front(mes, nx, pieces, n, FF)
    et, mixed, mixedt, mixedf, linv = attn_fwd(lengths, kv, qkvt, 0, NP, [])
    pieces2 = gather_direct(after(pack2, xht), n, linv)
    out, gx1, gmt, ka, sa, kb, sb = ffn(lengths, mes, tok, step, vec, upb, cot, mixed, mixedt, pieces2, n)
    bwd = lambda p, c, g, *deps: attn_bwd(kv, qkvt, after(gmt, *deps) if deps else gmt, mixedf, linv, et, p, c, g)
    ga, gb = swap(sa, 1), swap(sb, 1)
    g = bwd(0, 1, [])
    ga, gb, _ = lax.optimization_barrier((ga, gb, g))
    h = n // 4
    lo, hi = slice(0, h), slice(h, None)
    add = lambda a, b, s: add16(a[s], b[s])
    ka, xa = add(ka, ga, lo), add(ka, ga, hi)
    kb, gb, _ = lax.optimization_barrier((kb, gb, xa))
    kb, xb = add(kb, gb, lo), add(kb, gb, hi)
    g = bwd(1, NP - 1, [g], ka, xa, kb, xb)
    m = (n // 2).bit_length() - 1
    ga, gb = swap(xa, 2 << (m - 1)), swap(xb, 2)
    for t in range(1, m):
        dep = g if t == 1 else keep
        ga, gb, _ = lax.optimization_barrier((ga, gb, dep))
        h //= 2
        lo, hi = slice(0, h), slice(h, None)
        ka, xa = add(ka, ga, lo), add(ka, ga, hi)
        kb, gb, _ = lax.optimization_barrier((kb, gb, xa))
        kb, xb = add(kb, gb, lo), add(kb, gb, hi)
        ga, gb = swap(xa, 2 << (m - 1 - t)), swap(xb, 2 << t)
        if t == 1:
            keep, send = wqkv(mes, after(xht, ka, xa, kb, xb), g, n)
    got = swap(send, 1)
    p2 = [add16(keep[k], got[k]) for k in range(n // 2)]
    far2 = spread(p2)
    ga, gb, _ = lax.optimization_barrier((ga, gb, keep))
    got = swap(send, 1)
    p2 = [add16(keep[k], got[k]) for k in range(n // 2)]
    far2 = spread(p2)
    own1 = jnp.concatenate([add16(ka, ga)[0], add16(kb, gb)[0]], axis=0)
    m1, o1, x1 = rep_half(own1)
    z1 = add16(m1, after(o1, *p2[1:]))
    tg = back(tok, after(step, z1, *p2[1:]), vec, [w], g, gx1)
    own2 = total(p2[0], [after(a, tg) for a in far2])
    m2, o2, x2 = rep_half(own2)
    steps = rep_steps()
    z2 = None if steps else add16(m2, o2)
    for b in steps:
        z1 = add16(z1, after(rep_perm(z1, b), x2))
        if z2 is None:
            z2 = add16(m2, after(o2, z1))
        pz = rep_perm(z2, b)
        z2 = add16(z2, after(pz, z1))
    o1, o2 = rep_perm(z1, 1), rep_perm(z2, 1)
    ids = jnp.stack([me, (lax.axis_index("rep") % 2).astype(jnp.int32)])
    g_down, g_up, g_out, g_upb, g_ob, g_g2, g_b2, g_db = finish_rest(ids, z1, o1, r, rf, nc, n)
    g_qkv, g_g1, g_b1, g_q, g_v = finish_first(ids, z2, after(o2, g_out), qkv_weight, ln1_gain, ln1_bias)
    flat = lambda a: a.reshape(-1)
    return (out[None], tg[None], flat(g_g1), flat(g_b1), g_qkv, flat(g_q), flat(g_v), g_out, flat(g_ob), flat(g_g2), flat(g_b2), g_up, flat(g_upb), g_down, flat(g_db))


def solution(mesh):
    from jax.sharding import PartitionSpec as P

    in_specs = (
        P(("rep", "shard"), None, None),
        P(("rep", "shard"), None),
        P(("rep", "shard")),
        P(("rep", "shard"), None, None),
        P("shard"),
        P("shard"),
        P("shard", None),
        P("shard"),
        P("shard"),
        P("shard", None),
        P("shard"),
        P("shard"),
        P("shard"),
        P("shard", None),
        P("shard"),
        P("shard", None),
        P("shard"),
    )
    out_specs = (
        P(("rep", "shard"), None, None),
        P(("rep", "shard"), None, None),
        P("shard"),
        P("shard"),
        P("shard", None),
        P("shard"),
        P("shard"),
        P("shard", None),
        P("shard"),
        P("shard"),
        P("shard"),
        P("shard", None),
        P("shard"),
        P("shard", None),
        P("shard"),
    )
    return jax.shard_map(shards, mesh=mesh, in_specs=in_specs, out_specs=out_specs, check_vma=False)
```

```python
import functools, math
import jax, jax.numpy as jnp
from jax import lax
from jax.experimental import pallas as pl
from jax.experimental.pallas import tpu as pltpu

f32 = jnp.float32
bf16 = jnp.bfloat16
EPS = 1e-05
HEADS = 8

def dot(a, b):
    return jnp.dot(a, b, preferred_element_type=f32)

def dot_t(a, b):
    return lax.dot_general(a, b, (((1,), (1,)), ((), ())), preferred_element_type=f32)

def cp(mib=60):
    return pltpu.CompilerParams(dimension_semantics=("arbitrary",), vmem_limit_bytes=mib << 20)

def norm(x):
    c = x - jnp.mean(x, axis=-1, keepdims=True)
    r = lax.rsqrt(jnp.mean(c * c, axis=-1, keepdims=True) + EPS)
    return c * r, r

def row(v, i):
    return v[i : i + 1, :].astype(f32)


VROWS = 16
LANES = 128


def xor_perm(n, k):
    return [(i, i ^ k) for i in range(n)]


def rep_perm(x, b):
    return lax.ppermute(x, "rep", xor_perm(lax.axis_size("rep"), b))


def swap(x, k):
    return lax.ppermute(x, "shard", xor_perm(lax.axis_size("shard"), k))


def after(x, *deps):
    return lax.optimization_barrier((x,) + deps)[0]


def gather_direct(x, n, *gate):
    out = [(0, 0, x)]
    far = [(k, swap(x, k)) for k in range(2, n, 2)]
    out += [(k, 0, after(y, *gate) if gate else y) for k, y in far]
    return out + [(k ^ 1, 0, swap(y, 1)) for k, _, y in out]


def add16(a, b):
    return a + b


def spread(parts):
    return [swap(parts[k], 2 * k) for k in range(len(parts) - 1, 0, -1)]


def total(own, got):
    t = own.astype(f32)
    for a in got:
        t = t + a.astype(f32)
    return t.astype(bf16)


def rep_half(x):
    h = x.shape[0] // 2
    odd = lax.axis_index("rep") % 2
    mine = lax.dynamic_slice_in_dim(x, odd * h, h, 0)
    other = lax.dynamic_slice_in_dim(x, (1 - odd) * h, h, 0)
    return mine, rep_perm(other, 1), other


def rep_steps():
    nr = lax.axis_size("rep")
    return [b for b in (2 << i for i in range(16)) if b < nr]


GROUPS = 1


def pack_first_body(me, w, upb, *refs):
    vecs = refs[:-GROUPS]
    outs = refs[-GROUPS:]
    r, W = w.shape
    D = W // 3
    gw = D // GROUPS
    for g, out in enumerate(outs):
        for j in range(3):
            out[j * r : (j + 1) * r, :] = w[:, j * D + g * gw : j * D + (g + 1) * gw]

    def spot(v):
        w_ = v.shape[1]
        if w_ >= LANES:
            return [v[q : q + 1, :] for q in range(v.shape[0])]
        t = LANES // w_
        lane = lax.broadcasted_iota(jnp.int32, (1, LANES), 1)
        return [jnp.where(lane // w_ == me[0] % t, jnp.concatenate([v] * t, axis=1), jnp.zeros((1, LANES), f32))]

    rows = [a for v in vecs for a in spot(v[...].astype(f32))] + spot(upb[...].astype(f32))
    b = jnp.concatenate(rows + [jnp.zeros((VROWS - len(rows), LANES), f32)], axis=0).astype(bf16)
    outs[0][3 * r :, :] = jnp.concatenate([b, jnp.zeros((VROWS, gw - LANES), bf16)], axis=1) if gw > LANES else b


def whole(n):
    return [pl.BlockSpec(memory_space=pltpu.VMEM)] * n


def once(*arrays):
    return [pl.BlockSpec(a.shape, lambda i, *m, nd=len(a.shape): (0,) * nd) for a in arrays]


def pack_first(me, w, vecs, upb):
    r, W = w.shape
    gw = W // 3 // GROUPS
    lanes = lambda v: v.reshape(-1, min(LANES, v.shape[0]))
    args = [w] + [lanes(v) for v in [upb] + vecs]
    outs = [S((3 * r + (VROWS if g == 0 else 0), gw), bf16) for g in range(GROUPS)]
    return pl.pallas_call(
        pack_first_body,
        grid_spec=pltpu.PrefetchScalarGridSpec(num_scalar_prefetch=1, grid=(1,), in_specs=once(*args), out_specs=once(*outs)),
        out_shape=outs, compiler_params=cp(), name="pack_first", cost_estimate=cost(0, 4 * w.size),
    )(me, *args)


def pack_rest_body(wo, wu, wd, out):
    r, D = wo.shape
    out[:r, :] = wo[...]
    for j in range(wu.shape[1] // D):
        out[(1 + j) * r : (2 + j) * r, :] = wu[:, j * D : (j + 1) * D]
    out[(1 + wu.shape[1] // D) * r :, :] = wd[...]


def pack_rest(wo, wu, wd):
    D = wo.shape[1]
    out = S(((wo.size + wu.size + wd.size) // D, D), bf16)
    return pl.pallas_call(
        pack_rest_body, grid=(1,), in_specs=once(wo, wu, wd), out_specs=once(out)[0],
        out_shape=out, compiler_params=cp(), name="pack_rest", cost_estimate=cost(0, 4 * wu.size),
    )(wo, wu, wd)


def own_lanes(tiles, me, w):
    pick = lambda i: sum(jnp.where(i == t, a, jnp.zeros_like(a)) for t, a in enumerate(tiles))
    if w >= LANES:
        q = w // LANES
        return jnp.concatenate([pick(me * q + c) for c in range(q)], axis=1)
    per = LANES // w
    x = pick(me // per)
    off = me % per
    return sum(jnp.where(off == o, x[:, o * w : (o + 1) * w], 0.0) for o in range(per))


def rows_of(lo, hi, a, b):
    h = lo.shape[0]
    if b <= h:
        return lo[a:b, :]
    if a >= h:
        return hi[a - h : b - h, :]
    return jnp.concatenate([lo[a:h, :], hi[: b - h, :]], axis=0)


def finish_rest_body(r, rf, n, ids, s, o, down, up, out, upb, *vecs):
    D = out.shape[1]
    nf = up.shape[1] // D

    def run(lo, hi):
        f = lambda a, b: rows_of(lo, hi, a, b).astype(f32)
        down[...] = f(0, rf)
        out[...] = f(rf, rf + r)
        for j in range(nf):
            up[:, j * D : (j + 1) * D] = f(rf + (j + 1) * r, rf + (j + 2) * r)
        b = rf + (nf + 1) * r
        v = f(b, b + VROWS)
        me = ids[0]
        tiles = [v[0:8, t * LANES : (t + 1) * LANES] for t in range(D // LANES)]
        x = own_lanes(tiles, me, r)
        for q, ref in enumerate(vecs):
            ref[...] = x[q : q + 1, :]
        tiles = [v[4 + q : 5 + q, t * LANES : (t + 1) * LANES] for q in range(nf) for t in range(D // LANES)]
        upb[...] = own_lanes(tiles, me, nf * D // n)

    @pl.when(ids[1] == 0)
    def _():
        run(s, o)

    @pl.when(ids[1] == 1)
    def _():
        run(o, s)


def finish_rest(ids, s, o, r, rf, nf, n):
    D = s.shape[1]
    row1 = lambda w: S((1, w), f32)
    return pl.pallas_call(
        functools.partial(finish_rest_body, r, rf, n),
        in_specs=[pl.BlockSpec(memory_space=pltpu.SMEM)] + whole(2), out_specs=whole(8),
        out_shape=[S((rf, D), f32), S((r, nf * D), f32), S((r, D), f32), row1(nf * D // n)] + [row1(r)] * 4,
        compiler_params=pltpu.CompilerParams(vmem_limit_bytes=16 << 20), name="finish_rest", cost_estimate=cost(0, 8 * s.size),
    )(ids, s, o)


def finish_first_body(ids, s, o, w, gain, bias, qkv, gg, gb, qb, vb):
    r, W = w.shape
    D = s.shape[1]

    def run(lo, hi):
        f = lambda a, b: rows_of(lo, hi, a, b).astype(f32)
        v = f(3 * r, 3 * r + VROWS)
        nt = D // LANES
        accg = accb = jnp.zeros((r, LANES), f32)
        col = lambda g: jnp.concatenate([g[...].astype(f32), jnp.zeros((7, r), f32)], axis=0).T[:, 0:1]
        cg, cb = col(gain), col(bias)
        for j in range(3):
            m = f(j * r, (j + 1) * r)
            sq = v[j : j + 1, :]
            ww = w[:, j * D : (j + 1) * D].astype(f32)
            qkv[:, j * D : (j + 1) * D] = cg * m + cb * sq
            pg, pb = ww * m, ww * sq
            accg = accg + sum(pg[:, t * LANES : (t + 1) * LANES] for t in range(nt))
            accb = accb + sum(pb[:, t * LANES : (t + 1) * LANES] for t in range(nt))
        gg[...] = jnp.sum(accg.T, axis=0, keepdims=True)
        gb[...] = jnp.sum(accb.T, axis=0, keepdims=True)
        x = own_lanes([v[0:8, t * LANES : (t + 1) * LANES] for t in range(nt)], ids[0], r)
        qb[...] = x[0:1, :]
        vb[...] = x[2:3, :]

    @pl.when(ids[1] == 0)
    def _():
        run(s, o)

    @pl.when(ids[1] == 1)
    def _():
        run(o, s)


def finish_first(ids, s, o, w, gain, bias):
    r, W = w.shape
    return pl.pallas_call(
        finish_first_body,
        in_specs=[pl.BlockSpec(memory_space=pltpu.SMEM)] + whole(5), out_specs=whole(5),
        out_shape=[S((r, W), f32)] + [S((1, r), f32)] * 4,
        compiler_params=pltpu.CompilerParams(vmem_limit_bytes=16 << 20), name="finish_first", cost_estimate=cost(0, 8 * w.size),
    )(ids, s, o, w, gain[None], bias[None])


def pull(me, refs, meta, segs, sems):
    copies = []
    for ref, (k, r0) in zip(refs, meta):
        s = jnp.bitwise_xor(me, k)
        r1 = r0 + ref.shape[0]
        for a, c, dst, lanes in segs:
            lo, hi = max(a, r0), min(a + c, r1)
            if lo < hi:
                src = ref.at[pl.ds(lo - r0, hi - lo), pl.ds(0, lanes)]
                copies.append(pltpu.make_async_copy(src, dst(s, lo - a, hi - lo), sems.at[len(copies)]))
    return copies


def mult(x, m):
    return pl.multiple_of(x, m)


def weight_segs(w, r):
    gw = w.shape[1] // 3
    seg = lambda j: (j * r, r, lambda s, o, c: w.at[pl.ds(mult(s * r + o, 16), c), pl.ds(j * gw, gw)], gw)
    return [seg(j) for j in range(3)]


def start_body(tok, step, nx, xht):
    n, _ = norm(tok[...].astype(f32) + step[...].astype(f32))
    D = tok.shape[1]
    nx[...] = n
    xht[:D, :] = n.astype(bf16).T
    xht[D:, :] = jnp.ones((16, tok.shape[0]), bf16)


def start(tok, step, bm=256):
    T, D = tok.shape
    rows = pl.BlockSpec((bm, D), lambda i: (i, 0))
    return pl.pallas_call(
        start_body, grid=(T // bm,),
        in_specs=[rows, pl.BlockSpec((1, D), lambda i: (0, 0))], out_specs=[rows, pl.BlockSpec((D + 16, bm), lambda i: (0, i))],
        out_shape=[S((T, D), f32), S((D + 16, T), bf16)], compiler_params=cp(), name="start", cost_estimate=cost(20 * T * D, 8 * T * D),
    )(tok, step)


def front_body(scale, n, meta, me, nx, *refs):
    np_ = len(meta)
    pieces = refs[:np_]
    kv, qkvt, wout, vec, upb, nv, h, w, vbuf, sems, own = refs[np_:]
    T, D = nv.shape
    r = D // n
    FF = upb.shape[1]
    i = pl.program_id(0)
    cw = kv.shape[2]
    per_j = D // cw
    segs = [(3 * r, VROWS, lambda s, o, c: vbuf.at[s, pl.ds(o, c)], LANES)] + weight_segs(w, r)
    load = pltpu.make_async_copy(nx, nv, own.at[0])
    save = pltpu.make_async_copy(w, wout, own.at[1])

    @pl.when(i == 0)
    def _():
        cs = pull(me[0], pieces, meta, segs, sems)
        for c in cs:
            c.start()
        load.start()
        for c in cs:
            c.wait()
        save.start()
        per = LANES // r
        tiles = [sum(vbuf[s, 0:8, :].astype(f32) for s in range(t * per, (t + 1) * per)) for t in range(D // LANES)]
        vec[...] = jnp.concatenate(tiles, axis=1)
        wu = FF // n
        if wu >= LANES:
            rows = [vbuf[s, 8 + q : 9 + q, :].astype(f32) for s in range(n) for q in range(wu // LANES)]
        else:
            per = LANES // wu
            rows = [sum(vbuf[s, 8:9, :].astype(f32) for s in range(t * per, (t + 1) * per)) for t in range(FF // LANES)]
        upb[...] = jnp.concatenate(rows, axis=1)
        load.wait()
        v = vec[...]
        h[...] = (nv[...] * row(v, 0) + row(v, 1)).astype(bf16)

    cols = pl.ds(mult(i * cw, 128), cw)
    y = dot(h[...], w[:, cols])
    here = pl.ds(mult((i % per_j) * cw, 128), cw)
    kind = i // per_j
    y = (y + jnp.where(kind == 0, vec[2:3, here], jnp.where(kind == 2, vec[3:4, here], 0.0))).astype(bf16)
    kv[0] = y
    qkvt[0] = jnp.where(kind == 0, y * bf16(scale), y).T

    @pl.when(i == pl.num_programs(0) - 1)
    def _():
        save.wait()


S = jax.ShapeDtypeStruct
ANY = pl.BlockSpec(memory_space=pl.ANY)


def cost(flops, nbytes, tr=0):
    return pl.CostEstimate(flops=int(flops), bytes_accessed=int(nbytes), transcendentals=int(tr))


def front(me, nx, pieces, n, FF, cw=512):
    T, D = nx.shape
    scale = 1.0 / math.sqrt(D // HEADS)
    meta = tuple((k, r0) for k, r0, _ in pieces)
    q = D // cw
    keep = lambda *sh: pl.BlockSpec(sh, lambda i, m: (0,) * len(sh))
    rest = lambda i: jnp.maximum(i - q, 0)
    V = pltpu.VMEM
    return pl.pallas_call(
        functools.partial(front_body, scale, n, meta),
        grid_spec=pltpu.PrefetchScalarGridSpec(
            num_scalar_prefetch=1, grid=(3 * q,),
            in_specs=[ANY] * (1 + len(pieces)),
            out_specs=[pl.BlockSpec((1, T, cw), lambda i, m: (rest(i) // q, 0, rest(i) % q)), pl.BlockSpec((1, cw, T), lambda i, m: (i // q, i % q, 0)), ANY, keep(8, D), keep(1, FF)],
            scratch_shapes=[V((T, D), f32), V((T, D), bf16), V((D, 3 * D), bf16), V((n, VROWS, LANES), bf16), pltpu.SemaphoreType.DMA((8 * len(pieces),)), pltpu.SemaphoreType.DMA((2,))]),
        out_shape=[S((2, T, D), bf16), S((3, D, T), bf16), S((D, 3 * D), bf16), S((8, D), f32), S((1, FF), f32)],
        compiler_params=cp(), name="front", cost_estimate=cost(6 * T * D * D, 12 * T * D),
    )(me, nx, *[a for _, _, a in pieces])


def attn_fwd_body(HD, bi, CR, p0, ln, k, qt, vt, *refs):
    et, mixed, mixedt, mixedf, linv, scr, ka, eb, esem = refs[-9:]
    T, PW = k.shape
    n = ln[0]
    p = pl.program_id(0)
    last = p == pl.num_programs(0) - 1
    rid = lax.broadcasted_iota(jnp.int32, (PW, bi), 0)
    lane = lax.broadcasted_iota(jnp.int32, (T, PW), 1)
    rows = lax.broadcasted_iota(jnp.int32, (T, PW), 0)
    ka[:, :PW] = k[...]
    ka[:, PW:] = jnp.where((lane == 0) & (rows >= n), f32(-1e30), f32(0)).astype(bf16)
    ones = jnp.where(rid == 0, f32(1), f32(0)).astype(bf16)
    va = [jnp.concatenate([vt[h * HD : (h + 1) * HD, :], jnp.ones((16, T), bf16)], axis=0) for h in range(2)]
    tasks = [(b, h) for b in range(T // bi) for h in range(2)]
    nch = T // CR

    def query(t):
        b, h = tasks[t]
        q = qt[:, b * bi : (b + 1) * bi]
        return jnp.concatenate([jnp.where(rid // HD == h, q, jnp.zeros_like(q)), ones], axis=0)

    def score(t, c, q):
        s = dot(ka[c * CR : (c + 1) * CR, :], q)
        scr[t % 2, c * CR : (c + 1) * CR, :] = s
        return jnp.max(s, axis=0, keepdims=True)

    q = query(0)
    m = functools.reduce(jnp.maximum, [score(0, c, q) for c in range(nch)])
    half = None
    for t, (b, h) in enumerate(tasks):
        sl = slice(b * bi, (b + 1) * bi)
        more = t + 1 < len(tasks)
        put = pltpu.make_async_copy(eb.at[t % 2], et.at[2 * (p0 + p) + h, :, pl.ds(b * bi, bi)], esem.at[t % 2])
        if t < 2:

            @pl.when(p > 0)
            def _():
                put.wait()

        else:
            put.wait()
        if more:
            q = query(t + 1)
        nxt = []
        for c in range(nch):
            cs = slice(c * CR, (c + 1) * CR)
            if more:
                nxt.append(score(t + 1, c, q))
            eb[t % 2, cs, :] = jnp.exp(scr[t % 2, cs, :] - m).astype(bf16)
        put.start()
        o = dot(va[h], eb[t % 2])
        if more:
            m = functools.reduce(jnp.maximum, nxt)
        inv = 1.0 / o[HD : HD + 1, :]
        linv[h : h + 1, sl] = inv
        o = o[:HD, :] * inv
        if h == 0:
            half = o
        else:
            mt = jnp.concatenate([half, o], axis=0)
            mixedf[:, sl] = mt
            mt = mt.astype(bf16)
            mixedt[:, sl] = mt
            mixed[sl, :] = mt.T

    @pl.when(last)
    def _():
        for q in range(2):
            pltpu.make_async_copy(eb.at[q], et.at[0, :, pl.ds(0, bi)], esem.at[q]).wait()


def attn_fwd(ln, kv, qkvt, p0, cnt, prev):
    _, T, D = kv.shape
    HD = D // HEADS
    PW = 2 * HD
    NP = D // PW
    bi = T
    prev = list(prev)
    return pl.pallas_call(
        functools.partial(attn_fwd_body, HD, bi, min(512, T), p0),
        grid_spec=pltpu.PrefetchScalarGridSpec(
            num_scalar_prefetch=1, grid=(cnt,),
            in_specs=[pl.BlockSpec((None, T, PW), lambda p, r: (0, 0, p0 + p)), pl.BlockSpec((None, PW, T), lambda p, r: (0, p0 + p, 0)), pl.BlockSpec((None, PW, T), lambda p, r: (2, p0 + p, 0))] + [ANY] * len(prev),
            out_specs=[ANY, pl.BlockSpec((T, PW), lambda p, r: (0, p0 + p)), pl.BlockSpec((PW, T), lambda p, r: (p0 + p, 0)), pl.BlockSpec((PW, T), lambda p, r: (p0 + p, 0)), pl.BlockSpec((None, 8, T), lambda p, r: (p0 + p, 0, 0))],
            scratch_shapes=[pltpu.VMEM((2, T, bi), f32), pltpu.VMEM((T, 2 * PW), bf16), pltpu.VMEM((2, T, bi), bf16), pltpu.SemaphoreType.DMA((2,))]),
        out_shape=[S((HEADS, T, T), bf16), S((T, D), bf16), S((D, T), bf16), S((D, T), f32), S((NP, 8, T), f32)],
        input_output_aliases={4 + i: i for i in range(len(prev))},
        compiler_params=cp(), name="attn_fwd", cost_estimate=cost(cnt * 2 * 8 * T * T * 128, cnt * 2 * T * T * 2, cnt * 2 * T * T),
    )(ln, kv, qkvt, qkvt, *prev)


G0 = math.sqrt(2 / math.pi)


def bit_reverse(x, m):
    y = jnp.zeros_like(x)
    for t in range(m):
        y = y | (((x >> t) & 1) << (m - 1 - t))
    return y


def push(me, n, s, src, keep, send, row0, sem, reverse=False):
    k = jnp.bitwise_xor(me, s)
    p = k >> 1
    if reverse:
        p = bit_reverse(p, (n // 2).bit_length() - 1)
    put = lambda dst: pltpu.make_async_copy(src, dst.at[p, pl.ds(row0, src.shape[0])], sem)

    @pl.when(k & 1 == 0)
    def _():
        put(keep).start()

    @pl.when(k & 1 == 1)
    def _():
        put(send).start()


def ffn_body(n, meta, ch, ln, me, tok, step, vec, upb, cot, mixed, mixedt, *refs):
    np_ = len(meta)
    pieces = refs[:np_]
    out, gx1, gmt, ka, sa, kb, sb, wo, wu, wd, act, gup, h2t, gdt, gattn, sums, upsum, dn, up, gwo, vr, mtv, sems, psems = refs[np_:]
    i = pl.program_id(0)
    bm, D = tok.shape
    FF = wu.shape[1]
    r = D // n
    rf = FF // n
    nf = FF // D
    i0 = me[0]
    ro = pl.ds(mult(i * bm, 128), bm)
    first = i == 0
    seg = lambda j: (r + j * r, r, lambda s, o, c: wu.at[pl.ds(mult(s * r + o, 16), c), pl.ds(j * D, D)], D)
    seg_o = [(0, r, lambda s, o, c: wo.at[pl.ds(mult(s * r + o, 16), c)], D)]
    seg_u = [seg(j) for j in range(nf)]
    seg_d = [(r + r * nf, rf, lambda s, o, c: wd.at[pl.ds(mult(s * rf + o, 16), c)], D)]
    q = sems.shape[0] // 4
    parts = [(seg_o, sems.at[pl.ds(0, q)]), (seg_d, sems.at[pl.ds(q, q)]), (seg_u, sems.at[pl.ds(2 * q, 2 * q)])]
    load = pltpu.make_async_copy(mixedt, mtv, psems.at[psems.shape[0] - 1])

    @pl.when(first)
    def _():
        for sg, sm in parts:
            for c in pull(i0, pieces, meta, sg, sm):
                c.start()
        load.start()
        sums[...] = jnp.zeros_like(sums)
        upsum[...] = jnp.zeros_like(upsum)
        for c in pull(i0, pieces, meta, *parts[0]):
            c.wait()

    v = vec[...]
    x1 = tok[...].astype(f32) + step[...].astype(f32) + dot(mixed[...], wo[...]) + row(v, 4)
    nx, rr = norm(x1)
    h2 = (nx * row(v, 5) + row(v, 6)).astype(bf16)
    live = (lax.broadcasted_iota(jnp.int32, (bm, 1), 0) + i * bm) < ln[0]
    gd = jnp.where(live, cot[...], jnp.zeros_like(cot))
    acc = x1 + row(v, 7)
    gh = None
    nc = FF // ch
    sl = [slice(c * ch, (c + 1) * ch) for c in range(nc)]
    lead = lambda c: (dot(h2, wu[:, sl[c]]), dot_t(gd, wd[sl[c], :]))
    h2t[:, ro] = h2.T
    gdt[:, ro] = gd.T

    @pl.when(first)
    def _():
        for sg, sm in parts[1:]:
            for c in pull(i0, pieces, meta, sg, sm):
                c.wait()

    nxt = lead(0)
    for c in range(nc):
        u, ga = nxt
        nxt = lead(c + 1) if c + 1 < nc else None
        u = u + upb[:, sl[c]]
        u2 = u * u
        t = jnp.tanh(u * (f32(G0) + f32(G0 * 0.044715) * u2))
        half = 0.5 + 0.5 * t
        a = (u * half).astype(bf16)
        act[ro, sl[c]] = a
        dg = half + u * (half * (1.0 - half)) * (f32(2 * G0) + f32(6 * 0.044715 * G0) * u2)
        gu = (ga * dg).astype(bf16)
        gup[ro, sl[c]] = gu
        upsum[:, sl[c]] += jnp.sum(gu.astype(f32), axis=0, keepdims=True)
        acc = acc + dot(a, wd[sl[c], :])
        p = dot_t(gu, wu[:, sl[c]])
        gh = p if gh is None else gh + p
    out[...] = jnp.where(live, acc, 0.0).astype(bf16)
    gn = gh * row(v, 5)
    gx = gd.astype(f32) + rr * (gn - jnp.mean(gn, axis=-1, keepdims=True) - nx * jnp.mean(gn * nx, axis=-1, keepdims=True))
    gab = gx.astype(bf16)
    gx1[...] = gab
    gattn[ro, :] = gab
    gmt[...] = dot_t(gab, wo[...]).astype(bf16).T
    s_ = lambda a: jnp.sum(a.astype(f32), axis=0, keepdims=True)
    sums[...] += jnp.concatenate([s_(gab), s_(gh * nx), s_(gh), s_(gd), jnp.zeros((4, D), f32)], axis=0)

    @pl.when(i == pl.num_programs(0) - 1)
    def _():
        per = D // rf
        for j in range(nf):
            dn[j] = dot(gdt[...], act[:, j * D : (j + 1) * D]).astype(bf16).T
            for t in range(per):
                push(i0, n, j * per + t, dn.at[j, pl.ds(t * rf, rf)], ka, sa, 0, psems.at[j * per + t])
            up[j] = dot(h2t[...], gup[:, j * D : (j + 1) * D]).astype(bf16)
            for s in range(n):
                push(i0, n, s, up.at[j, pl.ds(s * r, r)], kb, sb, j * r, psems.at[n * (1 + j) + s], True)
        load.wait()
        gwo[...] = dot(mtv[...], gattn[...]).astype(bf16)
        vr[...] = jnp.concatenate([sums[0:4, :]] + [upsum[:, c * D : (c + 1) * D] for c in range(nf)] + [jnp.zeros((VROWS - 4 - nf, D), f32)], axis=0).astype(bf16)
        b = n * (1 + nf)
        for s in range(n):
            push(i0, n, s, gwo.at[pl.ds(s * r, r)], ka, sa, rf, psems.at[b + s])
            push(i0, n, s, vr, kb, sb, nf * r, psems.at[b + n + s], True)
        done = lambda src, q: pltpu.make_async_copy(src, (ka if src.shape[0] == rf else kb).at[0, pl.ds(0, src.shape[0])], psems.at[q]).wait()
        for s in range(n):
            done(dn.at[0, pl.ds(0, rf)], s)
            for c in range(nf):
                done(up.at[0, pl.ds(0, r)], n * (1 + c) + s)
            done(gwo.at[pl.ds(0, r)], b + s)
            done(vr, b + n + s)


def ffn(ln, me, tok, step, vec, upb, cot, mixed, mixedt, pieces, n):
    T, D = tok.shape
    FF = upb.shape[1]
    bm = min(512, T)
    nf = FF // D
    r = D // n
    meta = tuple((k, r0) for k, r0, _ in pieces)
    full = lambda a: pl.BlockSpec(a.shape, lambda i, l, m: (0,) * a.ndim)
    rows = pl.BlockSpec((bm, D), lambda i, l, m: (i, 0))
    A = S((n // 2, FF // n + r, D), bf16)
    B = S((n // 2, nf * r + VROWS, D), bf16)
    V = pltpu.VMEM
    return pl.pallas_call(
        functools.partial(ffn_body, n, meta, min(1024, FF)),
        grid_spec=pltpu.PrefetchScalarGridSpec(
            num_scalar_prefetch=2, grid=(T // bm,),
            in_specs=[rows, full(step), full(vec), full(upb), rows, rows, ANY] + [ANY] * len(pieces),
            out_specs=[rows, rows, pl.BlockSpec((D, bm), lambda i, l, m: (0, i))] + [ANY] * 4,
            scratch_shapes=[V((D, D), bf16), V((D, FF), bf16), V((FF, D), bf16), V((T, FF), bf16), V((T, FF), bf16), V((D, T), bf16), V((D, T), bf16), V((T, D), bf16), V((8, D), f32), V((1, FF), f32), V((nf, D, D), bf16), V((nf, D, D), bf16), V((D, D), bf16), V((VROWS, D), bf16), V((D, T), bf16), pltpu.SemaphoreType.DMA((16 * len(pieces),)), pltpu.SemaphoreType.DMA((n * (nf + 3) + 1,))]),
        out_shape=[S((T, D), bf16), S((T, D), bf16), S((D, T), bf16), A, A, B, B],
        compiler_params=cp(49), name="ffn", cost_estimate=cost(2 * T * D * (6 * FF + 3 * D), 16 * T * D, T * FF),
    )(ln, me, tok, step, vec, upb, cot, mixed, mixedt, *[a for _, _, a in pieces])


def attn_bwd_body(HD, scale, CR, v, kt, qt, gt, mt, linv, et, *refs):
    gq, ds = refs[-2:]
    T = v.shape[0]
    rid = lax.broadcasted_iota(jnp.int32, gt.shape, 0) // HD
    g = gt[...].astype(f32)
    q = qt[...]
    gv = gk = None
    for h in range(2):
        hs = slice(h * HD, (h + 1) * HD)
        gs = (g * linv[h : h + 1, :]).astype(bf16)
        gm = jnp.where(rid == h, gs, jnp.zeros_like(gs))
        dl = jnp.sum(gs[hs, :].astype(f32) * mt[hs, :], axis=0, keepdims=True)
        for c in range(T // CR):
            cs = slice(c * CR, (c + 1) * CR)
            ds[h, cs, :] = (et[h, cs, :].astype(f32) * (dot(v[cs, :], gm) - dl)).astype(bf16)
        a = dot(et[h], gm.T)
        b = dot(ds[h], jnp.where(rid == h, q, jnp.zeros_like(q)).T)
        gv = a if gv is None else gv + a
        gk = b if gk is None else gk + b
        gq[0, hs, :] = (dot(kt[hs, :], ds[h]) * scale).astype(bf16)
    gq[2] = gv.astype(bf16).T
    gq[1] = gk.astype(bf16).T


def attn_bwd(kv, qkvt, gmt, mixedf, linv, et, p0, cnt, prev):
    _, T, D = kv.shape
    HD = D // HEADS
    PW = 2 * HD
    NP = D // PW
    prev = list(prev)
    pr = pl.BlockSpec((PW, T), lambda p: (p0 + p, 0))
    of = lambda j: pl.BlockSpec((None, PW, T), lambda p: (j, p0 + p, 0))
    return pl.pallas_call(
        functools.partial(attn_bwd_body, HD, 1.0 / math.sqrt(HD), min(256, T)),
        grid=(cnt,),
        scratch_shapes=[pltpu.VMEM((2, T, T), bf16)],
        in_specs=[pl.BlockSpec((None, T, PW), lambda p: (1, 0, p0 + p)), of(1), of(0), pr, pr, pl.BlockSpec((None, 8, T), lambda p: (p0 + p, 0, 0)), pl.BlockSpec((2, T, T), lambda p: (p0 + p, 0, 0))] + [ANY] * len(prev),
        out_specs=pl.BlockSpec((3, PW, T), lambda p: (0, p0 + p, 0)),
        out_shape=S((3, D, T), bf16),
        input_output_aliases={7: 0} if prev else {},
        compiler_params=cp(56), name="attn_bwd", cost_estimate=cost(cnt * 2 * 16 * T * T * 128, cnt * 2 * T * T * 2),
    )(kv, qkvt, qkvt, gmt, mixedf, linv, et, *prev)


def wqkv_body(n, me, xht, g, keep, send, res, vr, sems):
    j = pl.program_id(0)
    D = g.shape[0]
    r = D // n
    i0 = me[0]
    y = dot_t(xht[...], g[...]).astype(bf16)
    res[j] = y[:D]
    vr[...] = jnp.where(lax.broadcasted_iota(jnp.int32, vr.shape, 0) == j, y[D:], jnp.where(j == 0, jnp.zeros_like(y[D:]), vr[...]))
    for s in range(n):
        push(i0, n, s, res.at[j, pl.ds(s * r, r)], keep, send, mult(j * r, 16), sems.at[j * n + s])

    @pl.when(j == 2)
    def _():
        for s in range(n):
            push(i0, n, s, vr, keep, send, 3 * r, sems.at[3 * n + s])
        for s in range(n):
            for q in range(3):
                pltpu.make_async_copy(res.at[0, pl.ds(0, r)], keep.at[0, pl.ds(0, r)], sems.at[q * n + s]).wait()
            pltpu.make_async_copy(vr, keep.at[0, pl.ds(0, VROWS)], sems.at[3 * n + s]).wait()


def wqkv(me, xht, g, n):
    _, D, T = g.shape
    A = S((n // 2, 3 * (D // n) + VROWS, D), bf16)
    return pl.pallas_call(
        functools.partial(wqkv_body, n),
        grid_spec=pltpu.PrefetchScalarGridSpec(
            num_scalar_prefetch=1, grid=(3,),
            in_specs=[pl.BlockSpec((D + 16, T), lambda j, m: (0, 0)), pl.BlockSpec((None, D, T), lambda j, m: (j, 0, 0))],
            out_specs=[ANY] * 2,
            scratch_shapes=[pltpu.VMEM((3, D, D), bf16), pltpu.VMEM((VROWS, D), bf16), pltpu.SemaphoreType.DMA((4 * n,))]),
        out_shape=[A, A],
        compiler_params=cp(), name="wqkv", cost_estimate=cost(6 * T * D * D, 10 * T * D),
    )(me, xht, g)


def back_body(tok, step, vec, g, gx1, *refs):
    ws, tg = refs[:-1], refs[-1]
    D = tok.shape[1]
    gw = D // GROUPS
    x = tok[...].astype(f32) + step[...].astype(f32)
    nx, rr = norm(x)
    gt = sum(dot(w[:, j * gw : (j + 1) * gw], g[j, q * gw : (q + 1) * gw, :]) for q, w in enumerate(ws) for j in range(3))
    gn = gt.T * row(vec[...], 0)
    tg[...] = gx1[...].astype(f32) + rr * (gn - jnp.mean(gn, axis=-1, keepdims=True) - nx * jnp.mean(gn * nx, axis=-1, keepdims=True))


def back(tok, step, vec, ws, g, gx1, bm=512):
    T, D = tok.shape
    full = lambda a: pl.BlockSpec(a.shape, lambda i: (0,) * a.ndim)
    rows = pl.BlockSpec((bm, D), lambda i: (i, 0))
    return pl.pallas_call(
        back_body, grid=(T // bm,),
        in_specs=[rows, full(step), full(vec), pl.BlockSpec((3, D, bm), lambda i: (0, 0, i)), rows] + [full(w) for w in ws],
        out_specs=rows, out_shape=S((T, D), f32), compiler_params=cp(), name="back", cost_estimate=cost(6 * T * D * D, 14 * T * D),
    )(tok, step, vec, g, gx1, *ws)


def shards(tokens, step_embed, lengths, cotangent, ln1_gain, ln1_bias, qkv_weight, q_bias, v_bias, out_weight, out_bias, ln2_gain, ln2_bias, up_weight, up_bias, down_weight, down_bias):
    n = lax.axis_size("shard")
    me = lax.axis_index("shard").astype(jnp.int32)
    mes = me[None]
    tok, cot, step = tokens[0], cotangent[0], step_embed
    T, D = tok.shape
    r = D // n
    FF = up_bias.shape[0] * n
    nc = FF // D
    rf = FF // n
    packs = pack_first(mes, qkv_weight, [ln1_gain, ln1_bias, q_bias, v_bias, out_bias, ln2_gain, ln2_bias, down_bias], up_bias)
    pack2 = pack_rest(out_weight, up_weight, down_weight)
    NP = HEADS // 2
    nx, xht = start(tok, step)
    pieces = gather_direct(packs[0], n, xht, pack2)
    kv, qkvt, w, vec, upb = front(mes, nx, pieces, n, FF)
    et, mixed, mixedt, mixedf, linv = attn_fwd(lengths, kv, qkvt, 0, NP, [])
    pieces2 = gather_direct(after(pack2, xht), n, linv)
    out, gx1, gmt, ka, sa, kb, sb = ffn(lengths, mes, tok, step, vec, upb, cot, mixed, mixedt, pieces2, n)
    bwd = lambda p, c, g, *deps: attn_bwd(kv, qkvt, after(gmt, *deps) if deps else gmt, mixedf, linv, et, p, c, g)
    ga, gb = swap(sa, 1), swap(sb, 1)
    g = bwd(0, 1, [])
    ga, gb, _ = lax.optimization_barrier((ga, gb, g))
    h = n // 4
    lo, hi = slice(0, h), slice(h, None)
    add = lambda a, b, s: add16(a[s], b[s])
    ka, xa, kb, xb = add(ka, ga, lo), add(ka, ga, hi), add(kb, gb, lo), add(kb, gb, hi)
    g = bwd(1, NP - 1, [g], ka, xa, kb, xb)
    m = (n // 2).bit_length() - 1
    ga, gb = swap(xa, 2 << (m - 1)), swap(xb, 2)
    for t in range(1, m):
        dep = g if t == 1 else keep
        ga, gb, _ = lax.optimization_barrier((ga, gb, dep))
        h //= 2
        lo, hi = slice(0, h), slice(h, None)
        ka, xa = add(ka, ga, lo), add(ka, ga, hi)
        kb, xb = add(kb, gb, lo), add(kb, gb, hi)
        ga, gb = swap(xa, 2 << (m - 1 - t)), swap(xb, 2 << t)
        if t == 1:
            keep, send = wqkv(mes, after(xht, ka, xa, kb, xb), g, n)
    got = swap(send, 1)
    p2 = [add16(keep[k], got[k]) for k in range(n // 2)]
    far2 = spread(p2)
    ga, gb, _ = lax.optimization_barrier((ga, gb, keep))
    got = swap(send, 1)
    p2 = [add16(keep[k], got[k]) for k in range(n // 2)]
    far2 = spread(p2)
    own1 = jnp.concatenate([add16(ka, ga)[0], add16(kb, gb)[0]], axis=0)
    m1, o1, x1 = rep_half(own1)
    z1 = add16(m1, after(o1, *p2[1:]))
    tg = back(tok, after(step, z1, *p2[1:]), vec, [w], g, gx1)
    own2 = total(p2[0], [after(a, tg) for a in far2])
    m2, o2, x2 = rep_half(own2)
    steps = rep_steps()
    z2 = None if steps else add16(m2, o2)
    for b in steps:
        z1 = add16(z1, after(rep_perm(z1, b), x2))
        if z2 is None:
            z2 = add16(m2, after(o2, z1))
        pz = rep_perm(z2, b)
        z2 = add16(z2, after(pz, z1))
    o1, o2 = rep_perm(z1, 1), rep_perm(z2, 1)
    ids = jnp.stack([me, (lax.axis_index("rep") % 2).astype(jnp.int32)])
    g_down, g_up, g_out, g_upb, g_ob, g_g2, g_b2, g_db = finish_rest(ids, z1, o1, r, rf, nc, n)
    g_qkv, g_g1, g_b1, g_q, g_v = finish_first(ids, z2, after(o2, g_out), qkv_weight, ln1_gain, ln1_bias)
    flat = lambda a: a.reshape(-1)
    return (out[None], tg[None], flat(g_g1), flat(g_b1), g_qkv, flat(g_q), flat(g_v), g_out, flat(g_ob), flat(g_g2), flat(g_b2), g_up, flat(g_upb), g_down, flat(g_db))


def solution(mesh):
    from jax.sharding import PartitionSpec as P

    in_specs = (
        P(("rep", "shard"), None, None),
        P(("rep", "shard"), None),
        P(("rep", "shard")),
        P(("rep", "shard"), None, None),
        P("shard"),
        P("shard"),
        P("shard", None),
        P("shard"),
        P("shard"),
        P("shard", None),
        P("shard"),
        P("shard"),
        P("shard"),
        P("shard", None),
        P("shard"),
        P("shard", None),
        P("shard"),
    )
    out_specs = (
        P(("rep", "shard"), None, None),
        P(("rep", "shard"), None, None),
        P("shard"),
        P("shard"),
        P("shard", None),
        P("shard"),
        P("shard"),
        P("shard", None),
        P("shard"),
        P("shard"),
        P("shard"),
        P("shard", None),
        P("shard"),
        P("shard", None),
        P("shard"),
    )
    return jax.shard_map(shards, mesh=mesh, in_specs=in_specs, out_specs=out_specs, check_vma=False)
```

```python
import functools, math
import jax, jax.numpy as jnp
from jax import lax
from jax.experimental import pallas as pl
from jax.experimental.pallas import tpu as pltpu

f32 = jnp.float32
bf16 = jnp.bfloat16
EPS = 1e-05
HEADS = 8

def dot(a, b):
    return jnp.dot(a, b, preferred_element_type=f32)

def dot_t(a, b):
    return lax.dot_general(a, b, (((1,), (1,)), ((), ())), preferred_element_type=f32)

def cp(mib=60):
    return pltpu.CompilerParams(dimension_semantics=("arbitrary",), vmem_limit_bytes=mib << 20)

def norm(x):
    c = x - jnp.mean(x, axis=-1, keepdims=True)
    r = lax.rsqrt(jnp.mean(c * c, axis=-1, keepdims=True) + EPS)
    return c * r, r

def row(v, i):
    return v[i : i + 1, :].astype(f32)


VROWS = 16
LANES = 128


def xor_perm(n, k):
    return [(i, i ^ k) for i in range(n)]


def rep_perm(x, b):
    return lax.ppermute(x, "rep", xor_perm(lax.axis_size("rep"), b))


def swap(x, k):
    return lax.ppermute(x, "shard", xor_perm(lax.axis_size("shard"), k))


def after(x, *deps):
    return lax.optimization_barrier((x,) + deps)[0]


def gather_direct(x, n, *gate):
    out = [(0, 0, x)]
    far = [(k, swap(x, k)) for k in range(2, n, 2)]
    out += [(k, 0, after(y, *gate) if gate else y) for k, y in far]
    return out + [(k ^ 1, 0, swap(y, 1)) for k, _, y in out]


def add16(a, b):
    return a + b


def spread(parts):
    return [swap(parts[k], 2 * k) for k in range(len(parts) - 1, 0, -1)]


def total(own, got):
    t = own.astype(f32)
    for a in got:
        t = t + a.astype(f32)
    return t.astype(bf16)


def rep_half(x):
    h = x.shape[0] // 2
    odd = lax.axis_index("rep") % 2
    mine = lax.dynamic_slice_in_dim(x, odd * h, h, 0)
    other = lax.dynamic_slice_in_dim(x, (1 - odd) * h, h, 0)
    return mine, rep_perm(other, 1), other


def rep_steps():
    nr = lax.axis_size("rep")
    return [b for b in (2 << i for i in range(16)) if b < nr]


GROUPS = 1


def pack_first_body(me, w, upb, *refs):
    vecs = refs[:-GROUPS]
    outs = refs[-GROUPS:]
    r, W = w.shape
    D = W // 3
    gw = D // GROUPS
    for g, out in enumerate(outs):
        for j in range(3):
            out[j * r : (j + 1) * r, :] = w[:, j * D + g * gw : j * D + (g + 1) * gw]

    def spot(v):
        w_ = v.shape[1]
        if w_ >= LANES:
            return [v[q : q + 1, :] for q in range(v.shape[0])]
        t = LANES // w_
        lane = lax.broadcasted_iota(jnp.int32, (1, LANES), 1)
        return [jnp.where(lane // w_ == me[0] % t, jnp.concatenate([v] * t, axis=1), jnp.zeros((1, LANES), f32))]

    rows = [a for v in vecs for a in spot(v[...].astype(f32))] + spot(upb[...].astype(f32))
    b = jnp.concatenate(rows + [jnp.zeros((VROWS - len(rows), LANES), f32)], axis=0).astype(bf16)
    outs[0][3 * r :, :] = jnp.concatenate([b, jnp.zeros((VROWS, gw - LANES), bf16)], axis=1) if gw > LANES else b


def whole(n):
    return [pl.BlockSpec(memory_space=pltpu.VMEM)] * n


def once(*arrays):
    return [pl.BlockSpec(a.shape, lambda i, *m, nd=len(a.shape): (0,) * nd) for a in arrays]


def pack_first(me, w, vecs, upb):
    r, W = w.shape
    gw = W // 3 // GROUPS
    lanes = lambda v: v.reshape(-1, min(LANES, v.shape[0]))
    args = [w] + [lanes(v) for v in [upb] + vecs]
    outs = [S((3 * r + (VROWS if g == 0 else 0), gw), bf16) for g in range(GROUPS)]
    return pl.pallas_call(
        pack_first_body,
        grid_spec=pltpu.PrefetchScalarGridSpec(num_scalar_prefetch=1, grid=(1,), in_specs=once(*args), out_specs=once(*outs)),
        out_shape=outs, compiler_params=cp(), name="pack_first", cost_estimate=cost(0, 4 * w.size),
    )(me, *args)


def pack_rest_body(wo, wu, wd, out):
    r, D = wo.shape
    out[:r, :] = wo[...]
    for j in range(wu.shape[1] // D):
        out[(1 + j) * r : (2 + j) * r, :] = wu[:, j * D : (j + 1) * D]
    out[(1 + wu.shape[1] // D) * r :, :] = wd[...]


def pack_rest(wo, wu, wd):
    D = wo.shape[1]
    out = S(((wo.size + wu.size + wd.size) // D, D), bf16)
    return pl.pallas_call(
        pack_rest_body, grid=(1,), in_specs=once(wo, wu, wd), out_specs=once(out)[0],
        out_shape=out, compiler_params=cp(), name="pack_rest", cost_estimate=cost(0, 4 * wu.size),
    )(wo, wu, wd)


def own_lanes(tiles, me, w):
    pick = lambda i: sum(jnp.where(i == t, a, jnp.zeros_like(a)) for t, a in enumerate(tiles))
    if w >= LANES:
        q = w // LANES
        return jnp.concatenate([pick(me * q + c) for c in range(q)], axis=1)
    per = LANES // w
    x = pick(me // per)
    off = me % per
    return sum(jnp.where(off == o, x[:, o * w : (o + 1) * w], 0.0) for o in range(per))


def rows_of(lo, hi, a, b):
    h = lo.shape[0]
    if b <= h:
        return lo[a:b, :]
    if a >= h:
        return hi[a - h : b - h, :]
    return jnp.concatenate([lo[a:h, :], hi[: b - h, :]], axis=0)


def finish_rest_body(r, rf, n, ids, s, o, down, up, out, upb, *vecs):
    D = out.shape[1]
    nf = up.shape[1] // D

    def run(lo, hi):
        f = lambda a, b: rows_of(lo, hi, a, b).astype(f32)
        down[...] = f(0, rf)
        out[...] = f(rf, rf + r)
        for j in range(nf):
            up[:, j * D : (j + 1) * D] = f(rf + (j + 1) * r, rf + (j + 2) * r)
        b = rf + (nf + 1) * r
        v = f(b, b + VROWS)
        me = ids[0]
        tiles = [v[0:8, t * LANES : (t + 1) * LANES] for t in range(D // LANES)]
        x = own_lanes(tiles, me, r)
        for q, ref in enumerate(vecs):
            ref[...] = x[q : q + 1, :]
        tiles = [v[4 + q : 5 + q, t * LANES : (t + 1) * LANES] for q in range(nf) for t in range(D // LANES)]
        upb[...] = own_lanes(tiles, me, nf * D // n)

    @pl.when(ids[1] == 0)
    def _():
        run(s, o)

    @pl.when(ids[1] == 1)
    def _():
        run(o, s)


def finish_rest(ids, s, o, r, rf, nf, n):
    D = s.shape[1]
    row1 = lambda w: S((1, w), f32)
    return pl.pallas_call(
        functools.partial(finish_rest_body, r, rf, n),
        in_specs=[pl.BlockSpec(memory_space=pltpu.SMEM)] + whole(2), out_specs=whole(8),
        out_shape=[S((rf, D), f32), S((r, nf * D), f32), S((r, D), f32), row1(nf * D // n)] + [row1(r)] * 4,
        compiler_params=pltpu.CompilerParams(vmem_limit_bytes=16 << 20), name="finish_rest", cost_estimate=cost(0, 8 * s.size),
    )(ids, s, o)


def finish_first_body(ids, s, o, w, gain, bias, qkv, gg, gb, qb, vb):
    r, W = w.shape
    D = s.shape[1]

    def run(lo, hi):
        f = lambda a, b: rows_of(lo, hi, a, b).astype(f32)
        v = f(3 * r, 3 * r + VROWS)
        nt = D // LANES
        accg = accb = jnp.zeros((r, LANES), f32)
        col = lambda g: jnp.concatenate([g[...].astype(f32), jnp.zeros((7, r), f32)], axis=0).T[:, 0:1]
        cg, cb = col(gain), col(bias)
        for j in range(3):
            m = f(j * r, (j + 1) * r)
            sq = v[j : j + 1, :]
            ww = w[:, j * D : (j + 1) * D].astype(f32)
            qkv[:, j * D : (j + 1) * D] = cg * m + cb * sq
            pg, pb = ww * m, ww * sq
            accg = accg + sum(pg[:, t * LANES : (t + 1) * LANES] for t in range(nt))
            accb = accb + sum(pb[:, t * LANES : (t + 1) * LANES] for t in range(nt))
        gg[...] = jnp.sum(accg.T, axis=0, keepdims=True)
        gb[...] = jnp.sum(accb.T, axis=0, keepdims=True)
        x = own_lanes([v[0:8, t * LANES : (t + 1) * LANES] for t in range(nt)], ids[0], r)
        qb[...] = x[0:1, :]
        vb[...] = x[2:3, :]

    @pl.when(ids[1] == 0)
    def _():
        run(s, o)

    @pl.when(ids[1] == 1)
    def _():
        run(o, s)


def finish_first(ids, s, o, w, gain, bias):
    r, W = w.shape
    return pl.pallas_call(
        finish_first_body,
        in_specs=[pl.BlockSpec(memory_space=pltpu.SMEM)] + whole(5), out_specs=whole(5),
        out_shape=[S((r, W), f32)] + [S((1, r), f32)] * 4,
        compiler_params=pltpu.CompilerParams(vmem_limit_bytes=16 << 20), name="finish_first", cost_estimate=cost(0, 8 * w.size),
    )(ids, s, o, w, gain[None], bias[None])


def pull(me, refs, meta, segs, sems):
    copies = []
    for ref, (k, r0) in zip(refs, meta):
        s = jnp.bitwise_xor(me, k)
        r1 = r0 + ref.shape[0]
        for a, c, dst, lanes in segs:
            lo, hi = max(a, r0), min(a + c, r1)
            if lo < hi:
                src = ref.at[pl.ds(lo - r0, hi - lo), pl.ds(0, lanes)]
                copies.append(pltpu.make_async_copy(src, dst(s, lo - a, hi - lo), sems.at[len(copies)]))
    return copies


def mult(x, m):
    return pl.multiple_of(x, m)


def weight_segs(w, r):
    gw = w.shape[1] // 3
    seg = lambda j: (j * r, r, lambda s, o, c: w.at[pl.ds(mult(s * r + o, 16), c), pl.ds(j * gw, gw)], gw)
    return [seg(j) for j in range(3)]


def start_body(tok, step, nx, xht):
    n, _ = norm(tok[...].astype(f32) + step[...].astype(f32))
    D = tok.shape[1]
    nx[...] = n
    xht[:D, :] = n.astype(bf16).T
    xht[D:, :] = jnp.ones((16, tok.shape[0]), bf16)


def start(tok, step, bm=256):
    T, D = tok.shape
    rows = pl.BlockSpec((bm, D), lambda i: (i, 0))
    return pl.pallas_call(
        start_body, grid=(T // bm,),
        in_specs=[rows, pl.BlockSpec((1, D), lambda i: (0, 0))], out_specs=[rows, pl.BlockSpec((D + 16, bm), lambda i: (0, i))],
        out_shape=[S((T, D), f32), S((D + 16, T), bf16)], compiler_params=cp(), name="start", cost_estimate=cost(20 * T * D, 8 * T * D),
    )(tok, step)


def front_body(scale, n, meta, me, nx, *refs):
    np_ = len(meta)
    pieces = refs[:np_]
    kv, qkvt, wout, vec, upb, nv, h, w, vbuf, sems, own = refs[np_:]
    T, D = nv.shape
    r = D // n
    FF = upb.shape[1]
    i = pl.program_id(0)
    cw = kv.shape[2]
    per_j = D // cw
    segs = [(3 * r, VROWS, lambda s, o, c: vbuf.at[s, pl.ds(o, c)], LANES)] + weight_segs(w, r)
    load = pltpu.make_async_copy(nx, nv, own.at[0])
    save = pltpu.make_async_copy(w, wout, own.at[1])

    @pl.when(i == 0)
    def _():
        cs = pull(me[0], pieces, meta, segs, sems)
        for c in cs:
            c.start()
        load.start()
        for c in cs:
            c.wait()
        save.start()
        per = LANES // r
        tiles = [sum(vbuf[s, 0:8, :].astype(f32) for s in range(t * per, (t + 1) * per)) for t in range(D // LANES)]
        vec[...] = jnp.concatenate(tiles, axis=1)
        wu = FF // n
        if wu >= LANES:
            rows = [vbuf[s, 8 + q : 9 + q, :].astype(f32) for s in range(n) for q in range(wu // LANES)]
        else:
            per = LANES // wu
            rows = [sum(vbuf[s, 8:9, :].astype(f32) for s in range(t * per, (t + 1) * per)) for t in range(FF // LANES)]
        upb[...] = jnp.concatenate(rows, axis=1)
        load.wait()
        v = vec[...]
        h[...] = (nv[...] * row(v, 0) + row(v, 1)).astype(bf16)

    cols = pl.ds(mult(i * cw, 128), cw)
    y = dot(h[...], w[:, cols])
    here = pl.ds(mult((i % per_j) * cw, 128), cw)
    kind = i // per_j
    y = (y + jnp.where(kind == 0, vec[2:3, here], jnp.where(kind == 2, vec[3:4, here], 0.0))).astype(bf16)
    kv[0] = y
    qkvt[0] = jnp.where(kind == 0, y * bf16(scale), y).T

    @pl.when(i == pl.num_programs(0) - 1)
    def _():
        save.wait()


S = jax.ShapeDtypeStruct
ANY = pl.BlockSpec(memory_space=pl.ANY)


def cost(flops, nbytes, tr=0):
    return pl.CostEstimate(flops=int(flops), bytes_accessed=int(nbytes), transcendentals=int(tr))


def front(me, nx, pieces, n, FF, cw=512):
    T, D = nx.shape
    scale = 1.0 / math.sqrt(D // HEADS)
    meta = tuple((k, r0) for k, r0, _ in pieces)
    q = D // cw
    keep = lambda *sh: pl.BlockSpec(sh, lambda i, m: (0,) * len(sh))
    rest = lambda i: jnp.maximum(i - q, 0)
    V = pltpu.VMEM
    return pl.pallas_call(
        functools.partial(front_body, scale, n, meta),
        grid_spec=pltpu.PrefetchScalarGridSpec(
            num_scalar_prefetch=1, grid=(3 * q,),
            in_specs=[ANY] * (1 + len(pieces)),
            out_specs=[pl.BlockSpec((1, T, cw), lambda i, m: (rest(i) // q, 0, rest(i) % q)), pl.BlockSpec((1, cw, T), lambda i, m: (i // q, i % q, 0)), ANY, keep(8, D), keep(1, FF)],
            scratch_shapes=[V((T, D), f32), V((T, D), bf16), V((D, 3 * D), bf16), V((n, VROWS, LANES), bf16), pltpu.SemaphoreType.DMA((8 * len(pieces),)), pltpu.SemaphoreType.DMA((2,))]),
        out_shape=[S((2, T, D), bf16), S((3, D, T), bf16), S((D, 3 * D), bf16), S((8, D), f32), S((1, FF), f32)],
        compiler_params=cp(), name="front", cost_estimate=cost(6 * T * D * D, 12 * T * D),
    )(me, nx, *[a for _, _, a in pieces])


def attn_fwd_body(HD, bi, CR, p0, ln, k, qt, vt, *refs):
    et, mixed, mixedt, mixedf, linv, scr, ka, eb, esem = refs[-9:]
    T, PW = k.shape
    n = ln[0]
    p = pl.program_id(0)
    last = p == pl.num_programs(0) - 1
    rid = lax.broadcasted_iota(jnp.int32, (PW, bi), 0)
    lane = lax.broadcasted_iota(jnp.int32, (T, PW), 1)
    rows = lax.broadcasted_iota(jnp.int32, (T, PW), 0)
    ka[:, :PW] = k[...]
    ka[:, PW:] = jnp.where((lane == 0) & (rows >= n), f32(-1e30), f32(0)).astype(bf16)
    ones = jnp.where(rid == 0, f32(1), f32(0)).astype(bf16)
    va = [jnp.concatenate([vt[h * HD : (h + 1) * HD, :], jnp.ones((16, T), bf16)], axis=0) for h in range(2)]
    tasks = [(b, h) for b in range(T // bi) for h in range(2)]
    nch = T // CR

    def query(t):
        b, h = tasks[t]
        q = qt[:, b * bi : (b + 1) * bi]
        return jnp.concatenate([jnp.where(rid // HD == h, q, jnp.zeros_like(q)), ones], axis=0)

    def score(t, c, q):
        s = dot(ka[c * CR : (c + 1) * CR, :], q)
        scr[t % 2, c * CR : (c + 1) * CR, :] = s
        return jnp.max(s, axis=0, keepdims=True)

    q = query(0)
    m = functools.reduce(jnp.maximum, [score(0, c, q) for c in range(nch)])
    half = None
    for t, (b, h) in enumerate(tasks):
        sl = slice(b * bi, (b + 1) * bi)
        more = t + 1 < len(tasks)
        put = pltpu.make_async_copy(eb.at[t % 2], et.at[2 * (p0 + p) + h, :, pl.ds(b * bi, bi)], esem.at[t % 2])
        if t < 2:

            @pl.when(p > 0)
            def _():
                put.wait()

        else:
            put.wait()
        if more:
            q = query(t + 1)
        nxt = []
        for c in range(nch):
            cs = slice(c * CR, (c + 1) * CR)
            if more:
                nxt.append(score(t + 1, c, q))
            eb[t % 2, cs, :] = jnp.exp(scr[t % 2, cs, :] - m).astype(bf16)
        put.start()
        o = dot(va[h], eb[t % 2])
        if more:
            m = functools.reduce(jnp.maximum, nxt)
        inv = 1.0 / o[HD : HD + 1, :]
        linv[h : h + 1, sl] = inv
        o = o[:HD, :] * inv
        if h == 0:
            half = o
        else:
            mt = jnp.concatenate([half, o], axis=0)
            mixedf[:, sl] = mt
            mt = mt.astype(bf16)
            mixedt[:, sl] = mt
            mixed[sl, :] = mt.T

    @pl.when(last)
    def _():
        for q in range(2):
            pltpu.make_async_copy(eb.at[q], et.at[0, :, pl.ds(0, bi)], esem.at[q]).wait()


def attn_fwd(ln, kv, qkvt, p0, cnt, prev):
    _, T, D = kv.shape
    HD = D // HEADS
    PW = 2 * HD
    NP = D // PW
    bi = T
    prev = list(prev)
    return pl.pallas_call(
        functools.partial(attn_fwd_body, HD, bi, min(512, T), p0),
        grid_spec=pltpu.PrefetchScalarGridSpec(
            num_scalar_prefetch=1, grid=(cnt,),
            in_specs=[pl.BlockSpec((None, T, PW), lambda p, r: (0, 0, p0 + p)), pl.BlockSpec((None, PW, T), lambda p, r: (0, p0 + p, 0)), pl.BlockSpec((None, PW, T), lambda p, r: (2, p0 + p, 0))] + [ANY] * len(prev),
            out_specs=[ANY, pl.BlockSpec((T, PW), lambda p, r: (0, p0 + p)), pl.BlockSpec((PW, T), lambda p, r: (p0 + p, 0)), pl.BlockSpec((PW, T), lambda p, r: (p0 + p, 0)), pl.BlockSpec((None, 8, T), lambda p, r: (p0 + p, 0, 0))],
            scratch_shapes=[pltpu.VMEM((2, T, bi), f32), pltpu.VMEM((T, 2 * PW), bf16), pltpu.VMEM((2, T, bi), bf16), pltpu.SemaphoreType.DMA((2,))]),
        out_shape=[S((HEADS, T, T), bf16), S((T, D), bf16), S((D, T), bf16), S((D, T), f32), S((NP, 8, T), f32)],
        input_output_aliases={4 + i: i for i in range(len(prev))},
        compiler_params=cp(), name="attn_fwd", cost_estimate=cost(cnt * 2 * 8 * T * T * 128, cnt * 2 * T * T * 2, cnt * 2 * T * T),
    )(ln, kv, qkvt, qkvt, *prev)


G0 = math.sqrt(2 / math.pi)


def bit_reverse(x, m):
    y = jnp.zeros_like(x)
    for t in range(m):
        y = y | (((x >> t) & 1) << (m - 1 - t))
    return y


def push(me, n, s, src, keep, send, row0, sem, reverse=False):
    k = jnp.bitwise_xor(me, s)
    p = k >> 1
    if reverse:
        p = bit_reverse(p, (n // 2).bit_length() - 1)
    put = lambda dst: pltpu.make_async_copy(src, dst.at[p, pl.ds(row0, src.shape[0])], sem)

    @pl.when(k & 1 == 0)
    def _():
        put(keep).start()

    @pl.when(k & 1 == 1)
    def _():
        put(send).start()


def ffn_body(n, meta, ch, ln, me, tok, step, vec, upb, cot, mixed, mixedt, *refs):
    np_ = len(meta)
    pieces = refs[:np_]
    out, gx1, gmt, ka, sa, kb, sb, wo, wu, wd, act, gup, h2t, gdt, gattn, sums, upsum, dn, up, gwo, vr, mtv, sems, psems = refs[np_:]
    i = pl.program_id(0)
    bm, D = tok.shape
    FF = wu.shape[1]
    r = D // n
    rf = FF // n
    nf = FF // D
    i0 = me[0]
    ro = pl.ds(mult(i * bm, 128), bm)
    first = i == 0
    seg = lambda j: (r + j * r, r, lambda s, o, c: wu.at[pl.ds(mult(s * r + o, 16), c), pl.ds(j * D, D)], D)
    seg_o = [(0, r, lambda s, o, c: wo.at[pl.ds(mult(s * r + o, 16), c)], D)]
    seg_u = [seg(j) for j in range(nf)]
    seg_d = [(r + r * nf, rf, lambda s, o, c: wd.at[pl.ds(mult(s * rf + o, 16), c)], D)]
    q = sems.shape[0] // 4
    parts = [(seg_o, sems.at[pl.ds(0, q)]), (seg_d, sems.at[pl.ds(q, q)]), (seg_u, sems.at[pl.ds(2 * q, 2 * q)])]
    load = pltpu.make_async_copy(mixedt, mtv, psems.at[psems.shape[0] - 1])

    @pl.when(first)
    def _():
        for sg, sm in parts:
            for c in pull(i0, pieces, meta, sg, sm):
                c.start()
        load.start()
        sums[...] = jnp.zeros_like(sums)
        upsum[...] = jnp.zeros_like(upsum)
        for c in pull(i0, pieces, meta, *parts[0]):
            c.wait()

    v = vec[...]
    x1 = tok[...].astype(f32) + step[...].astype(f32) + dot(mixed[...], wo[...]) + row(v, 4)
    nx, rr = norm(x1)
    h2 = (nx * row(v, 5) + row(v, 6)).astype(bf16)
    live = (lax.broadcasted_iota(jnp.int32, (bm, 1), 0) + i * bm) < ln[0]
    gd = jnp.where(live, cot[...], jnp.zeros_like(cot))
    acc = x1 + row(v, 7)
    gh = None
    nc = FF // ch
    sl = [slice(c * ch, (c + 1) * ch) for c in range(nc)]
    lead = lambda c: (dot(h2, wu[:, sl[c]]), dot_t(gd, wd[sl[c], :]))
    h2t[:, ro] = h2.T
    gdt[:, ro] = gd.T

    @pl.when(first)
    def _():
        for sg, sm in parts[1:]:
            for c in pull(i0, pieces, meta, sg, sm):
                c.wait()

    nxt = lead(0)
    for c in range(nc):
        u, ga = nxt
        nxt = lead(c + 1) if c + 1 < nc else None
        u = u + upb[:, sl[c]]
        u2 = u * u
        t = jnp.tanh(u * (f32(G0) + f32(G0 * 0.044715) * u2))
        half = 0.5 + 0.5 * t
        a = (u * half).astype(bf16)
        act[ro, sl[c]] = a
        dg = half + u * (half * (1.0 - half)) * (f32(2 * G0) + f32(6 * 0.044715 * G0) * u2)
        gu = (ga * dg).astype(bf16)
        gup[ro, sl[c]] = gu
        upsum[:, sl[c]] += jnp.sum(gu.astype(f32), axis=0, keepdims=True)
        acc = acc + dot(a, wd[sl[c], :])
        p = dot_t(gu, wu[:, sl[c]])
        gh = p if gh is None else gh + p
    out[...] = jnp.where(live, acc, 0.0).astype(bf16)
    gn = gh * row(v, 5)
    gx = gd.astype(f32) + rr * (gn - jnp.mean(gn, axis=-1, keepdims=True) - nx * jnp.mean(gn * nx, axis=-1, keepdims=True))
    gab = gx.astype(bf16)
    gx1[...] = gab
    gattn[ro, :] = gab
    gmt[...] = dot_t(gab, wo[...]).astype(bf16).T
    s_ = lambda a: jnp.sum(a.astype(f32), axis=0, keepdims=True)
    sums[...] += jnp.concatenate([s_(gab), s_(gh * nx), s_(gh), s_(gd), jnp.zeros((4, D), f32)], axis=0)

    @pl.when(i == pl.num_programs(0) - 1)
    def _():
        per = D // rf
        for j in range(nf):
            dn[j] = dot(gdt[...], act[:, j * D : (j + 1) * D]).astype(bf16).T
            for t in range(per):
                push(i0, n, j * per + t, dn.at[j, pl.ds(t * rf, rf)], ka, sa, 0, psems.at[j * per + t])
            up[j] = dot(h2t[...], gup[:, j * D : (j + 1) * D]).astype(bf16)
            for s in range(n):
                push(i0, n, s, up.at[j, pl.ds(s * r, r)], kb, sb, j * r, psems.at[n * (1 + j) + s], True)
        load.wait()
        gwo[...] = dot(mtv[...], gattn[...]).astype(bf16)
        vr[...] = jnp.concatenate([sums[0:4, :]] + [upsum[:, c * D : (c + 1) * D] for c in range(nf)] + [jnp.zeros((VROWS - 4 - nf, D), f32)], axis=0).astype(bf16)
        b = n * (1 + nf)
        for s in range(n):
            push(i0, n, s, gwo.at[pl.ds(s * r, r)], ka, sa, rf, psems.at[b + s])
            push(i0, n, s, vr, kb, sb, nf * r, psems.at[b + n + s], True)
        done = lambda src, q: pltpu.make_async_copy(src, (ka if src.shape[0] == rf else kb).at[0, pl.ds(0, src.shape[0])], psems.at[q]).wait()
        for s in range(n):
            done(dn.at[0, pl.ds(0, rf)], s)
            for c in range(nf):
                done(up.at[0, pl.ds(0, r)], n * (1 + c) + s)
            done(gwo.at[pl.ds(0, r)], b + s)
            done(vr, b + n + s)


def ffn(ln, me, tok, step, vec, upb, cot, mixed, mixedt, pieces, n):
    T, D = tok.shape
    FF = upb.shape[1]
    bm = min(512, T)
    nf = FF // D
    r = D // n
    meta = tuple((k, r0) for k, r0, _ in pieces)
    full = lambda a: pl.BlockSpec(a.shape, lambda i, l, m: (0,) * a.ndim)
    rows = pl.BlockSpec((bm, D), lambda i, l, m: (i, 0))
    A = S((n // 2, FF // n + r, D), bf16)
    B = S((n // 2, nf * r + VROWS, D), bf16)
    V = pltpu.VMEM
    return pl.pallas_call(
        functools.partial(ffn_body, n, meta, min(1024, FF)),
        grid_spec=pltpu.PrefetchScalarGridSpec(
            num_scalar_prefetch=2, grid=(T // bm,),
            in_specs=[rows, full(step), full(vec), full(upb), rows, rows, ANY] + [ANY] * len(pieces),
            out_specs=[rows, rows, pl.BlockSpec((D, bm), lambda i, l, m: (0, i))] + [ANY] * 4,
            scratch_shapes=[V((D, D), bf16), V((D, FF), bf16), V((FF, D), bf16), V((T, FF), bf16), V((T, FF), bf16), V((D, T), bf16), V((D, T), bf16), V((T, D), bf16), V((8, D), f32), V((1, FF), f32), V((nf, D, D), bf16), V((nf, D, D), bf16), V((D, D), bf16), V((VROWS, D), bf16), V((D, T), bf16), pltpu.SemaphoreType.DMA((16 * len(pieces),)), pltpu.SemaphoreType.DMA((n * (nf + 3) + 1,))]),
        out_shape=[S((T, D), bf16), S((T, D), bf16), S((D, T), bf16), A, A, B, B],
        compiler_params=cp(49), name="ffn", cost_estimate=cost(2 * T * D * (6 * FF + 3 * D), 16 * T * D, T * FF),
    )(ln, me, tok, step, vec, upb, cot, mixed, mixedt, *[a for _, _, a in pieces])


def attn_bwd_body(HD, scale, CR, v, kt, qt, gt, mt, linv, et, *refs):
    gq, ds = refs[-2:]
    T = v.shape[0]
    rid = lax.broadcasted_iota(jnp.int32, gt.shape, 0) // HD
    g = gt[...].astype(f32)
    q = qt[...]
    gv = gk = None
    for h in range(2):
        hs = slice(h * HD, (h + 1) * HD)
        gs = (g * linv[h : h + 1, :]).astype(bf16)
        gm = jnp.where(rid == h, gs, jnp.zeros_like(gs))
        dl = jnp.sum(gs[hs, :].astype(f32) * mt[hs, :], axis=0, keepdims=True)
        for c in range(T // CR):
            cs = slice(c * CR, (c + 1) * CR)
            ds[h, cs, :] = (et[h, cs, :].astype(f32) * (dot(v[cs, :], gm) - dl)).astype(bf16)
        a = dot(et[h], gm.T)
        b = dot(ds[h], jnp.where(rid == h, q, jnp.zeros_like(q)).T)
        gv = a if gv is None else gv + a
        gk = b if gk is None else gk + b
        gq[0, hs, :] = (dot(kt[hs, :], ds[h]) * scale).astype(bf16)
    gq[2] = gv.astype(bf16).T
    gq[1] = gk.astype(bf16).T


def attn_bwd(kv, qkvt, gmt, mixedf, linv, et, p0, cnt, prev):
    _, T, D = kv.shape
    HD = D // HEADS
    PW = 2 * HD
    NP = D // PW
    prev = list(prev)
    pr = pl.BlockSpec((PW, T), lambda p: (p0 + p, 0))
    of = lambda j: pl.BlockSpec((None, PW, T), lambda p: (j, p0 + p, 0))
    return pl.pallas_call(
        functools.partial(attn_bwd_body, HD, 1.0 / math.sqrt(HD), min(256, T)),
        grid=(cnt,),
        scratch_shapes=[pltpu.VMEM((2, T, T), bf16)],
        in_specs=[pl.BlockSpec((None, T, PW), lambda p: (1, 0, p0 + p)), of(1), of(0), pr, pr, pl.BlockSpec((None, 8, T), lambda p: (p0 + p, 0, 0)), pl.BlockSpec((2, T, T), lambda p: (p0 + p, 0, 0))] + [ANY] * len(prev),
        out_specs=pl.BlockSpec((3, PW, T), lambda p: (0, p0 + p, 0)),
        out_shape=S((3, D, T), bf16),
        input_output_aliases={7: 0} if prev else {},
        compiler_params=cp(56), name="attn_bwd", cost_estimate=cost(cnt * 2 * 16 * T * T * 128, cnt * 2 * T * T * 2),
    )(kv, qkvt, qkvt, gmt, mixedf, linv, et, *prev)


def wqkv_body(n, me, xht, g, keep, send, res, vr, sems):
    j = pl.program_id(0)
    D = g.shape[0]
    r = D // n
    i0 = me[0]
    y = dot_t(xht[...], g[...]).astype(bf16)
    res[j] = y[:D]
    vr[...] = jnp.where(lax.broadcasted_iota(jnp.int32, vr.shape, 0) == j, y[D:], jnp.where(j == 0, jnp.zeros_like(y[D:]), vr[...]))
    for s in range(n):
        push(i0, n, s, res.at[j, pl.ds(s * r, r)], keep, send, mult(j * r, 16), sems.at[j * n + s])

    @pl.when(j == 2)
    def _():
        for s in range(n):
            push(i0, n, s, vr, keep, send, 3 * r, sems.at[3 * n + s])
        for s in range(n):
            for q in range(3):
                pltpu.make_async_copy(res.at[0, pl.ds(0, r)], keep.at[0, pl.ds(0, r)], sems.at[q * n + s]).wait()
            pltpu.make_async_copy(vr, keep.at[0, pl.ds(0, VROWS)], sems.at[3 * n + s]).wait()


def wqkv(me, xht, g, n):
    _, D, T = g.shape
    A = S((n // 2, 3 * (D // n) + VROWS, D), bf16)
    return pl.pallas_call(
        functools.partial(wqkv_body, n),
        grid_spec=pltpu.PrefetchScalarGridSpec(
            num_scalar_prefetch=1, grid=(3,),
            in_specs=[pl.BlockSpec((D + 16, T), lambda j, m: (0, 0)), pl.BlockSpec((None, D, T), lambda j, m: (j, 0, 0))],
            out_specs=[ANY] * 2,
            scratch_shapes=[pltpu.VMEM((3, D, D), bf16), pltpu.VMEM((VROWS, D), bf16), pltpu.SemaphoreType.DMA((4 * n,))]),
        out_shape=[A, A],
        compiler_params=cp(), name="wqkv", cost_estimate=cost(6 * T * D * D, 10 * T * D),
    )(me, xht, g)


def back_body(tok, step, vec, g, gx1, *refs):
    ws, tg = refs[:-1], refs[-1]
    D = tok.shape[1]
    gw = D // GROUPS
    x = tok[...].astype(f32) + step[...].astype(f32)
    nx, rr = norm(x)
    gt = sum(dot(w[:, j * gw : (j + 1) * gw], g[j, q * gw : (q + 1) * gw, :]) for q, w in enumerate(ws) for j in range(3))
    gn = gt.T * row(vec[...], 0)
    tg[...] = gx1[...].astype(f32) + rr * (gn - jnp.mean(gn, axis=-1, keepdims=True) - nx * jnp.mean(gn * nx, axis=-1, keepdims=True))


def back(tok, step, vec, ws, g, gx1, bm=512):
    T, D = tok.shape
    full = lambda a: pl.BlockSpec(a.shape, lambda i: (0,) * a.ndim)
    rows = pl.BlockSpec((bm, D), lambda i: (i, 0))
    return pl.pallas_call(
        back_body, grid=(T // bm,),
        in_specs=[rows, full(step), full(vec), pl.BlockSpec((3, D, bm), lambda i: (0, 0, i)), rows] + [full(w) for w in ws],
        out_specs=rows, out_shape=S((T, D), f32), compiler_params=cp(56), name="back", cost_estimate=cost(6 * T * D * D, 14 * T * D),
    )(tok, step, vec, g, gx1, *ws)


def shards(tokens, step_embed, lengths, cotangent, ln1_gain, ln1_bias, qkv_weight, q_bias, v_bias, out_weight, out_bias, ln2_gain, ln2_bias, up_weight, up_bias, down_weight, down_bias):
    n = lax.axis_size("shard")
    me = lax.axis_index("shard").astype(jnp.int32)
    mes = me[None]
    tok, cot, step = tokens[0], cotangent[0], step_embed
    T, D = tok.shape
    r = D // n
    FF = up_bias.shape[0] * n
    nc = FF // D
    rf = FF // n
    packs = pack_first(mes, qkv_weight, [ln1_gain, ln1_bias, q_bias, v_bias, out_bias, ln2_gain, ln2_bias, down_bias], up_bias)
    pack2 = pack_rest(out_weight, up_weight, down_weight)
    NP = HEADS // 2
    nx, xht = start(tok, step)
    pieces = gather_direct(packs[0], n, xht, pack2)
    kv, qkvt, w, vec, upb = front(mes, nx, pieces, n, FF)
    et, mixed, mixedt, mixedf, linv = attn_fwd(lengths, kv, qkvt, 0, NP, [])
    pieces2 = gather_direct(after(pack2, xht), n, linv)
    out, gx1, gmt, ka, sa, kb, sb = ffn(lengths, mes, tok, step, vec, upb, cot, mixed, mixedt, pieces2, n)
    bwd = lambda p, c, g, *deps: attn_bwd(kv, qkvt, after(gmt, *deps) if deps else gmt, mixedf, linv, et, p, c, g)
    ga, gb = swap(sa, 1), swap(sb, 1)
    g = bwd(0, 1, [])
    ga, gb, _ = lax.optimization_barrier((ga, gb, g))
    h = n // 4
    lo, hi = slice(0, h), slice(h, None)
    add = lambda a, b, s: add16(a[s], b[s])
    ka, xa, kb, xb = add(ka, ga, lo), add(ka, ga, hi), add(kb, gb, lo), add(kb, gb, hi)
    g = bwd(1, NP - 1, [g], ka, xa, kb, xb)
    m = (n // 2).bit_length() - 1
    ga, gb = swap(xa, 2 << (m - 1)), swap(xb, 2)
    for t in range(1, m):
        dep = g if t == 1 else keep
        ga, gb, _ = lax.optimization_barrier((ga, gb, dep))
        h //= 2
        lo, hi = slice(0, h), slice(h, None)
        ka, xa = add(ka, ga, lo), add(ka, ga, hi)
        kb, xb = add(kb, gb, lo), add(kb, gb, hi)
        ga, gb = swap(xa, 2 << (m - 1 - t)), swap(xb, 2 << t)
        if t == 1:
            keep, send = wqkv(mes, after(xht, ka, xa, kb, xb), g, n)
    got = swap(send, 1)
    p2 = [add16(keep[k], got[k]) for k in range(n // 2)]
    far2 = spread(p2)
    ga, gb, _ = lax.optimization_barrier((ga, gb, keep))
    got = swap(send, 1)
    p2 = [add16(keep[k], got[k]) for k in range(n // 2)]
    far2 = spread(p2)
    own1 = jnp.concatenate([add16(ka, ga)[0], add16(kb, gb)[0]], axis=0)
    m1, o1, x1 = rep_half(own1)
    z1 = add16(m1, after(o1, *p2[1:]))
    tg = back(tok, after(step, z1, *p2[1:]), vec, [w], g, gx1)
    own2 = total(p2[0], [after(a, tg) for a in far2])
    m2, o2, x2 = rep_half(own2)
    steps = rep_steps()
    z2 = None if steps else add16(m2, o2)
    for b in steps:
        z1 = add16(z1, after(rep_perm(z1, b), x2))
        if z2 is None:
            z2 = add16(m2, after(o2, z1))
        pz = rep_perm(z2, b)
        z2 = add16(z2, after(pz, z1))
    o1, o2 = rep_perm(z1, 1), rep_perm(z2, 1)
    ids = jnp.stack([me, (lax.axis_index("rep") % 2).astype(jnp.int32)])
    g_down, g_up, g_out, g_upb, g_ob, g_g2, g_b2, g_db = finish_rest(ids, z1, o1, r, rf, nc, n)
    g_qkv, g_g1, g_b1, g_q, g_v = finish_first(ids, z2, after(o2, g_out), qkv_weight, ln1_gain, ln1_bias)
    flat = lambda a: a.reshape(-1)
    return (out[None], tg[None], flat(g_g1), flat(g_b1), g_qkv, flat(g_q), flat(g_v), g_out, flat(g_ob), flat(g_g2), flat(g_b2), g_up, flat(g_upb), g_down, flat(g_db))


def solution(mesh):
    from jax.sharding import PartitionSpec as P

    in_specs = (
        P(("rep", "shard"), None, None),
        P(("rep", "shard"), None),
        P(("rep", "shard")),
        P(("rep", "shard"), None, None),
        P("shard"),
        P("shard"),
        P("shard", None),
        P("shard"),
        P("shard"),
        P("shard", None),
        P("shard"),
        P("shard"),
        P("shard"),
        P("shard", None),
        P("shard"),
        P("shard", None),
        P("shard"),
    )
    out_specs = (
        P(("rep", "shard"), None, None),
        P(("rep", "shard"), None, None),
        P("shard"),
        P("shard"),
        P("shard", None),
        P("shard"),
        P("shard"),
        P("shard", None),
        P("shard"),
        P("shard"),
        P("shard"),
        P("shard", None),
        P("shard"),
        P("shard", None),
        P("shard"),
    )
    return jax.shard_map(shards, mesh=mesh, in_specs=in_specs, out_specs=out_specs, check_vma=False)
```
